32 devices in a mesh: cand: 8 (over z, y), query: 4 (over x, core).
Axes of the slice: x: 2, y: 2, z: 4, core: 2. Of those that a mesh axis runs over, the one named last changes fastest.
Arguments:
- hidden_in: float32 [2, 4, 8, 512, 768], P(None, 'query', 'cand'), may hold values from -6 to 6
- out_cotangent: float32 [2, 4, 8, 512, 768], P(None, 'query', 'cand'), may hold values from -6 to 6
- lengths: int32 [2, 4, 8], P(None, 'query', 'cand'), may hold values from 128 to 512, as said below
- labels: int32 [2, 4], P(None, 'query'), may hold values from 0 to 7
- buckets: int32 [1023], replicated, may hold values from 0 to 255
- w_qkv: float32 [768, 2304], P('query', 'cand'), may hold values from -0.21875 to 0.21875
- w_out: float32 [768, 768], P('query', 'cand'), may hold values from -2.5 to 2.5
- w_up: float32 [768, 3072], P('query', 'cand'), may hold values from -0.21875 to 0.21875
- w_down: float32 [3072, 768], P('query', 'cand'), may hold values from -0.109375 to 0.109375
- bias_q: float32 [768], P('query'), may hold values from -3 to 3
- bias_v: float32 [768], P('query'), may hold values from -3 to 3
- bias_out: float32 [768], P('query'), may hold values from -3 to 3
- norm1_gain: float32 [768], P('query'), may hold values from 0.5 to 1.5
- norm1_bias: float32 [768], P('query'), may hold values from -3 to 3
- bias_up: float32 [3072], P('query'), may hold values from -3 to 3
- bias_down: float32 [768], P('query'), may hold values from -3 to 3
- norm2_gain: float32 [768], P('query'), may hold values from 0.5 to 1.5
- score_vector: float32 [768], P('query'), may hold values from -0.4 to 0.4
- rel_table: float32 [256, 12], P('query'), may hold values from -5 to 5
Outputs:
- layer_out: float32 [2, 4, 8, 512, 768], P(None, 'query', 'cand')
- input_grad: float32 [2, 4, 8, 512, 768], P(None, 'query', 'cand')
- grad_w_qkv: float32 [768, 2304], P('query', 'cand')
- grad_w_out: float32 [768, 768], P('query', 'cand')
- grad_w_up: float32 [768, 3072], P('query', 'cand')
- grad_w_down: float32 [3072, 768], P('query', 'cand')
- grad_bias_q: float32 [768], P('query')
- grad_bias_v: float32 [768], P('query')
- grad_bias_out: float32 [768], P('query')
- grad_norm1_gain: float32 [768], P('query')
- grad_norm1_bias: float32 [768], P('query')
- grad_bias_up: float32 [3072], P('query')
- grad_bias_down: float32 [768], P('query')
- grad_norm2_gain: float32 [768], P('query')
- grad_score_vector: float32 [768], P('query')
- grad_rel_table: float32 [256, 12], P('query')
- loss: float32 [], replicated
The draws below stay inside these ranges and needn't reach their ends.
Inputs may be any that keep to these rules, and one draw needn't show every extreme that they name: `lengths`: some sequence has all 512 tokens and some has 128.
All inputs are finite; a program needn't handle non-finite values.
Results may differ from the reference program's by a relative error of at most 0.013.
The reference program's roundings to bfloat16 on the way count: a program that leaves them out, or rounds other values in their place, can miss the bound.
Values may be sent and summed in bfloat16 or wider, within the bound.
A program may use at most 384 MiB of HBM per device.

```python
import math
import jax
import jax.numpy as jnp
from jax import lax

D = 768
HEADS = 12
HEAD = 64
FF = 3072
BUCKETS = 256
SEQ = 512
MB = 2
QUERIES = 4
CANDS = 8


def draw_lengths(key, part):
    drawn = jax.random.randint(key, (MB, QUERIES, CANDS), SEQ // 4, SEQ + 1, dtype=jnp.int32)
    return drawn.at[0, 0, 0].set(SEQ).at[0, 0, 1].set(SEQ // 4)


def with_ends(array, own_key, smallest, top_value):
    longest = array.shape.index(max(array.shape))
    spots = []
    for shift in (0, 1):
        where = [jax.random.randint(jax.random.fold_in(own_key, axis), (), 0, length) for axis, length in enumerate(array.shape)]
        where[longest] = (where[longest] + shift) % array.shape[longest]
        spots.append(tuple(where))
    return array.at[spots[0]].set(smallest).at[spots[1]].set(top_value)


def levels(own_key, dims, shards, least, top_value):
    gain = 1.0
    for dim, blocks in shards:
        steps = jax.random.uniform(jax.random.fold_in(jax.random.fold_in(own_key, 6), dim), (blocks,), jnp.float32, least / len(shards), top_value / len(shards))
        gain = gain * jnp.repeat(jnp.exp(steps), dims[dim] // blocks).reshape((-1,) + (1,) * (len(dims) - 1 - dim))
    return gain


def noise(key, shape, deviation, most, split=(), held_as=jnp.bfloat16):
    values = jax.random.normal(key, shape, jnp.float32) * deviation
    if len(split) > 0:
        values = levels(key, shape, split, -0.22, 0.18) * values
    return jnp.clip(values, min=-most, max=most).astype(held_as)


def setup_inputs(seed: int = 0) -> dict:
    seeds = jax.random.split(jax.random.key(seed), 20)
    return {
        "hidden_in": noise(seeds[0], (MB, QUERIES, CANDS, SEQ, D), 1.0, 6.0, ((1, 4), (2, 8)), jnp.float32),
        "out_cotangent": noise(seeds[1], (MB, QUERIES, CANDS, SEQ, D), 1.0, 6.0, ((1, 4), (2, 8)), jnp.float32),
        "lengths": draw_lengths(jax.random.fold_in(seeds[19], 71), 0),
        "labels": with_ends(jax.random.randint(seeds[3], (MB, QUERIES), 0, CANDS), jax.random.fold_in(seeds[3], 1), 0, CANDS - 1).astype(jnp.int32),
        "buckets": with_ends(jax.random.randint(seeds[4], (2 * SEQ - 1,), 0, BUCKETS), jax.random.fold_in(seeds[4], 1), 0, BUCKETS - 1).astype(jnp.int32),
        "w_qkv": noise(seeds[5], (D, 3 * D), D ** -0.5, 0.21875, ((0, 4), (1, 8)), jnp.float32),
        "w_out": noise(seeds[6], (D, D), (D * 4 // SEQ) ** -0.5, 2.5, ((0, 4), (1, 8)), jnp.float32),
        "w_up": noise(seeds[7], (D, FF), D ** -0.5, 0.21875, ((0, 4), (1, 8)), jnp.float32),
        "w_down": noise(seeds[8], (FF, D), FF ** -0.5, 0.109375, ((0, 4), (1, 8)), jnp.float32),
        "bias_q": noise(seeds[9], (D,), 0.5, 3.0, ((0, 4),), jnp.float32),
        "bias_v": noise(seeds[10], (D,), 0.5, 3.0, ((0, 4),), jnp.float32),
        "bias_out": noise(seeds[11], (D,), 0.5, 3.0, ((0, 4),), jnp.float32),
        "norm1_gain": jnp.clip(1.0 + 0.1 * jax.random.normal(seeds[12], (D,), jnp.float32), 0.5, 1.5),
        "norm1_bias": noise(seeds[13], (D,), 0.5, 3.0, ((0, 4),), jnp.float32),
        "bias_up": noise(seeds[14], (FF,), 0.5, 3.0, ((0, 4),), jnp.float32),
        "bias_down": noise(seeds[15], (D,), 0.5, 3.0, ((0, 4),), jnp.float32),
        "norm2_gain": jnp.clip(1.0 + 0.1 * jax.random.normal(seeds[16], (D,), jnp.float32), 0.5, 1.5),
        "score_vector": noise(seeds[17], (D,), 0.07, 0.4, ((0, 4),), jnp.float32),
        "rel_table": noise(seeds[18], (BUCKETS, HEADS), 1.0, 5.0, ((0, 4),), jnp.float32),
    }


NORM_EPSILON = 1e-05
MASK_FILL = -1e+30

@jax.custom_vjp
def low(v):
    return lax.optimization_barrier(v.astype(jnp.bfloat16)).astype(jnp.float32)

@jax.custom_vjp
def low_back(v):
    return v

def low_keep(v):
    return (low(v), None)

def low_pass(kept, grad):
    return (grad,)

def back_keep(v):
    return (v, None)

def back_low(kept, grad):
    return (low(grad),)
low.defvjp(low_keep, low_pass)
low_back.defvjp(back_keep, back_low)

def layer_norm(values, gain_vector, shift_vector):
    row_mean = lax.optimization_barrier(jnp.mean(values, axis=-1, keepdims=True))
    centered = values - row_mean
    variance = lax.optimization_barrier(jnp.mean(centered * centered, axis=-1, keepdims=True))
    return centered * lax.rsqrt(variance + NORM_EPSILON) * gain_vector + shift_vector

def expand_bias(relative):
    seq_len = (relative.shape[0] + 1) // 2
    head_count = relative.shape[1]
    per_head = jnp.transpose(relative, (1, 0))
    padded = jnp.concatenate([per_head, jnp.zeros((head_count, 1), per_head.dtype)], axis=1)
    repeated = jnp.broadcast_to(padded[:, None, :], (head_count, seq_len, 2 * seq_len)).reshape(head_count, 2 * seq_len * seq_len)
    skewed = repeated[:, seq_len - 1:seq_len - 1 + seq_len * (2 * seq_len - 1)].reshape(head_count, seq_len, 2 * seq_len - 1)
    return skewed[:, :, :seq_len]

def exact_gelu(values):
    return jax.nn.gelu(values, approximate=False)

def split_heads(matrix):
    return jnp.transpose(matrix.reshape(matrix.shape[0], HEADS, HEAD), (1, 0, 2))

def one_sequence(matrices, vectors, position_bias, hidden, length):
    highest = lax.Precision.HIGHEST
    mixed_qkv, mixed_out, mixed_up, mixed_down = matrices
    bias_q, bias_v, bias_out, gain_one, shift_one, bias_up, bias_down, gain_two, score_vector = vectors
    seq_len, model_width = hidden.shape
    hidden_low = low(hidden)
    projected = jnp.dot(hidden_low, mixed_qkv, precision=highest)
    queries = low(low_back(projected[:, :model_width] + bias_q))
    key_rows = low(low_back(projected[:, model_width:2 * model_width]))
    value_rows = low(low_back(projected[:, 2 * model_width:] + bias_v))
    scale_factor = HEAD ** (-0.5)
    scores = jnp.einsum('hid,hjd->hij', split_heads(queries), split_heads(key_rows), precision=highest)
    scores = low_back(scores * scale_factor + position_bias)
    valid_keys = jnp.arange(seq_len, dtype=jnp.int32) < length
    scores = jnp.where(valid_keys[None, None, :], scores, MASK_FILL)
    probs_low = low(jax.nn.softmax(scores, axis=-1))
    context = jnp.einsum('hij,hjd->hid', probs_low, split_heads(value_rows), precision=highest)
    context = low(low_back(jnp.transpose(context, (1, 0, 2)).reshape(seq_len, model_width)))
    attended = low_back(jnp.dot(context, mixed_out, precision=highest) + bias_out)
    first_norm = layer_norm(hidden + attended, gain_one, shift_one)
    upward = low_back(jnp.dot(low(first_norm), mixed_up, precision=highest) + bias_up)
    activated = low(exact_gelu(upward))
    downward = low_back(jnp.dot(activated, mixed_down, precision=highest) + bias_down)
    output = layer_norm(first_norm + downward, gain_two, 0.0)
    return (output, jnp.dot(output[0], score_vector, precision=highest))

def reference(hidden_in, out_cotangent, lengths, labels, buckets, w_qkv, w_out, w_up, w_down, bias_q, bias_v, bias_out, norm1_gain, norm1_bias, bias_up, bias_down, norm2_gain, score_vector, rel_table):
    highest = lax.Precision.HIGHEST
    sequence_count = MB * QUERIES * CANDS
    group_size = math.gcd(sequence_count, max(1, 4096 // SEQ))
    hidden_groups = hidden_in.reshape(sequence_count // group_size, group_size, SEQ, D)
    cot_groups = out_cotangent.reshape(sequence_count // group_size, group_size, SEQ, D)
    length_groups = lengths.reshape(sequence_count // group_size, group_size)
    params = (w_qkv, w_out, w_up, w_down, bias_q, bias_v, bias_out, norm1_gain, norm1_bias, bias_up, bias_down, norm2_gain, score_vector, rel_table)

    def objective(params, hidden_all):
        matrices = (low(params[0]), low(params[1]), low(params[2]), low(params[3]))
        vectors = params[4:13]
        bucket_hot = jax.nn.one_hot(buckets, BUCKETS, dtype=jnp.float32)
        relative = jnp.dot(bucket_hot, params[13], precision=highest)
        position_bias = expand_bias(relative)

        def group_step(running, inputs_now):
            hidden_group, cot_group, length_group = inputs_now
            outputs, scores = jax.vmap(lambda hidden, length: one_sequence(matrices, vectors, position_bias, hidden, length))(hidden_group, length_group)
            return (running + jnp.sum(cot_group * outputs), (outputs, scores))
        inner_sum, (layer_outputs, scores) = lax.scan(jax.checkpoint(group_step), jnp.float32(0.0), (hidden_all, cot_groups, length_groups))
        scores = scores.reshape(MB, QUERIES, CANDS)
        log_sums = jax.nn.logsumexp(scores, axis=2)
        picked = lax.optimization_barrier(jnp.sum(jnp.where(jnp.arange(CANDS, dtype=jnp.int32)[None, None, :] == labels[:, :, None], scores, 0.0), axis=2))
        loss_value = jnp.sum(log_sums - picked) / QUERIES
        return (loss_value + inner_sum, (layer_outputs, loss_value))
    objective_value, pullback, (layer_outputs, loss_value) = jax.vjp(objective, params, hidden_groups, has_aux=True)
    param_grads, input_grads = pullback(jnp.ones_like(objective_value))
    return (layer_outputs.reshape(hidden_in.shape), input_grads.reshape(hidden_in.shape), param_grads[0], param_grads[1], param_grads[2], param_grads[3], param_grads[4], param_grads[5], param_grads[6], param_grads[7], param_grads[8], param_grads[9], param_grads[10], param_grads[11], param_grads[12], param_grads[13], loss_value)
```

```python
import functools

import jax
import jax.numpy as jnp
from jax import lax
from jax.experimental import pallas as pl
from jax.experimental.pallas import tpu as pltpu
from jax.sharding import PartitionSpec as P

F32 = jnp.float32
BF = jnp.bfloat16
NT = (((1,), (1,)), ((), ()))
NN = (((1,), (0,)), ((), ()))
TN = (((0,), (0,)), ((), ()))
VM = pl.BlockSpec(memory_space=pltpu.VMEM)
SM = pl.BlockSpec(memory_space=pltpu.SMEM)
ANY = pl.BlockSpec(memory_space=pl.ANY)
MESH = pl.DeviceIdType.MESH
EPS = 1e-5
FC = 512
HEADS = 12
PIECES = ["qa", "qb", "o", "u", "d"]
ORDER = {"qa": "x", "qb": "y", "o": "x", "u": "x", "d": "y"}
SHP = {"qa": (48, 384), "qb": (96, 384), "o": (48, 384), "u": (192, 384), "d": (96, 768)}
NB = 4 * len(PIECES)

def dg(a,b,d,prec=None): return lax.dot_general(a,b,d,preferred_element_type=F32,precision=prec)


def qkv_proj(x_ref, w_ref, bias_ref, xlow_ref, qkv_ref):
    S=x_ref.shape[1];
    for m in range(2):
        xlow_ref[m*S:(m+1)*S,:]=x_ref[m].astype(BF)
    def body(n,_):
        o=pl.multiple_of(n*256,256)
        y=dg(xlow_ref[...], w_ref[pl.ds(o,256),:], NT)
        y=(y+bias_ref[:,pl.ds(o,256)])*jnp.where(o<xlow_ref.shape[1],0.125,1.0)
        qkv_ref[:,pl.ds(o,256)]=y.astype(BF)
        return 0
    lax.fori_loop(0, w_ref.shape[0]//256, body, 0)


def rel_rows(tableT_ref, bk_ref, rel_ref):
    nb=tableT_ref.shape[1]; n=bk_ref.shape[1]
    hot=(lax.broadcasted_iota(jnp.int32,(nb,n),0)==bk_ref[...]).astype(F32)
    rel_ref[...]=dg(tableT_ref[...], hot, NN, lax.Precision.HIGHEST)


def bias_expand(row,S):
    R=pltpu.roll(jnp.broadcast_to(row,(128,2*S)), 2*S-127, 1, stride=1, stride_axis=0)
    nu=S//128
    return jnp.concatenate([R[:,128*(nu-1-u):128*(nu-1-u)+S] for u in range(nu)],axis=0)


def diag_sum(t,S):
    nu=S//128
    y=None
    for u in range(nu):
        a=128*(nu-1-u); parts=[]
        if a: parts.append(jnp.zeros((128,a),F32))
        parts.append(t[128*u:128*(u+1),:])
        if 2*S-a-S: parts.append(jnp.zeros((128,2*S-a-S),F32))
        v=jnp.concatenate(parts,axis=1) if len(parts)>1 else parts[0]
        y=v if y is None else y+v
    z=None
    for w in range(16):
        g=y[8*w:8*w+8,:]
        sh=120-8*w
        g=pltpu.roll(g,sh,1) if sh else g
        z=g if z is None else z+g
    out=None
    for b in range(8):
        g=z[b:b+1,:]
        g=pltpu.roll(g,7-b,1) if b<7 else g
        out=g if out is None else out+g
    return out


def attn_fwd(len_ref, qkv_ref, rel_ref, ctx_ref, lse_ref, bias_scr, S, D):
    lane=lax.broadcasted_iota(jnp.int32,(1,128),1)
    col=lax.broadcasted_iota(jnp.int32,(1,S),1)
    def body(p,_):
        o=pl.multiple_of(p*128,128)
        for hh in range(2):
            row=rel_ref[pl.ds(p*2+hh,1),:]
            bias_scr[hh]=bias_expand(row,S)
        for m in range(2):
            q=qkv_ref[m*S:(m+1)*S,pl.ds(o,128)]
            k=qkv_ref[m*S:(m+1)*S,pl.ds(D+o,128)]
            v=qkv_ref[m*S:(m+1)*S,pl.ds(2*D+o,128)]
            valid=col<len_ref[m]
            outs=[]
            for hh in range(2):
                mk=(lane//64)==hh
                qm=jnp.where(mk,q,jnp.zeros_like(q))
                s=dg(qm,k,NT)+bias_scr[hh]
                s=jnp.where(valid,s,-1e30)
                mx=jnp.max(s,axis=1,keepdims=True)
                e=jnp.exp(s-mx)
                tot=jnp.sum(e,axis=1,keepdims=True)
                pl_=(e*(1.0/tot)).astype(BF)
                outs.append(dg(pl_,v,NN))
                lse_ref[m,pl.ds(p*2+hh,1),:]=jnp.transpose(mx+jnp.log(tot),(1,0))
            ctx_ref[m*S:(m+1)*S,pl.ds(o,128)]=jnp.where((lane//64)==0,outs[0],outs[1]).astype(BF)
        return 0
    lax.fori_loop(0, D//128, body, 0)


def attn_bwd(len_ref, qkv_ref, dctx_ref, lse_ref, relf_ref, dqkv_ref, drelf_ref, bias_scr, acc_scr, S, D):
    lane=lax.broadcasted_iota(jnp.int32,(1,128),1)
    rowi=lax.broadcasted_iota(jnp.int32,(S,1),0)
    m0=(lane//64)==0
    def body(p,_):
        o=pl.multiple_of(p*128,128)
        for hh in range(2):
            row=relf_ref[pl.ds(p*2+hh,1),:]
            bias_scr[hh]=bias_expand(row,S)
        for m in range(2):
            q=qkv_ref[m*S:(m+1)*S,pl.ds(o,128)]
            k=qkv_ref[m*S:(m+1)*S,pl.ds(D+o,128)]
            v=qkv_ref[m*S:(m+1)*S,pl.ds(2*D+o,128)]
            do=dctx_ref[m*S:(m+1)*S,pl.ds(o,128)]
            valid=rowi<len_ref[m]
            oq=[];ok=[];ov=[]
            for hh in range(2):
                mk=(lane//64)==hh
                km=jnp.where(mk,k,jnp.zeros_like(k)); vm=jnp.where(mk,v,jnp.zeros_like(v))
                sT=dg(km,q,NT)+bias_scr[hh]
                sT=jnp.where(valid,sT,-1e30)
                pT=jnp.exp(sT-lse_ref[m,pl.ds(p*2+hh,1),:])
                dpT=dg(vm,do,NT)
                rd=jnp.sum(dpT*pT,axis=0,keepdims=True)
                ds=(pT*(dpT-rd)).astype(BF)
                ov.append(dg(pT.astype(BF),do,NN))
                ok.append(dg(ds,q,NN))
                oq.append(dg(ds,k,TN))
                if m==0: acc_scr[hh]=ds.astype(F32)
                else: acc_scr[hh]+=ds.astype(F32)
            dqkv_ref[m*S:(m+1)*S,pl.ds(o,128)]=(jnp.where(m0,oq[0],oq[1])*0.125).astype(BF)
            dqkv_ref[m*S:(m+1)*S,pl.ds(D+o,128)]=jnp.where(m0,ok[0],ok[1]).astype(BF)
            dqkv_ref[m*S:(m+1)*S,pl.ds(2*D+o,128)]=jnp.where(m0,ov[0],ov[1]).astype(BF)
        for hh in range(2):
            drelf_ref[pl.ds(p*2+hh,1),:]=diag_sum(acc_scr[hh],S)
        return 0
    lax.fori_loop(0, D//128, body, 0)


def stats(z):
    mu=jnp.mean(z,axis=-1,keepdims=True); c=z-mu
    var=jnp.mean(c*c,axis=-1,keepdims=True)
    r=lax.rsqrt(var+EPS)
    return c*r, r


def fwd_tile(slot, tile, x_ref, ctx_ref, wo_ref, wu_ref, wd_ref, vec_ref, bup_ref, out_ref, nl_scr, act_scr, gp_scr, z1_scr, z2_scr, r_scr, R):
    D=x_ref.shape[2]; FF=wu_ref.shape[1]
    row=pl.multiple_of(tile*R,R)
    ctx=ctx_ref[...].reshape(R,D)
    fs=x_ref[...].reshape(R,D)+(dg(ctx,wo_ref[...],NT)+vec_ref[0:1,:])
    z1,r1=stats(fs)
    z1_scr[slot]=z1
    fn=z1*vec_ref[1:2,:]+vec_ref[2:3,:]
    nl=fn.astype(BF)
    nl_scr[pl.ds(row,R),:]=nl
    def body(f,acc):
        o=pl.multiple_of(f*FC,FC)
        u=dg(nl_scr[pl.ds(row,R),:],wu_ref[:,pl.ds(o,FC)],NN)+bup_ref[:,pl.ds(o,FC)]
        phi=0.5*(1.0+lax.erf(u*(2.0**-0.5)))
        a=(u*phi).astype(BF)
        act_scr[pl.ds(row,R),pl.ds(o,FC)]=a
        gp_scr[slot,:,pl.ds(o,FC)]=phi+u*(jnp.exp(u*u*-0.5)*0.3989422804014327)
        return acc+dg(a,wd_ref[:,pl.ds(o,FC)],NT)
    acc=lax.fori_loop(0,FF//FC,body,fn+vec_ref[3:4,:])
    z2,r2=stats(acc)
    z2_scr[slot]=z2
    r_scr[slot,:,0:1]=r1
    r_scr[slot,:,1:2]=r2
    out_ref[...]=(z2*vec_ref[4:5,:]).reshape(out_ref.shape)


def lnb(u,z,r):
    return r*(u-jnp.mean(u,axis=-1,keepdims=True)-z*jnp.mean(u*z,axis=-1,keepdims=True))


def bwd_tile(slot, tile, ds_ref, cot_ref, wo_ref, wu_ref, wd_ref, vec_ref, dfs_ref, dctx_ref, gv_ref, gbu_ref, dl_scr, ul_scr, al_scr, gp_scr, z1_scr, z2_scr, r_scr, R):
    D=wu_ref.shape[0]; FF=wu_ref.shape[1]; Rh=R//2
    row=pl.multiple_of(tile*R,R)
    r1=r_scr[slot,:,0:1]; r2=r_scr[slot,:,1:2]
    z2=z2_scr[slot]
    do=cot_ref[...].reshape(R,D)
    ri=lax.broadcasted_iota(jnp.int32,(R,1),0)
    coef=jnp.where(ri==0,ds_ref[0:1,0:1],0.0)+jnp.where(ri==Rh,ds_ref[1:2,0:1],0.0)
    do=do+coef*vec_ref[5:6,:]
    gv_ref[4:5,:]+=jnp.sum(do*z2,axis=0,keepdims=True)
    gv_ref[5:6,:]+=jnp.sum(coef*(z2*vec_ref[4:5,:]),axis=0,keepdims=True)
    d2=lnb(do*vec_ref[4:5,:],z2,r2)
    dl=d2.astype(BF)
    dl_scr[pl.ds(row,R),:]=dl
    gv_ref[3:4,:]+=jnp.sum(dl.astype(F32),axis=0,keepdims=True)
    def body(f,acc):
        o=pl.multiple_of(f*FC,FC)
        da=dg(dl_scr[pl.ds(row,R),:],wd_ref[:,pl.ds(o,FC)],NN)
        ul=(da*gp_scr[slot,:,pl.ds(o,FC)]).astype(BF)
        ul_scr[pl.ds(row,R),pl.ds(o,FC)]=ul
        gbu_ref[:,pl.ds(o,FC)]+=jnp.sum(ul.astype(F32),axis=0,keepdims=True)
        return acc+dg(ul,wu_ref[:,pl.ds(o,FC)],NT)
    d1=lax.fori_loop(0,FF//FC,body,d2)
    z1=z1_scr[slot]
    gv_ref[1:2,:]+=jnp.sum(d1*z1,axis=0,keepdims=True)
    gv_ref[2:3,:]+=jnp.sum(d1,axis=0,keepdims=True)
    dfs=lnb(d1*vec_ref[1:2,:],z1,r1)
    dfs_ref[...]=dfs.reshape(dfs_ref.shape)
    al=dfs.astype(BF)
    al_scr[pl.ds(row,R),:]=al
    gv_ref[0:1,:]+=jnp.sum(al.astype(F32),axis=0,keepdims=True)
    dctx_ref[...]=dg(al,wo_ref[...],NN).astype(BF).reshape(dctx_ref.shape)


class Geo:
    def __init__(g, C, Q):
        g.C=C; g.Q=Q; g.nx=Q//2; g.nz=min(4,C); g.ny=C//g.nz
        c=lax.axis_index("cand"); q=lax.axis_index("query")
        g.z=c//g.ny; g.y=lax.rem(c,g.ny); g.x=q//2; g.k=lax.rem(q,2)
    def dev(g,z,y,x,k): return {"cand":z*g.ny+y,"query":x*2+k}


def mo(v,n): return pl.multiple_of(v,n)


def piece_slice(g, n, refs, z,y,x,k):
    wq,wo,wu,wd=refs
    c=z*g.ny+y; q=x*2+k
    if n=="qa": return wq.at[pl.ds(mo(c*288+k*144,16),48),pl.ds(mo(x*384,128),384)]
    if n=="qb": return wq.at[pl.ds(mo(c*288+k*144+48,16),96),pl.ds(mo(x*384,128),384)]
    if n=="o": return wo.at[pl.ds(mo(c*96+k*48,16),48),pl.ds(mo(x*384,128),384)]
    if n=="u": return wu.at[pl.ds(mo(q*192,16),192),pl.ds(mo(c*384,128),384)]
    if n=="d": return wd.at[pl.ds(mo(c*96,16),96),pl.ds(mo(q*768,128),768)]


def barrier(g, peers):
    b=pltpu.get_barrier_semaphore()
    for p in peers: pl.semaphore_signal(b,inc=1,device_id=p,device_id_type=MESH)
    pl.semaphore_wait(b,len(peers))


def kAG(p_ref,u_ref,d_ref,v_ref, wq,wo,wu,wd,vout, h_scr, pr_scr, ssem, rsem, csem, crsem, lsem, psem, vss, vrs, *, C, Q):
    g=Geo(C,Q); refs=(wq,wo,wu,wd)
    z,y,x,k=g.z,g.y,g.x,g.k
    oz=[lax.rem(z+i,g.nz) for i in range(1,g.nz)]
    partner=g.dev(z,y,x,1-k); xn=g.dev(z,y,1-x,k); yn=g.dev(z,1-y,x,k)
    barrier(g,[partner,xn,g.dev(z,y,1-x,1-k),yn]+[g.dev(zz,y,x,k) for zz in oz])
    q=x*2+k
    vcs=[]
    for j in range(1,Q):
        c=pltpu.make_async_remote_copy(v_ref,vout.at[q],vss.at[j-1],vrs.at[j-1],device_id={"query":lax.rem(q+j,Q)},device_id_type=MESH)
        c.start(); vcs.append(c)
    vout[q]=v_ref[...]
    pc=pltpu.make_async_remote_copy(p_ref.at[1-k],pr_scr,psem.at[0],psem.at[1],device_id=partner,device_id_type=MESH)
    pc.start()
    def own_src(n):
        if n=="qa": return h_scr.at[pl.ds(0,48)]
        if n=="qb": return h_scr.at[pl.ds(48,96)]
        if n=="o": return h_scr.at[pl.ds(144,48)]
        if n=="u": return u_ref
        if n=="d": return d_ref
    sends=[]
    def send(n,pi,src,zs,ys,xs,dst,sidx,ridx):
        c=pltpu.make_async_remote_copy(src,piece_slice(g,n,refs,zs,ys,xs,k),ssem.at[pi,sidx],rsem.at[pi,ridx],device_id=dst,device_id_type=MESH)
        c.start(); sends.append(c)
    def ri(zi,dy,dx): return zi*4+dy*2+dx
    def wait(n,pi,zi,dy,dx):
        zs=lax.rem(z+zi,g.nz); ys=jnp.where(dy==1,1-y,y) if dy else y; xs=1-x if dx else x
        s=piece_slice(g,n,refs,zs,ys,xs,k)
        pltpu.make_async_remote_copy(s,s,ssem.at[pi,0],rsem.at[pi,ri(zi,dy,dx)],device_id=partner,device_id_type=MESH).wait_recv()
    locs=[]; cores=[]
    def to_core(n,pi,zi,dy,dx,src=None):
        zs=lax.rem(z+zi,g.nz); ys=1-y if dy else y; xs=1-x if dx else x
        s=piece_slice(g,n,refs,zs,ys,xs,k)
        c=pltpu.make_async_remote_copy(s if src is None else src,s,csem.at[pi,ri(zi,dy,dx)],crsem.at[pi,ri(zi,dy,dx)],device_id=partner,device_id_type=MESH)
        c.start(); cores.append((c,n,zs,ys,xs))
    def own_z(pi,n):
        src=own_src(n)
        for i in range(1,g.nz):
            send(n,pi,src,z,y,x,g.dev(lax.rem(z+i,g.nz),y,x,k),i-1,ri(g.nz-i,0,0))
    def own_xy(pi,n):
        src=own_src(n)
        if ORDER[n]=="x": send(n,pi,src,z,y,x,xn,3,ri(0,0,1))
        else: send(n,pi,src,z,y,x,yn,3,ri(0,1,0))
    def own_second(pi,n):
        src=own_src(n)
        if ORDER[n]=="x": send(n,pi,src,z,y,x,yn,7,ri(0,1,0))
        else: send(n,pi,src,z,y,x,xn,7,ri(0,0,1))
        to_core(n,pi,0,0,0,src)
        c=pltpu.make_async_copy(src,piece_slice(g,n,refs,z,y,x,k),lsem.at[pi]); c.start(); locs.append(c)
    def fwd_z(pi,n,i):
        wait(n,pi,i,0,0)
        zs=lax.rem(z+i,g.nz); s=piece_slice(g,n,refs,zs,y,x,k)
        if ORDER[n]=="x":
            send(n,pi,s,zs,y,x,xn,3+i,ri(i,0,1)); send(n,pi,s,zs,y,x,yn,7+i,ri(i,1,0))
        else:
            send(n,pi,s,zs,y,x,yn,3+i,ri(i,1,0)); send(n,pi,s,zs,y,x,xn,7+i,ri(i,0,1))
        to_core(n,pi,i,0,0)
    def fwd_2(pi,n,i):
        zs=lax.rem(z+i,g.nz)
        if ORDER[n]=="x":
            wait(n,pi,i,0,1)
            s=piece_slice(g,n,refs,zs,y,1-x,k)
            send(n,pi,s,zs,y,1-x,yn,11+i,ri(i,1,1)); to_core(n,pi,i,0,1)
        else:
            wait(n,pi,i,1,0)
            s=piece_slice(g,n,refs,zs,1-y,x,k)
            send(n,pi,s,zs,1-y,x,xn,11+i,ri(i,1,1)); to_core(n,pi,i,1,0)
    def fin(pi,n,i):
        if ORDER[n]=="x":
            wait(n,pi,i,1,0); to_core(n,pi,i,1,0)
        else:
            wait(n,pi,i,0,1); to_core(n,pi,i,0,1)
        wait(n,pi,i,1,1); to_core(n,pi,i,1,1)
    P=list(enumerate(PIECES))
    big=[p for p in P if p[1] in "ud"]; small=[p for p in P if p[1] not in ("u","d")]
    for pi,n in big: own_xy(pi,n)
    for pi,n in big: own_z(pi,n)
    pc.wait()
    a=p_ref[k]; b=pr_scr[...]
    @pl.when(k==0)
    def _(): h_scr[...]=jnp.concatenate([a,b],axis=1)
    @pl.when(k==1)
    def _(): h_scr[...]=jnp.concatenate([b,a],axis=1)
    for pi,n in small: own_xy(pi,n)
    for pi,n in small: own_z(pi,n)
    PP=big+small
    for pi,n in PP: own_second(pi,n)
    for i in range(1,g.nz):
        for pi,n in PP: fwd_z(pi,n,i)
    for i in range(g.nz):
        for pi,n in PP: fwd_2(pi,n,i)
    for i in range(g.nz):
        for pi,n in PP: fin(pi,n,i)
    for c in vcs: c.wait()
    for c in locs: c.wait()
    for c in sends: c.wait_send()
    for c,n,zs,ys,xs in cores:
        c.wait_send()
        c.wait_recv()


def addto(dst, a, b, rows, st=48):
    def body(r,_):
        o=pl.multiple_of(r*st,16)
        dst[pl.ds(o,st),:]=(a[pl.ds(o,st),:].astype(F32)+b[pl.ds(o,st),:].astype(F32)).astype(BF)
        return 0
    lax.fori_loop(0,rows//st,body,0)


class RS:
    def __init__(s,g,refs,bufs,sems,esems):
        s.g=g; s.refs=refs; s.bufs=bufs; s.ss,s.rs=sems; s.es=esems
        s.pend=[]
        z,y,x,k=g.z,g.y,g.x,g.k
        s.partner=g.dev(z,y,x,1-k); s.xn=g.dev(z,y,1-x,k); s.yn=g.dev(z,1-y,x,k)
    def peers(s):
        g=s.g
        return [s.partner,s.xn,s.yn]+[g.dev(lax.rem(g.z+i,g.nz),g.y,g.x,g.k) for i in range(1,g.nz)]
    def sl(s,n,zi,dy,dx,k):
        g=s.g
        return piece_slice(g,n,s.refs,lax.rem(g.z+zi,g.nz),(1-g.y) if dy else g.y,(1-g.x) if dx else g.x,k)
    def copy(s,src,dst,n,i,dev):
        pi=PIECES.index(n)
        return pltpu.make_async_remote_copy(src,dst,s.ss.at[pi,i],s.rs.at[pi,i],device_id=dev,device_id_type=MESH)
    def bits(s,n,a,b): return (a,b) if ORDER[n]=="x" else (b,a)
    def n1(s,n): return s.yn if ORDER[n]=="x" else s.xn
    def n2(s,n): return s.xn if ORDER[n]=="x" else s.yn
    def c0(s,n,zi,a,b,k):
        dy,dx=s.bits(n,a,b); rc=s.bufs[n][0]
        return s.copy(s.sl(n,zi,dy,dx,k),rc.at[zi,a,b],n,zi*4+a*2+b,s.partner)
    def st0(s,n,zi,a,b):
        c=s.c0(n,zi,a,b,1-s.g.k); c.start(); s.pend.append(c)
    def add0(s,n,zi,a,b):
        dy,dx=s.bits(n,a,b); rc=s.bufs[n][0]
        s.c0(n,zi,a,b,1-s.g.k).wait_recv()
        addto(rc.at[zi,a,b],rc.at[zi,a,b],s.sl(n,zi,dy,dx,s.g.k),SHP[n][0])
    def c1(s,n,zi,b): return s.copy(s.bufs[n][0].at[zi,1,b],s.bufs[n][1].at[zi,b],n,16+zi*2+b,s.n1(n))
    def st1(s,n,zi,b):
        s.add0(n,zi,1,b); c=s.c1(n,zi,b); c.start(); s.pend.append(c)
    def add1(s,n,zi,b):
        s.add0(n,zi,0,b)
        s.c1(n,zi,b).wait_recv()
        r1=s.bufs[n][1].at[zi,b]
        addto(r1,r1,s.bufs[n][0].at[zi,0,b],SHP[n][0])
    def c2(s,n,zi): return s.copy(s.bufs[n][1].at[zi,1],s.bufs[n][2].at[zi],n,24+zi,s.n2(n))
    def st2(s,n,zi):
        s.add1(n,zi,1); c=s.c2(n,zi); c.start(); s.pend.append(c)
    def add2(s,n,zi):
        s.add1(n,zi,0)
        s.c2(n,zi).wait_recv()
        r2=s.bufs[n][2].at[zi]
        addto(r2,r2,s.bufs[n][1].at[zi,0],SHP[n][0])
    def c3(s,n,zi):
        g=s.g
        return s.copy(s.bufs[n][2].at[zi],s.bufs[n][3].at[zi-1],n,27+zi,g.dev(lax.rem(g.z+zi,g.nz),g.y,g.x,g.k))
    def st3(s,n,zi):
        s.add2(n,zi); c=s.c3(n,zi); c.start(); s.pend.append(c)
    def fin(s,n,dst):
        s.add2(n,0)
        for zi in range(1,s.g.nz): s.c3(n,zi).wait_recv()
        r2=s.bufs[n][2]; r3=s.bufs[n][3]; st=48
        def body(r,_):
            o=pl.multiple_of(r*st,16)
            t=r2[0,pl.ds(o,st),:].astype(F32)
            for j in range(s.g.nz-1): t=t+r3[j,pl.ds(o,st),:].astype(F32)
            dst[pl.ds(o,st),:]=t
            return 0
        lax.fori_loop(0,SHP[n][0]//st,body,0)
    def drain(s):
        for c in s.pend: c.wait_send()


def rs_bufs(nz=4):
    out=[]
    for n in PIECES:
        r,l=SHP[n]
        out+=[pltpu.VMEM((nz,2,2,r,l),BF),pltpu.VMEM((nz,2,r,l),BF),pltpu.VMEM((nz,r,l),BF),pltpu.VMEM((nz-1,r,l),BF)]
    return out


def kRS(gq,go,gu,gd,v_ref,p_out,u_out,d_out,v_out,*scr,C,Q):
    g=Geo(C,Q)
    bufs={n:scr[4*i:4*i+4] for i,n in enumerate(PIECES)}
    h_scr,e_snd,e_rcv,va,vs,vb,ss,rs,es,qs,qr,cs,cr=scr[NB:]
    R=RS(g,(gq,go,gu,gd),bufs,(ss,rs),es)
    c_=lax.axis_index("cand"); q_=lax.axis_index("query")
    barrier(g,[{"query":lax.rem(q_+j,Q)} for j in range(1,Q)]+[{"cand":lax.rem(c_+j,C)} for j in range(1,C)])
    vq=[]
    for j in range(1,Q):
        qq=lax.rem(q_+j,Q)
        c=pltpu.make_async_remote_copy(v_ref.at[qq],va.at[q_],qs.at[j-1],qr.at[j-1],device_id={"query":qq},device_id_type=MESH)
        c.start(); vq.append(c)
    va[q_]=v_ref[q_]
    PP=["u","d","o","qa","qb"]
    ZZ=[2,1,3,0]
    for n in PP:
        for zi in ZZ:
            for b in (1,0): R.st0(n,zi,1,b)
        for zi in ZZ:
            for b in (1,0): R.st0(n,zi,0,b)
    for c in vq: c.wait()
    t=va[0]
    for j in range(1,Q): t=t+va[j]
    vs[...]=t
    vb[c_]=t
    vc=[]
    for j in range(1,C):
        c=pltpu.make_async_remote_copy(vs,vb.at[c_],cs.at[j-1],cr.at[j-1],device_id={"cand":lax.rem(c_+j,C)},device_id_type=MESH)
        c.start(); vc.append(c)
    for zi in ZZ:
        for b in (1,0):
            for n in PP: R.st1(n,zi,b)
    for zi in ZZ:
        for n in PP: R.st2(n,zi)
    for zi in ZZ[:-1]:
        for n in PP: R.st3(n,zi)
    R.fin("u",u_out); R.fin("d",d_out)
    R.fin("qa",h_scr.at[pl.ds(0,48)]); R.fin("qb",h_scr.at[pl.ds(48,96)]); R.fin("o",h_scr.at[pl.ds(144,48)])
    k=g.k
    lo=h_scr[:,0:192]; hi=h_scr[:,192:384]
    e_snd[...]=jnp.where(k==0,hi,lo)
    c=pltpu.make_async_remote_copy(e_snd,e_rcv,es.at[0],es.at[1],device_id=R.partner,device_id_type=MESH)
    c.start()
    own=jnp.where(k==0,lo,hi)
    p_out[k]=own
    c.wait()
    p_out[1-k]=e_rcv[...]
    for c in vc: c.wait()
    t=vb[0]
    for j in range(1,C): t=t+vb[j]
    v_out[...]=t
    R.drain()


def attn_fwd_kernel(len_ref, x_ref, w_ref, bias_ref, tab_ref, bk_ref, xlow_ref, qkv_ref, ctx_ref, lse_ref, rel_ref, bias_scr):
    S, D = x_ref.shape[1:]
    qkv_proj(x_ref, w_ref, bias_ref, xlow_ref, qkv_ref)
    rel_rows(tab_ref, bk_ref, rel_ref)
    attn_fwd(len_ref, qkv_ref, rel_ref, ctx_ref, lse_ref, bias_scr, S, D)


def ffn_kernel(lab_ref, x_ref, ctx_ref, cot_ref, wo_ref, wu_ref, wd_ref, vec_ref, bup_ref,
               out_ref, dfs_ref, dctx_ref, gv_ref, gbu_ref, go_ref, gu_ref, gd_ref, loss_ref,
               cs_scr, nl_scr, dl_scr, al_scr, act_scr, ul_scr, gp_scr, z1_scr, z2_scr, r_scr,
               ds_scr, sc_snd, sc_all, sss, ssr, *, T, R, C, Q):
    i = pl.program_id(0)
    D, FF = wu_ref.shape
    cid = lax.axis_index("cand")

    def score_copy(j):
        return pltpu.make_async_remote_copy(sc_snd, sc_all.at[cid], sss.at[j - 1], ssr.at[j - 1], device_id={"cand": lax.rem(cid + j, C)}, device_id_type=MESH)

    @pl.when(i == 0)
    def _():
        b = pltpu.get_barrier_semaphore()
        for j in range(1, C):
            pl.semaphore_signal(b, inc=1, device_id={"cand": lax.rem(cid + j, C)}, device_id_type=MESH)
        pl.semaphore_wait(b, C - 1)
        gv_ref[...] = jnp.zeros_like(gv_ref)
        gbu_ref[...] = jnp.zeros_like(gbu_ref)
        ds_scr[...] = jnp.zeros_like(ds_scr)
        sc_snd[...] = jnp.zeros_like(sc_snd)

    @pl.when(i < T)
    def _():
        cs_scr[pl.ds(pl.multiple_of(i * R, R), R), :] = ctx_ref[...].reshape(R, D)
        fwd_tile(jnp.minimum(i, 1), i, x_ref, ctx_ref, wo_ref, wu_ref, wd_ref, vec_ref, bup_ref, out_ref, nl_scr, act_scr, gp_scr, z1_scr, z2_scr, r_scr, R)

    @pl.when(i == 0)
    def _():
        for m in range(2):
            sc = jnp.sum(out_ref[m, 0:1, :] * vec_ref[5:6, :], axis=1, keepdims=True)
            sc_snd[m:m + 1, :] = jnp.broadcast_to(sc, (1, 128))
        sc_all[cid] = sc_snd[...]
        for j in range(1, C):
            score_copy(j).start()

    @pl.when(i == T)
    def _():
        for j in range(1, C):
            score_copy(j).wait()
        total = jnp.zeros((1, 128), F32)
        own = sc_snd[...]
        for m in range(2):
            rows = [sc_all[j, m:m + 1, :] for j in range(C)]
            peak = functools.reduce(jnp.maximum, rows)
            lse = peak + jnp.log(functools.reduce(lambda a, b: a + b, [jnp.exp(r - peak) for r in rows]))
            lab = lab_ref[m]
            picked = functools.reduce(lambda a, b: a + b, [jnp.where(lab == j, r, 0.0) for j, r in enumerate(rows)])
            total = total + (lse - picked)
            ds_scr[m:m + 1, :] = (jnp.exp(own[m:m + 1, :] - lse) - jnp.where(lab == cid, 1.0, 0.0)) * (1.0 / Q)
        loss_ref[...] = jnp.broadcast_to(jnp.where(cid == 0, total * (1.0 / Q), 0.0), (8, 128))

    @pl.when((i >= 1) & (i <= T))
    def _():
        t = lax.rem(i, T)
        bwd_tile(jnp.minimum(t, 1), t, ds_scr, cot_ref, wo_ref, wu_ref, wd_ref, vec_ref, dfs_ref, dctx_ref, gv_ref, gbu_ref, dl_scr, ul_scr, al_scr, gp_scr, z1_scr, z2_scr, r_scr, R)

    @pl.when(i == T)
    def _():
        def b1(f, _):
            o = pl.multiple_of(f * FC, FC)
            gu_ref[:, pl.ds(o, FC)] = dg(nl_scr[...], ul_scr[:, pl.ds(o, FC)], TN).astype(BF)
            gd_ref[:, pl.ds(o, FC)] = dg(dl_scr[...], act_scr[:, pl.ds(o, FC)], TN).astype(BF)
            return 0
        lax.fori_loop(0, FF // FC, b1, 0)

        def b2(f, _):
            o = pl.multiple_of(f * 256, 256)
            go_ref[:, pl.ds(o, 256)] = dg(al_scr[...], cs_scr[:, pl.ds(o, 256)], TN).astype(BF)
            return 0
        lax.fori_loop(0, D // 256, b2, 0)


def attn_bwd_kernel(len_ref, qkv_ref, dctx_ref, lse_ref, tab_ref, bkf_ref, xlow_ref, w_ref, dfs_ref, gq_ref, gb_ref, gtab_ref, ig_ref, dqkv_ref, relf_ref, drelf_ref, bias_scr, acc_scr):
    S = lse_ref.shape[2]
    D = dctx_ref.shape[1]
    nb, n = tab_ref.shape[1], bkf_ref.shape[1]
    rel_rows(tab_ref, bkf_ref, relf_ref)
    drelf_ref[...] = jnp.zeros_like(drelf_ref)
    attn_bwd(len_ref, qkv_ref, dctx_ref, lse_ref, relf_ref, dqkv_ref, drelf_ref, bias_scr, acc_scr, S, D)
    hot = (lax.broadcasted_iota(jnp.int32, (nb, n), 0) == bkf_ref[...]).astype(F32)
    gtab_ref[...] = dg(hot, drelf_ref[...], NT, lax.Precision.HIGHEST)

    def b1(n, _):
        o = pl.multiple_of(n * 256, 256)
        g = dqkv_ref[:, pl.ds(o, 256)]
        gq_ref[pl.ds(o, 256), :] = dg(g, xlow_ref[...], TN).astype(BF)
        gb_ref[:, pl.ds(o, 256)] = jnp.sum(g.astype(F32), axis=0, keepdims=True)
        return 0
    lax.fori_loop(0, 3 * D // 256, b1, 0)

    def b2(r, _):
        o = pl.multiple_of(r * 256, 256)
        ig_ref[pl.ds(o, 256), :] = dfs_ref[pl.ds(o, 256), :] + dg(dqkv_ref[pl.ds(o, 256), :], w_ref[...], NN)
        return 0
    lax.fori_loop(0, 2 * S // 256, b2, 0)


def sds(shape, dtype=F32):
    return jax.ShapeDtypeStruct(shape, dtype)


def body(hidden_in, out_cotangent, lengths, labels, buckets, w_qkv, w_out, w_up, w_down, bias_q, bias_v, bias_out,
         norm1_gain, norm1_bias, bias_up, bias_down, norm2_gain, score_vector, rel_table):
    Q = lax.axis_size("query")
    C = lax.axis_size("cand")
    micro = hidden_in.shape[0]
    S, D = hidden_in.shape[3:]
    FF = w_up.shape[1] * C
    NBK = rel_table.shape[0] * Q
    dq, fq, bq = D // Q, FF // Q, NBK // Q
    fast = Q == 4 and C == 8 and D == 768 and FF == 3072
    x = hidden_in.reshape(micro, S, D)
    cot = out_cotangent.reshape(micro, S, D)
    lens = lengths.reshape(micro)
    labs = labels.reshape(micro)
    vflat = jnp.concatenate([bias_q, bias_v, bias_out, norm1_gain, norm1_bias, bias_down, norm2_gain, score_vector, bias_up, rel_table.reshape(-1)])
    nv = vflat.shape[0]
    if fast:
        a, b = w_qkv.astype(BF).T, w_out.astype(BF).T
        ha, hb = a.shape[0] // 2, b.shape[0] // 2
        p = jnp.stack([jnp.concatenate([a[i * ha:(i + 1) * ha], b[i * hb:(i + 1) * hb]], 0) for i in range(2)], 0)
        wq, wo, wu, wd, vall = pl.pallas_call(
            functools.partial(kAG, C=C, Q=Q), in_specs=[VM] * 4, out_specs=[ANY] * 4 + [VM],
            out_shape=[sds((3 * D, D), BF), sds((D, D), BF), sds((D, FF), BF), sds((D, FF), BF), sds((Q, nv // 128, 128))],
            scratch_shapes=[pltpu.VMEM((192, 384), BF), pltpu.VMEM((192, 192), BF)] + [pltpu.SemaphoreType.DMA((5, 16))] * 4
            + [pltpu.SemaphoreType.DMA((5,)), pltpu.SemaphoreType.DMA((2,)), pltpu.SemaphoreType.DMA((Q,)), pltpu.SemaphoreType.DMA((Q,))],
            compiler_params=pltpu.CompilerParams(collective_id=0, has_side_effects=True, vmem_limit_bytes=8 * 2**20),
        )(p, w_up.astype(BF), w_down.astype(BF).T, vflat.reshape(nv // 128, 128))
        vall = vall.reshape(Q, nv)
    else:
        def gather(w):
            part = lax.all_gather(w.astype(BF), "query", axis=0, tiled=True)
            return lax.all_gather(part, "cand", axis=1, tiled=True)
        wq, wo, wu, wd = gather(w_qkv).T, gather(w_out).T, gather(w_up), gather(w_down).T
        vall = lax.all_gather(vflat, "query", axis=0, tiled=False)
    vecs = vall[:, :8 * dq].reshape(Q, 8, dq).transpose(1, 0, 2).reshape(8, D)
    bup = vall[:, 8 * dq:8 * dq + fq].reshape(1, FF)
    table = vall[:, 8 * dq + fq:].reshape(NBK, HEADS)
    qkv_bias = jnp.concatenate([vecs[0:1], jnp.zeros((1, D), F32), vecs[1:2]], axis=1)
    vec = jnp.concatenate([vecs[2:], jnp.zeros((2, D), F32)], axis=0)
    tab = jnp.pad(table.T, ((0, 4), (0, 0)))
    nrel = buckets.shape[0]
    bk = jnp.pad(buckets, (0, 1), constant_values=-1)[None, :]
    bkf = jnp.pad(buckets[::-1], (0, 1), constant_values=-1)[None, :]
    NS = micro * S
    xlow, qkv, ctx, lse = pl.pallas_call(
        attn_fwd_kernel, in_specs=[SM] + [VM] * 5, out_specs=[VM] * 4,
        out_shape=[sds((NS, D), BF), sds((NS, 3 * D), BF), sds((NS, D), BF), sds((micro, 16, S))],
        scratch_shapes=[pltpu.VMEM((16, 2 * S), F32), pltpu.VMEM((2, S, S), F32)],
        compiler_params=pltpu.CompilerParams(vmem_limit_bytes=60 * 2**20))(lens, x, wq, qkv_bias, tab, bk)
    R = 256
    Rh, T = R // micro, NS // R
    tb = lambda im: pl.BlockSpec((micro, Rh, D), im)
    fw = lambda i: (0, jnp.minimum(i, T - 1), 0)
    bw = lambda i: (0, lax.rem(jnp.maximum(i, 1), T), 0)
    out, dfs, dctx, gv, gbu, go, gu, gd, lossv = pl.pallas_call(
        functools.partial(ffn_kernel, T=T, R=R, C=C, Q=Q), grid=(T + 1,),
        in_specs=[SM, tb(fw), tb(fw), tb(bw)] + [VM] * 5, out_specs=[tb(fw), tb(bw), tb(bw)] + [VM] * 6,
        out_shape=[sds((micro, S, D)), sds((micro, S, D)), sds((micro, S, D), BF), sds((8, D)), sds((1, FF)),
                   sds((D, D), BF), sds((D, FF), BF), sds((D, FF), BF), sds((8, 128))],
        scratch_shapes=[pltpu.VMEM((NS, D), BF)] * 4 + [pltpu.VMEM((NS, FF), BF)] * 2
        + [pltpu.VMEM((2, R, FF), F32), pltpu.VMEM((2, R, D), F32), pltpu.VMEM((2, R, D), F32), pltpu.VMEM((2, R, 128), F32),
           pltpu.VMEM((8, 128), F32), pltpu.VMEM((8, 128), F32), pltpu.VMEM((C, 8, 128), F32), pltpu.SemaphoreType.DMA((C,)), pltpu.SemaphoreType.DMA((C,))],
        compiler_params=pltpu.CompilerParams(collective_id=1, has_side_effects=True, vmem_limit_bytes=67043328),
    )(labs, x, ctx.reshape(micro, S, D), cot, wo, wu, wd, vec, bup)
    gq, gb, gtab, ig = pl.pallas_call(
        attn_bwd_kernel, in_specs=[SM] + [VM] * 8, out_specs=[VM] * 4,
        out_shape=[sds((3 * D, D), BF), sds((1, 3 * D)), sds((NBK, 16)), sds((NS, D))],
        scratch_shapes=[pltpu.VMEM((NS, 3 * D), BF), pltpu.VMEM((16, 2 * S), F32), pltpu.VMEM((16, 2 * S), F32), pltpu.VMEM((2, S, S), F32), pltpu.VMEM((2, S, S), F32)],
        compiler_params=pltpu.CompilerParams(vmem_limit_bytes=60 * 2**20))(lens, qkv, dctx.reshape(NS, D), lse, tab, bkf, xlow, wq, dfs.reshape(NS, D))
    gvecs = jnp.concatenate([gb[:, :D], gb[:, 2 * D:], gv[:6]], axis=0)
    vg = jnp.concatenate([gvecs.reshape(8, Q, dq).transpose(1, 0, 2).reshape(Q, 8 * dq), gbu.reshape(Q, fq), gtab[:, :HEADS].reshape(Q, bq * HEADS),
                          jnp.broadcast_to(lossv[0:1, 0:1], (Q, 1))], axis=1)
    pad = -vg.shape[1] % 1024
    vg = jnp.pad(vg, ((0, 0), (0, pad)))
    if fast:
        nr = vg.shape[1] // 128
        pg, ug, dng, vs = pl.pallas_call(
            functools.partial(kRS, C=C, Q=Q), in_specs=[VM] * 5, out_specs=[VM] * 4,
            out_shape=[sds((2, 192, 192)), sds((192, 384)), sds((96, 768)), sds((nr, 128))],
            scratch_shapes=rs_bufs() + [pltpu.VMEM((192, 384), F32), pltpu.VMEM((192, 192), F32), pltpu.VMEM((192, 192), F32),
                                        pltpu.VMEM((Q, nr, 128), F32), pltpu.VMEM((nr, 128), F32), pltpu.VMEM((C, nr, 128), F32),
                                        pltpu.SemaphoreType.DMA((5, 31)), pltpu.SemaphoreType.DMA((5, 31)), pltpu.SemaphoreType.DMA((2,))]
            + [pltpu.SemaphoreType.DMA((Q,))] * 2 + [pltpu.SemaphoreType.DMA((C,))] * 2,
            compiler_params=pltpu.CompilerParams(collective_id=2, has_side_effects=True, vmem_limit_bytes=50 * 2**20),
        )(gq, go, gu, gd, vg.reshape(Q, nr, 128))
        g_qkv = jnp.concatenate([pg[0, :ha], pg[1, :ha]], 0).T
        g_out = jnp.concatenate([pg[0, ha:], pg[1, ha:]], 0).T
        g_up, g_down = ug, dng.T
        vs = vs.reshape(-1)
    else:
        def scatter(g):
            rows, cols = g.shape[0] // Q, g.shape[1] // C
            tiles = g.astype(F32).reshape(Q, rows, C, cols).transpose(2, 0, 1, 3).reshape(C * Q, rows, cols)
            return lax.psum_scatter(tiles, ("cand", "query"), scatter_dimension=0, tiled=True)[0]
        g_qkv, g_out, g_up, g_down = scatter(gq.T), scatter(go.T), scatter(gu), scatter(gd.T)
        vs = lax.psum_scatter(lax.psum(vg, "cand"), "query", scatter_dimension=0, tiled=True)[0]
    small = [vs[i * dq:(i + 1) * dq] for i in range(8)]
    g_bup = vs[8 * dq:8 * dq + fq]
    g_tab = vs[8 * dq + fq:8 * dq + fq + bq * HEADS].reshape(bq, HEADS)
    loss = vs[8 * dq + fq + bq * HEADS]
    return (out.reshape(hidden_in.shape), ig.reshape(hidden_in.shape), g_qkv, g_out, g_up, g_down,
            small[0], small[1], small[2], small[3], small[4], g_bup, small[5], small[6], small[7], g_tab, loss)


def solution(mesh):
    seq, w, v = P(None, "query", "cand", None, None), P("query", "cand"), P("query")
    return jax.shard_map(
        body, mesh=mesh,
        in_specs=(seq, seq, P(None, "query", "cand"), P(None, "query"), P(), w, w, w, w) + (v,) * 9 + (P("query", None),),
        out_specs=(seq, seq, w, w, w, w) + (v,) * 9 + (P("query", None), P()),
        check_vma=False)
```

```python
import functools

import jax
import jax.numpy as jnp
from jax import lax
from jax.experimental import pallas as pl
from jax.experimental.pallas import tpu as pltpu
from jax.sharding import PartitionSpec as P

F32 = jnp.float32
BF = jnp.bfloat16
NT = (((1,), (1,)), ((), ()))
NN = (((1,), (0,)), ((), ()))
TN = (((0,), (0,)), ((), ()))
VM = pl.BlockSpec(memory_space=pltpu.VMEM)
SM = pl.BlockSpec(memory_space=pltpu.SMEM)
ANY = pl.BlockSpec(memory_space=pl.ANY)
MESH = pl.DeviceIdType.MESH
EPS = 1e-5
FC = 512
HEADS = 12
PIECES = ["qa", "qb", "o", "u", "d"]
ORDER = {"qa": "x", "qb": "y", "o": "x", "u": "x", "d": "y"}
SHP = {"qa": (48, 384), "qb": (96, 384), "o": (48, 384), "u": (192, 384), "d": (96, 768)}
NB = 4 * len(PIECES)

def dg(a,b,d,prec=None): return lax.dot_general(a,b,d,preferred_element_type=F32,precision=prec)


def qkv_proj(x_ref, w_ref, bias_ref, xlow_ref, qkv_ref):
    S=x_ref.shape[1];
    for m in range(2):
        xlow_ref[m*S:(m+1)*S,:]=x_ref[m].astype(BF)
    def body(n,_):
        o=pl.multiple_of(n*256,256)
        y=dg(xlow_ref[...], w_ref[pl.ds(o,256),:], NT)
        y=(y+bias_ref[:,pl.ds(o,256)])*jnp.where(o<xlow_ref.shape[1],0.125,1.0)
        qkv_ref[:,pl.ds(o,256)]=y.astype(BF)
        return 0
    lax.fori_loop(0, w_ref.shape[0]//256, body, 0)


def rel_rows(tableT_ref, bk_ref, rel_ref):
    nb=tableT_ref.shape[1]; n=bk_ref.shape[1]
    hot=(lax.broadcasted_iota(jnp.int32,(nb,n),0)==bk_ref[...]).astype(F32)
    rel_ref[...]=dg(tableT_ref[...], hot, NN, lax.Precision.HIGHEST)


def bias_expand(row,S):
    R=pltpu.roll(jnp.broadcast_to(row,(128,2*S)), 2*S-127, 1, stride=1, stride_axis=0)
    nu=S//128
    return jnp.concatenate([R[:,128*(nu-1-u):128*(nu-1-u)+S] for u in range(nu)],axis=0)


def diag_sum(t,S):
    nu=S//128
    y=None
    for u in range(nu):
        a=128*(nu-1-u); parts=[]
        if a: parts.append(jnp.zeros((128,a),F32))
        parts.append(t[128*u:128*(u+1),:])
        if 2*S-a-S: parts.append(jnp.zeros((128,2*S-a-S),F32))
        v=jnp.concatenate(parts,axis=1) if len(parts)>1 else parts[0]
        y=v if y is None else y+v
    z=None
    for w in range(16):
        g=y[8*w:8*w+8,:]
        sh=120-8*w
        g=pltpu.roll(g,sh,1) if sh else g
        z=g if z is None else z+g
    out=None
    for b in range(8):
        g=z[b:b+1,:]
        g=pltpu.roll(g,7-b,1) if b<7 else g
        out=g if out is None else out+g
    return out


def attn_fwd(len_ref, qkv_ref, rel_ref, ctx_ref, lse_ref, bias_scr, S, D):
    lane=lax.broadcasted_iota(jnp.int32,(1,128),1)
    col=lax.broadcasted_iota(jnp.int32,(1,S),1)
    def body(p,_):
        o=pl.multiple_of(p*128,128)
        for hh in range(2):
            row=rel_ref[pl.ds(p*2+hh,1),:]
            bias_scr[hh]=bias_expand(row,S)
        for m in range(2):
            q=qkv_ref[m*S:(m+1)*S,pl.ds(o,128)]
            k=qkv_ref[m*S:(m+1)*S,pl.ds(D+o,128)]
            v=qkv_ref[m*S:(m+1)*S,pl.ds(2*D+o,128)]
            valid=col<len_ref[m]
            outs=[]
            for hh in range(2):
                mk=(lane//64)==hh
                qm=jnp.where(mk,q,jnp.zeros_like(q))
                s=dg(qm,k,NT)+bias_scr[hh]
                s=jnp.where(valid,s,-1e30)
                mx=jnp.max(s,axis=1,keepdims=True)
                e=jnp.exp(s-mx)
                tot=jnp.sum(e,axis=1,keepdims=True)
                pl_=(e*(1.0/tot)).astype(BF)
                outs.append(dg(pl_,v,NN))
                lse_ref[m,pl.ds(p*2+hh,1),:]=jnp.transpose(mx+jnp.log(tot),(1,0))
            ctx_ref[m*S:(m+1)*S,pl.ds(o,128)]=jnp.where((lane//64)==0,outs[0],outs[1]).astype(BF)
        return 0
    lax.fori_loop(0, D//128, body, 0)


def attn_bwd(len_ref, qkv_ref, dctx_ref, lse_ref, relf_ref, drelf_ref, bias_scr, acc_scr, S, D, slots):
    lane=lax.broadcasted_iota(jnp.int32,(1,128),1)
    rowi=lax.broadcasted_iota(jnp.int32,(S,1),0)
    m0=(lane//64)==0
    def body(p,_):
        o=pl.multiple_of(p*128,128)
        for hh in range(2):
            row=relf_ref[pl.ds(p*2+hh,1),:]
            bias_scr[hh]=bias_expand(row,S)
        for m in range(2):
            q=qkv_ref[m*S:(m+1)*S,pl.ds(o,128)]
            k=qkv_ref[m*S:(m+1)*S,pl.ds(D+o,128)]
            v=qkv_ref[m*S:(m+1)*S,pl.ds(2*D+o,128)]
            do=dctx_ref[m*S:(m+1)*S,pl.ds(o,128)]
            valid=rowi<len_ref[m]
            oq=[];ok=[];ov=[]
            for hh in range(2):
                mk=(lane//64)==hh
                km=jnp.where(mk,k,jnp.zeros_like(k)); vm=jnp.where(mk,v,jnp.zeros_like(v))
                sT=dg(km,q,NT)+bias_scr[hh]
                sT=jnp.where(valid,sT,-1e30)
                pT=jnp.exp(sT-lse_ref[m,pl.ds(p*2+hh,1),:])
                dpT=dg(vm,do,NT)
                rd=jnp.sum(dpT*pT,axis=0,keepdims=True)
                ds=(pT*(dpT-rd)).astype(BF)
                ov.append(dg(pT.astype(BF),do,NN))
                ok.append(dg(ds,q,NN))
                oq.append(dg(ds,k,TN))
                if m==0: acc_scr[hh]=ds.astype(F32)
                else: acc_scr[hh]+=ds.astype(F32)
            qkv_ref[m*S:(m+1)*S,pl.ds(o,128)]=(jnp.where(m0,oq[0],oq[1])*0.125).astype(BF)
            qkv_ref[m*S:(m+1)*S,pl.ds(D+o,128)]=jnp.where(m0,ok[0],ok[1]).astype(BF)
            qkv_ref[m*S:(m+1)*S,pl.ds(2*D+o,128)]=jnp.where(m0,ov[0],ov[1]).astype(BF)
            for i in range(D//128):
                evs=slots.get((i,m),[])
                if evs:
                    @pl.when(p==i)
                    def _(evs=evs):
                        for e in evs: e()
        for hh in range(2):
            drelf_ref[pl.ds(p*2+hh,1),:]=diag_sum(acc_scr[hh],S)
        return 0
    lax.fori_loop(0, D//128, body, 0)


def stats(z):
    mu=jnp.mean(z,axis=-1,keepdims=True); c=z-mu
    var=jnp.mean(c*c,axis=-1,keepdims=True)
    r=lax.rsqrt(var+EPS)
    return c*r, r


def fwd_tile(slot, x_ref, ctx_ref, wo_ref, wu_ref, wd_ref, vec_ref, bup_ref, out_ref, nl_scr, act_scr, gp_scr, z1_scr, z2_scr, r_scr, R):
    D=x_ref.shape[2]; FF=wu_ref.shape[1]
    ctx=ctx_ref[...].reshape(R,D)
    fs=x_ref[...].reshape(R,D)+(dg(ctx,wo_ref[...],NT)+vec_ref[0:1,:])
    z1,r1=stats(fs)
    z1_scr[slot]=z1
    fn=z1*vec_ref[1:2,:]+vec_ref[2:3,:]
    nl=fn.astype(BF)
    nl_scr[...]=nl.reshape(nl_scr.shape)
    def body(f,acc):
        o=pl.multiple_of(f*FC,FC)
        u=dg(nl_scr[...].reshape(R,D),wu_ref[:,pl.ds(o,FC)],NN)+bup_ref[:,pl.ds(o,FC)]
        phi=0.5*(1.0+lax.erf(u*(2.0**-0.5)))
        a=(u*phi).astype(BF)
        act_scr[:,:,pl.ds(o,FC)]=a.reshape(2,R//2,FC)
        gp_scr[slot,:,pl.ds(o,FC)]=phi+u*(jnp.exp(u*u*-0.5)*0.3989422804014327)
        return acc+dg(a,wd_ref[:,pl.ds(o,FC)],NT)
    acc=lax.fori_loop(0,FF//FC,body,fn+vec_ref[3:4,:])
    z2,r2=stats(acc)
    z2_scr[slot]=z2
    r_scr[slot,:,0:1]=r1
    r_scr[slot,:,1:2]=r2
    out_ref[...]=(z2*vec_ref[4:5,:]).reshape(out_ref.shape)


def lnb(u,z,r):
    return r*(u-jnp.mean(u,axis=-1,keepdims=True)-z*jnp.mean(u*z,axis=-1,keepdims=True))


def bwd_tile(slot, ds_ref, cot_ref, wo_ref, wu_ref, wd_ref, vec_ref, dfs_ref, dctx_ref, gv_ref, gbu_ref, dl_scr, ul_scr, al_scr, gp_scr, z1_scr, z2_scr, r_scr, R):
    D=wu_ref.shape[0]; FF=wu_ref.shape[1]; Rh=R//2
    r1=r_scr[slot,:,0:1]; r2=r_scr[slot,:,1:2]
    z2=z2_scr[slot]
    do=cot_ref[...].reshape(R,D)
    ri=lax.broadcasted_iota(jnp.int32,(R,1),0)
    coef=jnp.where(ri==0,ds_ref[0:1,0:1],0.0)+jnp.where(ri==Rh,ds_ref[1:2,0:1],0.0)
    do=do+coef*vec_ref[5:6,:]
    gv_ref[4:5,:]+=jnp.sum(do*z2,axis=0,keepdims=True)
    gv_ref[5:6,:]+=jnp.sum(coef*(z2*vec_ref[4:5,:]),axis=0,keepdims=True)
    d2=lnb(do*vec_ref[4:5,:],z2,r2)
    dl=d2.astype(BF)
    dl_scr[...]=dl.reshape(dl_scr.shape)
    gv_ref[3:4,:]+=jnp.sum(dl.astype(F32),axis=0,keepdims=True)
    def body(f,acc):
        o=pl.multiple_of(f*FC,FC)
        da=dg(dl_scr[...].reshape(R,D),wd_ref[:,pl.ds(o,FC)],NN)
        ul=(da*gp_scr[slot,:,pl.ds(o,FC)]).astype(BF)
        ul_scr[:,:,pl.ds(o,FC)]=ul.reshape(2,R//2,FC)
        gbu_ref[:,pl.ds(o,FC)]+=jnp.sum(ul.astype(F32),axis=0,keepdims=True)
        return acc+dg(ul,wu_ref[:,pl.ds(o,FC)],NT)
    d1=lax.fori_loop(0,FF//FC,body,d2)
    z1=z1_scr[slot]
    gv_ref[1:2,:]+=jnp.sum(d1*z1,axis=0,keepdims=True)
    gv_ref[2:3,:]+=jnp.sum(d1,axis=0,keepdims=True)
    dfs=lnb(d1*vec_ref[1:2,:],z1,r1)
    dfs_ref[...]=dfs.reshape(dfs_ref.shape)
    al=dfs.astype(BF)
    al_scr[...]=al.reshape(al_scr.shape)
    gv_ref[0:1,:]+=jnp.sum(al.astype(F32),axis=0,keepdims=True)
    dctx_ref[...]=dg(al,wo_ref[...],NN).astype(BF).reshape(dctx_ref.shape)


class Geo:
    def __init__(g, C, Q):
        g.C=C; g.Q=Q; g.nx=Q//2; g.nz=min(4,C); g.ny=C//g.nz
        c=lax.axis_index("cand"); q=lax.axis_index("query")
        g.z=c//g.ny; g.y=lax.rem(c,g.ny); g.x=q//2; g.k=lax.rem(q,2)
    def dev(g,z,y,x,k): return {"cand":z*g.ny+y,"query":x*2+k}


def mo(v,n): return pl.multiple_of(v,n)


def piece_slice(g, n, refs, z,y,x,k):
    wq,wo,wu,wd=refs
    c=z*g.ny+y; q=x*2+k
    if n=="qa": return wq.at[pl.ds(mo(c*288+k*144,16),48),pl.ds(mo(x*384,128),384)]
    if n=="qb": return wq.at[pl.ds(mo(c*288+k*144+48,16),96),pl.ds(mo(x*384,128),384)]
    if n=="o": return wo.at[pl.ds(mo(c*96+k*48,16),48),pl.ds(mo(x*384,128),384)]
    if n=="u": return wu.at[pl.ds(mo(q*192,16),192),pl.ds(mo(c*384,128),384)]
    if n=="d": return wd.at[pl.ds(mo(c*96,16),96),pl.ds(mo(q*768,128),768)]


def barrier(g, peers):
    b=pltpu.get_barrier_semaphore()
    for p in peers: pl.semaphore_signal(b,inc=1,device_id=p,device_id_type=MESH)
    pl.semaphore_wait(b,len(peers))


def kAG(p_ref,u_ref,d_ref,v_ref, wq,wo,wu,wd,vout, h_scr, pr_scr, ssem, rsem, csem, crsem, lsem, psem, vss, vrs, *, C, Q):
    g=Geo(C,Q); refs=(wq,wo,wu,wd)
    z,y,x,k=g.z,g.y,g.x,g.k
    oz=[lax.rem(z+i,g.nz) for i in range(1,g.nz)]
    partner=g.dev(z,y,x,1-k); xn=g.dev(z,y,1-x,k); yn=g.dev(z,1-y,x,k)
    barrier(g,[partner,xn,g.dev(z,y,1-x,1-k),yn]+[g.dev(zz,y,x,k) for zz in oz])
    q=x*2+k
    vcs=[]
    for j in range(1,Q):
        c=pltpu.make_async_remote_copy(v_ref,vout.at[q],vss.at[j-1],vrs.at[j-1],device_id={"query":lax.rem(q+j,Q)},device_id_type=MESH)
        c.start(); vcs.append(c)
    vout[q]=v_ref[...]
    pc=pltpu.make_async_remote_copy(p_ref.at[1-k],pr_scr,psem.at[0],psem.at[1],device_id=partner,device_id_type=MESH)
    pc.start()
    def own_src(n):
        if n=="qa": return h_scr.at[pl.ds(0,48)]
        if n=="qb": return h_scr.at[pl.ds(48,96)]
        if n=="o": return h_scr.at[pl.ds(144,48)]
        if n=="u": return u_ref
        if n=="d": return d_ref
    sends=[]
    def send(n,pi,src,zs,ys,xs,dst,sidx,ridx):
        c=pltpu.make_async_remote_copy(src,piece_slice(g,n,refs,zs,ys,xs,k),ssem.at[pi,sidx],rsem.at[pi,ridx],device_id=dst,device_id_type=MESH)
        c.start(); sends.append(c)
    def ri(zi,dy,dx): return zi*4+dy*2+dx
    def wait(n,pi,zi,dy,dx):
        zs=lax.rem(z+zi,g.nz); ys=jnp.where(dy==1,1-y,y) if dy else y; xs=1-x if dx else x
        s=piece_slice(g,n,refs,zs,ys,xs,k)
        pltpu.make_async_remote_copy(s,s,ssem.at[pi,0],rsem.at[pi,ri(zi,dy,dx)],device_id=partner,device_id_type=MESH).wait_recv()
    locs=[]; cores=[]
    def to_core(n,pi,zi,dy,dx,src=None):
        zs=lax.rem(z+zi,g.nz); ys=1-y if dy else y; xs=1-x if dx else x
        s=piece_slice(g,n,refs,zs,ys,xs,k)
        c=pltpu.make_async_remote_copy(s if src is None else src,s,csem.at[pi,ri(zi,dy,dx)],crsem.at[pi,ri(zi,dy,dx)],device_id=partner,device_id_type=MESH)
        c.start(); cores.append((c,n,zs,ys,xs))
    def own_z(pi,n):
        src=own_src(n)
        for i in range(1,g.nz):
            send(n,pi,src,z,y,x,g.dev(lax.rem(z+i,g.nz),y,x,k),i-1,ri(g.nz-i,0,0))
    def own_xy(pi,n):
        src=own_src(n)
        if ORDER[n]=="x": send(n,pi,src,z,y,x,xn,3,ri(0,0,1))
        else: send(n,pi,src,z,y,x,yn,3,ri(0,1,0))
    def own_second(pi,n):
        src=own_src(n)
        if ORDER[n]=="x": send(n,pi,src,z,y,x,yn,7,ri(0,1,0))
        else: send(n,pi,src,z,y,x,xn,7,ri(0,0,1))
        to_core(n,pi,0,0,0,src)
        c=pltpu.make_async_copy(src,piece_slice(g,n,refs,z,y,x,k),lsem.at[pi]); c.start(); locs.append(c)
    def fwd_z(pi,n,i):
        wait(n,pi,i,0,0)
        zs=lax.rem(z+i,g.nz); s=piece_slice(g,n,refs,zs,y,x,k)
        if ORDER[n]=="x":
            send(n,pi,s,zs,y,x,xn,3+i,ri(i,0,1)); send(n,pi,s,zs,y,x,yn,7+i,ri(i,1,0))
        else:
            send(n,pi,s,zs,y,x,yn,3+i,ri(i,1,0)); send(n,pi,s,zs,y,x,xn,7+i,ri(i,0,1))
        to_core(n,pi,i,0,0)
    def fwd_2(pi,n,i):
        zs=lax.rem(z+i,g.nz)
        if ORDER[n]=="x":
            wait(n,pi,i,0,1)
            s=piece_slice(g,n,refs,zs,y,1-x,k)
            send(n,pi,s,zs,y,1-x,yn,11+i,ri(i,1,1)); to_core(n,pi,i,0,1)
        else:
            wait(n,pi,i,1,0)
            s=piece_slice(g,n,refs,zs,1-y,x,k)
            send(n,pi,s,zs,1-y,x,xn,11+i,ri(i,1,1)); to_core(n,pi,i,1,0)
    def fin(pi,n,i):
        if ORDER[n]=="x":
            wait(n,pi,i,1,0); to_core(n,pi,i,1,0)
        else:
            wait(n,pi,i,0,1); to_core(n,pi,i,0,1)
        wait(n,pi,i,1,1); to_core(n,pi,i,1,1)
    P=list(enumerate(PIECES))
    big=[p for p in P if p[1] in "ud"]; small=[p for p in P if p[1] not in ("u","d")]
    for pi,n in big: own_xy(pi,n)
    for pi,n in big: own_z(pi,n)
    pc.wait()
    a=p_ref[k]; b=pr_scr[...]
    @pl.when(k==0)
    def _(): h_scr[...]=jnp.concatenate([a,b],axis=1)
    @pl.when(k==1)
    def _(): h_scr[...]=jnp.concatenate([b,a],axis=1)
    for pi,n in small: own_xy(pi,n)
    for pi,n in small: own_z(pi,n)
    PP=big+small
    for pi,n in PP: own_second(pi,n)
    for i in range(1,g.nz):
        for pi,n in PP: fwd_z(pi,n,i)
    for i in range(g.nz):
        for pi,n in PP: fwd_2(pi,n,i)
    for i in range(g.nz):
        for pi,n in PP: fin(pi,n,i)
    for c in vcs: c.wait()
    for c in locs: c.wait()
    for c in sends: c.wait_send()
    for c,n,zs,ys,xs in cores:
        c.wait_send()
        c.wait_recv()


def addto(dst, a, b, rows, st=48):
    def body(r,_):
        o=pl.multiple_of(r*st,16)
        dst[pl.ds(o,st),:]=(a[pl.ds(o,st),:].astype(F32)+b[pl.ds(o,st),:].astype(F32)).astype(BF)
        return 0
    lax.fori_loop(0,rows//st,body,0)


class RS:
    def __init__(s,g,refs,bufs,sems,esems):
        s.g=g; s.refs=refs; s.bufs=bufs; s.ss,s.rs=sems; s.es=esems
        s.pend=[]
        z,y,x,k=g.z,g.y,g.x,g.k
        s.partner=g.dev(z,y,x,1-k); s.xn=g.dev(z,y,1-x,k); s.yn=g.dev(z,1-y,x,k)
    def peers(s):
        g=s.g
        return [s.partner,s.xn,s.yn]+[g.dev(jnp.bitwise_xor(g.z,i),g.y,g.x,g.k) for i in range(1,g.nz)]
    def sl(s,n,zi,dy,dx,k):
        g=s.g
        return piece_slice(g,n,s.refs,jnp.bitwise_xor(g.z,zi),(1-g.y) if dy else g.y,(1-g.x) if dx else g.x,k)
    def copy(s,src,dst,n,i,dev):
        pi=PIECES.index(n)
        return pltpu.make_async_remote_copy(src,dst,s.ss.at[pi,i],s.rs.at[pi,i],device_id=dev,device_id_type=MESH)
    def bits(s,n,a,b): return (a,b) if ORDER[n]=="x" else (b,a)
    def n1(s,n): return s.yn if ORDER[n]=="x" else s.xn
    def n2(s,n): return s.xn if ORDER[n]=="x" else s.yn
    def c0(s,n,zi,a,b,k):
        dy,dx=s.bits(n,a,b); rc=s.bufs[n][0]
        return s.copy(s.sl(n,zi,dy,dx,k),rc.at[zi,a,b],n,zi*4+a*2+b,s.partner)
    def st0(s,n,zi,a,b):
        s.c0(n,zi,a,b,1-s.g.k).start(); s.pend.append(lambda: s.c0(n,zi,a,b,1-s.g.k))
    def add0(s,n,zi,a,b):
        dy,dx=s.bits(n,a,b); rc=s.bufs[n][0]
        s.c0(n,zi,a,b,1-s.g.k).wait_recv()
        addto(rc.at[zi,a,b],rc.at[zi,a,b],s.sl(n,zi,dy,dx,s.g.k),SHP[n][0])
    def c1(s,n,zi,b): return s.copy(s.bufs[n][0].at[zi,1,b],s.bufs[n][1].at[zi,b],n,16+zi*2+b,s.n1(n))
    def st1(s,n,zi,b):
        s.add0(n,zi,1,b); s.c1(n,zi,b).start(); s.pend.append(lambda: s.c1(n,zi,b))
    def add1(s,n,zi,b):
        s.add0(n,zi,0,b)
        s.c1(n,zi,b).wait_recv()
        r1=s.bufs[n][1].at[zi,b]
        addto(r1,r1,s.bufs[n][0].at[zi,0,b],SHP[n][0])
    def c2(s,n,zi): return s.copy(s.bufs[n][1].at[zi,1],s.bufs[n][2].at[zi],n,24+zi,s.n2(n))
    def st2(s,n,zi):
        s.add1(n,zi,1); s.c2(n,zi).start(); s.pend.append(lambda: s.c2(n,zi))
    def add2(s,n,zi):
        s.add1(n,zi,0)
        s.c2(n,zi).wait_recv()
        r2=s.bufs[n][2].at[zi]
        addto(r2,r2,s.bufs[n][1].at[zi,0],SHP[n][0])
    def c3(s,n,zi):
        g=s.g
        return s.copy(s.bufs[n][2].at[zi],s.bufs[n][3].at[zi-1],n,27+zi,g.dev(jnp.bitwise_xor(g.z,zi),g.y,g.x,g.k))
    def st3(s,n,zi):
        s.add2(n,zi); s.c3(n,zi).start(); s.pend.append(lambda: s.c3(n,zi))
    def fin(s,n,dst):
        s.add2(n,0)
        for zi in range(1,s.g.nz): s.c3(n,zi).wait_recv()
        r2=s.bufs[n][2]; r3=s.bufs[n][3]; st=48
        def body(r,_):
            o=pl.multiple_of(r*st,16)
            t=r2[0,pl.ds(o,st),:].astype(F32)
            for j in range(s.g.nz-1): t=t+r3[j,pl.ds(o,st),:].astype(F32)
            dst[pl.ds(o,st),:]=t
            return 0
        lax.fori_loop(0,SHP[n][0]//st,body,0)
    def drain(s):
        for c in s.pend: c().wait_send()


def rs_bufs(nz=4):
    out=[]
    for n in PIECES:
        r,l=SHP[n]
        out+=[pltpu.VMEM((nz,2,2,r,l),BF),pltpu.VMEM((nz,2,r,l),BF),pltpu.VMEM((nz,r,l),BF),pltpu.VMEM((nz-1,r,l),BF)]
    return out


def attn_fwd_kernel(len_ref, x_ref, w_ref, bias_ref, tab_ref, bk_ref, xlow_ref, qkv_ref, ctx_ref, lse_ref, rel_ref, bias_scr):
    S, D = x_ref.shape[1:]
    qkv_proj(x_ref, w_ref, bias_ref, xlow_ref, qkv_ref)
    rel_rows(tab_ref, bk_ref, rel_ref)
    attn_fwd(len_ref, qkv_ref, rel_ref, ctx_ref, lse_ref, bias_scr, S, D)


def ffn_kernel(lab_ref, x_ref, ctx_ref, cot_ref, wo_ref, wu_ref, wd_ref, vec_ref, bup_ref,
               out_ref, dfs_ref, dctx_ref, nl_ref, act_ref, dl_ref, al_ref, ul_ref, gv_ref, gbu_ref, loss_ref,
               gp_scr, z1_scr, z2_scr, r_scr,
               ds_scr, sc_snd, sc_all, sss, ssr, *, T, R, C, Q):
    i = pl.program_id(0)
    D, FF = wu_ref.shape
    cid = lax.axis_index("cand")

    def score_copy(j):
        return pltpu.make_async_remote_copy(sc_snd, sc_all.at[cid], sss.at[j - 1], ssr.at[j - 1], device_id={"cand": lax.rem(cid + j, C)}, device_id_type=MESH)

    @pl.when(i == 0)
    def _():
        b = pltpu.get_barrier_semaphore()
        for j in range(1, C):
            pl.semaphore_signal(b, inc=1, device_id={"cand": lax.rem(cid + j, C)}, device_id_type=MESH)
        pl.semaphore_wait(b, C - 1)
        gv_ref[...] = jnp.zeros_like(gv_ref)
        gbu_ref[...] = jnp.zeros_like(gbu_ref)
        ds_scr[...] = jnp.zeros_like(ds_scr)
        sc_snd[...] = jnp.zeros_like(sc_snd)

    @pl.when(i < T)
    def _():
        fwd_tile(jnp.minimum(i, 1), x_ref, ctx_ref, wo_ref, wu_ref, wd_ref, vec_ref, bup_ref, out_ref, nl_ref, act_ref, gp_scr, z1_scr, z2_scr, r_scr, R)

    @pl.when(i == 0)
    def _():
        for m in range(2):
            sc = jnp.sum(out_ref[m, 0:1, :] * vec_ref[5:6, :], axis=1, keepdims=True)
            sc_snd[m:m + 1, :] = jnp.broadcast_to(sc, (1, 128))
        sc_all[cid] = sc_snd[...]
        for j in range(1, C):
            score_copy(j).start()

    @pl.when(i == T)
    def _():
        for j in range(1, C):
            score_copy(j).wait()
        total = jnp.zeros((1, 128), F32)
        own = sc_snd[...]
        for m in range(2):
            rows = [sc_all[j, m:m + 1, :] for j in range(C)]
            peak = functools.reduce(jnp.maximum, rows)
            lse = peak + jnp.log(functools.reduce(lambda a, b: a + b, [jnp.exp(r - peak) for r in rows]))
            lab = lab_ref[m]
            picked = functools.reduce(lambda a, b: a + b, [jnp.where(lab == j, r, 0.0) for j, r in enumerate(rows)])
            total = total + (lse - picked)
            ds_scr[m:m + 1, :] = (jnp.exp(own[m:m + 1, :] - lse) - jnp.where(lab == cid, 1.0, 0.0)) * (1.0 / Q)
        loss_ref[...] = jnp.broadcast_to(jnp.where(cid == 0, total * (1.0 / Q), 0.0), (8, 128))

    @pl.when((i >= 1) & (i <= T))
    def _():
        t = lax.rem(i, T)
        bwd_tile(jnp.minimum(t, 1), ds_scr, cot_ref, wo_ref, wu_ref, wd_ref, vec_ref, dfs_ref, dctx_ref, gv_ref, gbu_ref, dl_ref, ul_ref, al_ref, gp_scr, z1_scr, z2_scr, r_scr, R)


def back_kernel(len_ref, nl_h, dl_h, al_h, ctx_h, act_h, ul_h, qkv_h, dctx_h, xlow_h, wq_h, dfs_h, lse_ref, tab_ref, bkf_ref, gv_ref, gbu_ref, loss_ref,
                *rest, C, Q, fast):
    if fast:
        ig_h, p_out, u_out, d_out, v_out = rest[:5]
        scr = rest[5:]
    else:
        ig_h, gq_o, go_o, gu_o, gd_o, gb_o, gtab_o = rest[:7]
        scr = rest[7:]
    (nl, dl, al, ctx, ch, qkv, dctx, xlow, wq, dfs, igt, gq, go, gu, gd, relf, drelf, bias_scr, acc_scr, gb, gtab, ls, cs_, os_) = scr[:24]
    NS, D = nl.shape
    FF = gu.shape[1]
    S = NS // 2
    NZ = FF // 768
    load = lambda i, src, dst: pltpu.make_async_copy(src, dst, ls.at[i])
    big = [load(0, nl_h, nl), load(1, dl_h, dl), load(2, al_h, al), load(3, ctx_h, ctx), load(4, qkv_h, qkv), load(5, dctx_h, dctx),
           load(6, xlow_h, xlow), load(7, wq_h, wq), load(8, dfs_h, dfs)]
    if fast:
        g = Geo(C, Q)
        seq = [(ul_h, jnp.bitwise_xor(g.z, zi)) for zi in (3, 2, 1, 0)]
        qorder = [(1, 1), (1, 0), (0, 1), (0, 0)]
        seq += [(act_h, (1 - g.x if dx else g.x) * 2 + (1 - g.k if dk else g.k)) for dx, dk in qorder]
    else:
        seq = [(ul_h, i) for i in range(NZ)] + [(act_h, i) for i in range(NZ)]
    off = lambda i: pl.multiple_of(seq[i][1] * 768, 128)
    chunk = lambda i: pltpu.make_async_copy(seq[i][0].at[:, pl.ds(off(i), 768)], ch.at[i % 2], cs_.at[i % 2])
    big[0].start()
    chunk(0).start()
    chunk(1).start()
    for c in big[1:]:
        c.start()
    if fast:
        bufs = {n: scr[24 + 4 * i:28 + 4 * i] for i, n in enumerate(PIECES)}
        h_scr, e_snd, e_rcv, vb0, va, vs, vb, ss, rs, es, qs, qr, cs, cr = scr[24 + NB:]
        R = RS(g, (gq, go, gu, gd), bufs, (ss, rs), es)
        c_ = lax.axis_index("cand")
        q_ = lax.axis_index("query")
        barrier(g, [{"query": lax.rem(q_ + j, Q)} for j in range(1, Q)] + [{"cand": lax.rem(c_ + j, C)} for j in range(1, C)])
    ZZ = (3, 2, 1, 0)
    AB = ((1, 1), (1, 0), (0, 1), (0, 0))
    big[0].wait()
    for i in range(NZ):
        chunk(i).wait()
        gu[:, pl.ds(off(i), 768)] = dg(nl[...], ch[i % 2], TN).astype(BF)
        chunk(i + 2).start()
        if fast:
            for a, b in AB:
                R.st0("u", ZZ[i], a, b)
            if i:
                for b in (1, 0):
                    R.st1("u", ZZ[i - 1], b)
    big[1].wait()
    for i in range(NZ, 2 * NZ):
        chunk(i).wait()
        gd[:, pl.ds(off(i), 768)] = dg(dl[...], ch[i % 2], TN).astype(BF)
        if i + 2 < 2 * NZ:
            chunk(i + 2).start()
        if fast:
            j = i - NZ
            if j == 0:
                for b in (1, 0):
                    R.st1("u", ZZ[3], b)
            dx, dk = qorder[j]
            if dk:
                for zi in ZZ:
                    for b in (1, 0):
                        R.st0("d", zi, dx, b)
            if j == 1:
                for b in (1, 0):
                    R.st1("d", 3, b)
                R.st2("u", 3)
            if j == 2:
                for b in (1, 0):
                    R.st1("d", 2, b)
                R.st2("u", 2)
    big[2].wait()
    big[3].wait()
    go[...] = dg(al[...], ctx[...], TN).astype(BF)
    slots = {}
    if fast:
        for zi in ZZ:
            for a, b in AB:
                R.st0("o", zi, a, b)
        ev = []
        def E(f, *a):
            ev.append(lambda: f(*a))
        E(R.st2, "d", 3); E(R.st1, "d", 1, 1); E(R.st1, "d", 1, 0); E(R.st2, "u", 1)
        E(R.st3, "u", 3); E(R.st2, "d", 2); E(R.st1, "d", 0, 1); E(R.st1, "d", 0, 0); E(R.st2, "u", 0)
        E(R.st3, "d", 3); E(R.st3, "u", 2); E(R.st1, "o", 3, 1); E(R.st1, "o", 3, 0); E(R.st2, "d", 1)
        E(R.st3, "d", 2); E(R.st3, "u", 1); E(R.st1, "o", 2, 1); E(R.st1, "o", 2, 0); E(R.st2, "o", 3); E(R.st2, "d", 0)
        E(R.st3, "d", 1); E(R.st1, "o", 1, 1); E(R.st1, "o", 1, 0); E(R.st2, "o", 2); E(R.st3, "o", 3)
        E(R.st1, "o", 0, 1); E(R.st1, "o", 0, 0); E(R.st2, "o", 1); E(R.st3, "o", 2); E(R.st2, "o", 0); E(R.st3, "o", 1)
        ns = 11
        for i, e in enumerate(ev):
            t = i * ns // len(ev)
            slots.setdefault((t // 2, t % 2), []).append(e)
    rel_rows(tab_ref, bkf_ref, relf)
    drelf[...] = jnp.zeros_like(drelf)
    big[4].wait()
    big[5].wait()
    attn_bwd(len_ref, qkv, dctx, lse_ref, relf, drelf, bias_scr, acc_scr, S, D, slots)
    big[6].wait()

    def b1(n, _):
        o = pl.multiple_of(n * 256, 256)
        t = qkv[:, pl.ds(o, 256)]
        gq[pl.ds(o, 256), :] = dg(t, xlow[...], TN).astype(BF)
        gb[:, pl.ds(o, 256)] = jnp.sum(t.astype(F32), axis=0, keepdims=True)
        return 0
    lax.fori_loop(0, 3 * D // 256, b1, 0)
    QP = ("qa", "qb")
    if fast:
        for zi in ZZ:
            for a, b in AB:
                for n in QP:
                    R.st0(n, zi, a, b)
    nb, nn = tab_ref.shape[1], bkf_ref.shape[1]
    hot = (lax.broadcasted_iota(jnp.int32, (nb, nn), 0) == bkf_ref[...]).astype(F32)
    gtab[...] = dg(drelf[...], hot, NT, lax.Precision.HIGHEST)
    if fast:
        dq, fq, bq = D // Q, FF // Q, nb // Q
        vb0[...] = jnp.zeros_like(vb0)
        for q in range(Q):
            lo = slice(q * dq, (q + 1) * dq)
            vb0[q, 0:1, 0:dq] = gb[:, q * dq:(q + 1) * dq]
            vb0[q, 1:2, 0:dq] = gb[:, 2 * D + q * dq:2 * D + (q + 1) * dq]
            vb0[q, 2:8, 0:dq] = gv_ref[0:6, lo]
            for j in range(fq // 256):
                vb0[q, 8 + j:9 + j, :] = gbu_ref[:, q * fq + j * 256:q * fq + (j + 1) * 256]
            vb0[q, 11:12, 0:128] = loss_ref[0:1, :]
            vb0[q, 16:32, 0:bq] = gtab[:, q * bq:(q + 1) * bq]
        vq = []
        for j in range(1, Q):
            qq = lax.rem(q_ + j, Q)
            c = pltpu.make_async_remote_copy(vb0.at[qq], va.at[q_], qs.at[j - 1], qr.at[j - 1], device_id={"query": qq}, device_id_type=MESH)
            c.start()
            vq.append(c)
        va[q_] = vb0[q_]
        for n in QP:
            for b in (1, 0):
                R.st1(n, 3, b)
    big[7].wait()
    big[8].wait()
    steps = NS // 256
    outc = lambda r: pltpu.make_async_copy(igt.at[r % 2], ig_h.at[pl.ds(r * 256, 256), :], os_.at[r % 2])
    for r in range(steps):
        if r >= 2:
            outc(r - 2).wait()
        igt[r % 2] = dfs[r * 256:(r + 1) * 256, :] + dg(qkv[r * 256:(r + 1) * 256, :], wq[...], NN)
        outc(r).start()
        if fast:
            if r < 3:
                for n in QP:
                    for b in (1, 0):
                        R.st1(n, 2 - r, b)
            for n in QP:
                R.st2(n, 3 - r)
            if r >= 1:
                for n in QP:
                    R.st3(n, 4 - r)
    for r in range(max(0, steps - 2), steps):
        outc(r).wait()
    if fast:
        for c in vq:
            c.wait()
        t = functools.reduce(lambda a, b: a + b, [va[j] for j in range(Q)])
        vs[...] = t
        vb[c_] = t
        vc = []
        for j in range(1, C):
            c = pltpu.make_async_remote_copy(vs, vb.at[c_], cs.at[j - 1], cr.at[j - 1], device_id={"cand": lax.rem(c_ + j, C)}, device_id_type=MESH)
            c.start()
            vc.append(c)
        for i, n in enumerate(("qa", "qb", "o")):
            R.fin(n, h_scr.at[pl.ds((0, 48, 144)[i], SHP[n][0])])
        k = g.k
        lo = h_scr[:, 0:192]
        hi = h_scr[:, 192:384]
        e_snd[...] = jnp.where(k == 0, hi, lo)
        c = pltpu.make_async_remote_copy(e_snd, e_rcv, es.at[0], es.at[1], device_id=R.partner, device_id_type=MESH)
        c.start()
        p_out[k] = jnp.where(k == 0, lo, hi)
        R.fin("u", u_out)
        R.fin("d", d_out)
        c.wait()
        p_out[1 - k] = e_rcv[...]
        for c in vc:
            c.wait()
        v_out[...] = functools.reduce(lambda a, b: a + b, [vb[j] for j in range(C)])
        R.drain()
    else:
        gq_o[...] = gq[...]
        go_o[...] = go[...]
        gu_o[...] = gu[...]
        gd_o[...] = gd[...]
        gb_o[...] = gb[...]
        gtab_o[...] = gtab[...]


def sds(shape, dtype=F32):
    return jax.ShapeDtypeStruct(shape, dtype)


def body(hidden_in, out_cotangent, lengths, labels, buckets, w_qkv, w_out, w_up, w_down, bias_q, bias_v, bias_out,
         norm1_gain, norm1_bias, bias_up, bias_down, norm2_gain, score_vector, rel_table):
    Q = lax.axis_size("query")
    C = lax.axis_size("cand")
    micro = hidden_in.shape[0]
    S, D = hidden_in.shape[3:]
    FF = w_up.shape[1] * C
    NBK = rel_table.shape[0] * Q
    dq, fq, bq = D // Q, FF // Q, NBK // Q
    fast = Q == 4 and C == 8 and D == 768 and FF == 3072
    x = hidden_in.reshape(micro, S, D)
    cot = out_cotangent.reshape(micro, S, D)
    lens = lengths.reshape(micro)
    labs = labels.reshape(micro)
    vflat = jnp.concatenate([bias_q, bias_v, bias_out, norm1_gain, norm1_bias, bias_down, norm2_gain, score_vector, bias_up, rel_table.reshape(-1)])
    nv = vflat.shape[0]
    if fast:
        a, b = w_qkv.astype(BF).T, w_out.astype(BF).T
        ha, hb = a.shape[0] // 2, b.shape[0] // 2
        p = jnp.stack([jnp.concatenate([a[i * ha:(i + 1) * ha], b[i * hb:(i + 1) * hb]], 0) for i in range(2)], 0)
        wq, wo, wu, wd, vall = pl.pallas_call(
            functools.partial(kAG, C=C, Q=Q), in_specs=[VM] * 4, out_specs=[ANY] * 4 + [VM],
            out_shape=[sds((3 * D, D), BF), sds((D, D), BF), sds((D, FF), BF), sds((D, FF), BF), sds((Q, nv // 128, 128))],
            scratch_shapes=[pltpu.VMEM((192, 384), BF), pltpu.VMEM((192, 192), BF)] + [pltpu.SemaphoreType.DMA((5, 16))] * 4
            + [pltpu.SemaphoreType.DMA((5,)), pltpu.SemaphoreType.DMA((2,)), pltpu.SemaphoreType.DMA((Q,)), pltpu.SemaphoreType.DMA((Q,))],
            compiler_params=pltpu.CompilerParams(collective_id=0, has_side_effects=True, vmem_limit_bytes=8 * 2**20),
        )(p, w_up.astype(BF), w_down.astype(BF).T, vflat.reshape(nv // 128, 128))
        vall = vall.reshape(Q, nv)
    else:
        def gather(w):
            part = lax.all_gather(w.astype(BF), "query", axis=0, tiled=True)
            return lax.all_gather(part, "cand", axis=1, tiled=True)
        wq, wo, wu, wd = gather(w_qkv).T, gather(w_out).T, gather(w_up), gather(w_down).T
        vall = lax.all_gather(vflat, "query", axis=0, tiled=False)
    vecs = vall[:, :8 * dq].reshape(Q, 8, dq).transpose(1, 0, 2).reshape(8, D)
    bup = vall[:, 8 * dq:8 * dq + fq].reshape(1, FF)
    table = vall[:, 8 * dq + fq:].reshape(NBK, HEADS)
    qkv_bias = jnp.concatenate([vecs[0:1], jnp.zeros((1, D), F32), vecs[1:2]], axis=1)
    vec = jnp.concatenate([vecs[2:], jnp.zeros((2, D), F32)], axis=0)
    tab = jnp.pad(table.T, ((0, 4), (0, 0)))
    nrel = buckets.shape[0]
    bk = jnp.pad(buckets, (0, 1), constant_values=-1)[None, :]
    bkf = jnp.pad(buckets[::-1], (0, 1), constant_values=-1)[None, :]
    NS = micro * S
    xlow, qkv, ctx, lse = pl.pallas_call(
        attn_fwd_kernel, in_specs=[SM] + [VM] * 5, out_specs=[VM] * 4,
        out_shape=[sds((NS, D), BF), sds((NS, 3 * D), BF), sds((NS, D), BF), sds((micro, 16, S))],
        scratch_shapes=[pltpu.VMEM((16, 2 * S), F32), pltpu.VMEM((2, S, S), F32)],
        compiler_params=pltpu.CompilerParams(vmem_limit_bytes=60 * 2**20))(lens, x, wq, qkv_bias, tab, bk)
    R = 256
    Rh, T = R // micro, NS // R
    tb = lambda im, n=D: pl.BlockSpec((micro, Rh, n), im)
    fw = lambda i: (0, jnp.minimum(i, T - 1), 0)
    bw = lambda i: (0, lax.rem(jnp.maximum(i, 1), T), 0)
    tok = lambda n, dt=BF: sds((micro, S, n), dt)
    out, dfs, dctx, nl, act, dl, al, ul, gv, gbu, lossv = pl.pallas_call(
        functools.partial(ffn_kernel, T=T, R=R, C=C, Q=Q), grid=(T + 1,),
        in_specs=[SM, tb(fw), tb(fw), tb(bw)] + [VM] * 5, out_specs=[tb(fw), tb(bw), tb(bw), tb(fw), tb(fw, FF), tb(bw), tb(bw), tb(bw, FF)] + [VM] * 3,
        out_shape=[tok(D, F32), tok(D, F32), tok(D), tok(D), tok(FF), tok(D), tok(D), tok(FF), sds((8, D)), sds((1, FF)), sds((8, 128))],
        scratch_shapes=[pltpu.VMEM((2, R, FF), F32), pltpu.VMEM((2, R, D), F32), pltpu.VMEM((2, R, D), F32), pltpu.VMEM((2, R, 128), F32),
                        pltpu.VMEM((8, 128), F32), pltpu.VMEM((8, 128), F32), pltpu.VMEM((C, 8, 128), F32), pltpu.SemaphoreType.DMA((C,)), pltpu.SemaphoreType.DMA((C,))],
        compiler_params=pltpu.CompilerParams(collective_id=1, has_side_effects=True, vmem_limit_bytes=60 * 2**20),
    )(labs, x, ctx.reshape(micro, S, D), cot, wo, wu, wd, vec, bup)
    flat = lambda t: t.reshape(NS, t.shape[-1])
    gouts = [sds((2, 192, 192)), sds((192, 384)), sds((96, 768)), sds((32, 256))] if fast else \
        [sds((3 * D, D), BF), sds((D, D), BF), sds((D, FF), BF), sds((D, FF), BF), sds((1, 3 * D)), sds((16, NBK))]
    v = pltpu.VMEM
    dma = pltpu.SemaphoreType.DMA
    scr = [v((NS, D), BF)] * 4 + [v((2, NS, 768), BF), v((NS, 3 * D), BF), v((NS, D), BF), v((NS, D), BF), v((3 * D, D), BF), v((NS, D), F32), v((2, 256, D), F32),
                                  v((3 * D, D), BF), v((D, D), BF), v((D, FF), BF), v((D, FF), BF), v((16, 2 * S), F32), v((16, 2 * S), F32),
                                  v((2, S, S), F32), v((2, S, S), F32), v((1, 3 * D), F32), v((16, NBK), F32), dma((9,)), dma((2,)), dma((2,))]
    if fast:
        scr += rs_bufs() + [v((192, 384), F32), v((192, 192), F32), v((192, 192), F32), v((Q, 32, 256), F32), v((Q, 32, 256), F32), v((32, 256), F32), v((C, 32, 256), F32),
                            dma((5, 31)), dma((5, 31)), dma((2,)), dma((Q,)), dma((Q,)), dma((C,)), dma((C,))]
    res = pl.pallas_call(
        functools.partial(back_kernel, C=C, Q=Q, fast=fast), in_specs=[SM] + [ANY] * 11 + [VM] * 6, out_specs=[ANY] + [VM] * len(gouts),
        out_shape=[sds((NS, D))] + gouts, scratch_shapes=scr,
        compiler_params=pltpu.CompilerParams(collective_id=2 if fast else None, has_side_effects=True, vmem_limit_bytes=67043328),
    )(lens, flat(nl), flat(dl), flat(al), ctx, flat(act), flat(ul), qkv, flat(dctx), xlow, wq, flat(dfs), lse, tab, bkf, gv, gbu, lossv)
    ig = res[0]
    if fast:
        pg, ug, dng, vs = res[1:]
        g_qkv = jnp.concatenate([pg[0, :ha], pg[1, :ha]], 0).T
        g_out = jnp.concatenate([pg[0, ha:], pg[1, ha:]], 0).T
        g_up, g_down = ug, dng.T
        small = [vs[i, :dq] for i in range(8)]
        g_bup = vs[8:8 + fq // 256].reshape(fq)
        g_tab = vs[16:16 + HEADS, :bq].T
        loss = vs[11, 0]
    else:
        def scatter(g):
            rows, cols = g.shape[0] // Q, g.shape[1] // C
            tiles = g.astype(F32).reshape(Q, rows, C, cols).transpose(2, 0, 1, 3).reshape(C * Q, rows, cols)
            return lax.psum_scatter(tiles, ("cand", "query"), scatter_dimension=0, tiled=True)[0]
        gq, go, gu, gd, gb, gtab = res[1:]
        g_qkv, g_out, g_up, g_down = scatter(gq.T), scatter(go.T), scatter(gu), scatter(gd.T)
        gvecs = jnp.concatenate([gb[:, :D], gb[:, 2 * D:], gv[:6]], axis=0)
        vg = jnp.concatenate([gvecs.reshape(8, Q, dq).transpose(1, 0, 2).reshape(Q, 8 * dq), gbu.reshape(Q, fq), gtab[:HEADS].T.reshape(Q, bq * HEADS),
                              jnp.broadcast_to(lossv[0:1, 0:1], (Q, 1))], axis=1)
        vg = jnp.pad(vg, ((0, 0), (0, -vg.shape[1] % 1024)))
        vs = lax.psum_scatter(lax.psum(vg, "cand"), "query", scatter_dimension=0, tiled=True)[0]
        small = [vs[i * dq:(i + 1) * dq] for i in range(8)]
        g_bup = vs[8 * dq:8 * dq + fq]
        g_tab = vs[8 * dq + fq:8 * dq + fq + bq * HEADS].reshape(bq, HEADS)
        loss = vs[8 * dq + fq + bq * HEADS]
    return (out.reshape(hidden_in.shape), ig.reshape(hidden_in.shape), g_qkv, g_out, g_up, g_down,
            small[0], small[1], small[2], small[3], small[4], g_bup, small[5], small[6], small[7], g_tab, loss)


def solution(mesh):
    seq, w, v = P(None, "query", "cand", None, None), P("query", "cand"), P("query")
    return jax.shard_map(
        body, mesh=mesh,
        in_specs=(seq, seq, P(None, "query", "cand"), P(None, "query"), P(), w, w, w, w) + (v,) * 9 + (P("query", None),),
        out_specs=(seq, seq, w, w, w, w) + (v,) * 9 + (P("query", None), P()),
        check_vma=False)
```

```python
import functools

import jax
import jax.numpy as jnp
from jax import lax
from jax.experimental import pallas as pl
from jax.experimental.pallas import tpu as pltpu
from jax.sharding import PartitionSpec as P

F32 = jnp.float32
BF = jnp.bfloat16
NT = (((1,), (1,)), ((), ()))
NN = (((1,), (0,)), ((), ()))
TN = (((0,), (0,)), ((), ()))
VM = pl.BlockSpec(memory_space=pltpu.VMEM)
SM = pl.BlockSpec(memory_space=pltpu.SMEM)
ANY = pl.BlockSpec(memory_space=pl.ANY)
MESH = pl.DeviceIdType.MESH
EPS = 1e-5
FC = 512
HEADS = 12
NR = {"x": 2, "y": 2, "z": 4}
RPIECES = ["u", "d", "o", "qa", "qb", "qz"]
RORD = {"u": "yxz", "d": "xyz", "o": "zyx", "qa": "yxz", "qb": "xyz", "qz": "zyx"}
RSHP = {"u": (192, 384, 48), "d": (96, 768, 48), "o": (48, 384, 48), "qa": (64, 384, 32), "qb": (64, 384, 32), "qz": (16, 384, 16)}
QROW = {"qa": 0, "qb": 64, "qz": 128}
NB = 4 * len(RPIECES)
AGSLOTS = {
    "p": [("u", (0, 0, 0), (("k", 0), ("x", 1), ("y", 1), ("z", 1))), ("d", (0, 0, 0), (("k", 0),))],
    "w": [("o", (0, 0, 0), (("y", 1),)), ("qa", (0, 0, 0), (("x", 1), ("y", 1), ("z", 1), ("z", 2), ("z", 3))), ("qb", (0, 0, 0), (("k", 0), ("x", 1), ("y", 1), ("z", 1), ("z", 2), ("z", 3))), ("qz", (0, 0, 0), (("x", 1), ("y", 1))), ("qa", (0, 0, 0), (("k", 0),)), ("qz", (0, 0, 0), (("k", 0),)), ("o", (0, 0, 0), (("k", 0),)), ("qz", (0, 0, 0), (("z", 1),)), ("o", (0, 0, 0), (("x", 1),)), ("qz", (0, 0, 0), (("z", 3),)), ("u", (0, 0, 1), (("x", 1), ("y", 1), ("k", 0))), ("u", (0, 1, 0), (("y", 1), ("k", 0))), ("u", (1, 0, 0), (("k", 0),)), ("qz", (0, 0, 1), (("y", 1), ("z", 3), ("z", 2), ("z", 1), ("k", 0))), ("qz", (0, 0, 0), (("z", 2),)), ("qb", (0, 0, 1), (("y", 1), ("x", 1), ("k", 0))), ("qb", (0, 1, 0), (("x", 1), ("k", 0))), ("qa", (0, 1, 0), (("y", 1), ("k", 0))), ("qz", (0, 1, 0), (("z", 3), ("z", 2), ("z", 1), ("k", 0))), ("qa", (1, 0, 0), (("k", 0),)), ("qb", (1, 0, 0), (("k", 0),)), ("qb", (0, 0, 3), (("y", 1), ("x", 1), ("k", 0))), ("qb", (0, 1, 1), (("x", 1), ("k", 0))), ("qb", (1, 1, 0), (("k", 0),)), ("o", (0, 0, 0), (("z", 1),)), ("qa", (0, 0, 1), (("x", 1), ("y", 1), ("k", 0))), ("u", (0, 0, 0), (("z", 3),)), ("o", (0, 0, 0), (("z", 3),)), ("qb", (1, 0, 1), (("k", 0),)), ("qa", (1, 1, 0), (("k", 0),)), ("qz", (0, 1, 1), (("z", 3), ("z", 2), ("z", 1), ("k", 0))), ("qa", (0, 0, 3), (("x", 1), ("y", 1), ("k", 0))), ("qa", (0, 1, 1), (("y", 1), ("k", 0))), ("qb", (0, 1, 3), (("x", 1), ("k", 0))), ("qa", (1, 0, 1), (("k", 0),)), ("qb", (1, 1, 1), (("k", 0),)), ("o", (0, 0, 0), (("z", 2),)), ("d", (0, 0, 0), (("x", 1),)), ("qb", (1, 0, 3), (("k", 0),)), ("qb", (0, 0, 2), (("y", 1), ("x", 1), ("k", 0))), ("qa", (0, 1, 3), (("y", 1), ("k", 0))), ("o", (0, 1, 0), (("z", 3), ("z", 2), ("z", 1), ("k", 0))), ("qa", (1, 1, 1), (("k", 0),)), ("qz", (1, 0, 0), (("k", 0),)), ("qz", (1, 1, 0), (("k", 0),)), ("o", (0, 0, 1), (("y", 1), ("z", 3), ("z", 2), ("z", 1), ("k", 0))), ("qa", (1, 0, 3), (("k", 0),)), ("qb", (1, 1, 3), (("k", 0),)), ("qa", (0, 0, 2), (("x", 1), ("y", 1), ("k", 0))), ("qz", (1, 0, 1), (("k", 0),)), ("qz", (3, 0, 0), (("k", 0),)), ("qz", (3, 1, 0), (("k", 0),)), ("qb", (0, 1, 2), (("x", 1), ("k", 0))), ("qz", (2, 0, 0), (("k", 0),)), ("qb", (1, 0, 2), (("k", 0),)), ("qz", (1, 1, 1), (("k", 0),)), ("qz", (2, 1, 0), (("k", 0),)), ("qa", (1, 1, 3), (("k", 0),)), ("qa", (0, 1, 2), (("y", 1), ("k", 0))), ("qz", (3, 0, 1), (("k", 0),)), ("o", (0, 1, 1), (("z", 3), ("z", 2), ("z", 1), ("k", 0))), ("qa", (1, 0, 2), (("k", 0),)), ("qz", (3, 1, 1), (("k", 0),)), ("d", (0, 0, 0), (("z", 1),)), ("u", (1, 1, 0), (("k", 0),)), ("qz", (2, 0, 1), (("k", 0),)), ("u", (0, 1, 1), (("y", 1), ("k", 0))), ("qz", (2, 1, 1), (("k", 0),)), ("o", (1, 0, 0), (("k", 0),)), ("d", (0, 0, 0), (("y", 1),)), ("qb", (1, 1, 2), (("k", 0),)), ("o", (3, 0, 0), (("k", 0),)), ("qa", (1, 1, 2), (("k", 0),))],
    "n1": [("o", (3, 1, 0), (("k", 0),))],
    "n2": [("o", (1, 1, 0), (("k", 0),))],
    "n3": [("o", (2, 0, 0), (("k", 0),)), ("u", (0, 0, 3), (("x", 1), ("y", 1), ("k", 0)))],
    "n4": [("u", (0, 0, 0), (("z", 2),)), ("u", (1, 0, 1), (("k", 0),)), ("d", (1, 0, 0), (("k", 0),))],
    "n5": [("o", (2, 1, 0), (("k", 0),))],
    "n7": [("o", (1, 0, 1), (("k", 0),))],
    "n8": [("o", (3, 0, 1), (("k", 0),)), ("u", (1, 1, 1), (("k", 0),))],
    "t0": [("o", (3, 1, 1), (("k", 0),))],
    "t1": [("o", (1, 1, 1), (("k", 0),)), ("d", (0, 0, 0), (("z", 3),)), ("o", (2, 0, 1), (("k", 0),))],
    "t2": [("o", (2, 1, 1), (("k", 0),))],
    "t3": [("d", (0, 0, 1), (("y", 1), ("x", 1), ("k", 0)))],
    "t4": [("d", (0, 1, 0), (("x", 1), ("k", 0))), ("d", (0, 0, 0), (("z", 2),))],
    "t5": [("u", (0, 1, 3), (("y", 1), ("k", 0)))],
    "t7": [("d", (1, 1, 0), (("k", 0),))],
    "t8": [("u", (1, 0, 3), (("k", 0),)), ("u", (0, 0, 2), (("x", 1), ("y", 1), ("k", 0))), ("d", (1, 0, 1), (("k", 0),))],
    "t11": [("d", (0, 1, 1), (("x", 1), ("k", 0))), ("u", (1, 1, 3), (("k", 0),)), ("u", (1, 0, 2), (("k", 0),)), ("u", (0, 1, 2), (("y", 1), ("k", 0)))],
    "tail": [("d", (0, 0, 3), (("y", 1), ("x", 1), ("k", 0))), ("d", (0, 1, 3), (("x", 1), ("k", 0))), ("d", (1, 1, 1), (("k", 0),)), ("u", (1, 1, 2), (("k", 0),)), ("d", (0, 0, 2), (("y", 1), ("x", 1), ("k", 0))), ("d", (1, 0, 3), (("k", 0),)), ("d", (1, 1, 3), (("k", 0),)), ("d", (0, 1, 2), (("x", 1), ("k", 0))), ("d", (1, 0, 2), (("k", 0),)), ("d", (1, 1, 2), (("k", 0),))],
}
AGEARLY = 10
AGMID = 41
FIRST = {
    "o": [("s0", "o", 3, 0, 0), ("s0", "o", 2, 0, 0), ("s0", "o", 1, 0, 0), ("s0", "o", 0, 0, 0), ("s0", "o", 3, 1, 0), ("s0", "o", 2, 1, 0), ("s0", "o", 1, 1, 0), ("s0", "o", 0, 1, 0), ("s0", "o", 3, 0, 1), ("s0", "o", 2, 0, 1), ("s0", "o", 1, 0, 1), ("s0", "o", 0, 0, 1), ("s0", "o", 3, 1, 1), ("s0", "o", 2, 1, 1), ("s0", "o", 1, 1, 1), ("s0", "o", 0, 1, 1)],
    "u0": [("s0", "u", 1, 0, 3), ("s0", "u", 0, 0, 3), ("s0", "u", 1, 1, 3), ("s0", "u", 0, 1, 3)],
    "u1": [("s0", "u", 1, 0, 2), ("s0", "u", 0, 0, 2), ("s0", "u", 1, 1, 2), ("s0", "u", 0, 1, 2)],
    "u2": [("s0", "u", 1, 0, 1), ("s0", "u", 0, 0, 1), ("s0", "u", 1, 1, 1), ("s0", "u", 0, 1, 1)],
    "u3": [("s0", "u", 1, 0, 0), ("s0", "u", 0, 0, 0), ("s0", "u", 1, 1, 0), ("s0", "u", 0, 1, 0)],
    "d0": [("s0", "d", 1, 0, 3), ("s0", "d", 1, 1, 3), ("s0", "d", 1, 0, 2), ("s0", "d", 1, 1, 2), ("s0", "d", 1, 0, 1), ("s0", "d", 1, 1, 1), ("s0", "d", 1, 0, 0), ("s0", "d", 1, 1, 0)],
    "d2": [("s0", "d", 0, 0, 3), ("s0", "d", 0, 1, 3), ("s0", "d", 0, 0, 2), ("s0", "d", 0, 1, 2), ("s0", "d", 0, 0, 1), ("s0", "d", 0, 1, 1), ("s0", "d", 0, 0, 0), ("s0", "d", 0, 1, 0)],
    "g2": [("s0", "qa", 1, 0, 3), ("s0", "qa", 0, 0, 3), ("s0", "qa", 1, 1, 3), ("s0", "qa", 0, 1, 3), ("s0", "qa", 1, 0, 2), ("s0", "qa", 0, 0, 2), ("s0", "qa", 1, 1, 2), ("s0", "qa", 0, 1, 2), ("s0", "qa", 1, 0, 1), ("s0", "qa", 0, 0, 1), ("s0", "qa", 1, 1, 1), ("s0", "qa", 0, 1, 1), ("s0", "qa", 1, 0, 0), ("s0", "qa", 0, 0, 0), ("s0", "qa", 1, 1, 0), ("s0", "qa", 0, 1, 0), ("s0", "qb", 1, 0, 3), ("s0", "qb", 0, 0, 3), ("s0", "qb", 1, 1, 3), ("s0", "qb", 0, 1, 3), ("s0", "qb", 1, 0, 2), ("s0", "qb", 0, 0, 2), ("s0", "qb", 1, 1, 2), ("s0", "qb", 0, 1, 2), ("s0", "qb", 1, 0, 1), ("s0", "qb", 0, 0, 1), ("s0", "qb", 1, 1, 1), ("s0", "qb", 0, 1, 1), ("s0", "qb", 1, 0, 0), ("s0", "qb", 0, 0, 0), ("s0", "qb", 1, 1, 0), ("s0", "qb", 0, 1, 0), ("s0", "qz", 3, 0, 0), ("s0", "qz", 2, 0, 0), ("s0", "qz", 1, 0, 0), ("s0", "qz", 0, 0, 0), ("s0", "qz", 3, 1, 0), ("s0", "qz", 2, 1, 0), ("s0", "qz", 1, 1, 0), ("s0", "qz", 0, 1, 0), ("s0", "qz", 3, 0, 1), ("s0", "qz", 2, 0, 1), ("s0", "qz", 1, 0, 1), ("s0", "qz", 0, 0, 1), ("s0", "qz", 3, 1, 1), ("s0", "qz", 2, 1, 1), ("s0", "qz", 1, 1, 1), ("s0", "qz", 0, 1, 1)],
}
SLOTS = {
    "u1": [("s1", "o", 1, 1, 1), ("s1", "o", 2, 1, 1), ("s1", "o", 3, 1, 1)],
    "u2": [("s1", "o", 1, 0, 1), ("s1", "u", 1, 1, 3)],
    "u3": [("s1", "o", 2, 0, 1), ("s1", "u", 1, 0, 3), ("s1", "o", 1, 1, 0)],
    "d0": [("s1", "o", 3, 0, 1)],
    "d1": [("s1", "o", 2, 1, 0)],
    "d2": [("s1", "u", 1, 1, 2), ("s2", "u", 1, 3)],
    "d3": [("s1", "o", 3, 1, 0), ("s1", "d", 1, 1, 3)],
    "t0": [("s1", "u", 1, 0, 2), ("s1", "o", 1, 0, 0)],
    "t1": [("s1", "d", 1, 0, 3), ("s3", "u", 3)],
    "t2": [("s2", "u", 1, 2), ("s2", "d", 1, 3)],
    "t3": [("s1", "u", 1, 1, 1)],
    "t4": [("s1", "d", 1, 1, 2), ("s1", "u", 1, 0, 1)],
    "t5": [("s3", "d", 3)],
    "t6": [("s2", "o", 1, 1), ("s2", "u", 1, 1)],
    "t7": [("s3", "u", 2), ("s1", "d", 1, 0, 2), ("s2", "d", 1, 2), ("s1", "o", 2, 0, 0)],
    "t8": [("s1", "u", 1, 1, 0), ("s1", "o", 3, 0, 0), ("s1", "d", 1, 1, 1)],
    "t10": [("s1", "u", 1, 0, 0), ("s1", "d", 1, 0, 1), ("s3", "u", 1), ("s3", "d", 2)],
    "g0": [("s2", "u", 1, 0), ("s2", "d", 1, 1)],
    "g1": [("s2", "o", 1, 0), ("s1", "d", 1, 1, 0)],
    "i0": [("s3", "d", 1), ("s1", "d", 1, 0, 0), ("s1", "qa", 1, 0, 3), ("s1", "qa", 1, 1, 3), ("s1", "qa", 1, 1, 2)],
    "i2": [("s3", "o", 1), ("s1", "qz", 2, 1, 1), ("s1", "qz", 1, 1, 1), ("s1", "qz", 3, 1, 1), ("s2", "d", 1, 0)],
    "i3": [("s2", "qa", 1, 3), ("s1", "qz", 1, 0, 1), ("s1", "qz", 2, 0, 1)],
}
TAIL = [("s1", "qa", 1, 0, 2), ("s2", "qa", 1, 2), ("s1", "qb", 1, 1, 3), ("s1", "qa", 1, 1, 1), ("s1", "qz", 3, 0, 1), ("s1", "qz", 1, 1, 0), ("s1", "qz", 2, 1, 0), ("s1", "qb", 1, 0, 3), ("s1", "qz", 1, 0, 0), ("s1", "qz", 3, 1, 0), ("s1", "qa", 1, 0, 1), ("s1", "qz", 2, 0, 0), ("s1", "qb", 1, 1, 2), ("s1", "qa", 1, 1, 0), ("s3", "qa", 3), ("s1", "qb", 1, 0, 2), ("s3", "qa", 2), ("s2", "qb", 1, 3), ("s1", "qz", 3, 0, 0), ("s1", "qb", 1, 1, 1), ("s2", "qa", 1, 1), ("s2", "qz", 1, 1), ("s1", "qa", 1, 0, 0), ("s2", "qb", 1, 2), ("s1", "qb", 1, 0, 1), ("s2", "qa", 1, 0), ("s3", "qb", 3), ("s1", "qb", 1, 1, 0), ("s3", "qa", 1), ("s3", "qb", 2), ("s1", "qb", 1, 0, 0), ("s3", "qz", 1), ("s2", "qb", 1, 1), ("s2", "qz", 1, 0), ("s2", "qb", 1, 0), ("s3", "qb", 1)]


def dg(a,b,d,prec=None): return lax.dot_general(a,b,d,preferred_element_type=F32,precision=prec)


def hooks(i, table):
    for j, evs in table.items():
        if evs:
            @pl.when(i == j)
            def _(evs=evs):
                for e in evs: e()


def qkv_proj(w_ref, bias_ref, xlow_ref, qkv_ref, slots):
    def body(n,_):
        o=pl.multiple_of(n*256,256)
        y=dg(xlow_ref[...], w_ref[pl.ds(o,256),:], NT)
        y=(y+bias_ref[:,pl.ds(o,256)])*jnp.where(o<xlow_ref.shape[1],0.125,1.0)
        qkv_ref[:,pl.ds(o,256)]=y.astype(BF)
        hooks(n, slots)
        return 0
    lax.fori_loop(0, w_ref.shape[0]//256, body, 0)


def rel_rows(tableT_ref, bk_ref, rel_ref):
    nb=tableT_ref.shape[1]; n=bk_ref.shape[1]
    hot=(lax.broadcasted_iota(jnp.int32,(nb,n),0)==bk_ref[...]).astype(F32)
    rel_ref[...]=dg(tableT_ref[...], hot, NN, lax.Precision.HIGHEST)


def bias_expand(row,S):
    R=pltpu.roll(jnp.broadcast_to(row,(128,2*S)), 2*S-127, 1, stride=1, stride_axis=0)
    nu=S//128
    return jnp.concatenate([R[:,128*(nu-1-u):128*(nu-1-u)+S] for u in range(nu)],axis=0)


def diag_sum(t,S):
    nu=S//128
    y=None
    for u in range(nu):
        a=128*(nu-1-u); parts=[]
        if a: parts.append(jnp.zeros((128,a),F32))
        parts.append(t[128*u:128*(u+1),:])
        if 2*S-a-S: parts.append(jnp.zeros((128,2*S-a-S),F32))
        v=jnp.concatenate(parts,axis=1) if len(parts)>1 else parts[0]
        y=v if y is None else y+v
    z=None
    for w in range(16):
        g=y[8*w:8*w+8,:]
        sh=120-8*w
        g=pltpu.roll(g,sh,1) if sh else g
        z=g if z is None else z+g
    out=None
    for b in range(8):
        g=z[b:b+1,:]
        g=pltpu.roll(g,7-b,1) if b<7 else g
        out=g if out is None else out+g
    return out


def attn_fwd(len_ref, qkv_ref, rel_ref, ctx_ref, lse_ref, bias_scr, S, D, slots):
    lane=lax.broadcasted_iota(jnp.int32,(1,128),1)
    col=lax.broadcasted_iota(jnp.int32,(1,S),1)
    def body(p,_):
        o=pl.multiple_of(p*128,128)
        for hh in range(2):
            row=rel_ref[pl.ds(p*2+hh,1),:]
            bias_scr[hh]=bias_expand(row,S)
        for m in range(2):
            q=qkv_ref[m*S:(m+1)*S,pl.ds(o,128)]
            k=qkv_ref[m*S:(m+1)*S,pl.ds(D+o,128)]
            v=qkv_ref[m*S:(m+1)*S,pl.ds(2*D+o,128)]
            valid=col<len_ref[m]
            outs=[]
            for hh in range(2):
                mk=(lane//64)==hh
                qm=jnp.where(mk,q,jnp.zeros_like(q))
                s=dg(qm,k,NT)+bias_scr[hh]
                s=jnp.where(valid,s,-1e30)
                mx=jnp.max(s,axis=1,keepdims=True)
                e=jnp.exp(s-mx)
                tot=jnp.sum(e,axis=1,keepdims=True)
                pl_=(e*(1.0/tot)).astype(BF)
                outs.append(dg(pl_,v,NN))
                lse_ref[m,pl.ds(p*2+hh,1),:]=jnp.transpose(mx+jnp.log(tot),(1,0))
            ctx_ref[m*S:(m+1)*S,pl.ds(o,128)]=jnp.where((lane//64)==0,outs[0],outs[1]).astype(BF)
            hooks(p, {i: slots.get(2*i+m) for i in range(D//128)})
        return 0
    lax.fori_loop(0, D//128, body, 0)


def attn_bwd(len_ref, qkv_ref, dctx_ref, lse_ref, relf_ref, drelf_ref, bias_scr, acc_scr, S, D, slots):
    lane=lax.broadcasted_iota(jnp.int32,(1,128),1)
    rowi=lax.broadcasted_iota(jnp.int32,(S,1),0)
    m0=(lane//64)==0
    def body(p,_):
        o=pl.multiple_of(p*128,128)
        for hh in range(2):
            row=relf_ref[pl.ds(p*2+hh,1),:]
            bias_scr[hh]=bias_expand(row,S)
        for m in range(2):
            q=qkv_ref[m*S:(m+1)*S,pl.ds(o,128)]
            k=qkv_ref[m*S:(m+1)*S,pl.ds(D+o,128)]
            v=qkv_ref[m*S:(m+1)*S,pl.ds(2*D+o,128)]
            do=dctx_ref[m*S:(m+1)*S,pl.ds(o,128)]
            valid=rowi<len_ref[m]
            oq=[];ok=[];ov=[]
            for hh in range(2):
                mk=(lane//64)==hh
                km=jnp.where(mk,k,jnp.zeros_like(k)); vm=jnp.where(mk,v,jnp.zeros_like(v))
                sT=dg(km,q,NT)+bias_scr[hh]
                sT=jnp.where(valid,sT,-1e30)
                pT=jnp.exp(sT-lse_ref[m,pl.ds(p*2+hh,1),:])
                dpT=dg(vm,do,NT)
                rd=jnp.sum(dpT*pT,axis=0,keepdims=True)
                ds=(pT*(dpT-rd)).astype(BF)
                ov.append(dg(pT.astype(BF),do,NN))
                ok.append(dg(ds,q,NN))
                oq.append(dg(ds,k,TN))
                if m==0: acc_scr[hh]=ds.astype(F32)
                else: acc_scr[hh]+=ds.astype(F32)
            qkv_ref[m*S:(m+1)*S,pl.ds(o,128)]=(jnp.where(m0,oq[0],oq[1])*0.125).astype(BF)
            qkv_ref[m*S:(m+1)*S,pl.ds(D+o,128)]=jnp.where(m0,ok[0],ok[1]).astype(BF)
            qkv_ref[m*S:(m+1)*S,pl.ds(2*D+o,128)]=jnp.where(m0,ov[0],ov[1]).astype(BF)
            hooks(p, {i: slots.get(2*i+m) for i in range(D//128)})
        for hh in range(2):
            drelf_ref[pl.ds(p*2+hh,1),:]=diag_sum(acc_scr[hh],S)
        return 0
    lax.fori_loop(0, D//128, body, 0)


def stats(z):
    mu=jnp.mean(z,axis=-1,keepdims=True); c=z-mu
    var=jnp.mean(c*c,axis=-1,keepdims=True)
    r=lax.rsqrt(var+EPS)
    return c*r, r


def fwd_tile(slot, x_ref, ctx_ref, wo_ref, wu_ref, wd_ref, vec_ref, bup_ref, out_ref, nl_scr, act_scr, gp_scr, z1_scr, z2_scr, r_scr, R):
    D=x_ref.shape[2]; FF=wu_ref.shape[1]
    ctx=ctx_ref[...].reshape(R,D)
    fs=x_ref[...].reshape(R,D)+(dg(ctx,wo_ref[...],NT)+vec_ref[0:1,:])
    z1,r1=stats(fs)
    z1_scr[slot]=z1
    fn=z1*vec_ref[1:2,:]+vec_ref[2:3,:]
    nl=fn.astype(BF)
    nl_scr[...]=nl.reshape(nl_scr.shape)
    def body(f,acc):
        o=pl.multiple_of(f*FC,FC)
        u=dg(nl_scr[...].reshape(R,D),wu_ref[:,pl.ds(o,FC)],NN)+bup_ref[:,pl.ds(o,FC)]
        phi=0.5*(1.0+lax.erf(u*(2.0**-0.5)))
        a=(u*phi).astype(BF)
        act_scr[:,:,pl.ds(o,FC)]=a.reshape(2,R//2,FC)
        gp_scr[slot,:,pl.ds(o,FC)]=phi+u*(jnp.exp(u*u*-0.5)*0.3989422804014327)
        return acc+dg(a,wd_ref[:,pl.ds(o,FC)],NT)
    acc=lax.fori_loop(0,FF//FC,body,fn+vec_ref[3:4,:])
    z2,r2=stats(acc)
    z2_scr[slot]=z2
    r_scr[slot,:,0:1]=r1
    r_scr[slot,:,1:2]=r2
    out_ref[...]=(z2*vec_ref[4:5,:]).reshape(out_ref.shape)


def lnb(u,z,r):
    return r*(u-jnp.mean(u,axis=-1,keepdims=True)-z*jnp.mean(u*z,axis=-1,keepdims=True))


def bwd_tile(slot, ds_ref, cot_ref, wo_ref, wu_ref, wd_ref, vec_ref, dfs_ref, dctx_ref, gv_ref, gbu_ref, dl_scr, ul_scr, al_scr, gp_scr, z1_scr, z2_scr, r_scr, R):
    D=wu_ref.shape[0]; FF=wu_ref.shape[1]; Rh=R//2
    r1=r_scr[slot,:,0:1]; r2=r_scr[slot,:,1:2]
    z2=z2_scr[slot]
    do=cot_ref[...].reshape(R,D)
    ri=lax.broadcasted_iota(jnp.int32,(R,1),0)
    coef=jnp.where(ri==0,ds_ref[0:1,0:1],0.0)+jnp.where(ri==Rh,ds_ref[1:2,0:1],0.0)
    do=do+coef*vec_ref[5:6,:]
    gv_ref[4:5,:]+=jnp.sum(do*z2,axis=0,keepdims=True)
    gv_ref[5:6,:]+=jnp.sum(coef*(z2*vec_ref[4:5,:]),axis=0,keepdims=True)
    d2=lnb(do*vec_ref[4:5,:],z2,r2)
    dl=d2.astype(BF)
    dl_scr[...]=dl.reshape(dl_scr.shape)
    gv_ref[3:4,:]+=jnp.sum(dl.astype(F32),axis=0,keepdims=True)
    def body(f,acc):
        o=pl.multiple_of(f*FC,FC)
        da=dg(dl_scr[...].reshape(R,D),wd_ref[:,pl.ds(o,FC)],NN)
        ul=(da*gp_scr[slot,:,pl.ds(o,FC)]).astype(BF)
        ul_scr[:,:,pl.ds(o,FC)]=ul.reshape(2,R//2,FC)
        gbu_ref[:,pl.ds(o,FC)]+=jnp.sum(ul.astype(F32),axis=0,keepdims=True)
        return acc+dg(ul,wu_ref[:,pl.ds(o,FC)],NT)
    d1=lax.fori_loop(0,FF//FC,body,d2)
    z1=z1_scr[slot]
    gv_ref[1:2,:]+=jnp.sum(d1*z1,axis=0,keepdims=True)
    gv_ref[2:3,:]+=jnp.sum(d1,axis=0,keepdims=True)
    dfs=lnb(d1*vec_ref[1:2,:],z1,r1)
    dfs_ref[...]=dfs.reshape(dfs_ref.shape)
    al=dfs.astype(BF)
    al_scr[...]=al.reshape(al_scr.shape)
    gv_ref[0:1,:]+=jnp.sum(al.astype(F32),axis=0,keepdims=True)
    dctx_ref[...]=dg(al,wo_ref[...],NN).astype(BF).reshape(dctx_ref.shape)


class Geo:
    def __init__(g, C, Q):
        g.C=C; g.Q=Q; g.nx=Q//2; g.nz=min(4,C); g.ny=C//g.nz
        c=lax.axis_index("cand"); q=lax.axis_index("query")
        g.z=c//g.ny; g.y=lax.rem(c,g.ny); g.x=q//2; g.k=lax.rem(q,2)
    def dev(g,z,y,x,k): return {"cand":z*g.ny+y,"query":x*2+k}


def mo(v,n): return pl.multiple_of(v,n)


def barrier(g, peers):
    b=pltpu.get_barrier_semaphore()
    for p in peers: pl.semaphore_signal(b,inc=1,device_id=p,device_id_type=MESH)
    pl.semaphore_wait(b,len(peers))


class RS:
    def __init__(s, g, refs, bufs, ss, rs):
        s.g, s.refs, s.bufs, s.ss, s.rs = g, refs, bufs, ss, rs
        s.partner = g.dev(g.z, g.y, g.x, 1 - g.k)
        s.pend = []
    def dims(s, n): return [NR[d] for d in RORD[n]]
    def own(s, n, rel, k):
        g = s.g
        r = dict(zip(RORD[n], rel))
        return rs_slice(g, n, s.refs, jnp.bitwise_xor(g.z, r["z"]), 1 - g.y if r["y"] else g.y, 1 - g.x if r["x"] else g.x, k)
    def near(s, d, r):
        g = s.g
        return g.dev(jnp.bitwise_xor(g.z, r) if d == "z" else g.z, 1 - g.y if d == "y" else g.y, 1 - g.x if d == "x" else g.x, g.k)
    def copy(s, src, dst, n, i, dev):
        pi = RPIECES.index(n)
        return pltpu.make_async_remote_copy(src, dst, s.ss.at[pi, i], s.rs.at[pi, i], device_id=dev, device_id_type=MESH)
    def c0(s, n, r1, r2, r3):
        _, n2, n3 = s.dims(n)
        return s.copy(s.own(n, (r1, r2, r3), 1 - s.g.k), s.bufs[n][0].at[r1, r2, r3], n, (r1 * n2 + r2) * n3 + r3, s.partner)
    def c1(s, n, r1, r2, r3):
        _, n2, n3 = s.dims(n)
        return s.copy(s.bufs[n][0].at[r1, r2, r3], s.bufs[n][1].at[r1 - 1, r2, r3], n, 16 + ((r1 - 1) * n2 + r2) * n3 + r3, s.near(RORD[n][0], r1))
    def c2(s, n, r2, r3):
        n1, n2, n3 = s.dims(n)
        return s.copy(s.bufs[n][0].at[0, r2, r3], s.bufs[n][2].at[r2 - 1, r3], n, 16 + (n1 - 1) * n2 * n3 + (r2 - 1) * n3 + r3, s.near(RORD[n][1], r2))
    def c3(s, n, r3):
        n1, n2, n3 = s.dims(n)
        return s.copy(s.bufs[n][0].at[0, 0, r3], s.bufs[n][3].at[r3 - 1], n, 16 + (n1 - 1) * n2 * n3 + (n2 - 1) * n3 + r3 - 1, s.near(RORD[n][2], r3))
    def go(s, f, *a):
        f(*a).start()
        s.pend.append(lambda: f(*a))
    def add(s, n, dst, srcs):
        rows, st = RSHP[n][0], RSHP[n][2]
        def body(i, _):
            o = pl.multiple_of(i * st, 16)
            dst[pl.ds(o, st), :] = functools.reduce(lambda a, b: a + b, [r[pl.ds(o, st), :].astype(F32) for r in srcs]).astype(dst.dtype)
            return 0
        lax.fori_loop(0, rows // st, body, 0)
    def part1(s, n, r2, r3):
        s.c0(n, 0, r2, r3).wait_recv()
        n1 = s.dims(n)[0]
        for r1 in range(1, n1):
            s.c1(n, r1, r2, r3).wait_recv()
        return [s.own(n, (0, r2, r3), s.g.k), s.bufs[n][0].at[0, r2, r3]] + [s.bufs[n][1].at[r1 - 1, r2, r3] for r1 in range(1, n1)]
    def part2(s, n, r3):
        t = s.part1(n, 0, r3)
        n2 = s.dims(n)[1]
        for r2 in range(1, n2):
            s.c2(n, r2, r3).wait_recv()
        return t + [s.bufs[n][2].at[r2 - 1, r3] for r2 in range(1, n2)]
    def s0(s, n, r1, r2, r3): s.go(s.c0, n, r1, r2, r3)
    def s1(s, n, r1, r2, r3):
        s.c0(n, r1, r2, r3).wait_recv()
        b = s.bufs[n][0].at[r1, r2, r3]
        s.add(n, b, [s.own(n, (r1, r2, r3), s.g.k), b])
        s.go(s.c1, n, r1, r2, r3)
    def s2(s, n, r2, r3):
        s.add(n, s.bufs[n][0].at[0, r2, r3], s.part1(n, r2, r3))
        s.go(s.c2, n, r2, r3)
    def s3(s, n, r3):
        s.add(n, s.bufs[n][0].at[0, 0, r3], s.part2(n, r3))
        s.go(s.c3, n, r3)
    def fin(s, n, dst):
        t = s.part2(n, 0)
        n3 = s.dims(n)[2]
        for r3 in range(1, n3):
            s.c3(n, r3).wait_recv()
        s.add(n, dst, t + [s.bufs[n][3].at[r3 - 1] for r3 in range(1, n3)])
    def ev(s, e): getattr(s, e[0])(*e[1:])
    def drain(s):
        for c in s.pend: c().wait_send()


def rs_slice(g, n, refs, z, y, x, k):
    wq, wo, wu, wd = refs
    c = z * g.ny + y
    q = x * 2 + k
    if n in QROW:
        return wq.at[pl.ds(mo(c * 288 + k * 144 + QROW[n], 16), RSHP[n][0]), pl.ds(mo(x * 384, 128), 384)]
    if n == "o": return wo.at[pl.ds(mo(c * 96 + k * 48, 16), 48), pl.ds(mo(x * 384, 128), 384)]
    if n == "u": return wu.at[pl.ds(mo(q * 192, 16), 192), pl.ds(mo(c * 384, 128), 384)]
    if n == "d": return wd.at[pl.ds(mo(c * 96, 16), 96), pl.ds(mo(q * 768, 128), 768)]


def rs_bufs():
    out = []
    for n in RPIECES:
        n1, n2, n3 = [NR[d] for d in RORD[n]]
        sh = RSHP[n][:2]
        out += [pltpu.VMEM((n1, n2, n3) + sh, BF), pltpu.VMEM((n1 - 1, n2, n3) + sh, BF), pltpu.VMEM((n2 - 1, n3) + sh, BF), pltpu.VMEM((n3 - 1,) + sh, BF)]
    return out


def attn_fwd_kernel(len_ref, x_ref, w_ref, bias_ref, tab_ref, bk_ref, bkf_ref, xlow_ref, qkv_ref, ctx_ref, lse_ref, relf_ref, rel_ref, bias_scr):
    S, D = x_ref.shape[1:]
    for m in range(2):
        xlow_ref[m*S:(m+1)*S,:]=x_ref[m].astype(BF)
    qkv_proj(w_ref, bias_ref, xlow_ref, qkv_ref, {})
    rel_rows(tab_ref, bk_ref, rel_ref)
    rel_rows(tab_ref, bkf_ref, relf_ref)
    attn_fwd(len_ref, qkv_ref, rel_ref, ctx_ref, lse_ref, bias_scr, S, D, {})


class AG:
    def __init__(s, g, own, refs, ss, rs, cs, cr):
        s.g, s.own_, s.refs, s.ss, s.rs, s.cs, s.cr = g, own, refs, ss, rs, cs, cr
        s.partner = g.dev(g.z, g.y, g.x, 1 - g.k)
        s.pend = []
        s.got = set()
    def dst(s, n, rel, k):
        g = s.g
        r = dict(zip(RORD[n], rel))
        return rs_slice(g, n, s.refs, jnp.bitwise_xor(g.z, r["z"]), 1 - g.y if r["y"] else g.y, 1 - g.x if r["x"] else g.x, k)
    def idx(s, n, rel):
        _, n2, n3 = [NR[d] for d in RORD[n]]
        return (rel[0] * n2 + rel[1]) * n3 + rel[2]
    def src(s, n, rel): return s.own_(n) if rel == (0, 0, 0) else s.dst(n, rel, s.g.k)
    def near(s, d, r):
        g = s.g
        return g.dev(jnp.bitwise_xor(g.z, r) if d == "z" else g.z, 1 - g.y if d == "y" else g.y, 1 - g.x if d == "x" else g.x, g.k)
    def link(s, n, rel, d, k):
        new = tuple(k if a == d else r for a, r in zip(RORD[n], rel))
        pi, i = RPIECES.index(n), s.idx(n, new)
        return pltpu.make_async_remote_copy(s.src(n, rel), s.dst(n, rel, s.g.k), s.ss.at[pi, i], s.rs.at[pi, i], device_id=s.near(d, k), device_id_type=MESH)
    def core(s, n, rel):
        pi, i = RPIECES.index(n), s.idx(n, rel)
        return pltpu.make_async_remote_copy(s.src(n, rel), s.dst(n, rel, s.g.k), s.cs.at[pi, i], s.cr.at[pi, i], device_id=s.partner, device_id_type=MESH)
    def got_core(s, n, rel):
        pi, i = RPIECES.index(n), s.idx(n, rel)
        t = s.dst(n, rel, 1 - s.g.k)
        pltpu.make_async_remote_copy(t, t, s.cs.at[pi, i], s.cr.at[pi, i], device_id=s.partner, device_id_type=MESH).wait_recv()
    def go(s, f, *a):
        f(*a).start()
        s.pend.append(lambda: f(*a))
    def ev(s, e):
        n, rel, outs = e
        if rel != (0, 0, 0):
            t = s.dst(n, rel, s.g.k)
            pi, i = RPIECES.index(n), s.idx(n, rel)
            pltpu.make_async_remote_copy(t, t, s.ss.at[pi, i], s.rs.at[pi, i], device_id=s.partner, device_id_type=MESH).wait_recv()
        for d, k in outs:
            if d == "k": s.go(s.core, n, rel)
            else: s.go(s.link, n, rel, d, k)
    def rels(s, n):
        n1, n2, n3 = [NR[d] for d in RORD[n]]
        return [(a, b, c) for a in range(n1) for b in range(n2) for c in range(n3)]
    def drain(s):
        for c in s.pend: c().wait_send()


def front_kernel(len_ref, x_h, wqf_ref, wof_ref, wuf_ref, wdf_ref, v_ref, bk_ref, bkf_ref, wq_o, wo, wu, wd, vec_o, bup_o, xlow_o, qkv_o, ctx_ref, lse_ref, relf_ref,
                 x_v, xlow, qkv, wq, own_p, got_p, h_scr, u_bf, d_bf, vall, tab, rel, qb, bias_scr, ss, rs, cs, cr, vss, vrs, ps, ls, *, C, Q):
    g = Geo(C, Q)
    S, D = x_h.shape[1:]
    q_ = lax.axis_index("query")
    peers = [{"query": lax.rem(q_ + j, Q)} for j in range(1, Q)] + [g.dev(g.z, 1 - g.y, g.x, g.k)] + [g.dev(jnp.bitwise_xor(g.z, i), g.y, g.x, g.k) for i in range(1, g.nz)]
    bar = pltpu.get_barrier_semaphore()
    for p in peers:
        pl.semaphore_signal(bar, inc=1, device_id=p, device_id_type=MESH)
    xc = pltpu.make_async_copy(x_h, x_v, ls.at[0])
    xc.start()
    k = g.k

    def turn(w):
        n = w.shape[1]
        eye = (lax.broadcasted_iota(jnp.int32, (n, n), 0) == lax.broadcasted_iota(jnp.int32, (n, n), 1)).astype(BF)
        return dg(eye, w.astype(BF), NT).astype(BF)
    a, b = turn(wqf_ref[...]), turn(wof_ref[...])
    ha, hb = a.shape[0] // 2, b.shape[0] // 2
    for i in range(2):
        own_p[i, 0:ha, :] = a[i * ha:(i + 1) * ha]
        own_p[i, ha:ha + hb, :] = b[i * hb:(i + 1) * hb]
    d_bf[...] = turn(wdf_ref[...])
    u_bf[...] = wuf_ref[...].astype(BF)
    pl.semaphore_wait(bar, len(peers))
    pc = pltpu.make_async_remote_copy(own_p.at[1 - k], got_p, ps.at[0], ps.at[1], device_id=g.dev(g.z, g.y, g.x, 1 - k), device_id_type=MESH)
    pc.start()
    vcs = []
    for j in range(1, Q):
        c = pltpu.make_async_remote_copy(v_ref, vall.at[q_], vss.at[j - 1], vrs.at[j - 1], device_id={"query": lax.rem(q_ + j, Q)}, device_id_type=MESH)
        c.start()
        vcs.append(c)
    vall[q_] = v_ref[...]

    def own(n):
        if n == "u": return u_bf
        if n == "d": return d_bf
        return h_scr.at[pl.ds(QROW.get(n, 144), RSHP[n][0])]
    A = AG(g, own, (wq, wo, wu, wd), ss, rs, cs, cr)
    loc = [pltpu.make_async_copy(own(n), A.dst(n, (0, 0, 0), k), ls.at[1 + i]) for i, n in enumerate(RPIECES)]

    def after(name):
        for e in AGSLOTS.get(name, []):
            A.ev(e)
    after("p")
    loc[0].start()
    loc[1].start()
    pc.wait()
    t, r = own_p[k], got_p[...]
    @pl.when(k == 0)
    def _(): h_scr[...] = jnp.concatenate([t, r], axis=1)
    @pl.when(k == 1)
    def _(): h_scr[...] = jnp.concatenate([r, t], axis=1)
    for c in loc[2:]:
        c.start()
    for e in AGSLOTS["w"][:AGEARLY]:
        A.ev(e)
    xc.wait()
    for m in range(2):
        xlow[m*S:(m+1)*S,:]=x_v[m].astype(BF)
    xo = pltpu.make_async_copy(xlow, xlow_o, ls.at[7])
    xo.start()
    for e in AGSLOTS["w"][AGEARLY:AGMID]:
        A.ev(e)
    for c in vcs:
        c.wait()
    dq, bq = D // Q, tab.shape[1] // Q
    fq = bup_o.shape[1] // Q
    qb[...] = jnp.zeros_like(qb)
    vec_o[...] = jnp.zeros_like(vec_o)
    for q in range(Q):
        lo, hi = q * dq, (q + 1) * dq
        qb[:, lo:hi] = vall[q, 0:1, 0:dq]
        qb[:, 2 * D + lo:2 * D + hi] = vall[q, 1:2, 0:dq]
        vec_o[0:6, lo:hi] = vall[q, 2:8, 0:dq]
        for j in range(fq // 256):
            bup_o[:, q * fq + j * 256:q * fq + (j + 1) * 256] = vall[q, 8 + j:9 + j, :]
        tab[:, q * bq:(q + 1) * bq] = vall[q, 16:32, 0:bq]
    rel_rows(tab, bk_ref, rel)
    rel_rows(tab, bkf_ref, relf_ref)
    for e in AGSLOTS["w"][AGMID:]:
        A.ev(e)
    for i, n in enumerate(RPIECES):
        if n in QROW:
            loc[i].wait()
            for r in A.rels(n):
                A.got_core(n, r)
    qkv_proj(wq, qb, xlow, qkv, {i: [functools.partial(A.ev, e) for e in AGSLOTS.get(f"n{i}", [])] for i in range(3 * D // 256)})
    wc = pltpu.make_async_copy(wq, wq_o, ls.at[8])
    qc = pltpu.make_async_copy(qkv, qkv_o, ls.at[9])
    wc.start()
    qc.start()
    attn_fwd(len_ref, qkv, rel, ctx_ref, lse_ref, bias_scr, S, D, {i: [functools.partial(A.ev, e) for e in AGSLOTS.get(f"t{i}", [])] for i in range(D // 64)})
    after("tail")
    for c in (xo, wc, qc):
        c.wait()
    for i, n in enumerate(RPIECES):
        if n not in QROW:
            loc[i].wait()
            for r in A.rels(n):
                A.got_core(n, r)
    A.drain()


def ffn_kernel(lab_ref, x_ref, ctx_ref, cot_ref, wo_ref, wu_ref, wd_ref, vec_ref, bup_ref,
               out_ref, dfs_ref, dctx_ref, nl_ref, act_ref, dl_ref, al_ref, ul_ref, gv_ref, gbu_ref, loss_ref,
               gp_scr, z1_scr, z2_scr, r_scr,
               ds_scr, sc_snd, sc_all, sss, ssr, *, T, R, C, Q):
    i = pl.program_id(0)
    D, FF = wu_ref.shape
    cid = lax.axis_index("cand")

    def score_copy(j):
        return pltpu.make_async_remote_copy(sc_snd, sc_all.at[cid], sss.at[j - 1], ssr.at[j - 1], device_id={"cand": lax.rem(cid + j, C)}, device_id_type=MESH)

    @pl.when(i == 0)
    def _():
        b = pltpu.get_barrier_semaphore()
        for j in range(1, C):
            pl.semaphore_signal(b, inc=1, device_id={"cand": lax.rem(cid + j, C)}, device_id_type=MESH)
        pl.semaphore_wait(b, C - 1)
        gv_ref[...] = jnp.zeros_like(gv_ref)
        gbu_ref[...] = jnp.zeros_like(gbu_ref)
        ds_scr[...] = jnp.zeros_like(ds_scr)
        sc_snd[...] = jnp.zeros_like(sc_snd)

    @pl.when(i < T)
    def _():
        fwd_tile(jnp.minimum(i, 1), x_ref, ctx_ref, wo_ref, wu_ref, wd_ref, vec_ref, bup_ref, out_ref, nl_ref, act_ref, gp_scr, z1_scr, z2_scr, r_scr, R)

    @pl.when(i == 0)
    def _():
        for m in range(2):
            sc = jnp.sum(out_ref[m, 0:1, :] * vec_ref[5:6, :], axis=1, keepdims=True)
            sc_snd[m:m + 1, :] = jnp.broadcast_to(sc, (1, 128))
        sc_all[cid] = sc_snd[...]
        for j in range(1, C):
            score_copy(j).start()

    @pl.when(i == T)
    def _():
        for j in range(1, C):
            score_copy(j).wait()
        total = jnp.zeros((1, 128), F32)
        own = sc_snd[...]
        for m in range(2):
            rows = [sc_all[j, m:m + 1, :] for j in range(C)]
            peak = functools.reduce(jnp.maximum, rows)
            lse = peak + jnp.log(functools.reduce(lambda a, b: a + b, [jnp.exp(r - peak) for r in rows]))
            lab = lab_ref[m]
            picked = functools.reduce(lambda a, b: a + b, [jnp.where(lab == j, r, 0.0) for j, r in enumerate(rows)])
            total = total + (lse - picked)
            ds_scr[m:m + 1, :] = (jnp.exp(own[m:m + 1, :] - lse) - jnp.where(lab == cid, 1.0, 0.0)) * (1.0 / Q)
        loss_ref[...] = jnp.broadcast_to(jnp.where(cid == 0, total * (1.0 / Q), 0.0), (8, 128))

    @pl.when((i >= 1) & (i <= T))
    def _():
        t = lax.rem(i, T)
        bwd_tile(jnp.minimum(t, 1), ds_scr, cot_ref, wo_ref, wu_ref, wd_ref, vec_ref, dfs_ref, dctx_ref, gv_ref, gbu_ref, dl_ref, ul_ref, al_ref, gp_scr, z1_scr, z2_scr, r_scr, R)


def back_kernel(len_ref, nl_h, dl_h, al_h, ctx_h, act_h, ul_h, qkv_h, dctx_h, xlow_h, wq_h, dfs_h, lse_ref, relf, bkf_ref, gv_ref, gbu_ref, loss_ref,
                *rest, C, Q, fast):
    if fast:
        ig_h, p_out, u_out, d_out, v_out = rest[:5]
        scr = rest[5:]
    else:
        ig_h, gq_o, go_o, gu_o, gd_o, gb_o, gtab_o = rest[:7]
        scr = rest[7:]
    (nl, dl, al, ctx, ch, qkv, dctx, xlow, wq, dfs, igt, gq, go, gu, gd, drelf, bias_scr, acc_scr, gb, gtab, ls, cs_, os_) = scr[:23]
    NS, D = nl.shape
    FF = gu.shape[1]
    S = NS // 2
    NZ = FF // 768
    load = lambda i, src, dst: pltpu.make_async_copy(src, dst, ls.at[i])
    big = [load(0, nl_h, nl), load(1, dl_h, dl), load(2, al_h, al), load(3, ctx_h, ctx), load(4, qkv_h, qkv), load(5, dctx_h, dctx),
           load(6, xlow_h, xlow), load(7, wq_h, wq), load(8, dfs_h, dfs)]
    if fast:
        g = Geo(C, Q)
        seq = [(ul_h, jnp.bitwise_xor(g.z, zi)) for zi in (3, 2, 1, 0)]
        qorder = [(1, 1), (1, 0), (0, 1), (0, 0)]
        seq += [(act_h, (1 - g.x if dx else g.x) * 2 + (1 - g.k if dk else g.k)) for dx, dk in qorder]
    else:
        seq = [(ul_h, i) for i in range(NZ)] + [(act_h, i) for i in range(NZ)]
    off = lambda i: pl.multiple_of(seq[i][1] * 768, 128)
    chunk = lambda i: pltpu.make_async_copy(seq[i][0].at[:, pl.ds(off(i), 768)], ch.at[i % 2], cs_.at[i % 2])
    if fast:
        peers = [{"query": lax.rem(lax.axis_index("query") + j, Q)} for j in range(1, Q)] + [{"cand": lax.rem(lax.axis_index("cand") + j, C)} for j in range(1, C)]
        bar = pltpu.get_barrier_semaphore()
        for p in peers:
            pl.semaphore_signal(bar, inc=1, device_id=p, device_id_type=MESH)
    for c in (big[2], big[3], big[0], chunk(0), chunk(1), big[1]):
        c.start()
    if fast:
        bufs = {n: scr[23 + 4 * i:27 + 4 * i] for i, n in enumerate(RPIECES)}
        h_scr, e_snd, e_rcv, vb0, va, vs, vb, ss, rs, es, qs, qr, cs, cr = scr[23 + NB:]
        R = RS(g, (gq, go, gu, gd), bufs, ss, rs)
        c_ = lax.axis_index("cand")
        q_ = lax.axis_index("query")

    def after(name):
        if fast:
            for e in FIRST.get(name, []) + SLOTS.get(name, []):
                R.ev(e)
    big[2].wait()
    big[3].wait()
    go[...] = dg(al[...], ctx[...], TN).astype(BF)
    big[0].wait()
    for i in range(NZ):
        chunk(i).wait()
        gu[:, pl.ds(off(i), 768)] = dg(nl[...], ch[i % 2], TN).astype(BF)
        chunk(i + 2).start()
        if i == 0:
            if fast:
                pl.semaphore_wait(bar, len(peers))
            after("o")
        after(f"u{i}")
    big[1].wait()
    for i in range(NZ, 2 * NZ):
        chunk(i).wait()
        gd[:, pl.ds(off(i), 768)] = dg(dl[...], ch[i % 2], TN).astype(BF)
        if i + 2 < 2 * NZ:
            chunk(i + 2).start()
        if i == NZ:
            big[4].start()
            big[5].start()
        if i == NZ + 2:
            for c in big[6:]:
                c.start()
        after(f"d{i - NZ}")
    slots = {}
    if fast:
        for i in range(2 * (D // 128)):
            slots[i] = [functools.partial(R.ev, e) for e in SLOTS.get(f"t{i}", [])]
    drelf[...] = jnp.zeros_like(drelf)
    big[4].wait()
    big[5].wait()
    attn_bwd(len_ref, qkv, dctx, lse_ref, relf, drelf, bias_scr, acc_scr, S, D, slots)
    big[6].wait()

    def b1(n, _):
        o = pl.multiple_of(n * 256, 256)
        t = qkv[:, pl.ds(o, 256)]
        gq[pl.ds(o, 256), :] = dg(t, xlow[...], TN).astype(BF)
        gb[:, pl.ds(o, 256)] = jnp.sum(t.astype(F32), axis=0, keepdims=True)
        return 0
    for i in range(3):
        lax.fori_loop(i * D // 256, (i + 1) * D // 256, b1, 0)
        after(f"g{i}")
    nb, nn = gtab.shape[1], bkf_ref.shape[1]
    hot = (lax.broadcasted_iota(jnp.int32, (nb, nn), 0) == bkf_ref[...]).astype(F32)
    gtab[...] = dg(drelf[...], hot, NT, lax.Precision.HIGHEST)
    if fast:
        dq, fq, bq = D // Q, FF // Q, nb // Q
        vb0[...] = jnp.zeros_like(vb0)
        for q in range(Q):
            lo = slice(q * dq, (q + 1) * dq)
            vb0[q, 0:1, 0:dq] = gb[:, q * dq:(q + 1) * dq]
            vb0[q, 1:2, 0:dq] = gb[:, 2 * D + q * dq:2 * D + (q + 1) * dq]
            vb0[q, 2:8, 0:dq] = gv_ref[0:6, lo]
            for j in range(fq // 256):
                vb0[q, 8 + j:9 + j, :] = gbu_ref[:, q * fq + j * 256:q * fq + (j + 1) * 256]
            vb0[q, 11:12, 0:128] = loss_ref[0:1, :]
            vb0[q, 16:32, 0:bq] = gtab[:, q * bq:(q + 1) * bq]
        vq = []
        for j in range(1, Q):
            qq = lax.rem(q_ + j, Q)
            c = pltpu.make_async_remote_copy(vb0.at[qq], va.at[q_], qs.at[j - 1], qr.at[j - 1], device_id={"query": qq}, device_id_type=MESH)
            c.start()
            vq.append(c)
        va[q_] = vb0[q_]
        after("v")
    big[7].wait()
    big[8].wait()
    steps = NS // 256
    outc = lambda r: pltpu.make_async_copy(igt.at[r % 2], ig_h.at[pl.ds(r * 256, 256), :], os_.at[r % 2])
    for r in range(steps):
        if r >= 2:
            outc(r - 2).wait()
        igt[r % 2] = dfs[r * 256:(r + 1) * 256, :] + dg(qkv[r * 256:(r + 1) * 256, :], wq[...], NN)
        outc(r).start()
        after(f"i{r}")
    for r in range(max(0, steps - 2), steps):
        outc(r).wait()
    if fast:
        for c in vq:
            c.wait()
        t = functools.reduce(lambda a, b: a + b, [va[j] for j in range(Q)])
        vs[...] = t
        vb[c_] = t
        vc = []
        for j in range(1, C):
            c = pltpu.make_async_remote_copy(vs, vb.at[c_], cs.at[j - 1], cr.at[j - 1], device_id={"cand": lax.rem(c_ + j, C)}, device_id_type=MESH)
            c.start()
            vc.append(c)
        R.fin("u", u_out)
        R.fin("d", d_out)
        for e in TAIL:
            R.ev(e)
        for n in ("o", "qz", "qb", "qa"):
            R.fin(n, h_scr.at[pl.ds(QROW.get(n, 144), RSHP[n][0])])
        k = g.k
        lo = h_scr[:, 0:192]
        hi = h_scr[:, 192:384]
        e_snd[...] = jnp.where(k == 0, hi, lo)
        c = pltpu.make_async_remote_copy(e_snd, e_rcv, es.at[0], es.at[1], device_id=R.partner, device_id_type=MESH)
        c.start()
        p_out[k] = jnp.where(k == 0, lo, hi)
        c.wait()
        p_out[1 - k] = e_rcv[...]
        for c in vc:
            c.wait()
        v_out[...] = functools.reduce(lambda a, b: a + b, [vb[j] for j in range(C)])
        R.drain()
    else:
        gq_o[...] = gq[...]
        go_o[...] = go[...]
        gu_o[...] = gu[...]
        gd_o[...] = gd[...]
        gb_o[...] = gb[...]
        gtab_o[...] = gtab[...]


def sds(shape, dtype=F32):
    return jax.ShapeDtypeStruct(shape, dtype)


def back_scratch(fast, C, Q, NS=1024, S=512, D=768, FF=3072, NBK=256):
    v = pltpu.VMEM
    dma = pltpu.SemaphoreType.DMA
    scr = [v((NS, D), BF)] * 4 + [v((2, NS, 768), BF), v((NS, 3 * D), BF), v((NS, D), BF), v((NS, D), BF), v((3 * D, D), BF), v((NS, D), F32), v((2, 256, D), F32),
                                  v((3 * D, D), BF), v((D, D), BF), v((D, FF), BF), v((D, FF), BF), v((16, 2 * S), F32),
                                  v((2, S, S), F32), v((2, S, S), F32), v((1, 3 * D), F32), v((16, NBK), F32), dma((9,)), dma((2,)), dma((2,))]
    if fast:
        scr += rs_bufs() + [v((192, 384), F32), v((192, 192), F32), v((192, 192), F32), v((Q, 32, 256), F32), v((Q, 32, 256), F32), v((32, 256), F32), v((C, 32, 256), F32),
                            dma((len(RPIECES), 31)), dma((len(RPIECES), 31)), dma((2,)), dma((Q,)), dma((Q,)), dma((C,)), dma((C,))]
    return scr


def body(hidden_in, out_cotangent, lengths, labels, buckets, w_qkv, w_out, w_up, w_down, bias_q, bias_v, bias_out,
         norm1_gain, norm1_bias, bias_up, bias_down, norm2_gain, score_vector, rel_table):
    Q = lax.axis_size("query")
    C = lax.axis_size("cand")
    micro = hidden_in.shape[0]
    S, D = hidden_in.shape[3:]
    FF = w_up.shape[1] * C
    NBK = rel_table.shape[0] * Q
    dq, fq, bq = D // Q, FF // Q, NBK // Q
    fast = Q == 4 and C == 8 and D == 768 and FF == 3072
    x = hidden_in.reshape(micro, S, D)
    cot = out_cotangent.reshape(micro, S, D)
    lens = lengths.reshape(micro)
    labs = labels.reshape(micro)
    NS = micro * S
    bk = jnp.pad(buckets, (0, 1), constant_values=-1)[None, :]
    bkf = jnp.pad(buckets[::-1], (0, 1), constant_values=-1)[None, :]
    v = pltpu.VMEM
    dma = pltpu.SemaphoreType.DMA
    eight = jnp.stack([bias_q, bias_v, bias_out, norm1_gain, norm1_bias, bias_down, norm2_gain, score_vector])
    if fast:
        wide = lambda t, rows: jnp.pad(t, ((0, rows - t.shape[0]), (0, 256 - t.shape[1])))
        vb = jnp.concatenate([wide(eight, 8), wide(bias_up.reshape(-1, 256), 8), wide(rel_table.T, 16)], axis=0)
        np_ = len(RPIECES)
        wq, wo, wu, wd, vec, bup, xlow, qkv, ctx, lse, relf = pl.pallas_call(
            functools.partial(front_kernel, C=C, Q=Q), in_specs=[SM, ANY] + [VM] * 7, out_specs=[ANY] * 4 + [VM] * 2 + [ANY] * 2 + [VM] * 3,
            out_shape=[sds((3 * D, D), BF), sds((D, D), BF), sds((D, FF), BF), sds((D, FF), BF), sds((8, D)), sds((1, FF)), sds((NS, D), BF), sds((NS, 3 * D), BF),
                       sds((NS, D), BF), sds((micro, 16, S)), sds((16, 2 * S))],
            scratch_shapes=[v((micro, S, D), F32), v((NS, D), BF), v((NS, 3 * D), BF), v((3 * D, D), BF), v((2, 192, 192), BF), v((192, 192), BF), v((192, 384), BF),
                            v((192, 384), BF), v((96, 768), BF), v((Q, 32, 256), F32), v((16, NBK), F32), v((16, 2 * S), F32), v((1, 3 * D), F32), v((2, S, S), F32)]
            + [dma((np_, 16))] * 4 + [dma((Q,))] * 2 + [dma((2,)), dma((10,))],
            compiler_params=pltpu.CompilerParams(collective_id=0, has_side_effects=True, vmem_limit_bytes=40 * 2**20),
        )(lens, x, w_qkv, w_out, w_up, w_down, vb, bk, bkf)
    else:
        def gather(w):
            part = lax.all_gather(w.astype(BF), "query", axis=0, tiled=True)
            return lax.all_gather(part, "cand", axis=1, tiled=True)
        wq, wo, wu, wd = gather(w_qkv).T, gather(w_out).T, gather(w_up), gather(w_down).T
        vall = lax.all_gather(jnp.concatenate([eight.reshape(-1), bias_up, rel_table.reshape(-1)]), "query", axis=0, tiled=False)
        vecs = vall[:, :8 * dq].reshape(Q, 8, dq).transpose(1, 0, 2).reshape(8, D)
        bup = vall[:, 8 * dq:8 * dq + fq].reshape(1, FF)
        tab = jnp.pad(vall[:, 8 * dq + fq:].reshape(NBK, HEADS).T, ((0, 4), (0, 0)))
        qkv_bias = jnp.concatenate([vecs[0:1], jnp.zeros((1, D), F32), vecs[1:2]], axis=1)
        vec = jnp.concatenate([vecs[2:], jnp.zeros((2, D), F32)], axis=0)
        xlow, qkv, ctx, lse, relf = pl.pallas_call(
            attn_fwd_kernel, in_specs=[SM] + [VM] * 6, out_specs=[VM] * 5,
            out_shape=[sds((NS, D), BF), sds((NS, 3 * D), BF), sds((NS, D), BF), sds((micro, 16, S)), sds((16, 2 * S))],
            scratch_shapes=[v((16, 2 * S), F32), v((2, S, S), F32)],
            compiler_params=pltpu.CompilerParams(vmem_limit_bytes=60 * 2**20))(lens, x, wq, qkv_bias, tab, bk, bkf)
    R = 256
    Rh, T = R // micro, NS // R
    tb = lambda im, n=D: pl.BlockSpec((micro, Rh, n), im)
    fw = lambda i: (0, jnp.minimum(i, T - 1), 0)
    bw = lambda i: (0, lax.rem(jnp.maximum(i, 1), T), 0)
    tok = lambda n, dt=BF: sds((micro, S, n), dt)
    out, dfs, dctx, nl, act, dl, al, ul, gv, gbu, lossv = pl.pallas_call(
        functools.partial(ffn_kernel, T=T, R=R, C=C, Q=Q), grid=(T + 1,),
        in_specs=[SM, tb(fw), tb(fw), tb(bw)] + [VM] * 5, out_specs=[tb(fw), tb(bw), tb(bw), tb(fw), tb(fw, FF), tb(bw), tb(bw), tb(bw, FF)] + [VM] * 3,
        out_shape=[tok(D, F32), tok(D, F32), tok(D), tok(D), tok(FF), tok(D), tok(D), tok(FF), sds((8, D)), sds((1, FF)), sds((8, 128))],
        scratch_shapes=[pltpu.VMEM((2, R, FF), F32), pltpu.VMEM((2, R, D), F32), pltpu.VMEM((2, R, D), F32), pltpu.VMEM((2, R, 128), F32),
                        pltpu.VMEM((8, 128), F32), pltpu.VMEM((8, 128), F32), pltpu.VMEM((C, 8, 128), F32), pltpu.SemaphoreType.DMA((C,)), pltpu.SemaphoreType.DMA((C,))],
        compiler_params=pltpu.CompilerParams(collective_id=1, has_side_effects=True, vmem_limit_bytes=60 * 2**20),
    )(labs, x, ctx.reshape(micro, S, D), cot, wo, wu, wd, vec, bup)
    flat = lambda t: t.reshape(NS, t.shape[-1])
    gouts = [sds((2, 192, 192)), sds((192, 384)), sds((96, 768)), sds((32, 256))] if fast else \
        [sds((3 * D, D), BF), sds((D, D), BF), sds((D, FF), BF), sds((D, FF), BF), sds((1, 3 * D)), sds((16, NBK))]
    res = pl.pallas_call(
        functools.partial(back_kernel, C=C, Q=Q, fast=fast), in_specs=[SM] + [ANY] * 11 + [VM] * 6, out_specs=[ANY] + [VM] * len(gouts),
        out_shape=[sds((NS, D))] + gouts, scratch_shapes=back_scratch(fast, C, Q, NS, S, D, FF, NBK),
        compiler_params=pltpu.CompilerParams(collective_id=2 if fast else None, has_side_effects=True, vmem_limit_bytes=67043328),
    )(lens, flat(nl), flat(dl), flat(al), ctx, flat(act), flat(ul), qkv, flat(dctx), xlow, wq, flat(dfs), lse, relf, bkf, gv, gbu, lossv)
    ig = res[0]
    if fast:
        pg, ug, dng, vs = res[1:]
        ha = w_qkv.shape[1] // 2
        g_qkv = jnp.concatenate([pg[0, :ha], pg[1, :ha]], 0).T
        g_out = jnp.concatenate([pg[0, ha:], pg[1, ha:]], 0).T
        g_up, g_down = ug, dng.T
        small = [vs[i, :dq] for i in range(8)]
        g_bup = vs[8:8 + fq // 256].reshape(fq)
        g_tab = vs[16:16 + HEADS, :bq].T
        loss = vs[11, 0]
    else:
        def scatter(g):
            rows, cols = g.shape[0] // Q, g.shape[1] // C
            tiles = g.astype(F32).reshape(Q, rows, C, cols).transpose(2, 0, 1, 3).reshape(C * Q, rows, cols)
            return lax.psum_scatter(tiles, ("cand", "query"), scatter_dimension=0, tiled=True)[0]
        gq, go, gu, gd, gb, gtab = res[1:]
        g_qkv, g_out, g_up, g_down = scatter(gq.T), scatter(go.T), scatter(gu), scatter(gd.T)
        gvecs = jnp.concatenate([gb[:, :D], gb[:, 2 * D:], gv[:6]], axis=0)
        vg = jnp.concatenate([gvecs.reshape(8, Q, dq).transpose(1, 0, 2).reshape(Q, 8 * dq), gbu.reshape(Q, fq), gtab[:HEADS].T.reshape(Q, bq * HEADS),
                              jnp.broadcast_to(lossv[0:1, 0:1], (Q, 1))], axis=1)
        vg = jnp.pad(vg, ((0, 0), (0, -vg.shape[1] % 1024)))
        vs = lax.psum_scatter(lax.psum(vg, "cand"), "query", scatter_dimension=0, tiled=True)[0]
        small = [vs[i * dq:(i + 1) * dq] for i in range(8)]
        g_bup = vs[8 * dq:8 * dq + fq]
        g_tab = vs[8 * dq + fq:8 * dq + fq + bq * HEADS].reshape(bq, HEADS)
        loss = vs[8 * dq + fq + bq * HEADS]
    return (out.reshape(hidden_in.shape), ig.reshape(hidden_in.shape), g_qkv, g_out, g_up, g_down,
            small[0], small[1], small[2], small[3], small[4], g_bup, small[5], small[6], small[7], g_tab, loss)


def solution(mesh):
    seq, w, v = P(None, "query", "cand", None, None), P("query", "cand"), P("query")
    return jax.shard_map(
        body, mesh=mesh,
        in_specs=(seq, seq, P(None, "query", "cand"), P(None, "query"), P(), w, w, w, w) + (v,) * 9 + (P("query", None),),
        out_specs=(seq, seq, w, w, w, w) + (v,) * 9 + (P("query", None), P()),
        check_vma=False)
```

```python
import functools

import jax
import jax.numpy as jnp
from jax import lax
from jax.experimental import pallas as pl
from jax.experimental.pallas import tpu as pltpu
from jax.sharding import PartitionSpec as P

F32 = jnp.float32
BF = jnp.bfloat16
NT = (((1,), (1,)), ((), ()))
NN = (((1,), (0,)), ((), ()))
TN = (((0,), (0,)), ((), ()))
VM = pl.BlockSpec(memory_space=pltpu.VMEM)
SM = pl.BlockSpec(memory_space=pltpu.SMEM)
ANY = pl.BlockSpec(memory_space=pl.ANY)
MESH = pl.DeviceIdType.MESH
EPS = 1e-5
FC = 512
HEADS = 12
NR = {"x": 2, "y": 2, "z": 4}
RPIECES = ["u", "d", "o", "qa", "qb", "qz"]
RORD = {"u": "yxz", "d": "xyz", "o": "zyx", "qa": "yxz", "qb": "xyz", "qz": "zyx"}
RSHP = {"u": (192, 384, 48), "d": (96, 768, 48), "o": (48, 384, 48), "qa": (64, 384, 32), "qb": (64, 384, 32), "qz": (16, 384, 16)}
QROW = {"qa": 0, "qb": 64, "qz": 128}
NB = 4 * len(RPIECES)
AGSLOTS = {
    "p": [("u", (0, 0, 0), (("k", 0), ("x", 1), ("y", 1), ("z", 1))), ("d", (0, 0, 0), (("k", 0),))],
    "w": [("o", (0, 0, 0), (("y", 1),)), ("qa", (0, 0, 0), (("x", 1), ("y", 1), ("z", 1), ("z", 2), ("z", 3))), ("qb", (0, 0, 0), (("k", 0), ("x", 1), ("y", 1), ("z", 1), ("z", 2), ("z", 3))), ("qz", (0, 0, 0), (("x", 1), ("y", 1))), ("qa", (0, 0, 0), (("k", 0),)), ("qz", (0, 0, 0), (("k", 0),)), ("o", (0, 0, 0), (("k", 0),)), ("qz", (0, 0, 0), (("z", 1),)), ("o", (0, 0, 0), (("x", 1),)), ("qz", (0, 0, 0), (("z", 3),)), ("u", (0, 0, 1), (("x", 1), ("y", 1), ("k", 0))), ("u", (0, 1, 0), (("y", 1), ("k", 0))), ("u", (1, 0, 0), (("k", 0),)), ("qz", (0, 0, 1), (("y", 1), ("z", 3), ("z", 2), ("z", 1), ("k", 0))), ("qz", (0, 0, 0), (("z", 2),)), ("qb", (0, 0, 1), (("y", 1), ("x", 1), ("k", 0))), ("qb", (0, 1, 0), (("x", 1), ("k", 0))), ("qa", (0, 1, 0), (("y", 1), ("k", 0))), ("qz", (0, 1, 0), (("z", 3), ("z", 2), ("z", 1), ("k", 0))), ("qa", (1, 0, 0), (("k", 0),)), ("qb", (1, 0, 0), (("k", 0),)), ("qb", (0, 0, 3), (("y", 1), ("x", 1), ("k", 0))), ("qb", (0, 1, 1), (("x", 1), ("k", 0))), ("qb", (1, 1, 0), (("k", 0),)), ("o", (0, 0, 0), (("z", 1),)), ("qa", (0, 0, 1), (("x", 1), ("y", 1), ("k", 0))), ("u", (0, 0, 0), (("z", 3),)), ("o", (0, 0, 0), (("z", 3),)), ("qb", (1, 0, 1), (("k", 0),)), ("qa", (1, 1, 0), (("k", 0),)), ("qz", (0, 1, 1), (("z", 3), ("z", 2), ("z", 1), ("k", 0))), ("qa", (0, 0, 3), (("x", 1), ("y", 1), ("k", 0))), ("qa", (0, 1, 1), (("y", 1), ("k", 0))), ("qb", (0, 1, 3), (("x", 1), ("k", 0))), ("qa", (1, 0, 1), (("k", 0),)), ("qb", (1, 1, 1), (("k", 0),)), ("o", (0, 0, 0), (("z", 2),)), ("d", (0, 0, 0), (("x", 1),)), ("qb", (1, 0, 3), (("k", 0),)), ("qb", (0, 0, 2), (("y", 1), ("x", 1), ("k", 0))), ("qa", (0, 1, 3), (("y", 1), ("k", 0))), ("o", (0, 1, 0), (("z", 3), ("z", 2), ("z", 1), ("k", 0))), ("qa", (1, 1, 1), (("k", 0),)), ("qz", (1, 0, 0), (("k", 0),)), ("qz", (1, 1, 0), (("k", 0),)), ("o", (0, 0, 1), (("y", 1), ("z", 3), ("z", 2), ("z", 1), ("k", 0))), ("qa", (1, 0, 3), (("k", 0),)), ("qb", (1, 1, 3), (("k", 0),)), ("qa", (0, 0, 2), (("x", 1), ("y", 1), ("k", 0))), ("qz", (1, 0, 1), (("k", 0),)), ("qz", (3, 0, 0), (("k", 0),)), ("qz", (3, 1, 0), (("k", 0),)), ("qb", (0, 1, 2), (("x", 1), ("k", 0))), ("qz", (2, 0, 0), (("k", 0),)), ("qb", (1, 0, 2), (("k", 0),)), ("qz", (1, 1, 1), (("k", 0),)), ("qz", (2, 1, 0), (("k", 0),)), ("qa", (1, 1, 3), (("k", 0),)), ("qa", (0, 1, 2), (("y", 1), ("k", 0))), ("qz", (3, 0, 1), (("k", 0),)), ("o", (0, 1, 1), (("z", 3), ("z", 2), ("z", 1), ("k", 0))), ("qa", (1, 0, 2), (("k", 0),)), ("qz", (3, 1, 1), (("k", 0),)), ("d", (0, 0, 0), (("z", 1),)), ("u", (1, 1, 0), (("k", 0),)), ("qz", (2, 0, 1), (("k", 0),)), ("u", (0, 1, 1), (("y", 1), ("k", 0))), ("qz", (2, 1, 1), (("k", 0),)), ("o", (1, 0, 0), (("k", 0),)), ("d", (0, 0, 0), (("y", 1),)), ("qb", (1, 1, 2), (("k", 0),)), ("o", (3, 0, 0), (("k", 0),)), ("qa", (1, 1, 2), (("k", 0),))],
    "n1": [("o", (3, 1, 0), (("k", 0),))],
    "n2": [("o", (1, 1, 0), (("k", 0),))],
    "n3": [("o", (2, 0, 0), (("k", 0),)), ("u", (0, 0, 3), (("x", 1), ("y", 1), ("k", 0)))],
    "n4": [("u", (0, 0, 0), (("z", 2),)), ("u", (1, 0, 1), (("k", 0),)), ("d", (1, 0, 0), (("k", 0),))],
    "n5": [("o", (2, 1, 0), (("k", 0),))],
    "n7": [("o", (1, 0, 1), (("k", 0),))],
    "n8": [("o", (3, 0, 1), (("k", 0),)), ("u", (1, 1, 1), (("k", 0),))],
    "t0": [("o", (3, 1, 1), (("k", 0),))],
    "t1": [("o", (1, 1, 1), (("k", 0),)), ("d", (0, 0, 0), (("z", 3),)), ("o", (2, 0, 1), (("k", 0),))],
    "t2": [("o", (2, 1, 1), (("k", 0),))],
    "t3": [("d", (0, 0, 1), (("y", 1), ("x", 1), ("k", 0)))],
    "t4": [("d", (0, 1, 0), (("x", 1), ("k", 0))), ("d", (0, 0, 0), (("z", 2),))],
    "t5": [("u", (0, 1, 3), (("y", 1), ("k", 0)))],
    "t7": [("d", (1, 1, 0), (("k", 0),))],
    "t8": [("u", (1, 0, 3), (("k", 0),)), ("u", (0, 0, 2), (("x", 1), ("y", 1), ("k", 0))), ("d", (1, 0, 1), (("k", 0),))],
    "t11": [("d", (0, 1, 1), (("x", 1), ("k", 0))), ("u", (1, 1, 3), (("k", 0),)), ("u", (1, 0, 2), (("k", 0),)), ("u", (0, 1, 2), (("y", 1), ("k", 0)))],
    "tail": [("d", (0, 0, 3), (("y", 1), ("x", 1), ("k", 0))), ("d", (0, 1, 3), (("x", 1), ("k", 0))), ("d", (1, 1, 1), (("k", 0),)), ("u", (1, 1, 2), (("k", 0),)), ("d", (0, 0, 2), (("y", 1), ("x", 1), ("k", 0))), ("d", (1, 0, 3), (("k", 0),)), ("d", (1, 1, 3), (("k", 0),)), ("d", (0, 1, 2), (("x", 1), ("k", 0))), ("d", (1, 0, 2), (("k", 0),)), ("d", (1, 1, 2), (("k", 0),))],
}
AGEARLY = 10
AGMID = 41
FIRST = {
    "o": [("s0", "o", 3, 0, 0), ("s0", "o", 2, 0, 0), ("s0", "o", 1, 0, 0), ("s0", "o", 0, 0, 0), ("s0", "o", 3, 1, 0), ("s0", "o", 2, 1, 0), ("s0", "o", 1, 1, 0), ("s0", "o", 0, 1, 0), ("s0", "o", 3, 0, 1), ("s0", "o", 2, 0, 1), ("s0", "o", 1, 0, 1), ("s0", "o", 0, 0, 1), ("s0", "o", 3, 1, 1), ("s0", "o", 2, 1, 1), ("s0", "o", 1, 1, 1), ("s0", "o", 0, 1, 1)],
    "u0": [("s0", "u", 1, 0, 3), ("s0", "u", 0, 0, 3), ("s0", "u", 1, 1, 3), ("s0", "u", 0, 1, 3)],
    "u1": [("s0", "u", 1, 0, 2), ("s0", "u", 0, 0, 2), ("s0", "u", 1, 1, 2), ("s0", "u", 0, 1, 2)],
    "u2": [("s0", "u", 1, 0, 1), ("s0", "u", 0, 0, 1), ("s0", "u", 1, 1, 1), ("s0", "u", 0, 1, 1)],
    "u3": [("s0", "u", 1, 0, 0), ("s0", "u", 0, 0, 0), ("s0", "u", 1, 1, 0), ("s0", "u", 0, 1, 0)],
    "d0": [("s0", "d", 1, 0, 3), ("s0", "d", 1, 1, 3), ("s0", "d", 1, 0, 2), ("s0", "d", 1, 1, 2), ("s0", "d", 1, 0, 1), ("s0", "d", 1, 1, 1), ("s0", "d", 1, 0, 0), ("s0", "d", 1, 1, 0)],
    "d2": [("s0", "d", 0, 0, 3), ("s0", "d", 0, 1, 3), ("s0", "d", 0, 0, 2), ("s0", "d", 0, 1, 2), ("s0", "d", 0, 0, 1), ("s0", "d", 0, 1, 1), ("s0", "d", 0, 0, 0), ("s0", "d", 0, 1, 0)],
    "g2": [("s0", "qa", 1, 0, 3), ("s0", "qa", 0, 0, 3), ("s0", "qa", 1, 1, 3), ("s0", "qa", 0, 1, 3), ("s0", "qa", 1, 0, 2), ("s0", "qa", 0, 0, 2), ("s0", "qa", 1, 1, 2), ("s0", "qa", 0, 1, 2), ("s0", "qa", 1, 0, 1), ("s0", "qa", 0, 0, 1), ("s0", "qa", 1, 1, 1), ("s0", "qa", 0, 1, 1), ("s0", "qa", 1, 0, 0), ("s0", "qa", 0, 0, 0), ("s0", "qa", 1, 1, 0), ("s0", "qa", 0, 1, 0), ("s0", "qb", 1, 0, 3), ("s0", "qb", 0, 0, 3), ("s0", "qb", 1, 1, 3), ("s0", "qb", 0, 1, 3), ("s0", "qb", 1, 0, 2), ("s0", "qb", 0, 0, 2), ("s0", "qb", 1, 1, 2), ("s0", "qb", 0, 1, 2), ("s0", "qb", 1, 0, 1), ("s0", "qb", 0, 0, 1), ("s0", "qb", 1, 1, 1), ("s0", "qb", 0, 1, 1), ("s0", "qb", 1, 0, 0), ("s0", "qb", 0, 0, 0), ("s0", "qb", 1, 1, 0), ("s0", "qb", 0, 1, 0), ("s0", "qz", 3, 0, 0), ("s0", "qz", 2, 0, 0), ("s0", "qz", 1, 0, 0), ("s0", "qz", 0, 0, 0), ("s0", "qz", 3, 1, 0), ("s0", "qz", 2, 1, 0), ("s0", "qz", 1, 1, 0), ("s0", "qz", 0, 1, 0), ("s0", "qz", 3, 0, 1), ("s0", "qz", 2, 0, 1), ("s0", "qz", 1, 0, 1), ("s0", "qz", 0, 0, 1), ("s0", "qz", 3, 1, 1), ("s0", "qz", 2, 1, 1), ("s0", "qz", 1, 1, 1), ("s0", "qz", 0, 1, 1)],
}
SLOTS = {
    "u1": [("s1", "o", 1, 1, 1), ("s1", "o", 2, 1, 1), ("s1", "o", 3, 1, 1)],
    "u2": [("s1", "o", 1, 0, 1), ("s1", "u", 1, 1, 3)],
    "u3": [("s1", "o", 2, 0, 1), ("s1", "u", 1, 0, 3), ("s1", "o", 1, 1, 0)],
    "d0": [("s1", "o", 3, 0, 1)],
    "d1": [("s1", "o", 2, 1, 0)],
    "d2": [("s1", "u", 1, 1, 2), ("s2", "u", 1, 3)],
    "d3": [("s1", "o", 3, 1, 0), ("s1", "d", 1, 1, 3)],
    "t0": [("s1", "u", 1, 0, 2), ("s1", "o", 1, 0, 0)],
    "t1": [("s1", "d", 1, 0, 3), ("s3", "u", 3)],
    "t2": [("s2", "u", 1, 2), ("s2", "d", 1, 3)],
    "t3": [("s1", "u", 1, 1, 1)],
    "t4": [("s1", "d", 1, 1, 2), ("s1", "u", 1, 0, 1)],
    "t5": [("s3", "d", 3)],
    "t6": [("s2", "o", 1, 1), ("s2", "u", 1, 1)],
    "t7": [("s3", "u", 2), ("s1", "d", 1, 0, 2), ("s2", "d", 1, 2), ("s1", "o", 2, 0, 0)],
    "t8": [("s1", "u", 1, 1, 0), ("s1", "o", 3, 0, 0), ("s1", "d", 1, 1, 1)],
    "t10": [("s1", "u", 1, 0, 0), ("s1", "d", 1, 0, 1), ("s3", "u", 1), ("s3", "d", 2)],
    "g0": [("s2", "u", 1, 0), ("s2", "d", 1, 1)],
    "g1": [("s2", "o", 1, 0), ("s1", "d", 1, 1, 0)],
    "i0": [("s3", "d", 1), ("s1", "d", 1, 0, 0), ("s1", "qa", 1, 0, 3), ("s1", "qa", 1, 1, 3), ("s1", "qa", 1, 1, 2)],
    "i2": [("s3", "o", 1), ("s1", "qz", 2, 1, 1), ("s1", "qz", 1, 1, 1), ("s1", "qz", 3, 1, 1), ("s2", "d", 1, 0)],
    "i3": [("s2", "qa", 1, 3), ("s1", "qz", 1, 0, 1), ("s1", "qz", 2, 0, 1)],
}
TAIL = [("s1", "qa", 1, 0, 2), ("s2", "qa", 1, 2), ("s1", "qb", 1, 1, 3), ("s1", "qa", 1, 1, 1), ("s1", "qz", 3, 0, 1), ("s1", "qz", 1, 1, 0), ("s1", "qz", 2, 1, 0), ("s1", "qb", 1, 0, 3), ("s1", "qz", 1, 0, 0), ("s1", "qz", 3, 1, 0), ("s1", "qa", 1, 0, 1), ("s1", "qz", 2, 0, 0), ("s1", "qb", 1, 1, 2), ("s1", "qa", 1, 1, 0), ("s3", "qa", 3), ("s1", "qb", 1, 0, 2), ("s3", "qa", 2), ("s2", "qb", 1, 3), ("s1", "qz", 3, 0, 0), ("s1", "qb", 1, 1, 1), ("s2", "qa", 1, 1), ("s2", "qz", 1, 1), ("s1", "qa", 1, 0, 0), ("s2", "qb", 1, 2), ("s1", "qb", 1, 0, 1), ("s2", "qa", 1, 0), ("s3", "qb", 3), ("s1", "qb", 1, 1, 0), ("s3", "qa", 1), ("s3", "qb", 2), ("s1", "qb", 1, 0, 0), ("s3", "qz", 1), ("s2", "qb", 1, 1), ("s2", "qz", 1, 0), ("s2", "qb", 1, 0), ("s3", "qb", 1)]


def dg(a,b,d,prec=None): return lax.dot_general(a,b,d,preferred_element_type=F32,precision=prec)


def hooks(i, table):
    for j, evs in table.items():
        if evs:
            @pl.when(i == j)
            def _(evs=evs):
                for e in evs: e()


def qkv_proj(w_ref, bias_ref, xlow_ref, qkv_ref, slots):
    def body(n,_):
        o=pl.multiple_of(n*256,256)
        y=dg(xlow_ref[...], w_ref[pl.ds(o,256),:], NT)
        y=(y+bias_ref[:,pl.ds(o,256)])*jnp.where(o<xlow_ref.shape[1],0.125,1.0)
        qkv_ref[:,pl.ds(o,256)]=y.astype(BF)
        hooks(n, slots)
        return 0
    lax.fori_loop(0, w_ref.shape[0]//256, body, 0)


def rel_rows(tableT_ref, bk_ref, rel_ref):
    nb=tableT_ref.shape[1]; n=bk_ref.shape[1]
    hot=(lax.broadcasted_iota(jnp.int32,(nb,n),0)==bk_ref[...]).astype(F32)
    rel_ref[...]=dg(tableT_ref[...], hot, NN, lax.Precision.HIGHEST)


def bias_expand(row,S):
    R=pltpu.roll(jnp.broadcast_to(row,(128,2*S)), 2*S-127, 1, stride=1, stride_axis=0)
    nu=S//128
    return jnp.concatenate([R[:,128*(nu-1-u):128*(nu-1-u)+S] for u in range(nu)],axis=0)


def diag_sum(t,S):
    nu=S//128
    y=None
    for u in range(nu):
        a=128*(nu-1-u); parts=[]
        if a: parts.append(jnp.zeros((128,a),F32))
        parts.append(t[128*u:128*(u+1),:])
        if 2*S-a-S: parts.append(jnp.zeros((128,2*S-a-S),F32))
        v=jnp.concatenate(parts,axis=1) if len(parts)>1 else parts[0]
        y=v if y is None else y+v
    z=None
    for w in range(16):
        g=y[8*w:8*w+8,:]
        sh=120-8*w
        g=pltpu.roll(g,sh,1) if sh else g
        z=g if z is None else z+g
    out=None
    for b in range(8):
        g=z[b:b+1,:]
        g=pltpu.roll(g,7-b,1) if b<7 else g
        out=g if out is None else out+g
    return out


def attn_fwd(len_ref, qkv_ref, rel_ref, ctx_ref, lse_ref, bias_scr, S, D, slots):
    lane=lax.broadcasted_iota(jnp.int32,(1,128),1)
    col=lax.broadcasted_iota(jnp.int32,(1,S),1)
    def body(p,_):
        o=pl.multiple_of(p*128,128)
        for hh in range(2):
            row=rel_ref[pl.ds(p*2+hh,1),:]
            bias_scr[hh]=bias_expand(row,S)
        for m in range(2):
            q=qkv_ref[m*S:(m+1)*S,pl.ds(o,128)]
            k=qkv_ref[m*S:(m+1)*S,pl.ds(D+o,128)]
            v=qkv_ref[m*S:(m+1)*S,pl.ds(2*D+o,128)]
            valid=col<len_ref[m]
            outs=[]
            for hh in range(2):
                mk=(lane//64)==hh
                qm=jnp.where(mk,q,jnp.zeros_like(q))
                s=dg(qm,k,NT)+bias_scr[hh]
                s=jnp.where(valid,s,-1e30)
                mx=jnp.max(s,axis=1,keepdims=True)
                e=jnp.exp(s-mx)
                tot=jnp.sum(e,axis=1,keepdims=True)
                pl_=(e*(1.0/tot)).astype(BF)
                outs.append(dg(pl_,v,NN))
                lse_ref[m,pl.ds(p*2+hh,1),:]=jnp.transpose(mx+jnp.log(tot),(1,0))
            ctx_ref[m*S:(m+1)*S,pl.ds(o,128)]=jnp.where((lane//64)==0,outs[0],outs[1]).astype(BF)
            hooks(p, {i: slots.get(2*i+m) for i in range(D//128)})
        return 0
    lax.fori_loop(0, D//128, body, 0)


def attn_bwd(len_ref, qkv_ref, dctx_ref, lse_ref, relf_ref, drelf_ref, bias_scr, acc_scr, S, D, slots):
    lane=lax.broadcasted_iota(jnp.int32,(1,128),1)
    rowi=lax.broadcasted_iota(jnp.int32,(S,1),0)
    m0=(lane//64)==0
    def body(p,_):
        o=pl.multiple_of(p*128,128)
        for hh in range(2):
            row=relf_ref[pl.ds(p*2+hh,1),:]
            bias_scr[hh]=bias_expand(row,S)
        for m in range(2):
            q=qkv_ref[m*S:(m+1)*S,pl.ds(o,128)]
            k=qkv_ref[m*S:(m+1)*S,pl.ds(D+o,128)]
            v=qkv_ref[m*S:(m+1)*S,pl.ds(2*D+o,128)]
            do=dctx_ref[m*S:(m+1)*S,pl.ds(o,128)]
            valid=rowi<len_ref[m]
            oq=[];ok=[];ov=[]
            for hh in range(2):
                mk=(lane//64)==hh
                km=jnp.where(mk,k,jnp.zeros_like(k)); vm=jnp.where(mk,v,jnp.zeros_like(v))
                sT=dg(km,q,NT)+bias_scr[hh]
                sT=jnp.where(valid,sT,-1e30)
                pT=jnp.exp(sT-lse_ref[m,pl.ds(p*2+hh,1),:])
                dpT=dg(vm,do,NT)
                rd=jnp.sum(dpT*pT,axis=0,keepdims=True)
                ds=(pT*(dpT-rd)).astype(BF)
                ov.append(dg(pT.astype(BF),do,NN))
                ok.append(dg(ds,q,NN))
                oq.append(dg(ds,k,TN))
                if m==0: acc_scr[hh]=ds.astype(F32)
                else: acc_scr[hh]+=ds.astype(F32)
            qkv_ref[m*S:(m+1)*S,pl.ds(o,128)]=(jnp.where(m0,oq[0],oq[1])*0.125).astype(BF)
            qkv_ref[m*S:(m+1)*S,pl.ds(D+o,128)]=jnp.where(m0,ok[0],ok[1]).astype(BF)
            qkv_ref[m*S:(m+1)*S,pl.ds(2*D+o,128)]=jnp.where(m0,ov[0],ov[1]).astype(BF)
            hooks(p, {i: slots.get(2*i+m) for i in range(D//128)})
        for hh in range(2):
            drelf_ref[pl.ds(p*2+hh,1),:]=diag_sum(acc_scr[hh],S)
        return 0
    lax.fori_loop(0, D//128, body, 0)


def stats(z):
    mu=jnp.mean(z,axis=-1,keepdims=True); c=z-mu
    var=jnp.mean(c*c,axis=-1,keepdims=True)
    r=lax.rsqrt(var+EPS)
    return c*r, r


def fwd_tile(slot, x_ref, ctx_ref, wo_ref, wu_ref, wd_ref, vec_ref, bup_ref, out_ref, nl_scr, act_scr, gp_scr, z1_scr, z2_scr, r_scr, R):
    D=x_ref.shape[2]; FF=wu_ref.shape[1]
    ctx=ctx_ref[...].reshape(R,D)
    fs=x_ref[...].reshape(R,D)+(dg(ctx,wo_ref[...],NT)+vec_ref[0:1,:])
    z1,r1=stats(fs)
    z1_scr[slot]=z1
    fn=z1*vec_ref[1:2,:]+vec_ref[2:3,:]
    nl=fn.astype(BF)
    nl_scr[...]=nl.reshape(nl_scr.shape)
    def body(f,acc):
        o=pl.multiple_of(f*FC,FC)
        u=dg(nl_scr[...].reshape(R,D),wu_ref[:,pl.ds(o,FC)],NN)+bup_ref[:,pl.ds(o,FC)]
        phi=0.5*(1.0+lax.erf(u*(2.0**-0.5)))
        a=(u*phi).astype(BF)
        act_scr[:,:,pl.ds(o,FC)]=a.reshape(2,R//2,FC)
        gp_scr[slot,:,pl.ds(o,FC)]=phi+u*(jnp.exp(u*u*-0.5)*0.3989422804014327)
        return acc+dg(a,wd_ref[:,pl.ds(o,FC)],NT)
    acc=lax.fori_loop(0,FF//FC,body,fn+vec_ref[3:4,:])
    z2,r2=stats(acc)
    z2_scr[slot]=z2
    r_scr[slot,:,0:1]=r1
    r_scr[slot,:,1:2]=r2
    out_ref[...]=(z2*vec_ref[4:5,:]).reshape(out_ref.shape)


def lnb(u,z,r):
    return r*(u-jnp.mean(u,axis=-1,keepdims=True)-z*jnp.mean(u*z,axis=-1,keepdims=True))


def bwd_tile(slot, ds_ref, cot_ref, wo_ref, wu_ref, wd_ref, vec_ref, dfs_ref, dctx_ref, gv_ref, gbu_ref, dl_scr, ul_scr, al_scr, gp_scr, z1_scr, z2_scr, r_scr, R):
    D=wu_ref.shape[0]; FF=wu_ref.shape[1]; Rh=R//2
    r1=r_scr[slot,:,0:1]; r2=r_scr[slot,:,1:2]
    z2=z2_scr[slot]
    do=cot_ref[...].reshape(R,D)
    ri=lax.broadcasted_iota(jnp.int32,(R,1),0)
    coef=jnp.where(ri==0,ds_ref[0:1,0:1],0.0)+jnp.where(ri==Rh,ds_ref[1:2,0:1],0.0)
    do=do+coef*vec_ref[5:6,:]
    gv_ref[4:5,:]+=jnp.sum(do*z2,axis=0,keepdims=True)
    gv_ref[5:6,:]+=jnp.sum(coef*(z2*vec_ref[4:5,:]),axis=0,keepdims=True)
    d2=lnb(do*vec_ref[4:5,:],z2,r2)
    dl=d2.astype(BF)
    dl_scr[...]=dl.reshape(dl_scr.shape)
    gv_ref[3:4,:]+=jnp.sum(dl.astype(F32),axis=0,keepdims=True)
    def body(f,acc):
        o=pl.multiple_of(f*FC,FC)
        da=dg(dl_scr[...].reshape(R,D),wd_ref[:,pl.ds(o,FC)],NN)
        ul=(da*gp_scr[slot,:,pl.ds(o,FC)]).astype(BF)
        ul_scr[:,:,pl.ds(o,FC)]=ul.reshape(2,R//2,FC)
        gbu_ref[:,pl.ds(o,FC)]+=jnp.sum(ul.astype(F32),axis=0,keepdims=True)
        return acc+dg(ul,wu_ref[:,pl.ds(o,FC)],NT)
    d1=lax.fori_loop(0,FF//FC,body,d2)
    z1=z1_scr[slot]
    gv_ref[1:2,:]+=jnp.sum(d1*z1,axis=0,keepdims=True)
    gv_ref[2:3,:]+=jnp.sum(d1,axis=0,keepdims=True)
    dfs=lnb(d1*vec_ref[1:2,:],z1,r1)
    dfs_ref[...]=dfs.reshape(dfs_ref.shape)
    al=dfs.astype(BF)
    al_scr[...]=al.reshape(al_scr.shape)
    gv_ref[0:1,:]+=jnp.sum(al.astype(F32),axis=0,keepdims=True)
    dctx_ref[...]=dg(al,wo_ref[...],NN).astype(BF).reshape(dctx_ref.shape)


class Geo:
    def __init__(g, C, Q):
        g.C=C; g.Q=Q; g.nx=Q//2; g.nz=min(4,C); g.ny=C//g.nz
        c=lax.axis_index("cand"); q=lax.axis_index("query")
        g.z=c//g.ny; g.y=lax.rem(c,g.ny); g.x=q//2; g.k=lax.rem(q,2)
    def dev(g,z,y,x,k): return {"cand":z*g.ny+y,"query":x*2+k}


def mo(v,n): return pl.multiple_of(v,n)


def barrier(g, peers):
    b=pltpu.get_barrier_semaphore()
    for p in peers: pl.semaphore_signal(b,inc=1,device_id=p,device_id_type=MESH)
    pl.semaphore_wait(b,len(peers))


class RS:
    def __init__(s, g, refs, bufs, ss, rs):
        s.g, s.refs, s.bufs, s.ss, s.rs = g, refs, bufs, ss, rs
        s.partner = g.dev(g.z, g.y, g.x, 1 - g.k)
        s.pend = []
    def dims(s, n): return [NR[d] for d in RORD[n]]
    def own(s, n, rel, k):
        g = s.g
        r = dict(zip(RORD[n], rel))
        return rs_slice(g, n, s.refs, jnp.bitwise_xor(g.z, r["z"]), 1 - g.y if r["y"] else g.y, 1 - g.x if r["x"] else g.x, k)
    def near(s, d, r):
        g = s.g
        return g.dev(jnp.bitwise_xor(g.z, r) if d == "z" else g.z, 1 - g.y if d == "y" else g.y, 1 - g.x if d == "x" else g.x, g.k)
    def copy(s, src, dst, n, i, dev):
        pi = RPIECES.index(n)
        return pltpu.make_async_remote_copy(src, dst, s.ss.at[pi, i], s.rs.at[pi, i], device_id=dev, device_id_type=MESH)
    def c0(s, n, r1, r2, r3):
        _, n2, n3 = s.dims(n)
        return s.copy(s.own(n, (r1, r2, r3), 1 - s.g.k), s.bufs[n][0].at[r1, r2, r3], n, (r1 * n2 + r2) * n3 + r3, s.partner)
    def c1(s, n, r1, r2, r3):
        _, n2, n3 = s.dims(n)
        return s.copy(s.bufs[n][0].at[r1, r2, r3], s.bufs[n][1].at[r1 - 1, r2, r3], n, 16 + ((r1 - 1) * n2 + r2) * n3 + r3, s.near(RORD[n][0], r1))
    def c2(s, n, r2, r3):
        n1, n2, n3 = s.dims(n)
        return s.copy(s.bufs[n][0].at[0, r2, r3], s.bufs[n][2].at[r2 - 1, r3], n, 16 + (n1 - 1) * n2 * n3 + (r2 - 1) * n3 + r3, s.near(RORD[n][1], r2))
    def c3(s, n, r3):
        n1, n2, n3 = s.dims(n)
        return s.copy(s.bufs[n][0].at[0, 0, r3], s.bufs[n][3].at[r3 - 1], n, 16 + (n1 - 1) * n2 * n3 + (n2 - 1) * n3 + r3 - 1, s.near(RORD[n][2], r3))
    def go(s, f, *a):
        f(*a).start()
        s.pend.append(lambda: f(*a))
    def add(s, n, dst, srcs):
        rows, st = RSHP[n][0], RSHP[n][2]
        def body(i, _):
            o = pl.multiple_of(i * st, 16)
            dst[pl.ds(o, st), :] = functools.reduce(lambda a, b: a + b, [r[pl.ds(o, st), :].astype(F32) for r in srcs]).astype(dst.dtype)
            return 0
        lax.fori_loop(0, rows // st, body, 0)
    def part1(s, n, r2, r3):
        s.c0(n, 0, r2, r3).wait_recv()
        n1 = s.dims(n)[0]
        for r1 in range(1, n1):
            s.c1(n, r1, r2, r3).wait_recv()
        return [s.own(n, (0, r2, r3), s.g.k), s.bufs[n][0].at[0, r2, r3]] + [s.bufs[n][1].at[r1 - 1, r2, r3] for r1 in range(1, n1)]
    def part2(s, n, r3):
        t = s.part1(n, 0, r3)
        n2 = s.dims(n)[1]
        for r2 in range(1, n2):
            s.c2(n, r2, r3).wait_recv()
        return t + [s.bufs[n][2].at[r2 - 1, r3] for r2 in range(1, n2)]
    def s0(s, n, r1, r2, r3): s.go(s.c0, n, r1, r2, r3)
    def s1(s, n, r1, r2, r3):
        s.c0(n, r1, r2, r3).wait_recv()
        b = s.bufs[n][0].at[r1, r2, r3]
        s.add(n, b, [s.own(n, (r1, r2, r3), s.g.k), b])
        s.go(s.c1, n, r1, r2, r3)
    def s2(s, n, r2, r3):
        s.add(n, s.bufs[n][0].at[0, r2, r3], s.part1(n, r2, r3))
        s.go(s.c2, n, r2, r3)
    def s3(s, n, r3):
        s.add(n, s.bufs[n][0].at[0, 0, r3], s.part2(n, r3))
        s.go(s.c3, n, r3)
    def fin(s, n, dst):
        t = s.part2(n, 0)
        n3 = s.dims(n)[2]
        for r3 in range(1, n3):
            s.c3(n, r3).wait_recv()
        s.add(n, dst, t + [s.bufs[n][3].at[r3 - 1] for r3 in range(1, n3)])
    def ev(s, e): getattr(s, e[0])(*e[1:])
    def drain(s):
        for c in s.pend: c().wait_send()


def rs_slice(g, n, refs, z, y, x, k):
    wq, wo, wu, wd = refs
    c = z * g.ny + y
    q = x * 2 + k
    if n in QROW:
        return wq.at[pl.ds(mo(c * 288 + k * 144 + QROW[n], 16), RSHP[n][0]), pl.ds(mo(x * 384, 128), 384)]
    if n == "o": return wo.at[pl.ds(mo(c * 96 + k * 48, 16), 48), pl.ds(mo(x * 384, 128), 384)]
    if n == "u": return wu.at[pl.ds(mo(q * 192, 16), 192), pl.ds(mo(c * 384, 128), 384)]
    if n == "d": return wd.at[pl.ds(mo(c * 96, 16), 96), pl.ds(mo(q * 768, 128), 768)]


def rs_bufs():
    out = []
    for n in RPIECES:
        n1, n2, n3 = [NR[d] for d in RORD[n]]
        sh = RSHP[n][:2]
        out += [pltpu.VMEM((n1, n2, n3) + sh, BF), pltpu.VMEM((n1 - 1, n2, n3) + sh, BF), pltpu.VMEM((n2 - 1, n3) + sh, BF), pltpu.VMEM((n3 - 1,) + sh, BF)]
    return out


def attn_fwd_kernel(len_ref, x_ref, w_ref, bias_ref, tab_ref, bk_ref, bkf_ref, xlow_ref, qkv_ref, ctx_ref, lse_ref, relf_ref, rel_ref, bias_scr):
    S, D = x_ref.shape[1:]
    for m in range(2):
        xlow_ref[m*S:(m+1)*S,:]=x_ref[m].astype(BF)
    qkv_proj(w_ref, bias_ref, xlow_ref, qkv_ref, {})
    rel_rows(tab_ref, bk_ref, rel_ref)
    rel_rows(tab_ref, bkf_ref, relf_ref)
    attn_fwd(len_ref, qkv_ref, rel_ref, ctx_ref, lse_ref, bias_scr, S, D, {})


class AG:
    def __init__(s, g, own, refs, ss, rs, cs, cr):
        s.g, s.own_, s.refs, s.ss, s.rs, s.cs, s.cr = g, own, refs, ss, rs, cs, cr
        s.partner = g.dev(g.z, g.y, g.x, 1 - g.k)
        s.pend = []
        s.got = set()
    def dst(s, n, rel, k):
        g = s.g
        r = dict(zip(RORD[n], rel))
        return rs_slice(g, n, s.refs, jnp.bitwise_xor(g.z, r["z"]), 1 - g.y if r["y"] else g.y, 1 - g.x if r["x"] else g.x, k)
    def idx(s, n, rel):
        _, n2, n3 = [NR[d] for d in RORD[n]]
        return (rel[0] * n2 + rel[1]) * n3 + rel[2]
    def src(s, n, rel): return s.own_(n) if rel == (0, 0, 0) else s.dst(n, rel, s.g.k)
    def near(s, d, r):
        g = s.g
        return g.dev(jnp.bitwise_xor(g.z, r) if d == "z" else g.z, 1 - g.y if d == "y" else g.y, 1 - g.x if d == "x" else g.x, g.k)
    def link(s, n, rel, d, k):
        new = tuple(k if a == d else r for a, r in zip(RORD[n], rel))
        pi, i = RPIECES.index(n), s.idx(n, new)
        return pltpu.make_async_remote_copy(s.src(n, rel), s.dst(n, rel, s.g.k), s.ss.at[pi, i], s.rs.at[pi, i], device_id=s.near(d, k), device_id_type=MESH)
    def core(s, n, rel):
        pi, i = RPIECES.index(n), s.idx(n, rel)
        return pltpu.make_async_remote_copy(s.src(n, rel), s.dst(n, rel, s.g.k), s.cs.at[pi, i], s.cr.at[pi, i], device_id=s.partner, device_id_type=MESH)
    def got_core(s, n, rel):
        pi, i = RPIECES.index(n), s.idx(n, rel)
        t = s.dst(n, rel, 1 - s.g.k)
        pltpu.make_async_remote_copy(t, t, s.cs.at[pi, i], s.cr.at[pi, i], device_id=s.partner, device_id_type=MESH).wait_recv()
    def go(s, f, *a):
        f(*a).start()
        s.pend.append(lambda: f(*a))
    def ev(s, e):
        n, rel, outs = e
        if rel != (0, 0, 0):
            t = s.dst(n, rel, s.g.k)
            pi, i = RPIECES.index(n), s.idx(n, rel)
            pltpu.make_async_remote_copy(t, t, s.ss.at[pi, i], s.rs.at[pi, i], device_id=s.partner, device_id_type=MESH).wait_recv()
        for d, k in outs:
            if d == "k": s.go(s.core, n, rel)
            else: s.go(s.link, n, rel, d, k)
    def rels(s, n):
        n1, n2, n3 = [NR[d] for d in RORD[n]]
        return [(a, b, c) for a in range(n1) for b in range(n2) for c in range(n3)]
    def drain(s):
        for c in s.pend: c().wait_send()


def front_kernel(len_ref, x_h, wqf_h, wof_h, wuf_h, wdf_h, *rest, C, Q):
    vins, rest = rest[:11], rest[11:]
    (wq_o, wo, wu, wd, vec_o, bup_o, xlow_o, qkv_o, ctx_ref, lse_ref, relf_ref, bkf_o,
     wqf_ref, wof_ref, wuf_ref, wdf_ref, v_ref, bk_ref, x_v, xlow, qkv, wq, own_p, got_p, h_scr, u_bf, d_bf, vall, tab, rel, qb, bias_scr, ss, rs, cs, cr, vss, vrs, ps, ls) = rest
    g = Geo(C, Q)
    S, D = x_h.shape[1:]
    q_ = lax.axis_index("query")
    peers = [{"query": lax.rem(q_ + j, Q)} for j in range(1, Q)] + [g.dev(g.z, 1 - g.y, g.x, g.k)] + [g.dev(jnp.bitwise_xor(g.z, i), g.y, g.x, g.k) for i in range(1, g.nz)]
    bar = pltpu.get_barrier_semaphore()
    for p in peers:
        pl.semaphore_signal(bar, inc=1, device_id=p, device_id_type=MESH)
    wc = [pltpu.make_async_copy(a, b, ls.at[10 + i]) for i, (a, b) in enumerate(((wqf_h, wqf_ref), (wof_h, wof_ref), (wuf_h, wuf_ref), (wdf_h, wdf_ref)))]
    for c in wc:
        c.start()
    xc = pltpu.make_async_copy(x_h, x_v, ls.at[0])
    xc.start()
    k = g.k
    dq, bq = D // Q, tab.shape[1] // Q
    fq = bup_o.shape[1] // Q
    v_ref[...] = jnp.zeros_like(v_ref)
    for i in range(8):
        v_ref[i:i + 1, 0:dq] = vins[i][...]
    for j in range(fq // 256):
        v_ref[8 + j:9 + j, :] = vins[8][:, j * 256:(j + 1) * 256]
    v_ref[16:16 + vins[9].shape[0], 0:bq] = vins[9][...]
    nrel = vins[10].shape[1]
    bk_ref[...] = jnp.full(bk_ref.shape, -1, jnp.int32)
    bk_ref[:, 0:nrel] = vins[10][...]
    for c in wc:
        c.wait()

    def turn(w):
        n = w.shape[1]
        eye = (lax.broadcasted_iota(jnp.int32, (n, n), 0) == lax.broadcasted_iota(jnp.int32, (n, n), 1)).astype(BF)
        return dg(eye, w.astype(BF), NT).astype(BF)
    a, b = turn(wqf_ref[...]), turn(wof_ref[...])
    ha, hb = a.shape[0] // 2, b.shape[0] // 2
    for i in range(2):
        own_p[i, 0:ha, :] = a[i * ha:(i + 1) * ha]
        own_p[i, ha:ha + hb, :] = b[i * hb:(i + 1) * hb]
    d_bf[...] = wdf_ref[...].astype(BF)
    u_bf[...] = wuf_ref[...].astype(BF)
    pl.semaphore_wait(bar, len(peers))
    pc = pltpu.make_async_remote_copy(own_p.at[1 - k], got_p, ps.at[0], ps.at[1], device_id=g.dev(g.z, g.y, g.x, 1 - k), device_id_type=MESH)
    pc.start()
    vcs = []
    for j in range(1, Q):
        c = pltpu.make_async_remote_copy(v_ref, vall.at[q_], vss.at[j - 1], vrs.at[j - 1], device_id={"query": lax.rem(q_ + j, Q)}, device_id_type=MESH)
        c.start()
        vcs.append(c)
    vall[q_] = v_ref[...]

    def own(n):
        if n == "u": return u_bf
        if n == "d": return d_bf
        return h_scr.at[pl.ds(QROW.get(n, 144), RSHP[n][0])]
    A = AG(g, own, (wq, wo, wu, wd), ss, rs, cs, cr)
    loc = [pltpu.make_async_copy(own(n), A.dst(n, (0, 0, 0), k), ls.at[1 + i]) for i, n in enumerate(RPIECES)]

    def after(name):
        for e in AGSLOTS.get(name, []):
            A.ev(e)
    after("p")
    loc[0].start()
    loc[1].start()
    pc.wait()
    t, r = own_p[k], got_p[...]
    @pl.when(k == 0)
    def _(): h_scr[...] = jnp.concatenate([t, r], axis=1)
    @pl.when(k == 1)
    def _(): h_scr[...] = jnp.concatenate([r, t], axis=1)
    for c in loc[2:]:
        c.start()
    for e in AGSLOTS["w"][:AGEARLY]:
        A.ev(e)
    xc.wait()
    for m in range(2):
        xlow[m*S:(m+1)*S,:]=x_v[m].astype(BF)
    xo = pltpu.make_async_copy(xlow, xlow_o, ls.at[7])
    xo.start()
    ids = jnp.broadcast_to(bk_ref[...], (8, 2 * S)).astype(F32).astype(BF)
    for j in range(2 * S // 256):
        flip = (lax.broadcasted_iota(jnp.int32, (2 * S, 256), 0) + lax.broadcasted_iota(jnp.int32, (2 * S, 256), 1) == nrel - 1 - j * 256).astype(BF)
        bkf_o[:, j * 256:(j + 1) * 256] = dg(ids, flip, NN)[0:1].astype(jnp.int32)
    bkf_o[:, nrel:] = jnp.full((1, 2 * S - nrel), -1, jnp.int32)
    for e in AGSLOTS["w"][AGEARLY:AGMID]:
        A.ev(e)
    for c in vcs:
        c.wait()
    qb[...] = jnp.zeros_like(qb)
    vec_o[...] = jnp.zeros_like(vec_o)
    for q in range(Q):
        lo, hi = q * dq, (q + 1) * dq
        qb[:, lo:hi] = vall[q, 0:1, 0:dq]
        qb[:, 2 * D + lo:2 * D + hi] = vall[q, 1:2, 0:dq]
        vec_o[0:6, lo:hi] = vall[q, 2:8, 0:dq]
        for j in range(fq // 256):
            bup_o[:, q * fq + j * 256:q * fq + (j + 1) * 256] = vall[q, 8 + j:9 + j, :]
        tab[:, q * bq:(q + 1) * bq] = vall[q, 16:32, 0:bq]
    rel_rows(tab, bk_ref, rel)
    rel_rows(tab, bkf_o, relf_ref)
    for e in AGSLOTS["w"][AGMID:]:
        A.ev(e)
    for i, n in enumerate(RPIECES):
        if n in QROW:
            loc[i].wait()
            for r in A.rels(n):
                A.got_core(n, r)
    qkv_proj(wq, qb, xlow, qkv, {i: [functools.partial(A.ev, e) for e in AGSLOTS.get(f"n{i}", [])] for i in range(3 * D // 256)})
    wc = pltpu.make_async_copy(wq, wq_o, ls.at[8])
    qc = pltpu.make_async_copy(qkv, qkv_o, ls.at[9])
    wc.start()
    qc.start()
    attn_fwd(len_ref, qkv, rel, ctx_ref, lse_ref, bias_scr, S, D, {i: [functools.partial(A.ev, e) for e in AGSLOTS.get(f"t{i}", [])] for i in range(D // 64)})
    after("tail")
    for c in (xo, wc, qc):
        c.wait()
    for i, n in enumerate(RPIECES):
        if n not in QROW:
            loc[i].wait()
            for r in A.rels(n):
                A.got_core(n, r)
    A.drain()


def ffn_kernel(lab_ref, x_ref, ctx_ref, cot_ref, wo_ref, wu_ref, wd_ref, vec_ref, bup_ref,
               out_ref, dfs_ref, dctx_ref, nl_ref, act_ref, dl_ref, al_ref, ul_ref, gv_ref, gbu_ref, loss_ref,
               gp_scr, z1_scr, z2_scr, r_scr,
               ds_scr, sc_snd, sc_all, sss, ssr, *, T, R, C, Q):
    i = pl.program_id(0)
    D, FF = wu_ref.shape
    cid = lax.axis_index("cand")

    def score_copy(j):
        return pltpu.make_async_remote_copy(sc_snd, sc_all.at[cid], sss.at[j - 1], ssr.at[j - 1], device_id={"cand": lax.rem(cid + j, C)}, device_id_type=MESH)

    @pl.when(i == 0)
    def _():
        b = pltpu.get_barrier_semaphore()
        for j in range(1, C):
            pl.semaphore_signal(b, inc=1, device_id={"cand": lax.rem(cid + j, C)}, device_id_type=MESH)
        pl.semaphore_wait(b, C - 1)
        gv_ref[...] = jnp.zeros_like(gv_ref)
        gbu_ref[...] = jnp.zeros_like(gbu_ref)
        ds_scr[...] = jnp.zeros_like(ds_scr)
        sc_snd[...] = jnp.zeros_like(sc_snd)

    @pl.when(i < T)
    def _():
        fwd_tile(jnp.minimum(i, 1), x_ref, ctx_ref, wo_ref, wu_ref, wd_ref, vec_ref, bup_ref, out_ref, nl_ref, act_ref, gp_scr, z1_scr, z2_scr, r_scr, R)

    @pl.when(i == 0)
    def _():
        for m in range(2):
            sc = jnp.sum(out_ref[m, 0:1, :] * vec_ref[5:6, :], axis=1, keepdims=True)
            sc_snd[m:m + 1, :] = jnp.broadcast_to(sc, (1, 128))
        sc_all[cid] = sc_snd[...]
        for j in range(1, C):
            score_copy(j).start()

    @pl.when(i == T)
    def _():
        for j in range(1, C):
            score_copy(j).wait()
        total = jnp.zeros((1, 128), F32)
        own = sc_snd[...]
        for m in range(2):
            rows = [sc_all[j, m:m + 1, :] for j in range(C)]
            peak = functools.reduce(jnp.maximum, rows)
            lse = peak + jnp.log(functools.reduce(lambda a, b: a + b, [jnp.exp(r - peak) for r in rows]))
            lab = lab_ref[m]
            picked = functools.reduce(lambda a, b: a + b, [jnp.where(lab == j, r, 0.0) for j, r in enumerate(rows)])
            total = total + (lse - picked)
            ds_scr[m:m + 1, :] = (jnp.exp(own[m:m + 1, :] - lse) - jnp.where(lab == cid, 1.0, 0.0)) * (1.0 / Q)
        loss_ref[...] = jnp.broadcast_to(jnp.where(cid == 0, total * (1.0 / Q), 0.0), (8, 128))

    @pl.when((i >= 1) & (i <= T))
    def _():
        t = lax.rem(i, T)
        bwd_tile(jnp.minimum(t, 1), ds_scr, cot_ref, wo_ref, wu_ref, wd_ref, vec_ref, dfs_ref, dctx_ref, gv_ref, gbu_ref, dl_ref, ul_ref, al_ref, gp_scr, z1_scr, z2_scr, r_scr, R)


def back_kernel(len_ref, nl_h, dl_h, al_h, ctx_h, act_h, ul_h, qkv_h, dctx_h, xlow_h, wq_h, dfs_h, lse_ref, relf, bkf_ref, gv_ref, gbu_ref, loss_ref,
                *rest, C, Q, fast):
    if fast:
        ig_h, p_out, u_out, d_out, v_out = rest[:5]
        scr = rest[5:]
    else:
        ig_h, gq_o, go_o, gu_o, gd_o, gb_o, gtab_o = rest[:7]
        scr = rest[7:]
    (nl, dl, al, ctx, ch, qkv, dctx, xlow, wq, dfs, igt, gq, go, gu, gd, drelf, bias_scr, acc_scr, gb, gtab, ls, cs_, os_) = scr[:23]
    NS, D = nl.shape
    FF = gu.shape[1]
    S = NS // 2
    NZ = FF // 768
    load = lambda i, src, dst: pltpu.make_async_copy(src, dst, ls.at[i])
    big = [load(0, nl_h, nl), load(1, dl_h, dl), load(2, al_h, al), load(3, ctx_h, ctx), load(4, qkv_h, qkv), load(5, dctx_h, dctx),
           load(6, xlow_h, xlow), load(7, wq_h, wq), load(8, dfs_h, dfs)]
    if fast:
        g = Geo(C, Q)
        seq = [(ul_h, jnp.bitwise_xor(g.z, zi)) for zi in (3, 2, 1, 0)]
        qorder = [(1, 1), (1, 0), (0, 1), (0, 0)]
        seq += [(act_h, (1 - g.x if dx else g.x) * 2 + (1 - g.k if dk else g.k)) for dx, dk in qorder]
    else:
        seq = [(ul_h, i) for i in range(NZ)] + [(act_h, i) for i in range(NZ)]
    off = lambda i: pl.multiple_of(seq[i][1] * 768, 128)
    chunk = lambda i: pltpu.make_async_copy(seq[i][0].at[:, pl.ds(off(i), 768)], ch.at[i % 2], cs_.at[i % 2])
    if fast:
        peers = [{"query": lax.rem(lax.axis_index("query") + j, Q)} for j in range(1, Q)] + [{"cand": lax.rem(lax.axis_index("cand") + j, C)} for j in range(1, C)]
        bar = pltpu.get_barrier_semaphore()
        for p in peers:
            pl.semaphore_signal(bar, inc=1, device_id=p, device_id_type=MESH)
    for c in (big[2], big[3], big[0], chunk(0), chunk(1), big[1]):
        c.start()
    if fast:
        bufs = {n: scr[23 + 4 * i:27 + 4 * i] for i, n in enumerate(RPIECES)}
        h_scr, e_snd, e_rcv, vb0, va, vs, vb, ss, rs, es, qs, qr, cs, cr = scr[23 + NB:]
        R = RS(g, (gq, go, gu, gd), bufs, ss, rs)
        c_ = lax.axis_index("cand")
        q_ = lax.axis_index("query")

    def after(name):
        if fast:
            for e in FIRST.get(name, []) + SLOTS.get(name, []):
                R.ev(e)
    big[2].wait()
    big[3].wait()
    go[...] = dg(al[...], ctx[...], TN).astype(BF)
    big[0].wait()
    for i in range(NZ):
        chunk(i).wait()
        gu[:, pl.ds(off(i), 768)] = dg(nl[...], ch[i % 2], TN).astype(BF)
        chunk(i + 2).start()
        if i == 0:
            if fast:
                pl.semaphore_wait(bar, len(peers))
            after("o")
        after(f"u{i}")
    big[1].wait()
    for i in range(NZ, 2 * NZ):
        chunk(i).wait()
        gd[:, pl.ds(off(i), 768)] = dg(dl[...], ch[i % 2], TN).astype(BF)
        if i + 2 < 2 * NZ:
            chunk(i + 2).start()
        if i == NZ:
            big[4].start()
            big[5].start()
        if i == NZ + 2:
            for c in big[6:]:
                c.start()
        after(f"d{i - NZ}")
    slots = {}
    if fast:
        for i in range(2 * (D // 128)):
            slots[i] = [functools.partial(R.ev, e) for e in SLOTS.get(f"t{i}", [])]
    drelf[...] = jnp.zeros_like(drelf)
    big[4].wait()
    big[5].wait()
    attn_bwd(len_ref, qkv, dctx, lse_ref, relf, drelf, bias_scr, acc_scr, S, D, slots)
    big[6].wait()

    def b1(n, _):
        o = pl.multiple_of(n * 256, 256)
        t = qkv[:, pl.ds(o, 256)]
        gq[pl.ds(o, 256), :] = dg(t, xlow[...], TN).astype(BF)
        gb[:, pl.ds(o, 256)] = jnp.sum(t.astype(F32), axis=0, keepdims=True)
        return 0
    for i in range(3):
        lax.fori_loop(i * D // 256, (i + 1) * D // 256, b1, 0)
        after(f"g{i}")
    nb, nn = gtab.shape[1], bkf_ref.shape[1]
    hot = (lax.broadcasted_iota(jnp.int32, (nb, nn), 0) == bkf_ref[...]).astype(F32)
    gtab[...] = dg(drelf[...], hot, NT, lax.Precision.HIGHEST)
    if fast:
        dq, fq, bq = D // Q, FF // Q, nb // Q
        vb0[...] = jnp.zeros_like(vb0)
        for q in range(Q):
            lo = slice(q * dq, (q + 1) * dq)
            vb0[q, 0:1, 0:dq] = gb[:, q * dq:(q + 1) * dq]
            vb0[q, 1:2, 0:dq] = gb[:, 2 * D + q * dq:2 * D + (q + 1) * dq]
            vb0[q, 2:8, 0:dq] = gv_ref[0:6, lo]
            for j in range(fq // 256):
                vb0[q, 8 + j:9 + j, :] = gbu_ref[:, q * fq + j * 256:q * fq + (j + 1) * 256]
            vb0[q, 11:12, 0:128] = loss_ref[0:1, :]
            vb0[q, 16:32, 0:bq] = gtab[:, q * bq:(q + 1) * bq]
        vq = []
        for j in range(1, Q):
            qq = lax.rem(q_ + j, Q)
            c = pltpu.make_async_remote_copy(vb0.at[qq], va.at[q_], qs.at[j - 1], qr.at[j - 1], device_id={"query": qq}, device_id_type=MESH)
            c.start()
            vq.append(c)
        va[q_] = vb0[q_]
        after("v")
    big[7].wait()
    big[8].wait()
    steps = NS // 256
    outc = lambda r: pltpu.make_async_copy(igt.at[r % 2], ig_h.at[pl.ds(r * 256, 256), :], os_.at[r % 2])
    for r in range(steps):
        if r >= 2:
            outc(r - 2).wait()
        igt[r % 2] = dfs[r * 256:(r + 1) * 256, :] + dg(qkv[r * 256:(r + 1) * 256, :], wq[...], NN)
        outc(r).start()
        after(f"i{r}")
    for r in range(max(0, steps - 2), steps):
        outc(r).wait()
    if fast:
        for c in vq:
            c.wait()
        t = functools.reduce(lambda a, b: a + b, [va[j] for j in range(Q)])
        vs[...] = t
        vb[c_] = t
        vc = []
        for j in range(1, C):
            c = pltpu.make_async_remote_copy(vs, vb.at[c_], cs.at[j - 1], cr.at[j - 1], device_id={"cand": lax.rem(c_ + j, C)}, device_id_type=MESH)
            c.start()
            vc.append(c)
        R.fin("u", u_out)
        R.fin("d", d_out)
        for e in TAIL:
            R.ev(e)
        for n in ("o", "qz", "qb", "qa"):
            R.fin(n, h_scr.at[pl.ds(QROW.get(n, 144), RSHP[n][0])])
        k = g.k
        lo = h_scr[:, 0:192]
        hi = h_scr[:, 192:384]
        e_snd[...] = jnp.where(k == 0, hi, lo)
        c = pltpu.make_async_remote_copy(e_snd, e_rcv, es.at[0], es.at[1], device_id=R.partner, device_id_type=MESH)
        c.start()
        p_out[k] = jnp.where(k == 0, lo, hi)
        c.wait()
        p_out[1 - k] = e_rcv[...]
        for c in vc:
            c.wait()
        v_out[...] = functools.reduce(lambda a, b: a + b, [vb[j] for j in range(C)])
        R.drain()
    else:
        gq_o[...] = gq[...]
        go_o[...] = go[...]
        gu_o[...] = gu[...]
        gd_o[...] = gd[...]
        gb_o[...] = gb[...]
        gtab_o[...] = gtab[...]


def finish_kernel(out_h, ig_h, p_ref, u_ref, d_ref, v_ref, out_o, ig_o, gq_o, go_o, gu_o, gd_o, *rest):
    vec_o, bup_o, tab_o, loss_o = rest[:8], rest[8], rest[9], rest[10]
    buf, si, so = rest[11:]
    n, rows = buf.shape[0] // 2, buf.shape[1]
    src = [h.at[pl.ds(i * rows, rows), :] for h in (out_h, ig_h) for i in range(n)]
    dst = [h.at[pl.ds(i * rows, rows), :] for h in (out_o, ig_o) for i in range(n)]
    ins = [pltpu.make_async_copy(src[i], buf.at[i], si.at[i]) for i in range(2 * n)]
    outs = [pltpu.make_async_copy(buf.at[i], dst[i], so.at[i]) for i in range(2 * n)]
    for c in ins:
        c.start()
    for a, b in zip(ins, outs):
        a.wait()
        b.start()
    ha = gq_o.shape[1] // 2
    gq_o[...] = jnp.concatenate([p_ref[0, 0:ha, :], p_ref[1, 0:ha, :]], axis=0).T
    go_o[...] = jnp.concatenate([p_ref[0, ha:, :], p_ref[1, ha:, :]], axis=0).T
    gu_o[...] = u_ref[...]
    gd_o[...] = d_ref[...]
    for i in range(8):
        vec_o[i][...] = v_ref[i:i + 1, 0:vec_o[i].shape[1]]
    for j in range(bup_o.shape[1] // 256):
        bup_o[:, j * 256:(j + 1) * 256] = v_ref[8 + j:9 + j, :]
    loss_o[...] = v_ref[11:12, 0:1]
    tab_o[...] = v_ref[16:16 + tab_o.shape[0], 0:tab_o.shape[1]]
    for c in outs:
        c.wait()


def sds(shape, dtype=F32):
    return jax.ShapeDtypeStruct(shape, dtype)


def back_scratch(fast, C, Q, NS=1024, S=512, D=768, FF=3072, NBK=256):
    v = pltpu.VMEM
    dma = pltpu.SemaphoreType.DMA
    scr = [v((NS, D), BF)] * 4 + [v((2, NS, 768), BF), v((NS, 3 * D), BF), v((NS, D), BF), v((NS, D), BF), v((3 * D, D), BF), v((NS, D), F32), v((2, 256, D), F32),
                                  v((3 * D, D), BF), v((D, D), BF), v((D, FF), BF), v((D, FF), BF), v((16, 2 * S), F32),
                                  v((2, S, S), F32), v((2, S, S), F32), v((1, 3 * D), F32), v((16, NBK), F32), dma((9,)), dma((2,)), dma((2,))]
    if fast:
        scr += rs_bufs() + [v((192, 384), F32), v((192, 192), F32), v((192, 192), F32), v((Q, 32, 256), F32), v((Q, 32, 256), F32), v((32, 256), F32), v((C, 32, 256), F32),
                            dma((len(RPIECES), 31)), dma((len(RPIECES), 31)), dma((2,)), dma((Q,)), dma((Q,)), dma((C,)), dma((C,))]
    return scr


def body(hidden_in, out_cotangent, lengths, labels, buckets, w_qkv, w_out, w_up, w_down, bias_q, bias_v, bias_out,
         norm1_gain, norm1_bias, bias_up, bias_down, norm2_gain, score_vector, rel_table):
    Q = lax.axis_size("query")
    C = lax.axis_size("cand")
    micro = hidden_in.shape[0]
    S, D = hidden_in.shape[3:]
    FF = w_up.shape[1] * C
    NBK = rel_table.shape[0] * Q
    dq, fq, bq = D // Q, FF // Q, NBK // Q
    fast = Q == 4 and C == 8 and D == 768 and FF == 3072
    x = hidden_in.reshape(micro, S, D)
    cot = out_cotangent.reshape(micro, S, D)
    lens = lengths.reshape(micro)
    labs = labels.reshape(micro)
    NS = micro * S
    v = pltpu.VMEM
    dma = pltpu.SemaphoreType.DMA
    eight = [bias_q, bias_v, bias_out, norm1_gain, norm1_bias, bias_down, norm2_gain, score_vector]
    if fast:
        np_ = len(RPIECES)
        wq, wo, wu, wd, vec, bup, xlow, qkv, ctx, lse, relf, bkf = pl.pallas_call(
            functools.partial(front_kernel, C=C, Q=Q), in_specs=[SM] + [ANY] * 5 + [VM] * 11, out_specs=[ANY] * 4 + [VM] * 2 + [ANY] * 2 + [VM] * 4,
            out_shape=[sds((3 * D, D), BF), sds((D, D), BF), sds((D, FF), BF), sds((D, FF), BF), sds((8, D)), sds((1, FF)), sds((NS, D), BF), sds((NS, 3 * D), BF),
                       sds((NS, D), BF), sds((micro, 16, S)), sds((16, 2 * S)), sds((1, 2 * S), jnp.int32)],
            scratch_shapes=[v(w_qkv.shape, F32), v(w_out.shape, F32), v(w_up.shape, F32), v(w_down.shape[::-1], F32), v((32, 256), F32), v((1, 2 * S), jnp.int32),
                            v((micro, S, D), F32), v((NS, D), BF), v((NS, 3 * D), BF), v((3 * D, D), BF), v((2, 192, 192), BF), v((192, 192), BF), v((192, 384), BF),
                            v((192, 384), BF), v((96, 768), BF), v((Q, 32, 256), F32), v((16, NBK), F32), v((16, 2 * S), F32), v((1, 3 * D), F32), v((2, S, S), F32)]
            + [dma((np_, 16))] * 4 + [dma((Q,))] * 2 + [dma((2,)), dma((14,))],
            compiler_params=pltpu.CompilerParams(collective_id=0, has_side_effects=True, vmem_limit_bytes=67043328),
        )(lens, x, w_qkv, w_out, w_up, w_down.T, *[t.reshape(1, -1) for t in eight], bias_up.reshape(1, -1), rel_table.T, buckets.reshape(1, -1))
    else:
        bk = jnp.pad(buckets, (0, 1), constant_values=-1)[None, :]
        bkf = jnp.pad(buckets[::-1], (0, 1), constant_values=-1)[None, :]
        def gather(w):
            part = lax.all_gather(w.astype(BF), "query", axis=0, tiled=True)
            return lax.all_gather(part, "cand", axis=1, tiled=True)
        wq, wo, wu, wd = gather(w_qkv).T, gather(w_out).T, gather(w_up), gather(w_down).T
        vall = lax.all_gather(jnp.concatenate(eight + [bias_up, rel_table.reshape(-1)]), "query", axis=0, tiled=False)
        vecs = vall[:, :8 * dq].reshape(Q, 8, dq).transpose(1, 0, 2).reshape(8, D)
        bup = vall[:, 8 * dq:8 * dq + fq].reshape(1, FF)
        tab = jnp.pad(vall[:, 8 * dq + fq:].reshape(NBK, HEADS).T, ((0, 4), (0, 0)))
        qkv_bias = jnp.concatenate([vecs[0:1], jnp.zeros((1, D), F32), vecs[1:2]], axis=1)
        vec = jnp.concatenate([vecs[2:], jnp.zeros((2, D), F32)], axis=0)
        xlow, qkv, ctx, lse, relf = pl.pallas_call(
            attn_fwd_kernel, in_specs=[SM] + [VM] * 6, out_specs=[VM] * 5,
            out_shape=[sds((NS, D), BF), sds((NS, 3 * D), BF), sds((NS, D), BF), sds((micro, 16, S)), sds((16, 2 * S))],
            scratch_shapes=[v((16, 2 * S), F32), v((2, S, S), F32)],
            compiler_params=pltpu.CompilerParams(vmem_limit_bytes=60 * 2**20))(lens, x, wq, qkv_bias, tab, bk, bkf)
    R = 256
    Rh, T = R // micro, NS // R
    tb = lambda im, n=D: pl.BlockSpec((micro, Rh, n), im)
    fw = lambda i: (0, jnp.minimum(i, T - 1), 0)
    bw = lambda i: (0, lax.rem(jnp.maximum(i, 1), T), 0)
    tok = lambda n, dt=BF: sds((micro, S, n), dt)
    out, dfs, dctx, nl, act, dl, al, ul, gv, gbu, lossv = pl.pallas_call(
        functools.partial(ffn_kernel, T=T, R=R, C=C, Q=Q), grid=(T + 1,),
        in_specs=[SM, tb(fw), tb(fw), tb(bw)] + [VM] * 5, out_specs=[tb(fw), tb(bw), tb(bw), tb(fw), tb(fw, FF), tb(bw), tb(bw), tb(bw, FF)] + [VM] * 3,
        out_shape=[tok(D, F32), tok(D, F32), tok(D), tok(D), tok(FF), tok(D), tok(D), tok(FF), sds((8, D)), sds((1, FF)), sds((8, 128))],
        scratch_shapes=[pltpu.VMEM((2, R, FF), F32), pltpu.VMEM((2, R, D), F32), pltpu.VMEM((2, R, D), F32), pltpu.VMEM((2, R, 128), F32),
                        pltpu.VMEM((8, 128), F32), pltpu.VMEM((8, 128), F32), pltpu.VMEM((C, 8, 128), F32), pltpu.SemaphoreType.DMA((C,)), pltpu.SemaphoreType.DMA((C,))],
        compiler_params=pltpu.CompilerParams(collective_id=1, has_side_effects=True, vmem_limit_bytes=67043328),
    )(labs, x, ctx.reshape(micro, S, D), cot, wo, wu, wd, vec, bup)
    flat = lambda t: t.reshape(NS, t.shape[-1])
    gouts = [sds((2, 192, 192)), sds((192, 384)), sds((96, 768)), sds((32, 256))] if fast else \
        [sds((3 * D, D), BF), sds((D, D), BF), sds((D, FF), BF), sds((D, FF), BF), sds((1, 3 * D)), sds((16, NBK))]
    res = pl.pallas_call(
        functools.partial(back_kernel, C=C, Q=Q, fast=fast), in_specs=[SM] + [ANY] * 11 + [VM] * 6, out_specs=[ANY] + [VM] * len(gouts),
        out_shape=[sds((NS, D))] + gouts, scratch_shapes=back_scratch(fast, C, Q, NS, S, D, FF, NBK),
        compiler_params=pltpu.CompilerParams(collective_id=2 if fast else None, has_side_effects=True, vmem_limit_bytes=67043328),
    )(lens, flat(nl), flat(dl), flat(al), ctx, flat(act), flat(ul), qkv, flat(dctx), xlow, wq, flat(dfs), lse, relf, bkf, gv, gbu, lossv)
    ig = res[0]
    if fast:
        fin = pl.pallas_call(
            finish_kernel, in_specs=[ANY] * 2 + [VM] * 4, out_specs=[ANY] * 2 + [VM] * 15,
            out_shape=[sds((NS, D)), sds((NS, D)), sds(w_qkv.shape), sds(w_out.shape), sds(w_up.shape), sds(w_down.shape[::-1])] + [sds((1, dq))] * 8
            + [sds((1, fq)), sds((HEADS, bq)), sds((1, 1))],
            scratch_shapes=[v((8, NS // 4, D), F32), dma((8,)), dma((8,))],
            compiler_params=pltpu.CompilerParams(vmem_limit_bytes=67043328))(flat(out), ig, *res[1:])
        out, ig, g_qkv, g_out, g_up = fin[:5]
        g_down = fin[5].T
        small = [t.reshape(dq) for t in fin[6:14]]
        g_bup, g_tab, loss = fin[14].reshape(fq), fin[15].T, fin[16].reshape(())
    else:
        def scatter(g):
            rows, cols = g.shape[0] // Q, g.shape[1] // C
            tiles = g.astype(F32).reshape(Q, rows, C, cols).transpose(2, 0, 1, 3).reshape(C * Q, rows, cols)
            return lax.psum_scatter(tiles, ("cand", "query"), scatter_dimension=0, tiled=True)[0]
        gq, go, gu, gd, gb, gtab = res[1:]
        g_qkv, g_out, g_up, g_down = scatter(gq.T), scatter(go.T), scatter(gu), scatter(gd.T)
        gvecs = jnp.concatenate([gb[:, :D], gb[:, 2 * D:], gv[:6]], axis=0)
        vg = jnp.concatenate([gvecs.reshape(8, Q, dq).transpose(1, 0, 2).reshape(Q, 8 * dq), gbu.reshape(Q, fq), gtab[:HEADS].T.reshape(Q, bq * HEADS),
                              jnp.broadcast_to(lossv[0:1, 0:1], (Q, 1))], axis=1)
        vg = jnp.pad(vg, ((0, 0), (0, -vg.shape[1] % 1024)))
        vs = lax.psum_scatter(lax.psum(vg, "cand"), "query", scatter_dimension=0, tiled=True)[0]
        small = [vs[i * dq:(i + 1) * dq] for i in range(8)]
        g_bup = vs[8 * dq:8 * dq + fq]
        g_tab = vs[8 * dq + fq:8 * dq + fq + bq * HEADS].reshape(bq, HEADS)
        loss = vs[8 * dq + fq + bq * HEADS]
    return (out.reshape(hidden_in.shape), ig.reshape(hidden_in.shape), g_qkv, g_out, g_up, g_down,
            small[0], small[1], small[2], small[3], small[4], g_bup, small[5], small[6], small[7], g_tab, loss)


def solution(mesh):
    seq, w, v = P(None, "query", "cand", None, None), P("query", "cand"), P("query")
    return jax.shard_map(
        body, mesh=mesh,
        in_specs=(seq, seq, P(None, "query", "cand"), P(None, "query"), P(), w, w, w, w) + (v,) * 9 + (P("query", None),),
        out_specs=(seq, seq, w, w, w, w) + (v,) * 9 + (P("query", None), P()),
        check_vma=False)
```

```python
import functools

import jax
import jax.numpy as jnp
from jax import lax
from jax.experimental import pallas as pl
from jax.experimental.pallas import tpu as pltpu
from jax.sharding import PartitionSpec as P

F32 = jnp.float32
BF = jnp.bfloat16
NT = (((1,), (1,)), ((), ()))
NN = (((1,), (0,)), ((), ()))
TN = (((0,), (0,)), ((), ()))
VM = pl.BlockSpec(memory_space=pltpu.VMEM)
SM = pl.BlockSpec(memory_space=pltpu.SMEM)
ANY = pl.BlockSpec(memory_space=pl.ANY)
MESH = pl.DeviceIdType.MESH
EPS = 1e-5
FC = 512
HEADS = 12
NR = {"x": 2, "y": 2, "z": 4}
RPIECES = ["u", "d", "o", "qa", "qb", "qz"]
RORD = {"u": "yxz", "d": "xyz", "o": "zyx", "qa": "yxz", "qb": "xyz", "qz": "zyx"}
RSHP = {"u": (192, 384, 48), "d": (96, 768, 48), "o": (48, 384, 48), "qa": (64, 384, 32), "qb": (64, 384, 32), "qz": (16, 384, 16)}
QROW = {"qa": 0, "qb": 64, "qz": 128}
NB = 4 * len(RPIECES)
AGSLOTS = {
    "b": [("u", (0, 0, 0), (("z", 1),)), ("d", (0, 0, 0), (("y", 1),)), ("u", (0, 0, 0), (("x", 1),))],
    "h": [("qa", (0, 0, 0), (("y", 1),)), ("qb", (0, 0, 0), (("x", 1),)), ("qa", (0, 0, 0), (("z", 3),)), ("qz", (0, 0, 0), (("z", 3), ("k", 0))), ("qb", (0, 0, 0), (("y", 1),)), ("u", (0, 0, 1), (("x", 1), ("y", 1), ("k", 0))), ("qb", (0, 0, 0), (("z", 2),)), ("qa", (0, 0, 0), (("z", 1),)), ("qb", (0, 0, 0), (("z", 3), ("z", 1))), ("qa", (0, 0, 0), (("x", 1),)), ("u", (0, 1, 0), (("y", 1), ("k", 0))), ("qz", (0, 0, 0), (("x", 1),)), ("qb", (0, 0, 2), (("y", 1), ("x", 1), ("k", 0))), ("qz", (0, 0, 0), (("y", 1),)), ("qb", (0, 0, 0), (("k", 0),)), ("qa", (0, 0, 0), (("z", 2),)), ("qb", (0, 1, 0), (("x", 1), ("k", 0))), ("qz", (0, 0, 1), (("y", 1), ("z", 1), ("z", 2), ("z", 3), ("k", 0))), ("d", (0, 0, 0), (("x", 1),)), ("qb", (0, 0, 3), (("y", 1), ("x", 1), ("k", 0))), ("qa", (0, 0, 1), (("x", 1), ("y", 1), ("k", 0))), ("u", (0, 0, 0), (("k", 0),)), ("d", (0, 0, 0), (("z", 1),)), ("qb", (0, 0, 1), (("y", 1), ("x", 1), ("k", 0))), ("qz", (0, 0, 0), (("z", 1),)), ("o", (0, 0, 0), (("k", 0),)), ("d", (0, 0, 0), (("z", 3),)), ("qa", (0, 0, 2), (("x", 1), ("y", 1), ("k", 0))), ("qz", (2, 0, 1), (("k", 0),)), ("qz", (0, 1, 1), (("z", 1), ("z", 2), ("z", 3), ("k", 0))), ("qz", (0, 1, 0), (("z", 1), ("z", 2), ("z", 3), ("k", 0))), ("d", (0, 0, 1), (("y", 1), ("x", 1), ("k", 0))), ("qa", (0, 0, 3), (("x", 1), ("y", 1), ("k", 0)))],
    "p0": [("qa", (0, 0, 0), (("k", 0),)), ("qz", (1, 0, 1), (("k", 0),)), ("qa", (1, 0, 1), (("k", 0),)), ("o", (0, 0, 0), (("x", 1),))],
    "p1": [("qz", (0, 0, 0), (("z", 2),)), ("o", (0, 0, 0), (("y", 1),)), ("qz", (2, 1, 1), (("k", 0),)), ("qb", (0, 1, 1), (("x", 1), ("k", 0))), ("qa", (0, 1, 0), (("y", 1), ("k", 0))), ("qa", (0, 1, 2), (("y", 1), ("k", 0))), ("qz", (1, 0, 0), (("k", 0),))],
    "p2": [("qb", (1, 0, 1), (("k", 0),)), ("u", (0, 0, 0), (("z", 2),)), ("qa", (1, 0, 3), (("k", 0),)), ("qb", (0, 1, 2), (("x", 1), ("k", 0))), ("qz", (3, 0, 0), (("k", 0),)), ("o", (0, 0, 0), (("z", 1),)), ("qb", (1, 0, 2), (("k", 0),)), ("qz", (2, 1, 0), (("k", 0),)), ("qz", (1, 1, 0), (("k", 0),)), ("qa", (0, 1, 3), (("y", 1), ("k", 0))), ("qa", (1, 0, 0), (("k", 0),)), ("qb", (1, 1, 0), (("k", 0),)), ("qb", (0, 1, 3), (("x", 1), ("k", 0))), ("d", (0, 1, 1), (("x", 1), ("k", 0))), ("qz", (2, 0, 0), (("k", 0),)), ("qa", (0, 1, 1), (("y", 1), ("k", 0))), ("qz", (3, 0, 1), (("k", 0),)), ("u", (0, 0, 0), (("z", 3),)), ("d", (0, 0, 0), (("z", 2),)), ("d", (0, 0, 3), (("y", 1), ("x", 1), ("k", 0))), ("u", (0, 1, 1), (("y", 1), ("k", 0))), ("qa", (1, 1, 0), (("k", 0),)), ("qz", (3, 1, 0), (("k", 0),)), ("qz", (3, 1, 1), (("k", 0),)), ("qb", (1, 1, 2), (("k", 0),)), ("qa", (1, 0, 2), (("k", 0),)), ("qa", (1, 1, 3), (("k", 0),)), ("qa", (1, 1, 2), (("k", 0),)), ("qb", (1, 0, 3), (("k", 0),)), ("qb", (1, 1, 3), (("k", 0),)), ("qb", (1, 1, 1), (("k", 0),)), ("qb", (1, 0, 0), (("k", 0),)), ("qz", (1, 1, 1), (("k", 0),)), ("qa", (1, 1, 1), (("k", 0),))],
    "n0": [("o", (0, 1, 0), (("z", 1), ("z", 2), ("z", 3), ("k", 0))), ("d", (1, 0, 1), (("k", 0),))],
    "n1": [("d", (0, 1, 0), (("x", 1), ("k", 0))), ("o", (0, 0, 1), (("y", 1), ("z", 1), ("z", 2), ("z", 3), ("k", 0)))],
    "n2": [("u", (1, 0, 1), (("k", 0),)), ("u", (0, 0, 2), (("x", 1), ("y", 1), ("k", 0)))],
    "n5": [("o", (0, 1, 1), (("z", 1), ("z", 2), ("z", 3), ("k", 0))), ("u", (0, 0, 0), (("y", 1),))],
    "n8": [("u", (0, 0, 3), (("x", 1), ("y", 1), ("k", 0))), ("d", (0, 1, 3), (("x", 1), ("k", 0))), ("o", (1, 0, 0), (("k", 0),)), ("d", (1, 0, 0), (("k", 0),))],
    "t3": [("d", (0, 0, 2), (("y", 1), ("x", 1), ("k", 0))), ("d", (1, 0, 3), (("k", 0),))],
    "t4": [("d", (0, 0, 0), (("k", 0),)), ("o", (0, 0, 0), (("z", 3),)), ("u", (1, 0, 0), (("k", 0),))],
    "t5": [("u", (0, 1, 2), (("y", 1), ("k", 0)))],
    "t6": [("o", (3, 1, 0), (("k", 0),)), ("u", (0, 1, 3), (("y", 1), ("k", 0))), ("d", (0, 1, 2), (("x", 1), ("k", 0))), ("u", (1, 0, 2), (("k", 0),)), ("o", (2, 1, 0), (("k", 0),)), ("d", (1, 1, 1), (("k", 0),)), ("u", (1, 1, 1), (("k", 0),))],
    "t8": [("u", (1, 1, 0), (("k", 0),)), ("u", (1, 0, 3), (("k", 0),)), ("o", (0, 0, 0), (("z", 2),)), ("d", (1, 1, 3), (("k", 0),)), ("o", (3, 0, 1), (("k", 0),)), ("d", (1, 1, 0), (("k", 0),)), ("u", (1, 1, 2), (("k", 0),)), ("o", (2, 1, 1), (("k", 0),))],
    "t9": [("d", (1, 0, 2), (("k", 0),))],
    "t10": [("o", (1, 1, 0), (("k", 0),)), ("o", (2, 0, 1), (("k", 0),)), ("d", (1, 1, 2), (("k", 0),)), ("o", (1, 1, 1), (("k", 0),)), ("o", (3, 1, 1), (("k", 0),)), ("u", (1, 1, 3), (("k", 0),)), ("o", (1, 0, 1), (("k", 0),)), ("o", (3, 0, 0), (("k", 0),)), ("o", (2, 0, 0), (("k", 0),))],
}
SLOTS = {
    "u0": [("s0", "o", 0, 0, 1), ("s0", "o", 3, 1, 1), ("s0", "u", 0, 0, 3)],
    "u1": [("s0", "u", 1, 1, 3), ("s0", "o", 1, 0, 0), ("s0", "u", 1, 1, 2), ("s0", "u", 1, 0, 3), ("s0", "u", 0, 1, 2), ("s0", "o", 2, 0, 1), ("s0", "o", 1, 1, 1)],
    "u2": [("s0", "o", 2, 1, 1), ("s0", "o", 2, 1, 0), ("s0", "u", 1, 1, 1), ("s0", "o", 2, 0, 0), ("s0", "u", 0, 1, 3), ("s1", "u", 1, 1, 3)],
    "u3": [("s1", "u", 1, 1, 2), ("s0", "o", 3, 0, 1), ("s1", "o", 2, 0, 1)],
    "d1": [("s0", "d", 1, 0, 3), ("s0", "d", 1, 1, 1), ("s0", "o", 3, 1, 0), ("s0", "d", 1, 1, 3), ("s1", "u", 1, 0, 3), ("s0", "d", 1, 0, 2), ("s1", "o", 3, 1, 1), ("s0", "d", 1, 0, 1)],
    "d2": [("s0", "u", 0, 0, 1), ("s0", "u", 1, 0, 0), ("s1", "d", 1, 0, 3), ("s0", "o", 3, 0, 0), ("s0", "d", 1, 1, 2)],
    "d3": [("s1", "o", 3, 0, 1), ("s1", "u", 1, 1, 1), ("s1", "o", 2, 0, 0), ("s1", "d", 1, 1, 3), ("s0", "d", 0, 1, 3), ("s2", "u", 1, 3), ("s0", "d", 1, 1, 0), ("s1", "o", 2, 1, 1), ("s1", "u", 1, 0, 0), ("s0", "o", 1, 1, 0), ("s0", "u", 1, 1, 0), ("s0", "u", 1, 0, 1), ("s0", "o", 1, 0, 1), ("s1", "o", 1, 1, 1), ("s1", "o", 3, 1, 0), ("s0", "d", 0, 1, 2), ("s0", "u", 0, 1, 0), ("s1", "o", 3, 0, 0)],
    "t0": [("s0", "o", 0, 1, 0), ("s0", "d", 0, 0, 1), ("s1", "d", 1, 1, 2)],
    "t2": [("s2", "d", 1, 3), ("s1", "o", 2, 1, 0)],
    "t3": [("s0", "u", 0, 0, 2), ("s1", "d", 1, 0, 2), ("s0", "u", 0, 1, 1), ("s1", "o", 1, 1, 0), ("s3", "u", 3), ("s0", "u", 1, 0, 2), ("s0", "d", 0, 0, 3), ("s0", "d", 0, 0, 2), ("s0", "o", 0, 1, 1), ("s1", "d", 1, 1, 1)],
    "t4": [("s3", "d", 3), ("s1", "o", 1, 0, 0), ("s2", "u", 1, 2), ("s2", "o", 1, 1), ("s1", "u", 1, 0, 2), ("s2", "d", 1, 2), ("s0", "d", 0, 1, 1)],
    "t7": [("s1", "u", 1, 1, 0), ("s1", "o", 1, 0, 1), ("s2", "u", 1, 1), ("s2", "o", 1, 0)],
    "t8": [("s1", "d", 1, 0, 1), ("s2", "d", 1, 1), ("s3", "d", 2), ("s0", "o", 0, 0, 0)],
    "t9": [("s1", "d", 1, 1, 0), ("s3", "u", 2)],
    "g2": [("s0", "qb", 1, 0, 3), ("s0", "qa", 1, 1, 2), ("s0", "d", 0, 1, 0), ("s1", "u", 1, 0, 1), ("s0", "qb", 1, 1, 2), ("s0", "qb", 1, 1, 3), ("s0", "d", 1, 0, 0), ("s0", "qz", 3, 1, 0), ("s0", "qa", 0, 1, 2), ("s0", "qz", 2, 1, 0), ("s3", "o", 1)],
    "g3": [("s0", "d", 0, 0, 0), ("s0", "qa", 1, 1, 3), ("s0", "qz", 3, 0, 0), ("s0", "qz", 2, 0, 0), ("s1", "qb", 1, 0, 3)],
    "g4": [("s1", "qb", 1, 1, 3), ("s0", "qz", 3, 1, 1)],
    "g5": [("s0", "qz", 1, 1, 1), ("s0", "qz", 0, 0, 0), ("s1", "qz", 2, 0, 0), ("s1", "qa", 1, 1, 2), ("s0", "qz", 1, 1, 0), ("s0", "qb", 0, 0, 0), ("s0", "qa", 1, 1, 1), ("s1", "qz", 3, 0, 0), ("s0", "qb", 1, 0, 2), ("s0", "qa", 1, 0, 1), ("s1", "qb", 1, 1, 2), ("s0", "qb", 1, 1, 0), ("s0", "qb", 0, 0, 3), ("s0", "qb", 0, 1, 3), ("s0", "qa", 1, 0, 3), ("s0", "qa", 0, 0, 3), ("s0", "qb", 0, 0, 2), ("s0", "qz", 1, 0, 1), ("s2", "u", 1, 0), ("s0", "qz", 3, 0, 1), ("s0", "qb", 0, 1, 1), ("s0", "qa", 0, 1, 1), ("s0", "qb", 1, 0, 1), ("s0", "qa", 0, 1, 3), ("s3", "d", 1), ("s0", "qa", 0, 0, 1), ("s1", "qa", 1, 1, 3), ("s0", "qb", 1, 1, 1), ("s0", "qa", 1, 1, 0), ("s0", "qb", 0, 1, 0), ("s0", "qb", 0, 0, 1), ("s0", "qz", 2, 1, 1)],
    "v": [("s2", "qb", 1, 3), ("s1", "qz", 2, 1, 0), ("s0", "qz", 2, 0, 1), ("s1", "qb", 1, 1, 0), ("s0", "qa", 1, 0, 2), ("s1", "qa", 1, 1, 1), ("s1", "qz", 3, 1, 0), ("s1", "qz", 3, 0, 1), ("s1", "qa", 1, 1, 0), ("s1", "qz", 1, 0, 1), ("s1", "qz", 1, 1, 1), ("fin_", "o")],
    "i0": [("s0", "qa", 0, 0, 2), ("s2", "qa", 1, 3), ("s1", "qz", 2, 1, 1), ("s1", "qz", 1, 1, 0), ("s1", "qz", 3, 1, 1), ("s2", "qa", 1, 2), ("s1", "qa", 1, 0, 3), ("s0", "u", 0, 0, 0), ("s0", "qa", 1, 0, 0), ("s1", "qa", 1, 0, 2), ("s0", "qb", 0, 1, 2), ("s1", "qb", 1, 1, 1), ("s1", "qz", 2, 0, 1), ("s0", "qa", 0, 1, 0), ("s2", "d", 1, 0), ("s3", "u", 1), ("s2", "qa", 1, 1)],
    "i1": [("s1", "qb", 1, 0, 2), ("s2", "qa", 1, 0), ("s0", "qa", 0, 0, 0), ("s0", "qz", 0, 1, 1), ("s3", "qb", 3), ("s3", "qa", 3), ("s1", "qb", 1, 0, 1), ("s3", "qa", 2), ("s1", "qa", 1, 0, 1), ("s0", "qb", 1, 0, 0), ("s1", "d", 1, 0, 0), ("s2", "qb", 1, 2), ("s2", "qb", 1, 1)],
    "i2": [("s3", "qa", 1), ("s2", "qz", 1, 1), ("s0", "qz", 0, 1, 0), ("s1", "qa", 1, 0, 0), ("s1", "qb", 1, 0, 0), ("s0", "qz", 1, 0, 0), ("s3", "qb", 2), ("s2", "qb", 1, 0)],
    "i3": [("s0", "qz", 0, 0, 1), ("s3", "qb", 1), ("s1", "qz", 1, 0, 0), ("s3", "qz", 1), ("fin_", "qa"), ("s2", "qz", 1, 0), ("fin_", "u"), ("fin_", "d"), ("fin_", "qb"), ("fin_", "qz")],
}


def dg(a,b,d,prec=None): return lax.dot_general(a,b,d,preferred_element_type=F32,precision=prec)


def hooks(i, table):
    for j, evs in table.items():
        if evs:
            @pl.when(i == j)
            def _(evs=evs):
                for e in evs: e()


def qkv_proj(w_ref, bias_ref, xlow_ref, qkv_ref, slots):
    def body(n,_):
        o=pl.multiple_of(n*256,256)
        y=dg(xlow_ref[...], w_ref[pl.ds(o,256),:], NT)
        y=(y+bias_ref[:,pl.ds(o,256)])*jnp.where(o<xlow_ref.shape[1],0.125,1.0)
        qkv_ref[:,pl.ds(o,256)]=y.astype(BF)
        hooks(n, slots)
        return 0
    lax.fori_loop(0, w_ref.shape[0]//256, body, 0)


def rel_rows(tableT_ref, bk_ref, rel_ref):
    nb=tableT_ref.shape[1]; n=bk_ref.shape[1]
    hot=(lax.broadcasted_iota(jnp.int32,(nb,n),0)==bk_ref[...]).astype(F32)
    rel_ref[...]=dg(tableT_ref[...], hot, NN, lax.Precision.HIGHEST)


def bias_expand(row,S):
    R=pltpu.roll(jnp.broadcast_to(row,(128,2*S)), 2*S-127, 1, stride=1, stride_axis=0)
    nu=S//128
    return jnp.concatenate([R[:,128*(nu-1-u):128*(nu-1-u)+S] for u in range(nu)],axis=0)


def diag_sum(t,S):
    nu=S//128
    y=None
    for u in range(nu):
        a=128*(nu-1-u); parts=[]
        if a: parts.append(jnp.zeros((128,a),F32))
        parts.append(t[128*u:128*(u+1),:])
        if 2*S-a-S: parts.append(jnp.zeros((128,2*S-a-S),F32))
        v=jnp.concatenate(parts,axis=1) if len(parts)>1 else parts[0]
        y=v if y is None else y+v
    z=None
    for w in range(16):
        g=y[8*w:8*w+8,:]
        sh=120-8*w
        g=pltpu.roll(g,sh,1) if sh else g
        z=g if z is None else z+g
    out=None
    for b in range(8):
        g=z[b:b+1,:]
        g=pltpu.roll(g,7-b,1) if b<7 else g
        out=g if out is None else out+g
    return out


def attn_fwd(len_ref, qkv_ref, rel_ref, ctx_ref, lse_ref, bias_scr, S, D, slots):
    lane=lax.broadcasted_iota(jnp.int32,(1,128),1)
    col=lax.broadcasted_iota(jnp.int32,(1,S),1)
    def body(p,_):
        o=pl.multiple_of(p*128,128)
        for hh in range(2):
            row=rel_ref[pl.ds(p*2+hh,1),:]
            bias_scr[hh]=bias_expand(row,S)
        for m in range(2):
            q=qkv_ref[m*S:(m+1)*S,pl.ds(o,128)]
            k=qkv_ref[m*S:(m+1)*S,pl.ds(D+o,128)]
            v=qkv_ref[m*S:(m+1)*S,pl.ds(2*D+o,128)]
            valid=col<len_ref[m]
            outs=[]
            for hh in range(2):
                mk=(lane//64)==hh
                qm=jnp.where(mk,q,jnp.zeros_like(q))
                s=dg(qm,k,NT)+bias_scr[hh]
                s=jnp.where(valid,s,-1e30)
                mx=jnp.max(s,axis=1,keepdims=True)
                e=jnp.exp(s-mx)
                tot=jnp.sum(e,axis=1,keepdims=True)
                pl_=(e*(1.0/tot)).astype(BF)
                outs.append(dg(pl_,v,NN))
                lse_ref[m,pl.ds(p*2+hh,1),:]=jnp.transpose(mx+jnp.log(tot),(1,0))
            ctx_ref[m*S:(m+1)*S,pl.ds(o,128)]=jnp.where((lane//64)==0,outs[0],outs[1]).astype(BF)
            hooks(p, {i: slots.get(2*i+m) for i in range(D//128)})
        return 0
    lax.fori_loop(0, D//128, body, 0)


def attn_bwd(len_ref, qkv_ref, dctx_ref, lse_ref, relf_ref, drelf_ref, bias_scr, acc_scr, S, D, slots):
    lane=lax.broadcasted_iota(jnp.int32,(1,128),1)
    rowi=lax.broadcasted_iota(jnp.int32,(S,1),0)
    m0=(lane//64)==0
    def body(p,_):
        o=pl.multiple_of(p*128,128)
        for hh in range(2):
            row=relf_ref[pl.ds(p*2+hh,1),:]
            bias_scr[hh]=bias_expand(row,S)
        for m in range(2):
            q=qkv_ref[m*S:(m+1)*S,pl.ds(o,128)]
            k=qkv_ref[m*S:(m+1)*S,pl.ds(D+o,128)]
            v=qkv_ref[m*S:(m+1)*S,pl.ds(2*D+o,128)]
            do=dctx_ref[m*S:(m+1)*S,pl.ds(o,128)]
            valid=rowi<len_ref[m]
            oq=[];ok=[];ov=[]
            for hh in range(2):
                mk=(lane//64)==hh
                km=jnp.where(mk,k,jnp.zeros_like(k)); vm=jnp.where(mk,v,jnp.zeros_like(v))
                sT=dg(km,q,NT)+bias_scr[hh]
                sT=jnp.where(valid,sT,-1e30)
                pT=jnp.exp(sT-lse_ref[m,pl.ds(p*2+hh,1),:])
                dpT=dg(vm,do,NT)
                rd=jnp.sum(dpT*pT,axis=0,keepdims=True)
                ds=(pT*(dpT-rd)).astype(BF)
                ov.append(dg(pT.astype(BF),do,NN))
                ok.append(dg(ds,q,NN))
                oq.append(dg(ds,k,TN))
                if m==0: acc_scr[hh]=ds.astype(F32)
                else: acc_scr[hh]+=ds.astype(F32)
            qkv_ref[m*S:(m+1)*S,pl.ds(o,128)]=(jnp.where(m0,oq[0],oq[1])*0.125).astype(BF)
            qkv_ref[m*S:(m+1)*S,pl.ds(D+o,128)]=jnp.where(m0,ok[0],ok[1]).astype(BF)
            qkv_ref[m*S:(m+1)*S,pl.ds(2*D+o,128)]=jnp.where(m0,ov[0],ov[1]).astype(BF)
            hooks(p, {i: slots.get(2*i+m) for i in range(D//128)})
        for hh in range(2):
            drelf_ref[pl.ds(p*2+hh,1),:]=diag_sum(acc_scr[hh],S)
        return 0
    lax.fori_loop(0, D//128, body, 0)


def stats(z):
    mu=jnp.mean(z,axis=-1,keepdims=True); c=z-mu
    var=jnp.mean(c*c,axis=-1,keepdims=True)
    r=lax.rsqrt(var+EPS)
    return c*r, r


def fwd_tile(slot, x_ref, ctx_ref, wo_ref, wu_ref, wd_ref, vec_ref, bup_ref, out_ref, nl_scr, act_scr, gp_scr, z1_scr, z2_scr, r_scr, R):
    D=x_ref.shape[2]; FF=wu_ref.shape[1]
    ctx=ctx_ref[...].reshape(R,D)
    fs=x_ref[...].reshape(R,D)+(dg(ctx,wo_ref[...],NT)+vec_ref[0:1,:])
    z1,r1=stats(fs)
    z1_scr[slot]=z1
    fn=z1*vec_ref[1:2,:]+vec_ref[2:3,:]
    nl=fn.astype(BF)
    nl_scr[...]=nl.reshape(nl_scr.shape)
    def body(f,acc):
        o=pl.multiple_of(f*FC,FC)
        u=dg(nl_scr[...].reshape(R,D),wu_ref[:,pl.ds(o,FC)],NN)+bup_ref[:,pl.ds(o,FC)]
        phi=0.5*(1.0+lax.erf(u*(2.0**-0.5)))
        a=(u*phi).astype(BF)
        act_scr[:,:,pl.ds(o,FC)]=a.reshape(2,R//2,FC)
        gp_scr[slot,:,pl.ds(o,FC)]=phi+u*(jnp.exp(u*u*-0.5)*0.3989422804014327)
        return acc+dg(a,wd_ref[:,pl.ds(o,FC)],NT)
    acc=lax.fori_loop(0,FF//FC,body,fn+vec_ref[3:4,:])
    z2,r2=stats(acc)
    z2_scr[slot]=z2
    r_scr[slot,:,0:1]=r1
    r_scr[slot,:,1:2]=r2
    out_ref[...]=(z2*vec_ref[4:5,:]).reshape(out_ref.shape)


def lnb(u,z,r):
    return r*(u-jnp.mean(u,axis=-1,keepdims=True)-z*jnp.mean(u*z,axis=-1,keepdims=True))


def bwd_tile(slot, ds_ref, cot_ref, wo_ref, wu_ref, wd_ref, vec_ref, dfs_ref, dctx_ref, gv_ref, gbu_ref, dl_scr, ul_scr, al_scr, gp_scr, z1_scr, z2_scr, r_scr, R):
    D=wu_ref.shape[0]; FF=wu_ref.shape[1]; Rh=R//2
    r1=r_scr[slot,:,0:1]; r2=r_scr[slot,:,1:2]
    z2=z2_scr[slot]
    do=cot_ref[...].reshape(R,D)
    ri=lax.broadcasted_iota(jnp.int32,(R,1),0)
    coef=jnp.where(ri==0,ds_ref[0:1,0:1],0.0)+jnp.where(ri==Rh,ds_ref[1:2,0:1],0.0)
    do=do+coef*vec_ref[5:6,:]
    gv_ref[4:5,:]+=jnp.sum(do*z2,axis=0,keepdims=True)
    gv_ref[5:6,:]+=jnp.sum(coef*(z2*vec_ref[4:5,:]),axis=0,keepdims=True)
    d2=lnb(do*vec_ref[4:5,:],z2,r2)
    dl=d2.astype(BF)
    dl_scr[...]=dl.reshape(dl_scr.shape)
    gv_ref[3:4,:]+=jnp.sum(dl.astype(F32),axis=0,keepdims=True)
    def body(f,acc):
        o=pl.multiple_of(f*FC,FC)
        da=dg(dl_scr[...].reshape(R,D),wd_ref[:,pl.ds(o,FC)],NN)
        ul=(da*gp_scr[slot,:,pl.ds(o,FC)]).astype(BF)
        ul_scr[:,:,pl.ds(o,FC)]=ul.reshape(2,R//2,FC)
        gbu_ref[:,pl.ds(o,FC)]+=jnp.sum(ul.astype(F32),axis=0,keepdims=True)
        return acc+dg(ul,wu_ref[:,pl.ds(o,FC)],NT)
    d1=lax.fori_loop(0,FF//FC,body,d2)
    z1=z1_scr[slot]
    gv_ref[1:2,:]+=jnp.sum(d1*z1,axis=0,keepdims=True)
    gv_ref[2:3,:]+=jnp.sum(d1,axis=0,keepdims=True)
    dfs=lnb(d1*vec_ref[1:2,:],z1,r1)
    dfs_ref[...]=dfs.reshape(dfs_ref.shape)
    al=dfs.astype(BF)
    al_scr[...]=al.reshape(al_scr.shape)
    gv_ref[0:1,:]+=jnp.sum(al.astype(F32),axis=0,keepdims=True)
    dctx_ref[...]=dg(al,wo_ref[...],NN).astype(BF).reshape(dctx_ref.shape)


class Geo:
    def __init__(g, C, Q):
        g.C=C; g.Q=Q; g.nx=Q//2; g.nz=min(4,C); g.ny=C//g.nz
        c=lax.axis_index("cand"); q=lax.axis_index("query")
        g.z=c//g.ny; g.y=lax.rem(c,g.ny); g.x=q//2; g.k=lax.rem(q,2)
    def dev(g,z,y,x,k): return {"cand":z*g.ny+y,"query":x*2+k}


def mo(v,n): return pl.multiple_of(v,n)


def barrier(g, peers):
    b=pltpu.get_barrier_semaphore()
    for p in peers: pl.semaphore_signal(b,inc=1,device_id=p,device_id_type=MESH)
    pl.semaphore_wait(b,len(peers))


class RS:
    def __init__(s, g, refs, bufs, ss, rs):
        s.g, s.refs, s.bufs, s.ss, s.rs = g, refs, bufs, ss, rs
        s.partner = g.dev(g.z, g.y, g.x, 1 - g.k)
        s.pend = []
    def dims(s, n): return [NR[d] for d in RORD[n]]
    def own(s, n, rel, k):
        g = s.g
        r = dict(zip(RORD[n], rel))
        return rs_slice(g, n, s.refs, jnp.bitwise_xor(g.z, r["z"]), 1 - g.y if r["y"] else g.y, 1 - g.x if r["x"] else g.x, k)
    def near(s, d, r):
        g = s.g
        return g.dev(jnp.bitwise_xor(g.z, r) if d == "z" else g.z, 1 - g.y if d == "y" else g.y, 1 - g.x if d == "x" else g.x, g.k)
    def copy(s, src, dst, n, i, dev):
        pi = RPIECES.index(n)
        return pltpu.make_async_remote_copy(src, dst, s.ss.at[pi, i], s.rs.at[pi, i], device_id=dev, device_id_type=MESH)
    def c0(s, n, r1, r2, r3):
        _, n2, n3 = s.dims(n)
        return s.copy(s.own(n, (r1, r2, r3), 1 - s.g.k), s.bufs[n][0].at[r1, r2, r3], n, (r1 * n2 + r2) * n3 + r3, s.partner)
    def c1(s, n, r1, r2, r3):
        _, n2, n3 = s.dims(n)
        return s.copy(s.bufs[n][0].at[r1, r2, r3], s.bufs[n][1].at[r1 - 1, r2, r3], n, 16 + ((r1 - 1) * n2 + r2) * n3 + r3, s.near(RORD[n][0], r1))
    def c2(s, n, r2, r3):
        n1, n2, n3 = s.dims(n)
        return s.copy(s.bufs[n][0].at[0, r2, r3], s.bufs[n][2].at[r2 - 1, r3], n, 16 + (n1 - 1) * n2 * n3 + (r2 - 1) * n3 + r3, s.near(RORD[n][1], r2))
    def c3(s, n, r3):
        n1, n2, n3 = s.dims(n)
        return s.copy(s.bufs[n][0].at[0, 0, r3], s.bufs[n][3].at[r3 - 1], n, 16 + (n1 - 1) * n2 * n3 + (n2 - 1) * n3 + r3 - 1, s.near(RORD[n][2], r3))
    def go(s, f, *a):
        f(*a).start()
        s.pend.append(lambda: f(*a))
    def add(s, n, dst, srcs):
        rows, st = RSHP[n][0], RSHP[n][2]
        def body(i, _):
            o = pl.multiple_of(i * st, 16)
            dst[pl.ds(o, st), :] = functools.reduce(lambda a, b: a + b, [r[pl.ds(o, st), :].astype(F32) for r in srcs]).astype(dst.dtype)
            return 0
        lax.fori_loop(0, rows // st, body, 0)
    def part1(s, n, r2, r3):
        s.c0(n, 0, r2, r3).wait_recv()
        n1 = s.dims(n)[0]
        for r1 in range(1, n1):
            s.c1(n, r1, r2, r3).wait_recv()
        return [s.own(n, (0, r2, r3), s.g.k), s.bufs[n][0].at[0, r2, r3]] + [s.bufs[n][1].at[r1 - 1, r2, r3] for r1 in range(1, n1)]
    def part2(s, n, r3):
        t = s.part1(n, 0, r3)
        n2 = s.dims(n)[1]
        for r2 in range(1, n2):
            s.c2(n, r2, r3).wait_recv()
        return t + [s.bufs[n][2].at[r2 - 1, r3] for r2 in range(1, n2)]
    def s0(s, n, r1, r2, r3): s.go(s.c0, n, r1, r2, r3)
    def s1(s, n, r1, r2, r3):
        s.c0(n, r1, r2, r3).wait_recv()
        b = s.bufs[n][0].at[r1, r2, r3]
        s.add(n, b, [s.own(n, (r1, r2, r3), s.g.k), b])
        s.go(s.c1, n, r1, r2, r3)
    def s2(s, n, r2, r3):
        s.add(n, s.bufs[n][0].at[0, r2, r3], s.part1(n, r2, r3))
        s.go(s.c2, n, r2, r3)
    def s3(s, n, r3):
        s.add(n, s.bufs[n][0].at[0, 0, r3], s.part2(n, r3))
        s.go(s.c3, n, r3)
    def fin(s, n, dst):
        t = s.part2(n, 0)
        n3 = s.dims(n)[2]
        for r3 in range(1, n3):
            s.c3(n, r3).wait_recv()
        s.add(n, dst, t + [s.bufs[n][3].at[r3 - 1] for r3 in range(1, n3)])
    def fin_(s, n): s.fin(n, s.outs[n])
    def ev(s, e): getattr(s, e[0])(*e[1:])
    def drain(s):
        for c in s.pend: c().wait_send()


def rs_slice(g, n, refs, z, y, x, k):
    wq, wo, wu, wd = refs
    c = z * g.ny + y
    q = x * 2 + k
    if n in QROW:
        return wq.at[pl.ds(mo(c * 288 + k * 144 + QROW[n], 16), RSHP[n][0]), pl.ds(mo(x * 384, 128), 384)]
    if n == "o": return wo.at[pl.ds(mo(c * 96 + k * 48, 16), 48), pl.ds(mo(x * 384, 128), 384)]
    if n == "u": return wu.at[pl.ds(mo(q * 192, 16), 192), pl.ds(mo(c * 384, 128), 384)]
    if n == "d": return wd.at[pl.ds(mo(c * 96, 16), 96), pl.ds(mo(q * 768, 128), 768)]


def rs_bufs():
    out = []
    for n in RPIECES:
        n1, n2, n3 = [NR[d] for d in RORD[n]]
        sh = RSHP[n][:2]
        out += [pltpu.VMEM((n1, n2, n3) + sh, BF), pltpu.VMEM((n1 - 1, n2, n3) + sh, BF), pltpu.VMEM((n2 - 1, n3) + sh, BF), pltpu.VMEM((n3 - 1,) + sh, BF)]
    return out


def attn_fwd_kernel(len_ref, x_ref, w_ref, bias_ref, tab_ref, bk_ref, bkf_ref, xlow_ref, qkv_ref, ctx_ref, lse_ref, relf_ref, rel_ref, bias_scr):
    S, D = x_ref.shape[1:]
    for m in range(2):
        xlow_ref[m*S:(m+1)*S,:]=x_ref[m].astype(BF)
    qkv_proj(w_ref, bias_ref, xlow_ref, qkv_ref, {})
    rel_rows(tab_ref, bk_ref, rel_ref)
    rel_rows(tab_ref, bkf_ref, relf_ref)
    attn_fwd(len_ref, qkv_ref, rel_ref, ctx_ref, lse_ref, bias_scr, S, D, {})


class AG:
    def __init__(s, g, own, refs, ss, rs, cs, cr):
        s.g, s.own_, s.refs, s.ss, s.rs, s.cs, s.cr = g, own, refs, ss, rs, cs, cr
        s.partner = g.dev(g.z, g.y, g.x, 1 - g.k)
        s.pend = []
        s.got = set()
    def dst(s, n, rel, k):
        g = s.g
        r = dict(zip(RORD[n], rel))
        return rs_slice(g, n, s.refs, jnp.bitwise_xor(g.z, r["z"]), 1 - g.y if r["y"] else g.y, 1 - g.x if r["x"] else g.x, k)
    def idx(s, n, rel):
        _, n2, n3 = [NR[d] for d in RORD[n]]
        return (rel[0] * n2 + rel[1]) * n3 + rel[2]
    def src(s, n, rel): return s.own_(n) if rel == (0, 0, 0) else s.dst(n, rel, s.g.k)
    def near(s, d, r):
        g = s.g
        return g.dev(jnp.bitwise_xor(g.z, r) if d == "z" else g.z, 1 - g.y if d == "y" else g.y, 1 - g.x if d == "x" else g.x, g.k)
    def link(s, n, rel, d, k):
        new = tuple(k if a == d else r for a, r in zip(RORD[n], rel))
        pi, i = RPIECES.index(n), s.idx(n, new)
        return pltpu.make_async_remote_copy(s.src(n, rel), s.dst(n, rel, s.g.k), s.ss.at[pi, i], s.rs.at[pi, i], device_id=s.near(d, k), device_id_type=MESH)
    def core(s, n, rel):
        pi, i = RPIECES.index(n), s.idx(n, rel)
        return pltpu.make_async_remote_copy(s.src(n, rel), s.dst(n, rel, s.g.k), s.cs.at[pi, i], s.cr.at[pi, i], device_id=s.partner, device_id_type=MESH)
    def got_core(s, n, rel):
        pi, i = RPIECES.index(n), s.idx(n, rel)
        t = s.dst(n, rel, 1 - s.g.k)
        pltpu.make_async_remote_copy(t, t, s.cs.at[pi, i], s.cr.at[pi, i], device_id=s.partner, device_id_type=MESH).wait_recv()
    def go(s, f, *a):
        f(*a).start()
        s.pend.append(lambda: f(*a))
    def ev(s, e):
        n, rel, outs = e
        if rel != (0, 0, 0):
            t = s.dst(n, rel, s.g.k)
            pi, i = RPIECES.index(n), s.idx(n, rel)
            pltpu.make_async_remote_copy(t, t, s.ss.at[pi, i], s.rs.at[pi, i], device_id=s.partner, device_id_type=MESH).wait_recv()
        for d, k in outs:
            if d == "k": s.go(s.core, n, rel)
            else: s.go(s.link, n, rel, d, k)
    def rels(s, n):
        n1, n2, n3 = [NR[d] for d in RORD[n]]
        return [(a, b, c) for a in range(n1) for b in range(n2) for c in range(n3)]
    def drain(s):
        for c in s.pend: c().wait_send()


def front_kernel(len_ref, x_h, wqf_h, wof_h, wuf_h, wdf_h, *rest, C, Q):
    vins, rest = rest[:11], rest[11:]
    (wq_o, wo, wu, wd, vec_o, bup_o, xlow_o, qkv_o, ctx_ref, lse_ref, relf_ref, bkf_o,
     wqf_ref, wof_ref, wuf_ref, wdf_ref, v_ref, bk_ref, x_v, xlow, qkv, wq, own_p, got_p, h_scr, u_bf, d_bf, vall, tab, rel, qb, bias_scr, ss, rs, cs, cr, vss, vrs, ps, ls) = rest
    g = Geo(C, Q)
    S, D = x_h.shape[1:]
    q_ = lax.axis_index("query")
    peers = [{"query": lax.rem(q_ + j, Q)} for j in range(1, Q)] + [g.dev(g.z, 1 - g.y, g.x, g.k)] + [g.dev(jnp.bitwise_xor(g.z, i), g.y, g.x, g.k) for i in range(1, g.nz)]
    bar = pltpu.get_barrier_semaphore()
    for p in peers:
        pl.semaphore_signal(bar, inc=1, device_id=p, device_id_type=MESH)
    wc = [pltpu.make_async_copy(a, b, ls.at[10 + i]) for i, (a, b) in enumerate(((wqf_h, wqf_ref), (wof_h, wof_ref), (wuf_h, wuf_ref), (wdf_h, wdf_ref)))]
    for c in wc:
        c.start()
    xc = pltpu.make_async_copy(x_h, x_v, ls.at[0])
    xc.start()
    k = g.k
    dq, bq = D // Q, tab.shape[1] // Q
    fq = bup_o.shape[1] // Q
    v_ref[...] = jnp.zeros_like(v_ref)
    for i in range(8):
        v_ref[i:i + 1, 0:dq] = vins[i][...]
    for j in range(fq // 256):
        v_ref[8 + j:9 + j, :] = vins[8][:, j * 256:(j + 1) * 256]
    v_ref[16:16 + vins[9].shape[0], 0:bq] = vins[9][...]
    nrel = vins[10].shape[1]
    bk_ref[...] = jnp.full(bk_ref.shape, -1, jnp.int32)
    bk_ref[:, 0:nrel] = vins[10][...]
    for c in wc:
        c.wait()

    def turn(w):
        n = w.shape[1]
        eye = (lax.broadcasted_iota(jnp.int32, (n, n), 0) == lax.broadcasted_iota(jnp.int32, (n, n), 1)).astype(BF)
        return dg(eye, w.astype(BF), NT).astype(BF)
    a, b = turn(wqf_ref[...]), turn(wof_ref[...])
    ha, hb = a.shape[0] // 2, b.shape[0] // 2
    for i in range(2):
        own_p[i, 0:ha, :] = a[i * ha:(i + 1) * ha]
        own_p[i, ha:ha + hb, :] = b[i * hb:(i + 1) * hb]
    d_bf[...] = wdf_ref[...].astype(BF)
    u_bf[...] = wuf_ref[...].astype(BF)
    pl.semaphore_wait(bar, len(peers))
    pc = pltpu.make_async_remote_copy(own_p.at[1 - k], got_p, ps.at[0], ps.at[1], device_id=g.dev(g.z, g.y, g.x, 1 - k), device_id_type=MESH)
    pc.start()
    vcs = []
    for j in range(1, Q):
        c = pltpu.make_async_remote_copy(v_ref, vall.at[q_], vss.at[j - 1], vrs.at[j - 1], device_id={"query": lax.rem(q_ + j, Q)}, device_id_type=MESH)
        c.start()
        vcs.append(c)
    vall[q_] = v_ref[...]

    def own(n):
        if n == "u": return u_bf
        if n == "d": return d_bf
        return h_scr.at[pl.ds(QROW.get(n, 144), RSHP[n][0])]
    A = AG(g, own, (wq, wo, wu, wd), ss, rs, cs, cr)
    loc = [pltpu.make_async_copy(own(n), A.dst(n, (0, 0, 0), k), ls.at[1 + i]) for i, n in enumerate(RPIECES)]

    def after(name):
        for e in AGSLOTS.get(name, []):
            A.ev(e)
    after("b")
    loc[0].start()
    loc[1].start()
    pc.wait()
    t, r = own_p[k], got_p[...]
    @pl.when(k == 0)
    def _(): h_scr[...] = jnp.concatenate([t, r], axis=1)
    @pl.when(k == 1)
    def _(): h_scr[...] = jnp.concatenate([r, t], axis=1)
    for c in loc[2:]:
        c.start()
    after("h")
    xc.wait()
    for m in range(2):
        xlow[m*S:(m+1)*S,:]=x_v[m].astype(BF)
    xo = pltpu.make_async_copy(xlow, xlow_o, ls.at[7])
    xo.start()
    after("p0")
    ids = jnp.broadcast_to(bk_ref[...], (8, 2 * S)).astype(F32).astype(BF)
    for j in range(2 * S // 256):
        flip = (lax.broadcasted_iota(jnp.int32, (2 * S, 256), 0) + lax.broadcasted_iota(jnp.int32, (2 * S, 256), 1) == nrel - 1 - j * 256).astype(BF)
        bkf_o[:, j * 256:(j + 1) * 256] = dg(ids, flip, NN)[0:1].astype(jnp.int32)
    bkf_o[:, nrel:] = jnp.full((1, 2 * S - nrel), -1, jnp.int32)
    after("p1")
    for c in vcs:
        c.wait()
    qb[...] = jnp.zeros_like(qb)
    vec_o[...] = jnp.zeros_like(vec_o)
    for q in range(Q):
        lo, hi = q * dq, (q + 1) * dq
        qb[:, lo:hi] = vall[q, 0:1, 0:dq]
        qb[:, 2 * D + lo:2 * D + hi] = vall[q, 1:2, 0:dq]
        vec_o[0:6, lo:hi] = vall[q, 2:8, 0:dq]
        for j in range(fq // 256):
            bup_o[:, q * fq + j * 256:q * fq + (j + 1) * 256] = vall[q, 8 + j:9 + j, :]
        tab[:, q * bq:(q + 1) * bq] = vall[q, 16:32, 0:bq]
    rel_rows(tab, bk_ref, rel)
    rel_rows(tab, bkf_o, relf_ref)
    after("p2")
    for i, n in enumerate(RPIECES):
        if n in QROW:
            loc[i].wait()
            for r in A.rels(n):
                A.got_core(n, r)
    qkv_proj(wq, qb, xlow, qkv, {i: [functools.partial(A.ev, e) for e in AGSLOTS.get(f"n{i}", [])] for i in range(3 * D // 256)})
    wc = pltpu.make_async_copy(wq, wq_o, ls.at[8])
    qc = pltpu.make_async_copy(qkv, qkv_o, ls.at[9])
    wc.start()
    qc.start()
    attn_fwd(len_ref, qkv, rel, ctx_ref, lse_ref, bias_scr, S, D, {i: [functools.partial(A.ev, e) for e in AGSLOTS.get(f"t{i}", [])] for i in range(D // 64)})
    for c in (xo, wc, qc):
        c.wait()
    for i, n in enumerate(RPIECES):
        if n not in QROW:
            loc[i].wait()
            for r in A.rels(n):
                A.got_core(n, r)
    A.drain()


def ffn_kernel(lab_ref, x_ref, ctx_ref, cot_ref, wo_ref, wu_ref, wd_ref, vec_ref, bup_ref,
               out_ref, dfs_ref, dctx_ref, nl_ref, act_ref, dl_ref, al_ref, ul_ref, gv_ref, gbu_ref, loss_ref,
               gp_scr, z1_scr, z2_scr, r_scr,
               ds_scr, sc_snd, sc_all, sss, ssr, *, T, R, C, Q):
    i = pl.program_id(0)
    D, FF = wu_ref.shape
    cid = lax.axis_index("cand")

    def score_copy(j):
        return pltpu.make_async_remote_copy(sc_snd, sc_all.at[cid], sss.at[j - 1], ssr.at[j - 1], device_id={"cand": lax.rem(cid + j, C)}, device_id_type=MESH)

    @pl.when(i == 0)
    def _():
        b = pltpu.get_barrier_semaphore()
        for j in range(1, C):
            pl.semaphore_signal(b, inc=1, device_id={"cand": lax.rem(cid + j, C)}, device_id_type=MESH)
        pl.semaphore_wait(b, C - 1)
        gv_ref[...] = jnp.zeros_like(gv_ref)
        gbu_ref[...] = jnp.zeros_like(gbu_ref)
        ds_scr[...] = jnp.zeros_like(ds_scr)
        sc_snd[...] = jnp.zeros_like(sc_snd)

    @pl.when(i < T)
    def _():
        fwd_tile(jnp.minimum(i, 1), x_ref, ctx_ref, wo_ref, wu_ref, wd_ref, vec_ref, bup_ref, out_ref, nl_ref, act_ref, gp_scr, z1_scr, z2_scr, r_scr, R)

    @pl.when(i == 0)
    def _():
        for m in range(2):
            sc = jnp.sum(out_ref[m, 0:1, :] * vec_ref[5:6, :], axis=1, keepdims=True)
            sc_snd[m:m + 1, :] = jnp.broadcast_to(sc, (1, 128))
        sc_all[cid] = sc_snd[...]
        for j in range(1, C):
            score_copy(j).start()

    @pl.when(i == T)
    def _():
        for j in range(1, C):
            score_copy(j).wait()
        total = jnp.zeros((1, 128), F32)
        own = sc_snd[...]
        for m in range(2):
            rows = [sc_all[j, m:m + 1, :] for j in range(C)]
            peak = functools.reduce(jnp.maximum, rows)
            lse = peak + jnp.log(functools.reduce(lambda a, b: a + b, [jnp.exp(r - peak) for r in rows]))
            lab = lab_ref[m]
            picked = functools.reduce(lambda a, b: a + b, [jnp.where(lab == j, r, 0.0) for j, r in enumerate(rows)])
            total = total + (lse - picked)
            ds_scr[m:m + 1, :] = (jnp.exp(own[m:m + 1, :] - lse) - jnp.where(lab == cid, 1.0, 0.0)) * (1.0 / Q)
        loss_ref[...] = jnp.broadcast_to(jnp.where(cid == 0, total * (1.0 / Q), 0.0), (8, 128))

    @pl.when((i >= 1) & (i <= T))
    def _():
        t = lax.rem(i, T)
        bwd_tile(jnp.minimum(t, 1), ds_scr, cot_ref, wo_ref, wu_ref, wd_ref, vec_ref, dfs_ref, dctx_ref, gv_ref, gbu_ref, dl_ref, ul_ref, al_ref, gp_scr, z1_scr, z2_scr, r_scr, R)


def back_kernel(len_ref, nl_h, dl_h, al_h, ctx_h, act_h, ul_h, qkv_h, dctx_h, xlow_h, wq_h, dfs_h, lse_ref, relf, bkf_ref, gv_ref, gbu_ref, loss_ref,
                *rest, C, Q, fast):
    if fast:
        ig_h, p_out, u_out, d_out, v_out = rest[:5]
        scr = rest[5:]
    else:
        ig_h, gq_o, go_o, gu_o, gd_o, gb_o, gtab_o = rest[:7]
        scr = rest[7:]
    (nl, dl, al, ctx, ch, qkv, dctx, xlow, wq, dfs, igt, gq, go, gu, gd, drelf, bias_scr, acc_scr, gb, gtab, ls, cs_, os_) = scr[:23]
    NS, D = nl.shape
    FF = gu.shape[1]
    S = NS // 2
    NZ = FF // 768
    load = lambda i, src, dst: pltpu.make_async_copy(src, dst, ls.at[i])
    big = [load(0, nl_h, nl), load(1, dl_h, dl), load(2, al_h, al), load(3, ctx_h, ctx), load(4, qkv_h, qkv), load(5, dctx_h, dctx),
           load(6, xlow_h, xlow), load(7, wq_h, wq), load(8, dfs_h, dfs)]
    if fast:
        g = Geo(C, Q)
        seq = [(ul_h, jnp.bitwise_xor(g.z, zi)) for zi in (3, 2, 1, 0)]
        qorder = [(1, 1), (1, 0), (0, 1), (0, 0)]
        seq += [(act_h, (1 - g.x if dx else g.x) * 2 + (1 - g.k if dk else g.k)) for dx, dk in qorder]
    else:
        seq = [(ul_h, i) for i in range(NZ)] + [(act_h, i) for i in range(NZ)]
    off = lambda i: pl.multiple_of(seq[i][1] * 768, 128)
    chunk = lambda i: pltpu.make_async_copy(seq[i][0].at[:, pl.ds(off(i), 768)], ch.at[i % 2], cs_.at[i % 2])
    if fast:
        peers = [{"query": lax.rem(lax.axis_index("query") + j, Q)} for j in range(1, Q)] + [{"cand": lax.rem(lax.axis_index("cand") + j, C)} for j in range(1, C)]
        bar = pltpu.get_barrier_semaphore()
        for p in peers:
            pl.semaphore_signal(bar, inc=1, device_id=p, device_id_type=MESH)
    for c in (big[2], big[3], big[0], chunk(0), chunk(1), big[1]):
        c.start()
    if fast:
        bufs = {n: scr[23 + 4 * i:27 + 4 * i] for i, n in enumerate(RPIECES)}
        h_scr, e_snd, e_rcv, vb0, va, vs, vb, ss, rs, es, qs, qr, cs, cr = scr[23 + NB:]
        R = RS(g, (gq, go, gu, gd), bufs, ss, rs)
        R.outs = {n: h_scr.at[pl.ds(QROW.get(n, 144), RSHP[n][0])] for n in ("qa", "qb", "qz", "o")}
        R.outs.update(u=u_out, d=d_out)
        c_ = lax.axis_index("cand")
        q_ = lax.axis_index("query")

    def after(name):
        if fast:
            for e in SLOTS.get(name, []):
                R.ev(e)
    big[2].wait()
    big[3].wait()
    go[...] = dg(al[...], ctx[...], TN).astype(BF)
    big[0].wait()
    for i in range(NZ):
        chunk(i).wait()
        gu[:, pl.ds(off(i), 768)] = dg(nl[...], ch[i % 2], TN).astype(BF)
        chunk(i + 2).start()
        if i == 0:
            if fast:
                pl.semaphore_wait(bar, len(peers))
            after("o")
        after(f"u{i}")
    big[1].wait()
    for i in range(NZ, 2 * NZ):
        chunk(i).wait()
        gd[:, pl.ds(off(i), 768)] = dg(dl[...], ch[i % 2], TN).astype(BF)
        if i + 2 < 2 * NZ:
            chunk(i + 2).start()
        if i == NZ:
            big[4].start()
            big[5].start()
        if i == NZ + 2:
            for c in big[6:]:
                c.start()
        after(f"d{i - NZ}")
    slots = {}
    if fast:
        for i in range(2 * (D // 128)):
            slots[i] = [functools.partial(R.ev, e) for e in SLOTS.get(f"t{i}", [])]
    drelf[...] = jnp.zeros_like(drelf)
    big[4].wait()
    big[5].wait()
    attn_bwd(len_ref, qkv, dctx, lse_ref, relf, drelf, bias_scr, acc_scr, S, D, slots)
    big[6].wait()

    half = 3 * D // 2
    zh = g.z // 2 if fast else 0

    def b1(n, _):
        o = pl.multiple_of(jnp.where(n < 3, 1 - zh, zh) * half + lax.rem(n, 3) * 384, 128)
        t = qkv[:, pl.ds(o, 384)]
        gq[pl.ds(o, 384), :] = dg(t, xlow[...], TN).astype(BF)
        gb[:, pl.ds(o, 384)] = jnp.sum(t.astype(F32), axis=0, keepdims=True)
        hooks(n, {i: [functools.partial(R.ev, e) for e in SLOTS.get(f"g{i}", [])] for i in range(6)} if fast else {})
        return 0
    lax.fori_loop(0, 6, b1, 0)
    nb, nn = gtab.shape[1], bkf_ref.shape[1]
    hot = (lax.broadcasted_iota(jnp.int32, (nb, nn), 0) == bkf_ref[...]).astype(F32)
    gtab[...] = dg(drelf[...], hot, NT, lax.Precision.HIGHEST)
    if fast:
        dq, fq, bq = D // Q, FF // Q, nb // Q
        vb0[...] = jnp.zeros_like(vb0)
        for q in range(Q):
            lo = slice(q * dq, (q + 1) * dq)
            vb0[q, 0:1, 0:dq] = gb[:, q * dq:(q + 1) * dq]
            vb0[q, 1:2, 0:dq] = gb[:, 2 * D + q * dq:2 * D + (q + 1) * dq]
            vb0[q, 2:8, 0:dq] = gv_ref[0:6, lo]
            for j in range(fq // 256):
                vb0[q, 8 + j:9 + j, :] = gbu_ref[:, q * fq + j * 256:q * fq + (j + 1) * 256]
            vb0[q, 11:12, 0:128] = loss_ref[0:1, :]
            vb0[q, 16:32, 0:bq] = gtab[:, q * bq:(q + 1) * bq]
        vq = []
        for j in range(1, Q):
            qq = lax.rem(q_ + j, Q)
            c = pltpu.make_async_remote_copy(vb0.at[qq], va.at[q_], qs.at[j - 1], qr.at[j - 1], device_id={"query": qq}, device_id_type=MESH)
            c.start()
            vq.append(c)
        va[q_] = vb0[q_]
        after("v")
    big[7].wait()
    big[8].wait()
    steps = NS // 256
    outc = lambda r: pltpu.make_async_copy(igt.at[r % 2], ig_h.at[pl.ds(r * 256, 256), :], os_.at[r % 2])
    for r in range(steps):
        if r >= 2:
            outc(r - 2).wait()
        igt[r % 2] = dfs[r * 256:(r + 1) * 256, :] + dg(qkv[r * 256:(r + 1) * 256, :], wq[...], NN)
        outc(r).start()
        after(f"i{r}")
    for r in range(max(0, steps - 2), steps):
        outc(r).wait()
    if fast:
        for c in vq:
            c.wait()
        t = functools.reduce(lambda a, b: a + b, [va[j] for j in range(Q)])
        vs[...] = t
        vb[c_] = t
        vc = []
        for j in range(1, C):
            c = pltpu.make_async_remote_copy(vs, vb.at[c_], cs.at[j - 1], cr.at[j - 1], device_id={"cand": lax.rem(c_ + j, C)}, device_id_type=MESH)
            c.start()
            vc.append(c)
        k = g.k
        lo = h_scr[:, 0:192]
        hi = h_scr[:, 192:384]
        e_snd[...] = jnp.where(k == 0, hi, lo)
        c = pltpu.make_async_remote_copy(e_snd, e_rcv, es.at[0], es.at[1], device_id=R.partner, device_id_type=MESH)
        c.start()
        p_out[k] = jnp.where(k == 0, lo, hi)
        c.wait()
        p_out[1 - k] = e_rcv[...]
        for c in vc:
            c.wait()
        v_out[...] = functools.reduce(lambda a, b: a + b, [vb[j] for j in range(C)])
        R.drain()
    else:
        gq_o[...] = gq[...]
        go_o[...] = go[...]
        gu_o[...] = gu[...]
        gd_o[...] = gd[...]
        gb_o[...] = gb[...]
        gtab_o[...] = gtab[...]


def finish_kernel(out_h, ig_h, p_ref, u_ref, d_ref, v_ref, out_o, ig_o, gq_o, go_o, gu_o, gd_o, *rest):
    vec_o, bup_o, tab_o, loss_o = rest[:8], rest[8], rest[9], rest[10]
    buf, si, so = rest[11:]
    n, rows = buf.shape[0] // 2, buf.shape[1]
    src = [h.at[pl.ds(i * rows, rows), :] for h in (out_h, ig_h) for i in range(n)]
    dst = [h.at[pl.ds(i * rows, rows), :] for h in (out_o, ig_o) for i in range(n)]
    ins = [pltpu.make_async_copy(src[i], buf.at[i], si.at[i]) for i in range(2 * n)]
    outs = [pltpu.make_async_copy(buf.at[i], dst[i], so.at[i]) for i in range(2 * n)]
    for c in ins:
        c.start()
    for a, b in zip(ins, outs):
        a.wait()
        b.start()
    ha = gq_o.shape[1] // 2
    gq_o[...] = jnp.concatenate([p_ref[0, 0:ha, :], p_ref[1, 0:ha, :]], axis=0).T
    go_o[...] = jnp.concatenate([p_ref[0, ha:, :], p_ref[1, ha:, :]], axis=0).T
    gu_o[...] = u_ref[...]
    gd_o[...] = d_ref[...]
    for i in range(8):
        vec_o[i][...] = v_ref[i:i + 1, 0:vec_o[i].shape[1]]
    for j in range(bup_o.shape[1] // 256):
        bup_o[:, j * 256:(j + 1) * 256] = v_ref[8 + j:9 + j, :]
    loss_o[...] = v_ref[11:12, 0:1]
    tab_o[...] = v_ref[16:16 + tab_o.shape[0], 0:tab_o.shape[1]]
    for c in outs:
        c.wait()


def sds(shape, dtype=F32):
    return jax.ShapeDtypeStruct(shape, dtype)


def back_scratch(fast, C, Q, NS=1024, S=512, D=768, FF=3072, NBK=256):
    v = pltpu.VMEM
    dma = pltpu.SemaphoreType.DMA
    scr = [v((NS, D), BF)] * 4 + [v((2, NS, 768), BF), v((NS, 3 * D), BF), v((NS, D), BF), v((NS, D), BF), v((3 * D, D), BF), v((NS, D), F32), v((2, 256, D), F32),
                                  v((3 * D, D), BF), v((D, D), BF), v((D, FF), BF), v((D, FF), BF), v((16, 2 * S), F32),
                                  v((2, S, S), F32), v((2, S, S), F32), v((1, 3 * D), F32), v((16, NBK), F32), dma((9,)), dma((2,)), dma((2,))]
    if fast:
        scr += rs_bufs() + [v((192, 384), F32), v((192, 192), F32), v((192, 192), F32), v((Q, 32, 256), F32), v((Q, 32, 256), F32), v((32, 256), F32), v((C, 32, 256), F32),
                            dma((len(RPIECES), 31)), dma((len(RPIECES), 31)), dma((2,)), dma((Q,)), dma((Q,)), dma((C,)), dma((C,))]
    return scr


def body(hidden_in, out_cotangent, lengths, labels, buckets, w_qkv, w_out, w_up, w_down, bias_q, bias_v, bias_out,
         norm1_gain, norm1_bias, bias_up, bias_down, norm2_gain, score_vector, rel_table):
    Q = lax.axis_size("query")
    C = lax.axis_size("cand")
    micro = hidden_in.shape[0]
    S, D = hidden_in.shape[3:]
    FF = w_up.shape[1] * C
    NBK = rel_table.shape[0] * Q
    dq, fq, bq = D // Q, FF // Q, NBK // Q
    fast = Q == 4 and C == 8 and D == 768 and FF == 3072
    x = hidden_in.reshape(micro, S, D)
    cot = out_cotangent.reshape(micro, S, D)
    lens = lengths.reshape(micro)
    labs = labels.reshape(micro)
    NS = micro * S
    v = pltpu.VMEM
    dma = pltpu.SemaphoreType.DMA
    eight = [bias_q, bias_v, bias_out, norm1_gain, norm1_bias, bias_down, norm2_gain, score_vector]
    if fast:
        np_ = len(RPIECES)
        wq, wo, wu, wd, vec, bup, xlow, qkv, ctx, lse, relf, bkf = pl.pallas_call(
            functools.partial(front_kernel, C=C, Q=Q), in_specs=[SM] + [ANY] * 5 + [VM] * 11, out_specs=[ANY] * 4 + [VM] * 2 + [ANY] * 2 + [VM] * 4,
            out_shape=[sds((3 * D, D), BF), sds((D, D), BF), sds((D, FF), BF), sds((D, FF), BF), sds((8, D)), sds((1, FF)), sds((NS, D), BF), sds((NS, 3 * D), BF),
                       sds((NS, D), BF), sds((micro, 16, S)), sds((16, 2 * S)), sds((1, 2 * S), jnp.int32)],
            scratch_shapes=[v(w_qkv.shape, F32), v(w_out.shape, F32), v(w_up.shape, F32), v(w_down.shape[::-1], F32), v((32, 256), F32), v((1, 2 * S), jnp.int32),
                            v((micro, S, D), F32), v((NS, D), BF), v((NS, 3 * D), BF), v((3 * D, D), BF), v((2, 192, 192), BF), v((192, 192), BF), v((192, 384), BF),
                            v((192, 384), BF), v((96, 768), BF), v((Q, 32, 256), F32), v((16, NBK), F32), v((16, 2 * S), F32), v((1, 3 * D), F32), v((2, S, S), F32)]
            + [dma((np_, 16))] * 4 + [dma((Q,))] * 2 + [dma((2,)), dma((14,))],
            compiler_params=pltpu.CompilerParams(collective_id=0, has_side_effects=True, vmem_limit_bytes=67043328),
        )(lens, x, w_qkv, w_out, w_up, w_down.T, *[t.reshape(1, -1) for t in eight], bias_up.reshape(1, -1), rel_table.T, buckets.reshape(1, -1))
    else:
        bk = jnp.pad(buckets, (0, 1), constant_values=-1)[None, :]
        bkf = jnp.pad(buckets[::-1], (0, 1), constant_values=-1)[None, :]
        def gather(w):
            part = lax.all_gather(w.astype(BF), "query", axis=0, tiled=True)
            return lax.all_gather(part, "cand", axis=1, tiled=True)
        wq, wo, wu, wd = gather(w_qkv).T, gather(w_out).T, gather(w_up), gather(w_down).T
        vall = lax.all_gather(jnp.concatenate(eight + [bias_up, rel_table.reshape(-1)]), "query", axis=0, tiled=False)
        vecs = vall[:, :8 * dq].reshape(Q, 8, dq).transpose(1, 0, 2).reshape(8, D)
        bup = vall[:, 8 * dq:8 * dq + fq].reshape(1, FF)
        tab = jnp.pad(vall[:, 8 * dq + fq:].reshape(NBK, HEADS).T, ((0, 4), (0, 0)))
        qkv_bias = jnp.concatenate([vecs[0:1], jnp.zeros((1, D), F32), vecs[1:2]], axis=1)
        vec = jnp.concatenate([vecs[2:], jnp.zeros((2, D), F32)], axis=0)
        xlow, qkv, ctx, lse, relf = pl.pallas_call(
            attn_fwd_kernel, in_specs=[SM] + [VM] * 6, out_specs=[VM] * 5,
            out_shape=[sds((NS, D), BF), sds((NS, 3 * D), BF), sds((NS, D), BF), sds((micro, 16, S)), sds((16, 2 * S))],
            scratch_shapes=[v((16, 2 * S), F32), v((2, S, S), F32)],
            compiler_params=pltpu.CompilerParams(vmem_limit_bytes=60 * 2**20))(lens, x, wq, qkv_bias, tab, bk, bkf)
    R = 256
    Rh, T = R // micro, NS // R
    tb = lambda im, n=D: pl.BlockSpec((micro, Rh, n), im)
    fw = lambda i: (0, jnp.minimum(i, T - 1), 0)
    bw = lambda i: (0, lax.rem(jnp.maximum(i, 1), T), 0)
    tok = lambda n, dt=BF: sds((micro, S, n), dt)
    out, dfs, dctx, nl, act, dl, al, ul, gv, gbu, lossv = pl.pallas_call(
        functools.partial(ffn_kernel, T=T, R=R, C=C, Q=Q), grid=(T + 1,),
        in_specs=[SM, tb(fw), tb(fw), tb(bw)] + [VM] * 5, out_specs=[tb(fw), tb(bw), tb(bw), tb(fw), tb(fw, FF), tb(bw), tb(bw), tb(bw, FF)] + [VM] * 3,
        out_shape=[tok(D, F32), tok(D, F32), tok(D), tok(D), tok(FF), tok(D), tok(D), tok(FF), sds((8, D)), sds((1, FF)), sds((8, 128))],
        scratch_shapes=[pltpu.VMEM((2, R, FF), F32), pltpu.VMEM((2, R, D), F32), pltpu.VMEM((2, R, D), F32), pltpu.VMEM((2, R, 128), F32),
                        pltpu.VMEM((8, 128), F32), pltpu.VMEM((8, 128), F32), pltpu.VMEM((C, 8, 128), F32), pltpu.SemaphoreType.DMA((C,)), pltpu.SemaphoreType.DMA((C,))],
        compiler_params=pltpu.CompilerParams(collective_id=1, has_side_effects=True, vmem_limit_bytes=67043328),
    )(labs, x, ctx.reshape(micro, S, D), cot, wo, wu, wd, vec, bup)
    flat = lambda t: t.reshape(NS, t.shape[-1])
    gouts = [sds((2, 192, 192)), sds((192, 384)), sds((96, 768)), sds((32, 256))] if fast else \
        [sds((3 * D, D), BF), sds((D, D), BF), sds((D, FF), BF), sds((D, FF), BF), sds((1, 3 * D)), sds((16, NBK))]
    res = pl.pallas_call(
        functools.partial(back_kernel, C=C, Q=Q, fast=fast), in_specs=[SM] + [ANY] * 11 + [VM] * 6, out_specs=[ANY] + [VM] * len(gouts),
        out_shape=[sds((NS, D))] + gouts, scratch_shapes=back_scratch(fast, C, Q, NS, S, D, FF, NBK),
        compiler_params=pltpu.CompilerParams(collective_id=2 if fast else None, has_side_effects=True, vmem_limit_bytes=67043328),
    )(lens, flat(nl), flat(dl), flat(al), ctx, flat(act), flat(ul), qkv, flat(dctx), xlow, wq, flat(dfs), lse, relf, bkf, gv, gbu, lossv)
    ig = res[0]
    if fast:
        fin = pl.pallas_call(
            finish_kernel, in_specs=[ANY] * 2 + [VM] * 4, out_specs=[ANY] * 2 + [VM] * 15,
            out_shape=[sds((NS, D)), sds((NS, D)), sds(w_qkv.shape), sds(w_out.shape), sds(w_up.shape), sds(w_down.shape[::-1])] + [sds((1, dq))] * 8
            + [sds((1, fq)), sds((HEADS, bq)), sds((1, 1))],
            scratch_shapes=[v((8, NS // 4, D), F32), dma((8,)), dma((8,))],
            compiler_params=pltpu.CompilerParams(vmem_limit_bytes=67043328))(flat(out), ig, *res[1:])
        out, ig, g_qkv, g_out, g_up = fin[:5]
        g_down = fin[5].T
        small = [t.reshape(dq) for t in fin[6:14]]
        g_bup, g_tab, loss = fin[14].reshape(fq), fin[15].T, fin[16].reshape(())
    else:
        def scatter(g):
            rows, cols = g.shape[0] // Q, g.shape[1] // C
            tiles = g.astype(F32).reshape(Q, rows, C, cols).transpose(2, 0, 1, 3).reshape(C * Q, rows, cols)
            return lax.psum_scatter(tiles, ("cand", "query"), scatter_dimension=0, tiled=True)[0]
        gq, go, gu, gd, gb, gtab = res[1:]
        g_qkv, g_out, g_up, g_down = scatter(gq.T), scatter(go.T), scatter(gu), scatter(gd.T)
        gvecs = jnp.concatenate([gb[:, :D], gb[:, 2 * D:], gv[:6]], axis=0)
        vg = jnp.concatenate([gvecs.reshape(8, Q, dq).transpose(1, 0, 2).reshape(Q, 8 * dq), gbu.reshape(Q, fq), gtab[:HEADS].T.reshape(Q, bq * HEADS),
                              jnp.broadcast_to(lossv[0:1, 0:1], (Q, 1))], axis=1)
        vg = jnp.pad(vg, ((0, 0), (0, -vg.shape[1] % 1024)))
        vs = lax.psum_scatter(lax.psum(vg, "cand"), "query", scatter_dimension=0, tiled=True)[0]
        small = [vs[i * dq:(i + 1) * dq] for i in range(8)]
        g_bup = vs[8 * dq:8 * dq + fq]
        g_tab = vs[8 * dq + fq:8 * dq + fq + bq * HEADS].reshape(bq, HEADS)
        loss = vs[8 * dq + fq + bq * HEADS]
    return (out.reshape(hidden_in.shape), ig.reshape(hidden_in.shape), g_qkv, g_out, g_up, g_down,
            small[0], small[1], small[2], small[3], small[4], g_bup, small[5], small[6], small[7], g_tab, loss)


def solution(mesh):
    seq, w, v = P(None, "query", "cand", None, None), P("query", "cand"), P("query")
    return jax.shard_map(
        body, mesh=mesh,
        in_specs=(seq, seq, P(None, "query", "cand"), P(None, "query"), P(), w, w, w, w) + (v,) * 9 + (P("query", None),),
        out_specs=(seq, seq, w, w, w, w) + (v,) * 9 + (P("query", None), P()),
        check_vma=False)
```

```python
import functools

import jax
import jax.numpy as jnp
from jax import lax
from jax.experimental import pallas as pl
from jax.experimental.pallas import tpu as pltpu
from jax.sharding import PartitionSpec as P

F32 = jnp.float32
BF = jnp.bfloat16
NT = (((1,), (1,)), ((), ()))
NN = (((1,), (0,)), ((), ()))
TN = (((0,), (0,)), ((), ()))
VM = pl.BlockSpec(memory_space=pltpu.VMEM)
SM = pl.BlockSpec(memory_space=pltpu.SMEM)
ANY = pl.BlockSpec(memory_space=pl.ANY)
MESH = pl.DeviceIdType.MESH
EPS = 1e-5
FC = 1536
HEADS = 12
NR = {"x": 2, "y": 2, "z": 4}
RPIECES = ["u", "d", "o", "qa", "qb", "qz"]
RORD = {"u": "yxz", "d": "xyz", "o": "zyx", "qa": "yxz", "qb": "xyz", "qz": "zyx"}
RSHP = {"u": (192, 384, 48), "d": (96, 768, 48), "o": (48, 384, 48), "qa": (64, 384, 32), "qb": (64, 384, 32), "qz": (16, 384, 16)}
QROW = {"qa": 0, "qb": 64, "qz": 128}
NB = 4 * len(RPIECES)
AGSLOTS = {
    "b": [("u", (0, 0, 0), (("z", 1),)), ("d", (0, 0, 0), (("y", 1),)), ("u", (0, 0, 0), (("x", 1),))],
    "h": [("qa", (0, 0, 0), (("y", 1),)), ("qb", (0, 0, 0), (("x", 1),)), ("qa", (0, 0, 0), (("z", 3),)), ("qz", (0, 0, 0), (("z", 3), ("k", 0))), ("qb", (0, 0, 0), (("y", 1),)), ("u", (0, 0, 1), (("x", 1), ("y", 1), ("k", 0))), ("qb", (0, 0, 0), (("z", 2),)), ("qa", (0, 0, 0), (("z", 1),)), ("qb", (0, 0, 0), (("z", 3), ("z", 1))), ("qa", (0, 0, 0), (("x", 1),)), ("u", (0, 1, 0), (("y", 1), ("k", 0))), ("qz", (0, 0, 0), (("x", 1),)), ("qb", (0, 0, 2), (("y", 1), ("x", 1), ("k", 0))), ("qz", (0, 0, 0), (("y", 1),)), ("qb", (0, 0, 0), (("k", 0),)), ("qa", (0, 0, 0), (("z", 2),)), ("qb", (0, 1, 0), (("x", 1), ("k", 0))), ("qz", (0, 0, 1), (("y", 1), ("z", 1), ("z", 2), ("z", 3), ("k", 0))), ("d", (0, 0, 0), (("x", 1),)), ("qb", (0, 0, 3), (("y", 1), ("x", 1), ("k", 0))), ("qa", (0, 0, 1), (("x", 1), ("y", 1), ("k", 0))), ("u", (0, 0, 0), (("k", 0),)), ("d", (0, 0, 0), (("z", 1),)), ("qb", (0, 0, 1), (("y", 1), ("x", 1), ("k", 0))), ("qz", (0, 0, 0), (("z", 1),)), ("o", (0, 0, 0), (("k", 0),)), ("d", (0, 0, 0), (("z", 3),)), ("qa", (0, 0, 2), (("x", 1), ("y", 1), ("k", 0))), ("qz", (2, 0, 1), (("k", 0),)), ("qz", (0, 1, 1), (("z", 1), ("z", 2), ("z", 3), ("k", 0))), ("qz", (0, 1, 0), (("z", 1), ("z", 2), ("z", 3), ("k", 0))), ("d", (0, 0, 1), (("y", 1), ("x", 1), ("k", 0))), ("qa", (0, 0, 3), (("x", 1), ("y", 1), ("k", 0)))],
    "p0": [("qa", (0, 0, 0), (("k", 0),)), ("qz", (1, 0, 1), (("k", 0),)), ("qa", (1, 0, 1), (("k", 0),)), ("o", (0, 0, 0), (("x", 1),))],
    "p1": [("qz", (0, 0, 0), (("z", 2),)), ("o", (0, 0, 0), (("y", 1),)), ("qz", (2, 1, 1), (("k", 0),)), ("qb", (0, 1, 1), (("x", 1), ("k", 0))), ("qa", (0, 1, 0), (("y", 1), ("k", 0))), ("qa", (0, 1, 2), (("y", 1), ("k", 0))), ("qz", (1, 0, 0), (("k", 0),))],
    "p2": [("qb", (1, 0, 1), (("k", 0),)), ("u", (0, 0, 0), (("z", 2),)), ("qa", (1, 0, 3), (("k", 0),)), ("qb", (0, 1, 2), (("x", 1), ("k", 0))), ("qz", (3, 0, 0), (("k", 0),)), ("o", (0, 0, 0), (("z", 1),)), ("qb", (1, 0, 2), (("k", 0),)), ("qz", (2, 1, 0), (("k", 0),)), ("qz", (1, 1, 0), (("k", 0),)), ("qa", (0, 1, 3), (("y", 1), ("k", 0))), ("qa", (1, 0, 0), (("k", 0),)), ("qb", (1, 1, 0), (("k", 0),)), ("qb", (0, 1, 3), (("x", 1), ("k", 0))), ("d", (0, 1, 1), (("x", 1), ("k", 0))), ("qz", (2, 0, 0), (("k", 0),)), ("qa", (0, 1, 1), (("y", 1), ("k", 0))), ("qz", (3, 0, 1), (("k", 0),)), ("u", (0, 0, 0), (("z", 3),)), ("d", (0, 0, 0), (("z", 2),)), ("d", (0, 0, 3), (("y", 1), ("x", 1), ("k", 0))), ("u", (0, 1, 1), (("y", 1), ("k", 0))), ("qa", (1, 1, 0), (("k", 0),)), ("qz", (3, 1, 0), (("k", 0),)), ("qz", (3, 1, 1), (("k", 0),)), ("qb", (1, 1, 2), (("k", 0),)), ("qa", (1, 0, 2), (("k", 0),)), ("qa", (1, 1, 3), (("k", 0),)), ("qa", (1, 1, 2), (("k", 0),)), ("qb", (1, 0, 3), (("k", 0),)), ("qb", (1, 1, 3), (("k", 0),)), ("qb", (1, 1, 1), (("k", 0),)), ("qb", (1, 0, 0), (("k", 0),)), ("qz", (1, 1, 1), (("k", 0),)), ("qa", (1, 1, 1), (("k", 0),))],
    "n0": [("o", (0, 1, 0), (("z", 1), ("z", 2), ("z", 3), ("k", 0))), ("d", (1, 0, 1), (("k", 0),))],
    "n1": [("d", (0, 1, 0), (("x", 1), ("k", 0))), ("o", (0, 0, 1), (("y", 1), ("z", 1), ("z", 2), ("z", 3), ("k", 0)))],
    "n2": [("u", (1, 0, 1), (("k", 0),)), ("u", (0, 0, 2), (("x", 1), ("y", 1), ("k", 0)))],
    "n5": [("o", (0, 1, 1), (("z", 1), ("z", 2), ("z", 3), ("k", 0))), ("u", (0, 0, 0), (("y", 1),))],
    "n8": [("u", (0, 0, 3), (("x", 1), ("y", 1), ("k", 0))), ("d", (0, 1, 3), (("x", 1), ("k", 0))), ("o", (1, 0, 0), (("k", 0),)), ("d", (1, 0, 0), (("k", 0),))],
    "t3": [("d", (0, 0, 2), (("y", 1), ("x", 1), ("k", 0))), ("d", (1, 0, 3), (("k", 0),))],
    "t4": [("d", (0, 0, 0), (("k", 0),)), ("o", (0, 0, 0), (("z", 3),)), ("u", (1, 0, 0), (("k", 0),))],
    "t5": [("u", (0, 1, 2), (("y", 1), ("k", 0)))],
    "t6": [("o", (3, 1, 0), (("k", 0),)), ("u", (0, 1, 3), (("y", 1), ("k", 0))), ("d", (0, 1, 2), (("x", 1), ("k", 0))), ("u", (1, 0, 2), (("k", 0),)), ("o", (2, 1, 0), (("k", 0),)), ("d", (1, 1, 1), (("k", 0),)), ("u", (1, 1, 1), (("k", 0),))],
    "t8": [("u", (1, 1, 0), (("k", 0),)), ("u", (1, 0, 3), (("k", 0),)), ("o", (0, 0, 0), (("z", 2),)), ("d", (1, 1, 3), (("k", 0),)), ("o", (3, 0, 1), (("k", 0),)), ("d", (1, 1, 0), (("k", 0),)), ("u", (1, 1, 2), (("k", 0),)), ("o", (2, 1, 1), (("k", 0),))],
    "t9": [("d", (1, 0, 2), (("k", 0),))],
    "t10": [("o", (1, 1, 0), (("k", 0),)), ("o", (2, 0, 1), (("k", 0),)), ("d", (1, 1, 2), (("k", 0),)), ("o", (1, 1, 1), (("k", 0),)), ("o", (3, 1, 1), (("k", 0),)), ("u", (1, 1, 3), (("k", 0),)), ("o", (1, 0, 1), (("k", 0),)), ("o", (3, 0, 0), (("k", 0),)), ("o", (2, 0, 0), (("k", 0),))],
}
SLOTS = {
    "u0": [("s0", "o", 0, 0, 1), ("s0", "o", 3, 1, 1), ("s0", "u", 0, 0, 3)],
    "u1": [("s0", "u", 1, 1, 3), ("s0", "o", 1, 0, 0), ("s0", "u", 1, 1, 2), ("s0", "u", 1, 0, 3), ("s0", "u", 0, 1, 2), ("s0", "o", 2, 0, 1), ("s0", "o", 1, 1, 1)],
    "u2": [("s0", "o", 2, 1, 1), ("s0", "o", 2, 1, 0), ("s0", "u", 1, 1, 1), ("s0", "o", 2, 0, 0), ("s0", "u", 0, 1, 3), ("s1", "u", 1, 1, 3)],
    "u3": [("s1", "u", 1, 1, 2), ("s0", "o", 3, 0, 1), ("s1", "o", 2, 0, 1)],
    "d1": [("s0", "d", 1, 0, 3), ("s0", "d", 1, 1, 1), ("s0", "o", 3, 1, 0), ("s0", "d", 1, 1, 3), ("s1", "u", 1, 0, 3), ("s0", "d", 1, 0, 2), ("s1", "o", 3, 1, 1), ("s0", "d", 1, 0, 1)],
    "d2": [("s0", "u", 0, 0, 1), ("s0", "u", 1, 0, 0), ("s1", "d", 1, 0, 3), ("s0", "o", 3, 0, 0), ("s0", "d", 1, 1, 2)],
    "d3": [("s1", "o", 3, 0, 1), ("s1", "u", 1, 1, 1), ("s1", "o", 2, 0, 0), ("s1", "d", 1, 1, 3), ("s0", "d", 0, 1, 3), ("s2", "u", 1, 3), ("s0", "d", 1, 1, 0), ("s1", "o", 2, 1, 1), ("s1", "u", 1, 0, 0), ("s0", "o", 1, 1, 0), ("s0", "u", 1, 1, 0), ("s0", "u", 1, 0, 1), ("s0", "o", 1, 0, 1), ("s1", "o", 1, 1, 1), ("s1", "o", 3, 1, 0), ("s0", "d", 0, 1, 2), ("s0", "u", 0, 1, 0), ("s1", "o", 3, 0, 0)],
    "t0": [("s0", "o", 0, 1, 0), ("s0", "d", 0, 0, 1), ("s1", "d", 1, 1, 2)],
    "t2": [("s2", "d", 1, 3), ("s1", "o", 2, 1, 0)],
    "t3": [("s0", "u", 0, 0, 2), ("s1", "d", 1, 0, 2), ("s0", "u", 0, 1, 1), ("s1", "o", 1, 1, 0), ("s3", "u", 3), ("s0", "u", 1, 0, 2), ("s0", "d", 0, 0, 3), ("s0", "d", 0, 0, 2), ("s0", "o", 0, 1, 1), ("s1", "d", 1, 1, 1)],
    "t4": [("s3", "d", 3), ("s1", "o", 1, 0, 0), ("s2", "u", 1, 2), ("s2", "o", 1, 1), ("s1", "u", 1, 0, 2), ("s2", "d", 1, 2), ("s0", "d", 0, 1, 1)],
    "t7": [("s1", "u", 1, 1, 0), ("s1", "o", 1, 0, 1), ("s2", "u", 1, 1), ("s2", "o", 1, 0)],
    "t8": [("s1", "d", 1, 0, 1), ("s2", "d", 1, 1), ("s3", "d", 2), ("s0", "o", 0, 0, 0)],
    "t9": [("s1", "d", 1, 1, 0), ("s3", "u", 2)],
    "g2": [("s0", "qb", 1, 0, 3), ("s0", "qa", 1, 1, 2), ("s0", "d", 0, 1, 0), ("s1", "u", 1, 0, 1), ("s0", "qb", 1, 1, 2), ("s0", "qb", 1, 1, 3), ("s0", "d", 1, 0, 0), ("s0", "qz", 3, 1, 0), ("s0", "qa", 0, 1, 2), ("s0", "qz", 2, 1, 0), ("s3", "o", 1)],
    "g3": [("s0", "d", 0, 0, 0), ("s0", "qa", 1, 1, 3), ("s0", "qz", 3, 0, 0), ("s0", "qz", 2, 0, 0), ("s1", "qb", 1, 0, 3)],
    "g4": [("s1", "qb", 1, 1, 3), ("s0", "qz", 3, 1, 1)],
    "g5": [("s0", "qz", 1, 1, 1), ("s0", "qz", 0, 0, 0), ("s1", "qz", 2, 0, 0), ("s1", "qa", 1, 1, 2), ("s0", "qz", 1, 1, 0), ("s0", "qb", 0, 0, 0), ("s0", "qa", 1, 1, 1), ("s1", "qz", 3, 0, 0), ("s0", "qb", 1, 0, 2), ("s0", "qa", 1, 0, 1), ("s1", "qb", 1, 1, 2), ("s0", "qb", 1, 1, 0), ("s0", "qb", 0, 0, 3), ("s0", "qb", 0, 1, 3), ("s0", "qa", 1, 0, 3), ("s0", "qa", 0, 0, 3), ("s0", "qb", 0, 0, 2), ("s0", "qz", 1, 0, 1), ("s2", "u", 1, 0), ("s0", "qz", 3, 0, 1), ("s0", "qb", 0, 1, 1), ("s0", "qa", 0, 1, 1), ("s0", "qb", 1, 0, 1), ("s0", "qa", 0, 1, 3), ("s3", "d", 1), ("s0", "qa", 0, 0, 1), ("s1", "qa", 1, 1, 3), ("s0", "qb", 1, 1, 1), ("s0", "qa", 1, 1, 0), ("s0", "qb", 0, 1, 0), ("s0", "qb", 0, 0, 1), ("s0", "qz", 2, 1, 1)],
    "v": [("s2", "qb", 1, 3), ("s1", "qz", 2, 1, 0), ("s0", "qz", 2, 0, 1), ("s1", "qb", 1, 1, 0), ("s0", "qa", 1, 0, 2), ("s1", "qa", 1, 1, 1), ("s1", "qz", 3, 1, 0), ("s1", "qz", 3, 0, 1), ("s1", "qa", 1, 1, 0), ("s1", "qz", 1, 0, 1), ("s1", "qz", 1, 1, 1), ("fin_", "o")],
    "i0": [("s0", "qa", 0, 0, 2), ("s2", "qa", 1, 3), ("s1", "qz", 2, 1, 1), ("s1", "qz", 1, 1, 0), ("s1", "qz", 3, 1, 1), ("s2", "qa", 1, 2), ("s1", "qa", 1, 0, 3), ("s0", "u", 0, 0, 0), ("s0", "qa", 1, 0, 0), ("s1", "qa", 1, 0, 2), ("s0", "qb", 0, 1, 2), ("s1", "qb", 1, 1, 1), ("s1", "qz", 2, 0, 1), ("s0", "qa", 0, 1, 0), ("s2", "d", 1, 0), ("s3", "u", 1), ("s2", "qa", 1, 1)],
    "i1": [("s1", "qb", 1, 0, 2), ("s2", "qa", 1, 0), ("s0", "qa", 0, 0, 0), ("s0", "qz", 0, 1, 1), ("s3", "qb", 3), ("s3", "qa", 3), ("s1", "qb", 1, 0, 1), ("s3", "qa", 2), ("s1", "qa", 1, 0, 1), ("s0", "qb", 1, 0, 0), ("s1", "d", 1, 0, 0), ("s2", "qb", 1, 2), ("s2", "qb", 1, 1)],
    "i2": [("s3", "qa", 1), ("s2", "qz", 1, 1), ("s0", "qz", 0, 1, 0), ("s1", "qa", 1, 0, 0), ("s1", "qb", 1, 0, 0), ("s0", "qz", 1, 0, 0), ("s3", "qb", 2), ("s2", "qb", 1, 0)],
    "i3": [("s0", "qz", 0, 0, 1), ("s3", "qb", 1), ("s1", "qz", 1, 0, 0), ("s3", "qz", 1), ("fin_", "qa"), ("s2", "qz", 1, 0), ("fin_", "u"), ("fin_", "d"), ("fin_", "qb"), ("fin_", "qz")],
}


def dg(a,b,d,prec=None): return lax.dot_general(a,b,d,preferred_element_type=F32,precision=prec)


def hooks(i, table):
    for j, evs in table.items():
        if evs:
            @pl.when(i == j)
            def _(evs=evs):
                for e in evs: e()


def qkv_proj(w_ref, bias_ref, xlow_ref, qkv_ref, slots):
    def body(n,_):
        o=pl.multiple_of(n*256,256)
        y=dg(xlow_ref[...], w_ref[pl.ds(o,256),:], NT)
        y=(y+bias_ref[:,pl.ds(o,256)])*jnp.where(o<xlow_ref.shape[1],0.125,1.0)
        qkv_ref[:,pl.ds(o,256)]=y.astype(BF)
        hooks(n, slots)
        return 0
    lax.fori_loop(0, w_ref.shape[0]//256, body, 0)


def rel_rows(tableT_ref, bk_ref, rel_ref):
    nb=tableT_ref.shape[1]; n=bk_ref.shape[1]
    hot=(lax.broadcasted_iota(jnp.int32,(nb,n),0)==bk_ref[...]).astype(F32)
    rel_ref[...]=dg(tableT_ref[...], hot, NN, lax.Precision.HIGHEST)


def bias_expand(row,S):
    R=pltpu.roll(jnp.broadcast_to(row,(128,2*S)), 2*S-127, 1, stride=1, stride_axis=0)
    nu=S//128
    return jnp.concatenate([R[:,128*(nu-1-u):128*(nu-1-u)+S] for u in range(nu)],axis=0)


def diag_sum(t,S):
    nu=S//128
    y=None
    for u in range(nu):
        a=128*(nu-1-u); parts=[]
        if a: parts.append(jnp.zeros((128,a),F32))
        parts.append(t[128*u:128*(u+1),:])
        if 2*S-a-S: parts.append(jnp.zeros((128,2*S-a-S),F32))
        v=jnp.concatenate(parts,axis=1) if len(parts)>1 else parts[0]
        y=v if y is None else y+v
    z=None
    for w in range(16):
        g=y[8*w:8*w+8,:]
        sh=120-8*w
        g=pltpu.roll(g,sh,1) if sh else g
        z=g if z is None else z+g
    out=None
    for b in range(8):
        g=z[b:b+1,:]
        g=pltpu.roll(g,7-b,1) if b<7 else g
        out=g if out is None else out+g
    return out


def attn_fwd(len_ref, qkv_ref, rel_ref, ctx_ref, lse_ref, bias_scr, S, D, slots):
    lane=lax.broadcasted_iota(jnp.int32,(1,128),1)
    col=lax.broadcasted_iota(jnp.int32,(1,S),1)
    def body(p,_):
        o=pl.multiple_of(p*128,128)
        for hh in range(2):
            row=rel_ref[pl.ds(p*2+hh,1),:]
            bias_scr[hh]=bias_expand(row,S)
        for m in range(2):
            q=qkv_ref[m*S:(m+1)*S,pl.ds(o,128)]
            k=qkv_ref[m*S:(m+1)*S,pl.ds(D+o,128)]
            v=qkv_ref[m*S:(m+1)*S,pl.ds(2*D+o,128)]
            valid=col<len_ref[m]
            outs=[]
            for hh in range(2):
                mk=(lane//64)==hh
                qm=jnp.where(mk,q,jnp.zeros_like(q))
                s=dg(qm,k,NT)+bias_scr[hh]
                s=jnp.where(valid,s,-1e30)
                mx=jnp.max(s,axis=1,keepdims=True)
                e=jnp.exp(s-mx)
                tot=jnp.sum(e,axis=1,keepdims=True)
                pl_=(e*(1.0/tot)).astype(BF)
                outs.append(dg(pl_,v,NN))
                lse_ref[m,pl.ds(p*2+hh,1),:]=jnp.transpose(mx+jnp.log(tot),(1,0))
            ctx_ref[m*S:(m+1)*S,pl.ds(o,128)]=jnp.where((lane//64)==0,outs[0],outs[1]).astype(BF)
            hooks(p, {i: slots.get(2*i+m) for i in range(D//128)})
        return 0
    lax.fori_loop(0, D//128, body, 0)


def attn_bwd(len_ref, qkv_ref, dctx_ref, lse_ref, relf_ref, drelf_ref, bias_scr, acc_scr, S, D, slots):
    lane=lax.broadcasted_iota(jnp.int32,(1,128),1)
    rowi=lax.broadcasted_iota(jnp.int32,(S,1),0)
    m0=(lane//64)==0
    def body(p,_):
        o=pl.multiple_of(p*128,128)
        for hh in range(2):
            row=relf_ref[pl.ds(p*2+hh,1),:]
            bias_scr[hh]=bias_expand(row,S)
        for m in range(2):
            q=qkv_ref[m*S:(m+1)*S,pl.ds(o,128)]
            k=qkv_ref[m*S:(m+1)*S,pl.ds(D+o,128)]
            v=qkv_ref[m*S:(m+1)*S,pl.ds(2*D+o,128)]
            do=dctx_ref[m*S:(m+1)*S,pl.ds(o,128)]
            valid=rowi<len_ref[m]
            oq=[];ok=[];ov=[]
            for hh in range(2):
                mk=(lane//64)==hh
                km=jnp.where(mk,k,jnp.zeros_like(k)); vm=jnp.where(mk,v,jnp.zeros_like(v))
                sT=dg(km,q,NT)+bias_scr[hh]
                sT=jnp.where(valid,sT,-1e30)
                pT=jnp.exp(sT-lse_ref[m,pl.ds(p*2+hh,1),:])
                dpT=dg(vm,do,NT)
                rd=jnp.sum(dpT*pT,axis=0,keepdims=True)
                ds=(pT*(dpT-rd)).astype(BF)
                ov.append(dg(pT.astype(BF),do,NN))
                ok.append(dg(ds,q,NN))
                oq.append(dg(ds,k,TN))
                if m==0: acc_scr[hh]=ds.astype(F32)
                else: acc_scr[hh]+=ds.astype(F32)
            qkv_ref[m*S:(m+1)*S,pl.ds(o,128)]=(jnp.where(m0,oq[0],oq[1])*0.125).astype(BF)
            qkv_ref[m*S:(m+1)*S,pl.ds(D+o,128)]=jnp.where(m0,ok[0],ok[1]).astype(BF)
            qkv_ref[m*S:(m+1)*S,pl.ds(2*D+o,128)]=jnp.where(m0,ov[0],ov[1]).astype(BF)
            hooks(p, {i: slots.get(2*i+m) for i in range(D//128)})
        for hh in range(2):
            drelf_ref[pl.ds(p*2+hh,1),:]=diag_sum(acc_scr[hh],S)
        return 0
    lax.fori_loop(0, D//128, body, 0)


def stats(z):
    mu=jnp.mean(z,axis=-1,keepdims=True); c=z-mu
    var=jnp.mean(c*c,axis=-1,keepdims=True)
    r=lax.rsqrt(var+EPS)
    return c*r, r


def fwd_tile(slot, x_ref, ctx_ref, wo_ref, wu_ref, wd_ref, vec_ref, bup_ref, out_ref, nl_scr, act_scr, gp_scr, z1_scr, z2_scr, r_scr, R):
    D=x_ref.shape[2]; FF=wu_ref.shape[1]
    ctx=ctx_ref[...].reshape(R,D)
    fs=x_ref[...].reshape(R,D)+(dg(ctx,wo_ref[...],NT)+vec_ref[0:1,:])
    z1,r1=stats(fs)
    z1_scr[slot]=z1
    fn=z1*vec_ref[1:2,:]+vec_ref[2:3,:]
    nl=fn.astype(BF)
    nl_scr[...]=nl.reshape(nl_scr.shape)
    def body(f,acc):
        o=pl.multiple_of(f*FC,FC)
        u=dg(nl_scr[...].reshape(R,D),wu_ref[:,pl.ds(o,FC)],NN)+bup_ref[:,pl.ds(o,FC)]
        phi=0.5*(1.0+lax.erf(u*(2.0**-0.5)))
        a=(u*phi).astype(BF)
        act_scr[:,:,pl.ds(o,FC)]=a.reshape(2,R//2,FC)
        gp_scr[slot,:,pl.ds(o,FC)]=phi+u*(jnp.exp(u*u*-0.5)*0.3989422804014327)
        return acc+dg(a,wd_ref[:,pl.ds(o,FC)],NT)
    acc=lax.fori_loop(0,FF//FC,body,fn+vec_ref[3:4,:],unroll=True)
    z2,r2=stats(acc)
    z2_scr[slot]=z2
    r_scr[slot,:,0:1]=r1
    r_scr[slot,:,1:2]=r2
    out_ref[...]=(z2*vec_ref[4:5,:]).reshape(out_ref.shape)


def lnb(u,z,r):
    return r*(u-jnp.mean(u,axis=-1,keepdims=True)-z*jnp.mean(u*z,axis=-1,keepdims=True))


def bwd_tile(slot, ds_ref, cot_ref, wo_ref, wu_ref, wd_ref, vec_ref, dfs_ref, dctx_ref, gv_ref, gbu_ref, dl_scr, ul_scr, al_scr, gp_scr, z1_scr, z2_scr, r_scr, R):
    D=wu_ref.shape[0]; FF=wu_ref.shape[1]; Rh=R//2
    r1=r_scr[slot,:,0:1]; r2=r_scr[slot,:,1:2]
    z2=z2_scr[slot]
    do=cot_ref[...].reshape(R,D)
    ri=lax.broadcasted_iota(jnp.int32,(R,1),0)
    coef=jnp.where(ri==0,ds_ref[0:1,0:1],0.0)+jnp.where(ri==Rh,ds_ref[1:2,0:1],0.0)
    do=do+coef*vec_ref[5:6,:]
    gv_ref[4:5,:]+=jnp.sum(do*z2,axis=0,keepdims=True)
    gv_ref[5:6,:]+=jnp.sum(coef*(z2*vec_ref[4:5,:]),axis=0,keepdims=True)
    d2=lnb(do*vec_ref[4:5,:],z2,r2)
    dl=d2.astype(BF)
    dl_scr[...]=dl.reshape(dl_scr.shape)
    gv_ref[3:4,:]+=jnp.sum(dl.astype(F32),axis=0,keepdims=True)
    def body(f,acc):
        o=pl.multiple_of(f*FC,FC)
        da=dg(dl_scr[...].reshape(R,D),wd_ref[:,pl.ds(o,FC)],NN)
        ul=(da*gp_scr[slot,:,pl.ds(o,FC)]).astype(BF)
        ul_scr[:,:,pl.ds(o,FC)]=ul.reshape(2,R//2,FC)
        gbu_ref[:,pl.ds(o,FC)]+=jnp.sum(ul.astype(F32),axis=0,keepdims=True)
        return acc+dg(ul,wu_ref[:,pl.ds(o,FC)],NT)
    d1=lax.fori_loop(0,FF//FC,body,d2,unroll=True)
    z1=z1_scr[slot]
    gv_ref[1:2,:]+=jnp.sum(d1*z1,axis=0,keepdims=True)
    gv_ref[2:3,:]+=jnp.sum(d1,axis=0,keepdims=True)
    dfs=lnb(d1*vec_ref[1:2,:],z1,r1)
    dfs_ref[...]=dfs.reshape(dfs_ref.shape)
    al=dfs.astype(BF)
    al_scr[...]=al.reshape(al_scr.shape)
    gv_ref[0:1,:]+=jnp.sum(al.astype(F32),axis=0,keepdims=True)
    dctx_ref[...]=dg(al,wo_ref[...],NN).astype(BF).reshape(dctx_ref.shape)


class Geo:
    def __init__(g, C, Q):
        g.C=C; g.Q=Q; g.nx=Q//2; g.nz=min(4,C); g.ny=C//g.nz
        c=lax.axis_index("cand"); q=lax.axis_index("query")
        g.z=c//g.ny; g.y=lax.rem(c,g.ny); g.x=q//2; g.k=lax.rem(q,2)
    def dev(g,z,y,x,k): return {"cand":z*g.ny+y,"query":x*2+k}


def mo(v,n): return pl.multiple_of(v,n)


def barrier(g, peers):
    b=pltpu.get_barrier_semaphore()
    for p in peers: pl.semaphore_signal(b,inc=1,device_id=p,device_id_type=MESH)
    pl.semaphore_wait(b,len(peers))


class RS:
    def __init__(s, g, refs, bufs, ss, rs):
        s.g, s.refs, s.bufs, s.ss, s.rs = g, refs, bufs, ss, rs
        s.partner = g.dev(g.z, g.y, g.x, 1 - g.k)
        s.pend = []
    def dims(s, n): return [NR[d] for d in RORD[n]]
    def own(s, n, rel, k):
        g = s.g
        r = dict(zip(RORD[n], rel))
        return rs_slice(g, n, s.refs, jnp.bitwise_xor(g.z, r["z"]), 1 - g.y if r["y"] else g.y, 1 - g.x if r["x"] else g.x, k)
    def near(s, d, r):
        g = s.g
        return g.dev(jnp.bitwise_xor(g.z, r) if d == "z" else g.z, 1 - g.y if d == "y" else g.y, 1 - g.x if d == "x" else g.x, g.k)
    def copy(s, src, dst, n, i, dev):
        pi = RPIECES.index(n)
        return pltpu.make_async_remote_copy(src, dst, s.ss.at[pi, i], s.rs.at[pi, i], device_id=dev, device_id_type=MESH)
    def c0(s, n, r1, r2, r3):
        _, n2, n3 = s.dims(n)
        return s.copy(s.own(n, (r1, r2, r3), 1 - s.g.k), s.bufs[n][0].at[r1, r2, r3], n, (r1 * n2 + r2) * n3 + r3, s.partner)
    def c1(s, n, r1, r2, r3):
        _, n2, n3 = s.dims(n)
        return s.copy(s.bufs[n][0].at[r1, r2, r3], s.bufs[n][1].at[r1 - 1, r2, r3], n, 16 + ((r1 - 1) * n2 + r2) * n3 + r3, s.near(RORD[n][0], r1))
    def c2(s, n, r2, r3):
        n1, n2, n3 = s.dims(n)
        return s.copy(s.bufs[n][0].at[0, r2, r3], s.bufs[n][2].at[r2 - 1, r3], n, 16 + (n1 - 1) * n2 * n3 + (r2 - 1) * n3 + r3, s.near(RORD[n][1], r2))
    def c3(s, n, r3):
        n1, n2, n3 = s.dims(n)
        return s.copy(s.bufs[n][0].at[0, 0, r3], s.bufs[n][3].at[r3 - 1], n, 16 + (n1 - 1) * n2 * n3 + (n2 - 1) * n3 + r3 - 1, s.near(RORD[n][2], r3))
    def go(s, f, *a):
        f(*a).start()
        s.pend.append(lambda: f(*a))
    def add(s, n, dst, srcs):
        rows, st = RSHP[n][0], RSHP[n][2]
        def body(i, _):
            o = pl.multiple_of(i * st, 16)
            dst[pl.ds(o, st), :] = functools.reduce(lambda a, b: a + b, [r[pl.ds(o, st), :].astype(F32) for r in srcs]).astype(dst.dtype)
            return 0
        lax.fori_loop(0, rows // st, body, 0)
    def part1(s, n, r2, r3):
        s.c0(n, 0, r2, r3).wait_recv()
        n1 = s.dims(n)[0]
        for r1 in range(1, n1):
            s.c1(n, r1, r2, r3).wait_recv()
        return [s.own(n, (0, r2, r3), s.g.k), s.bufs[n][0].at[0, r2, r3]] + [s.bufs[n][1].at[r1 - 1, r2, r3] for r1 in range(1, n1)]
    def part2(s, n, r3):
        t = s.part1(n, 0, r3)
        n2 = s.dims(n)[1]
        for r2 in range(1, n2):
            s.c2(n, r2, r3).wait_recv()
        return t + [s.bufs[n][2].at[r2 - 1, r3] for r2 in range(1, n2)]
    def s0(s, n, r1, r2, r3): s.go(s.c0, n, r1, r2, r3)
    def s1(s, n, r1, r2, r3):
        s.c0(n, r1, r2, r3).wait_recv()
        b = s.bufs[n][0].at[r1, r2, r3]
        s.add(n, b, [s.own(n, (r1, r2, r3), s.g.k), b])
        s.go(s.c1, n, r1, r2, r3)
    def s2(s, n, r2, r3):
        s.add(n, s.bufs[n][0].at[0, r2, r3], s.part1(n, r2, r3))
        s.go(s.c2, n, r2, r3)
    def s3(s, n, r3):
        s.add(n, s.bufs[n][0].at[0, 0, r3], s.part2(n, r3))
        s.go(s.c3, n, r3)
    def fin(s, n, dst):
        t = s.part2(n, 0)
        n3 = s.dims(n)[2]
        for r3 in range(1, n3):
            s.c3(n, r3).wait_recv()
        s.add(n, dst, t + [s.bufs[n][3].at[r3 - 1] for r3 in range(1, n3)])
    def fin_(s, n): s.fin(n, s.outs[n])
    def ev(s, e): getattr(s, e[0])(*e[1:])
    def drain(s):
        for c in s.pend: c().wait_send()


def rs_slice(g, n, refs, z, y, x, k):
    wq, wo, wu, wd = refs
    c = z * g.ny + y
    q = x * 2 + k
    if n in QROW:
        return wq.at[pl.ds(mo(c * 288 + k * 144 + QROW[n], 16), RSHP[n][0]), pl.ds(mo(x * 384, 128), 384)]
    if n == "o": return wo.at[pl.ds(mo(c * 96 + k * 48, 16), 48), pl.ds(mo(x * 384, 128), 384)]
    if n == "u": return wu.at[pl.ds(mo(q * 192, 16), 192), pl.ds(mo(c * 384, 128), 384)]
    if n == "d": return wd.at[pl.ds(mo(c * 96, 16), 96), pl.ds(mo(q * 768, 128), 768)]


def rs_bufs():
    out = []
    for n in RPIECES:
        n1, n2, n3 = [NR[d] for d in RORD[n]]
        sh = RSHP[n][:2]
        out += [pltpu.VMEM((n1, n2, n3) + sh, BF), pltpu.VMEM((n1 - 1, n2, n3) + sh, BF), pltpu.VMEM((n2 - 1, n3) + sh, BF), pltpu.VMEM((n3 - 1,) + sh, BF)]
    return out


def attn_fwd_kernel(len_ref, x_ref, w_ref, bias_ref, tab_ref, bk_ref, bkf_ref, xlow_ref, qkv_ref, ctx_ref, lse_ref, relf_ref, rel_ref, bias_scr):
    S, D = x_ref.shape[1:]
    for m in range(2):
        xlow_ref[m*S:(m+1)*S,:]=x_ref[m].astype(BF)
    qkv_proj(w_ref, bias_ref, xlow_ref, qkv_ref, {})
    rel_rows(tab_ref, bk_ref, rel_ref)
    rel_rows(tab_ref, bkf_ref, relf_ref)
    attn_fwd(len_ref, qkv_ref, rel_ref, ctx_ref, lse_ref, bias_scr, S, D, {})


class AG:
    def __init__(s, g, own, refs, ss, rs, cs, cr):
        s.g, s.own_, s.refs, s.ss, s.rs, s.cs, s.cr = g, own, refs, ss, rs, cs, cr
        s.partner = g.dev(g.z, g.y, g.x, 1 - g.k)
        s.pend = []
        s.got = set()
    def dst(s, n, rel, k):
        g = s.g
        r = dict(zip(RORD[n], rel))
        return rs_slice(g, n, s.refs, jnp.bitwise_xor(g.z, r["z"]), 1 - g.y if r["y"] else g.y, 1 - g.x if r["x"] else g.x, k)
    def idx(s, n, rel):
        _, n2, n3 = [NR[d] for d in RORD[n]]
        return (rel[0] * n2 + rel[1]) * n3 + rel[2]
    def src(s, n, rel): return s.own_(n) if rel == (0, 0, 0) else s.dst(n, rel, s.g.k)
    def near(s, d, r):
        g = s.g
        return g.dev(jnp.bitwise_xor(g.z, r) if d == "z" else g.z, 1 - g.y if d == "y" else g.y, 1 - g.x if d == "x" else g.x, g.k)
    def link(s, n, rel, d, k):
        new = tuple(k if a == d else r for a, r in zip(RORD[n], rel))
        pi, i = RPIECES.index(n), s.idx(n, new)
        return pltpu.make_async_remote_copy(s.src(n, rel), s.dst(n, rel, s.g.k), s.ss.at[pi, i], s.rs.at[pi, i], device_id=s.near(d, k), device_id_type=MESH)
    def core(s, n, rel):
        pi, i = RPIECES.index(n), s.idx(n, rel)
        return pltpu.make_async_remote_copy(s.src(n, rel), s.dst(n, rel, s.g.k), s.cs.at[pi, i], s.cr.at[pi, i], device_id=s.partner, device_id_type=MESH)
    def got_core(s, n, rel):
        pi, i = RPIECES.index(n), s.idx(n, rel)
        t = s.dst(n, rel, 1 - s.g.k)
        pltpu.make_async_remote_copy(t, t, s.cs.at[pi, i], s.cr.at[pi, i], device_id=s.partner, device_id_type=MESH).wait_recv()
    def go(s, f, *a):
        f(*a).start()
        s.pend.append(lambda: f(*a))
    def ev(s, e):
        n, rel, outs = e
        if rel != (0, 0, 0):
            t = s.dst(n, rel, s.g.k)
            pi, i = RPIECES.index(n), s.idx(n, rel)
            pltpu.make_async_remote_copy(t, t, s.ss.at[pi, i], s.rs.at[pi, i], device_id=s.partner, device_id_type=MESH).wait_recv()
        for d, k in outs:
            if d == "k": s.go(s.core, n, rel)
            else: s.go(s.link, n, rel, d, k)
    def rels(s, n):
        n1, n2, n3 = [NR[d] for d in RORD[n]]
        return [(a, b, c) for a in range(n1) for b in range(n2) for c in range(n3)]
    def drain(s):
        for c in s.pend: c().wait_send()


def front_kernel(len_ref, x_h, wqf_h, wof_h, wuf_h, wdf_h, *rest, C, Q):
    vins, rest = rest[:11], rest[11:]
    (wq_o, wo, wu, wd, vec_o, bup_o, xlow_o, qkv_o, ctx_ref, lse_ref, relf_ref, bkf_o,
     wqf_ref, wof_ref, wuf_ref, wdf_ref, v_ref, bk_ref, x_v, xlow, qkv, wq, own_p, got_p, h_scr, u_bf, d_bf, vall, tab, rel, qb, bias_scr, ss, rs, cs, cr, vss, vrs, ps, ls) = rest
    g = Geo(C, Q)
    S, D = x_h.shape[1:]
    q_ = lax.axis_index("query")
    peers = [{"query": lax.rem(q_ + j, Q)} for j in range(1, Q)] + [g.dev(g.z, 1 - g.y, g.x, g.k)] + [g.dev(jnp.bitwise_xor(g.z, i), g.y, g.x, g.k) for i in range(1, g.nz)]
    bar = pltpu.get_barrier_semaphore()
    for p in peers:
        pl.semaphore_signal(bar, inc=1, device_id=p, device_id_type=MESH)
    wc = [pltpu.make_async_copy(a, b, ls.at[10 + i]) for i, (a, b) in enumerate(((wqf_h, wqf_ref), (wof_h, wof_ref), (wuf_h, wuf_ref), (wdf_h, wdf_ref)))]
    for c in wc:
        c.start()
    xc = pltpu.make_async_copy(x_h, x_v, ls.at[0])
    xc.start()
    k = g.k
    dq, bq = D // Q, tab.shape[1] // Q
    fq = bup_o.shape[1] // Q
    v_ref[...] = jnp.zeros_like(v_ref)
    for i in range(8):
        v_ref[i:i + 1, 0:dq] = vins[i][...]
    for j in range(fq // 256):
        v_ref[8 + j:9 + j, :] = vins[8][:, j * 256:(j + 1) * 256]
    v_ref[16:16 + vins[9].shape[0], 0:bq] = vins[9][...]
    nrel = vins[10].shape[1]
    bk_ref[...] = jnp.full(bk_ref.shape, -1, jnp.int32)
    bk_ref[:, 0:nrel] = vins[10][...]
    for c in wc:
        c.wait()

    def turn(w):
        n = w.shape[1]
        eye = (lax.broadcasted_iota(jnp.int32, (n, n), 0) == lax.broadcasted_iota(jnp.int32, (n, n), 1)).astype(BF)
        return dg(eye, w.astype(BF), NT).astype(BF)
    a, b = turn(wqf_ref[...]), turn(wof_ref[...])
    ha, hb = a.shape[0] // 2, b.shape[0] // 2
    for i in range(2):
        own_p[i, 0:ha, :] = a[i * ha:(i + 1) * ha]
        own_p[i, ha:ha + hb, :] = b[i * hb:(i + 1) * hb]
    d_bf[...] = wdf_ref[...].astype(BF)
    u_bf[...] = wuf_ref[...].astype(BF)
    pl.semaphore_wait(bar, len(peers))
    pc = pltpu.make_async_remote_copy(own_p.at[1 - k], got_p, ps.at[0], ps.at[1], device_id=g.dev(g.z, g.y, g.x, 1 - k), device_id_type=MESH)
    pc.start()
    vcs = []
    for j in range(1, Q):
        c = pltpu.make_async_remote_copy(v_ref, vall.at[q_], vss.at[j - 1], vrs.at[j - 1], device_id={"query": lax.rem(q_ + j, Q)}, device_id_type=MESH)
        c.start()
        vcs.append(c)
    vall[q_] = v_ref[...]

    def own(n):
        if n == "u": return u_bf
        if n == "d": return d_bf
        return h_scr.at[pl.ds(QROW.get(n, 144), RSHP[n][0])]
    A = AG(g, own, (wq, wo, wu, wd), ss, rs, cs, cr)
    loc = [pltpu.make_async_copy(own(n), A.dst(n, (0, 0, 0), k), ls.at[1 + i]) for i, n in enumerate(RPIECES)]

    def after(name):
        for e in AGSLOTS.get(name, []):
            A.ev(e)
    after("b")
    loc[0].start()
    loc[1].start()
    pc.wait()
    t, r = own_p[k], got_p[...]
    @pl.when(k == 0)
    def _(): h_scr[...] = jnp.concatenate([t, r], axis=1)
    @pl.when(k == 1)
    def _(): h_scr[...] = jnp.concatenate([r, t], axis=1)
    for c in loc[2:]:
        c.start()
    after("h")
    xc.wait()
    for m in range(2):
        xlow[m*S:(m+1)*S,:]=x_v[m].astype(BF)
    xo = pltpu.make_async_copy(xlow, xlow_o, ls.at[7])
    xo.start()
    after("p0")
    ids = jnp.broadcast_to(bk_ref[...], (8, 2 * S)).astype(F32).astype(BF)
    for j in range(2 * S // 256):
        flip = (lax.broadcasted_iota(jnp.int32, (2 * S, 256), 0) + lax.broadcasted_iota(jnp.int32, (2 * S, 256), 1) == nrel - 1 - j * 256).astype(BF)
        bkf_o[:, j * 256:(j + 1) * 256] = dg(ids, flip, NN)[0:1].astype(jnp.int32)
    bkf_o[:, nrel:] = jnp.full((1, 2 * S - nrel), -1, jnp.int32)
    after("p1")
    for c in vcs:
        c.wait()
    qb[...] = jnp.zeros_like(qb)
    vec_o[...] = jnp.zeros_like(vec_o)
    for q in range(Q):
        lo, hi = q * dq, (q + 1) * dq
        qb[:, lo:hi] = vall[q, 0:1, 0:dq]
        qb[:, 2 * D + lo:2 * D + hi] = vall[q, 1:2, 0:dq]
        vec_o[0:6, lo:hi] = vall[q, 2:8, 0:dq]
        for j in range(fq // 256):
            bup_o[:, q * fq + j * 256:q * fq + (j + 1) * 256] = vall[q, 8 + j:9 + j, :]
        tab[:, q * bq:(q + 1) * bq] = vall[q, 16:32, 0:bq]
    rel_rows(tab, bk_ref, rel)
    rel_rows(tab, bkf_o, relf_ref)
    after("p2")
    for i, n in enumerate(RPIECES):
        if n in QROW:
            loc[i].wait()
            for r in A.rels(n):
                A.got_core(n, r)
    qkv_proj(wq, qb, xlow, qkv, {i: [functools.partial(A.ev, e) for e in AGSLOTS.get(f"n{i}", [])] for i in range(3 * D // 256)})
    wc = pltpu.make_async_copy(wq, wq_o, ls.at[8])
    qc = pltpu.make_async_copy(qkv, qkv_o, ls.at[9])
    wc.start()
    qc.start()
    attn_fwd(len_ref, qkv, rel, ctx_ref, lse_ref, bias_scr, S, D, {i: [functools.partial(A.ev, e) for e in AGSLOTS.get(f"t{i}", [])] for i in range(D // 64)})
    for c in (xo, wc, qc):
        c.wait()
    for i, n in enumerate(RPIECES):
        if n not in QROW:
            loc[i].wait()
            for r in A.rels(n):
                A.got_core(n, r)
    A.drain()


def ffn_kernel(lab_ref, x_ref, ctx_ref, cot_ref, wo_ref, wu_ref, wd_ref, vec_ref, bup_ref,
               out_ref, dfs_ref, dctx_ref, nl_ref, act_ref, dl_ref, al_ref, ul_ref, gv_ref, gbu_ref, loss_ref,
               gp_scr, z1_scr, z2_scr, r_scr,
               ds_scr, sc_snd, sc_all, sss, ssr, *, T, R, C, Q):
    i = pl.program_id(0)
    D, FF = wu_ref.shape
    cid = lax.axis_index("cand")

    def score_copy(j):
        return pltpu.make_async_remote_copy(sc_snd, sc_all.at[cid], sss.at[j - 1], ssr.at[j - 1], device_id={"cand": lax.rem(cid + j, C)}, device_id_type=MESH)

    @pl.when(i == 0)
    def _():
        b = pltpu.get_barrier_semaphore()
        for j in range(1, C):
            pl.semaphore_signal(b, inc=1, device_id={"cand": lax.rem(cid + j, C)}, device_id_type=MESH)
        pl.semaphore_wait(b, C - 1)
        gv_ref[...] = jnp.zeros_like(gv_ref)
        gbu_ref[...] = jnp.zeros_like(gbu_ref)
        ds_scr[...] = jnp.zeros_like(ds_scr)
        sc_snd[...] = jnp.zeros_like(sc_snd)

    @pl.when(i < T)
    def _():
        fwd_tile(jnp.minimum(i, 1), x_ref, ctx_ref, wo_ref, wu_ref, wd_ref, vec_ref, bup_ref, out_ref, nl_ref, act_ref, gp_scr, z1_scr, z2_scr, r_scr, R)

    @pl.when(i == 0)
    def _():
        for m in range(2):
            sc = jnp.sum(out_ref[m, 0:1, :] * vec_ref[5:6, :], axis=1, keepdims=True)
            sc_snd[m:m + 1, :] = jnp.broadcast_to(sc, (1, 128))
        sc_all[cid] = sc_snd[...]
        for j in range(1, C):
            score_copy(j).start()

    @pl.when(i == T)
    def _():
        for j in range(1, C):
            score_copy(j).wait()
        total = jnp.zeros((1, 128), F32)
        own = sc_snd[...]
        for m in range(2):
            rows = [sc_all[j, m:m + 1, :] for j in range(C)]
            peak = functools.reduce(jnp.maximum, rows)
            lse = peak + jnp.log(functools.reduce(lambda a, b: a + b, [jnp.exp(r - peak) for r in rows]))
            lab = lab_ref[m]
            picked = functools.reduce(lambda a, b: a + b, [jnp.where(lab == j, r, 0.0) for j, r in enumerate(rows)])
            total = total + (lse - picked)
            ds_scr[m:m + 1, :] = (jnp.exp(own[m:m + 1, :] - lse) - jnp.where(lab == cid, 1.0, 0.0)) * (1.0 / Q)
        loss_ref[...] = jnp.broadcast_to(jnp.where(cid == 0, total * (1.0 / Q), 0.0), (8, 128))

    @pl.when((i >= 1) & (i <= T))
    def _():
        t = lax.rem(i, T)
        bwd_tile(jnp.minimum(t, 1), ds_scr, cot_ref, wo_ref, wu_ref, wd_ref, vec_ref, dfs_ref, dctx_ref, gv_ref, gbu_ref, dl_ref, ul_ref, al_ref, gp_scr, z1_scr, z2_scr, r_scr, R)


class VecSum:
    def __init__(s, C, Q, src, va, snd, rcv, qs, qr, rs, rr):
        s.C, s.Q, s.src, s.va, s.snd, s.rcv, s.qs, s.qr, s.rs, s.rr = C, Q, src, va, snd, rcv, qs, qr, rs, rr
        s.c, s.q = lax.axis_index("cand"), lax.axis_index("query")
        s.rounds = C.bit_length() - 1
    def qcopy(s, j):
        to = lax.rem(s.q + j, s.Q)
        return pltpu.make_async_remote_copy(s.src.at[to], s.va.at[s.q], s.qs.at[j - 1], s.qr.at[j - 1], device_id={"query": to}, device_id_type=MESH)
    def rcopy(s, i):
        return pltpu.make_async_remote_copy(s.snd.at[i], s.rcv.at[i], s.rs.at[i], s.rr.at[i], device_id={"cand": jnp.bitwise_xor(s.c, 1 << i)}, device_id_type=MESH)
    def start(s):
        for j in range(1, s.Q):
            s.qcopy(j).start()
        s.va[s.q] = s.src[s.q]
    def take(s, i):
        if i == 0:
            for j in range(1, s.Q):
                s.qcopy(j).wait()
            return functools.reduce(lambda a, b: a + b, [s.va[j] for j in range(s.Q)])
        s.rcopy(i - 1).wait()
        return s.snd[i - 1] + s.rcv[i - 1]
    def step(s, i):
        s.snd[i] = s.take(i)
        s.rcopy(i).start()
    def finish(s, dst):
        dst[...] = s.take(s.rounds)


def back_kernel(len_ref, nl_h, dl_h, al_h, ctx_h, act_h, ul_h, qkv_h, dctx_h, xlow_h, wq_h, dfs_h, lse_ref, relf, bkf_ref, gv_ref, gbu_ref, loss_ref,
                *rest, C, Q, fast):
    if fast:
        ig_h, p_out, u_out, d_out, ve_out, vl_out = rest[:6]
        scr = rest[6:]
    else:
        ig_h, gq_o, go_o, gu_o, gd_o, gb_o, gtab_o = rest[:7]
        scr = rest[7:]
    (nl, dl, al, ctx, ch, qkv, dctx, xlow, wq, dfs, igt, gq, go, gu, gd, drelf, bias_scr, acc_scr, gb, gtab, ls, cs_, os_) = scr[:23]
    NS, D = nl.shape
    FF = gu.shape[1]
    S = NS // 2
    NZ = FF // 768
    load = lambda i, src, dst: pltpu.make_async_copy(src, dst, ls.at[i])
    big = [load(0, nl_h, nl), load(1, dl_h, dl), load(2, al_h, al), load(3, ctx_h, ctx), load(4, qkv_h, qkv), load(5, dctx_h, dctx),
           load(6, xlow_h, xlow), load(7, wq_h, wq), load(8, dfs_h, dfs)]
    if fast:
        g = Geo(C, Q)

    def offs(d, i):
        if not fast: c = i
        elif d: c = jnp.bitwise_xor(g.x, 1 - i // 2) * 2 + jnp.bitwise_xor(g.k, 1 - lax.rem(i, 2))
        else: c = jnp.bitwise_xor(g.z, 3 - i)
        return pl.multiple_of(c * 768, 128)

    def chunk(d, i):
        return pltpu.make_async_copy((act_h if d else ul_h).at[:, pl.ds(offs(d, i), 768)], ch.at[lax.rem(i, 2)], cs_.at[lax.rem(i, 2)])
    if fast:
        peers = [{"query": lax.rem(lax.axis_index("query") + j, Q)} for j in range(1, Q)] + [{"cand": lax.rem(lax.axis_index("cand") + j, C)} for j in range(1, C)]
        bar = pltpu.get_barrier_semaphore()
        for p in peers:
            pl.semaphore_signal(bar, inc=1, device_id=p, device_id_type=MESH)
    for c in (big[2], big[3], big[0], chunk(0, jnp.int32(0)), chunk(0, jnp.int32(1)), big[1]):
        c.start()
    if fast:
        bufs = {n: scr[23 + 4 * i:27 + 4 * i] for i, n in enumerate(RPIECES)}
        h_scr, e_snd, e_rcv, ve, vea, ves, ver, vl, vla, vls, vlr, ss, rs, es, qs, qr, cs, cr = scr[23 + NB:]
        R = RS(g, (gq, go, gu, gd), bufs, ss, rs)
        R.outs = {n: h_scr.at[pl.ds(QROW.get(n, 144), RSHP[n][0])] for n in ("qa", "qb", "qz", "o")}
        R.outs.update(u=u_out, d=d_out)
        dq, fq, bq = D // Q, FF // Q, gtab.shape[1] // Q
        early = VecSum(C, Q, ve, vea, ves, ver, qs.at[0], qr.at[0], cs.at[0], cr.at[0])
        late = VecSum(C, Q, vl, vla, vls, vlr, qs.at[1], qr.at[1], cs.at[1], cr.at[1])
        ve[...] = jnp.zeros_like(ve)
        vl[...] = jnp.zeros_like(vl)
        for q in range(Q):
            ve[q, 0:6, 0:dq] = gv_ref[0:6, q * dq:(q + 1) * dq]
            for j in range(fq // 256):
                ve[q, 6 + j:7 + j, :] = gbu_ref[:, q * fq + j * 256:q * fq + (j + 1) * 256]
            ve[q, 9:10, 0:128] = loss_ref[0:1, :]
        vec_at = {"o": early.start, "u3": functools.partial(early.step, 0), "d1": functools.partial(early.step, 1), "d3": functools.partial(early.step, 2),
                  "v": late.start, "i0": functools.partial(late.step, 0), "i1": functools.partial(late.step, 1), "i2": functools.partial(late.step, 2)}

    def after(name):
        if fast:
            for e in SLOTS.get(name, []):
                R.ev(e)
            if name in vec_at:
                vec_at[name]()
    big[2].wait()
    big[3].wait()
    go[...] = dg(al[...], ctx[...], TN).astype(BF)
    big[0].wait()

    def table(names):
        return {i: [functools.partial(after, n) for n in t] for i, t in enumerate(names)} if fast else {}

    def up(i, _):
        chunk(0, i).wait()
        gu[:, pl.ds(offs(0, i), 768)] = dg(nl[...], ch[lax.rem(i, 2)], TN).astype(BF)
        @pl.when(i < NZ - 2)
        def _(): chunk(0, i + 2).start()
        @pl.when(i >= NZ - 2)
        def _(): chunk(1, i + 2 - NZ).start()
        if fast:
            @pl.when(i == 0)
            def _(): pl.semaphore_wait(bar, len(peers))
        hooks(i, table([("o", "u0"), ("u1",), ("u2",), ("u3",)]))
        return 0
    lax.fori_loop(0, NZ, up, 0)
    big[1].wait()
    big[4].start()
    big[5].start()

    def down(i, _):
        chunk(1, i).wait()
        gd[:, pl.ds(offs(1, i), 768)] = dg(dl[...], ch[lax.rem(i, 2)], TN).astype(BF)
        @pl.when(i < NZ - 2)
        def _(): chunk(1, i + 2).start()
        @pl.when(i == 2)
        def _():
            for c in big[6:]:
                c.start()
        hooks(i, table([("d0",), ("d1",), ("d2",), ("d3",)]))
        return 0
    lax.fori_loop(0, NZ, down, 0)
    slots = {}
    if fast:
        for i in range(2 * (D // 128)):
            slots[i] = [functools.partial(R.ev, e) for e in SLOTS.get(f"t{i}", [])]
    drelf[...] = jnp.zeros_like(drelf)
    big[4].wait()
    big[5].wait()
    attn_bwd(len_ref, qkv, dctx, lse_ref, relf, drelf, bias_scr, acc_scr, S, D, slots)
    big[6].wait()

    half = 3 * D // 2
    zh = g.z // 2 if fast else 0

    def b1(n, _):
        o = pl.multiple_of(jnp.where(n < 3, 1 - zh, zh) * half + lax.rem(n, 3) * 384, 128)
        t = qkv[:, pl.ds(o, 384)]
        gq[pl.ds(o, 384), :] = dg(t, xlow[...], TN).astype(BF)
        gb[:, pl.ds(o, 384)] = jnp.sum(t.astype(F32), axis=0, keepdims=True)
        hooks(n, {i: [functools.partial(R.ev, e) for e in SLOTS.get(f"g{i}", [])] for i in range(6)} if fast else {})
        return 0
    lax.fori_loop(0, 6, b1, 0)
    nb, nn = gtab.shape[1], bkf_ref.shape[1]
    hot = (lax.broadcasted_iota(jnp.int32, (nb, nn), 0) == bkf_ref[...]).astype(F32)
    gtab[...] = dg(drelf[...], hot, NT, lax.Precision.HIGHEST)
    if fast:
        for q in range(Q):
            vl[q, 0:1, 0:dq] = gb[:, q * dq:(q + 1) * dq]
            vl[q, 1:2, 0:dq] = gb[:, 2 * D + q * dq:2 * D + (q + 1) * dq]
            for h in range(HEADS):
                vl[q, 2 + h // 4:3 + h // 4, h % 4 * bq:(h % 4 + 1) * bq] = gtab[h:h + 1, q * bq:(q + 1) * bq]
        after("v")
    big[7].wait()
    big[8].wait()
    steps = NS // 256
    outc = lambda r: pltpu.make_async_copy(igt.at[lax.rem(r, 2)], ig_h.at[pl.ds(pl.multiple_of(r * 256, 256), 256), :], os_.at[lax.rem(r, 2)])

    def rows(r, _):
        o = pl.multiple_of(r * 256, 256)
        @pl.when(r >= 2)
        def _(): outc(r - 2).wait()
        igt[lax.rem(r, 2)] = dfs[pl.ds(o, 256), :] + dg(qkv[pl.ds(o, 256), :], wq[...], NN)
        outc(r).start()
        hooks(r, table([("i0",), ("i1",), ("i2",), ("i3",)]))
        return 0
    lax.fori_loop(0, steps, rows, 0)
    for r in range(max(0, steps - 2), steps):
        outc(jnp.int32(r)).wait()
    if fast:
        k = g.k
        lo = h_scr[:, 0:192]
        hi = h_scr[:, 192:384]
        e_snd[...] = jnp.where(k == 0, hi, lo)
        c = pltpu.make_async_remote_copy(e_snd, e_rcv, es.at[0], es.at[1], device_id=R.partner, device_id_type=MESH)
        c.start()
        p_out[k] = jnp.where(k == 0, lo, hi)
        c.wait()
        p_out[1 - k] = e_rcv[...]
        early.finish(ve_out)
        late.finish(vl_out)
        R.drain()
    else:
        gq_o[...] = gq[...]
        go_o[...] = go[...]
        gu_o[...] = gu[...]
        gd_o[...] = gd[...]
        gb_o[...] = gb[...]
        gtab_o[...] = gtab[...]


def finish_kernel(out_h, ig_h, p_ref, u_ref, d_ref, ve_ref, vl_ref, out_o, ig_o, gq_o, go_o, gu_o, gd_o, *rest):
    vec_o, bup_o, tab_o, loss_o = rest[:8], rest[8], rest[9], rest[10]
    buf, si, so = rest[11:]
    n, rows = buf.shape[0] // 2, buf.shape[1]
    src = [h.at[pl.ds(i * rows, rows), :] for h in (out_h, ig_h) for i in range(n)]
    dst = [h.at[pl.ds(i * rows, rows), :] for h in (out_o, ig_o) for i in range(n)]
    ins = [pltpu.make_async_copy(src[i], buf.at[i], si.at[i]) for i in range(2 * n)]
    outs = [pltpu.make_async_copy(buf.at[i], dst[i], so.at[i]) for i in range(2 * n)]
    for c in ins:
        c.start()
    for a, b in zip(ins, outs):
        a.wait()
        b.start()
    ha = gq_o.shape[1] // 2
    gq_o[...] = jnp.concatenate([p_ref[0, 0:ha, :], p_ref[1, 0:ha, :]], axis=0).T
    go_o[...] = jnp.concatenate([p_ref[0, ha:, :], p_ref[1, ha:, :]], axis=0).T
    gu_o[...] = u_ref[...]
    gd_o[...] = d_ref[...]
    for i in range(8):
        n = vec_o[i].shape[1]
        vec_o[i][...] = vl_ref[i:i + 1, 0:n] if i < 2 else ve_ref[i - 2:i - 1, 0:n]
    for j in range(bup_o.shape[1] // 256):
        bup_o[:, j * 256:(j + 1) * 256] = ve_ref[6 + j:7 + j, :]
    loss_o[0] = ve_ref[9, 0]
    bq = tab_o.shape[1]
    for h in range(HEADS):
        tab_o[h:h + 1, :] = vl_ref[2 + h // 4:3 + h // 4, h % 4 * bq:(h % 4 + 1) * bq]
    for c in outs:
        c.wait()


def sds(shape, dtype=F32):
    return jax.ShapeDtypeStruct(shape, dtype)


def back_scratch(fast, C, Q, NS=1024, S=512, D=768, FF=3072, NBK=256):
    v = pltpu.VMEM
    dma = pltpu.SemaphoreType.DMA
    scr = [v((NS, D), BF)] * 4 + [v((2, NS, 768), BF), v((NS, 3 * D), BF), v((NS, D), BF), v((NS, D), BF), v((3 * D, D), BF), v((NS, D), F32), v((2, 256, D), F32),
                                  v((3 * D, D), BF), v((D, D), BF), v((D, FF), BF), v((D, FF), BF), v((16, 2 * S), F32),
                                  v((2, S, S), F32), v((2, S, S), F32), v((1, 3 * D), F32), v((16, NBK), F32), dma((9,)), dma((2,)), dma((2,))]
    if fast:
        scr += rs_bufs() + [v((192, 384), F32), v((192, 192), F32), v((192, 192), F32), v((Q, 16, 256), F32), v((Q, 16, 256), F32), v((3, 16, 256), F32), v((3, 16, 256), F32),
                v((Q, 8, 256), F32), v((Q, 8, 256), F32), v((3, 8, 256), F32), v((3, 8, 256), F32),
                            dma((len(RPIECES), 31)), dma((len(RPIECES), 31)), dma((2,)), dma((2, Q)), dma((2, Q)), dma((2, 3)), dma((2, 3))]
    return scr


def body(hidden_in, out_cotangent, lengths, labels, buckets, w_qkv, w_out, w_up, w_down, bias_q, bias_v, bias_out,
         norm1_gain, norm1_bias, bias_up, bias_down, norm2_gain, score_vector, rel_table):
    Q = lax.axis_size("query")
    C = lax.axis_size("cand")
    micro = hidden_in.shape[0]
    S, D = hidden_in.shape[3:]
    FF = w_up.shape[1] * C
    NBK = rel_table.shape[0] * Q
    dq, fq, bq = D // Q, FF // Q, NBK // Q
    fast = Q == 4 and C == 8 and D == 768 and FF == 3072
    x = hidden_in.reshape(micro, S, D)
    cot = out_cotangent.reshape(micro, S, D)
    lens = lengths.reshape(micro)
    labs = labels.reshape(micro)
    NS = micro * S
    v = pltpu.VMEM
    dma = pltpu.SemaphoreType.DMA
    eight = [bias_q, bias_v, bias_out, norm1_gain, norm1_bias, bias_down, norm2_gain, score_vector]
    if fast:
        np_ = len(RPIECES)
        wq, wo, wu, wd, vec, bup, xlow, qkv, ctx, lse, relf, bkf = pl.pallas_call(
            functools.partial(front_kernel, C=C, Q=Q), in_specs=[SM] + [ANY] * 5 + [VM] * 11, out_specs=[ANY] * 4 + [VM] * 2 + [ANY] * 2 + [VM] * 4,
            out_shape=[sds((3 * D, D), BF), sds((D, D), BF), sds((D, FF), BF), sds((D, FF), BF), sds((8, D)), sds((1, FF)), sds((NS, D), BF), sds((NS, 3 * D), BF),
                       sds((NS, D), BF), sds((micro, 16, S)), sds((16, 2 * S)), sds((1, 2 * S), jnp.int32)],
            scratch_shapes=[v(w_qkv.shape, F32), v(w_out.shape, F32), v(w_up.shape, F32), v(w_down.shape[::-1], F32), v((32, 256), F32), v((1, 2 * S), jnp.int32),
                            v((micro, S, D), F32), v((NS, D), BF), v((NS, 3 * D), BF), v((3 * D, D), BF), v((2, 192, 192), BF), v((192, 192), BF), v((192, 384), BF),
                            v((192, 384), BF), v((96, 768), BF), v((Q, 32, 256), F32), v((16, NBK), F32), v((16, 2 * S), F32), v((1, 3 * D), F32), v((2, S, S), F32)]
            + [dma((np_, 16))] * 4 + [dma((Q,))] * 2 + [dma((2,)), dma((14,))],
            compiler_params=pltpu.CompilerParams(collective_id=0, has_side_effects=True, vmem_limit_bytes=67043328),
        )(lens, x, w_qkv, w_out, w_up, w_down.T, *[t.reshape(1, -1) for t in eight], bias_up.reshape(1, -1), rel_table.T, buckets.reshape(1, -1))
    else:
        bk = jnp.pad(buckets, (0, 1), constant_values=-1)[None, :]
        bkf = jnp.pad(buckets[::-1], (0, 1), constant_values=-1)[None, :]
        def gather(w):
            part = lax.all_gather(w.astype(BF), "query", axis=0, tiled=True)
            return lax.all_gather(part, "cand", axis=1, tiled=True)
        wq, wo, wu, wd = gather(w_qkv).T, gather(w_out).T, gather(w_up), gather(w_down).T
        vall = lax.all_gather(jnp.concatenate(eight + [bias_up, rel_table.reshape(-1)]), "query", axis=0, tiled=False)
        vecs = vall[:, :8 * dq].reshape(Q, 8, dq).transpose(1, 0, 2).reshape(8, D)
        bup = vall[:, 8 * dq:8 * dq + fq].reshape(1, FF)
        tab = jnp.pad(vall[:, 8 * dq + fq:].reshape(NBK, HEADS).T, ((0, 4), (0, 0)))
        qkv_bias = jnp.concatenate([vecs[0:1], jnp.zeros((1, D), F32), vecs[1:2]], axis=1)
        vec = jnp.concatenate([vecs[2:], jnp.zeros((2, D), F32)], axis=0)
        xlow, qkv, ctx, lse, relf = pl.pallas_call(
            attn_fwd_kernel, in_specs=[SM] + [VM] * 6, out_specs=[VM] * 5,
            out_shape=[sds((NS, D), BF), sds((NS, 3 * D), BF), sds((NS, D), BF), sds((micro, 16, S)), sds((16, 2 * S))],
            scratch_shapes=[v((16, 2 * S), F32), v((2, S, S), F32)],
            compiler_params=pltpu.CompilerParams(vmem_limit_bytes=60 * 2**20))(lens, x, wq, qkv_bias, tab, bk, bkf)
    R = 256
    Rh, T = R // micro, NS // R
    tb = lambda im, n=D: pl.BlockSpec((micro, Rh, n), im)
    fw = lambda i: (0, jnp.minimum(i, T - 1), 0)
    bw = lambda i: (0, lax.rem(jnp.maximum(i, 1), T), 0)
    tok = lambda n, dt=BF: sds((micro, S, n), dt)
    out, dfs, dctx, nl, act, dl, al, ul, gv, gbu, lossv = pl.pallas_call(
        functools.partial(ffn_kernel, T=T, R=R, C=C, Q=Q), grid=(T + 1,),
        in_specs=[SM, tb(fw), tb(fw), tb(bw)] + [VM] * 5, out_specs=[tb(fw), tb(bw), tb(bw), tb(fw), tb(fw, FF), tb(bw), tb(bw), tb(bw, FF)] + [VM] * 3,
        out_shape=[tok(D, F32), tok(D, F32), tok(D), tok(D), tok(FF), tok(D), tok(D), tok(FF), sds((8, D)), sds((1, FF)), sds((8, 128))],
        scratch_shapes=[pltpu.VMEM((2, R, FF), F32), pltpu.VMEM((2, R, D), F32), pltpu.VMEM((2, R, D), F32), pltpu.VMEM((2, R, 128), F32),
                        pltpu.VMEM((8, 128), F32), pltpu.VMEM((8, 128), F32), pltpu.VMEM((C, 8, 128), F32), pltpu.SemaphoreType.DMA((C,)), pltpu.SemaphoreType.DMA((C,))],
        compiler_params=pltpu.CompilerParams(collective_id=1, has_side_effects=True, vmem_limit_bytes=67043328),
    )(labs, x, ctx.reshape(micro, S, D), cot, wo, wu, wd, vec, bup)
    flat = lambda t: t.reshape(NS, t.shape[-1])
    gouts = [sds((2, 192, 192)), sds((192, 384)), sds((96, 768)), sds((16, 256)), sds((8, 256))] if fast else \
        [sds((3 * D, D), BF), sds((D, D), BF), sds((D, FF), BF), sds((D, FF), BF), sds((1, 3 * D)), sds((16, NBK))]
    res = pl.pallas_call(
        functools.partial(back_kernel, C=C, Q=Q, fast=fast), in_specs=[SM] + [ANY] * 11 + [VM] * 6, out_specs=[ANY] + [VM] * len(gouts),
        out_shape=[sds((NS, D))] + gouts, scratch_shapes=back_scratch(fast, C, Q, NS, S, D, FF, NBK),
        compiler_params=pltpu.CompilerParams(collective_id=2 if fast else None, has_side_effects=True, vmem_limit_bytes=67043328),
    )(lens, flat(nl), flat(dl), flat(al), ctx, flat(act), flat(ul), qkv, flat(dctx), xlow, wq, flat(dfs), lse, relf, bkf, gv, gbu, lossv)
    ig = res[0]
    if fast:
        fin = pl.pallas_call(
            finish_kernel, in_specs=[ANY] * 2 + [VM] * 5, out_specs=[ANY] * 2 + [VM] * 14 + [SM],
            out_shape=[sds((NS, D)), sds((NS, D)), sds(w_qkv.shape), sds(w_out.shape), sds(w_up.shape), sds(w_down.shape[::-1])] + [sds((1, dq))] * 8
            + [sds((1, fq)), sds((HEADS, bq)), sds((1,))],
            scratch_shapes=[v((8, NS // 4, D), F32), dma((8,)), dma((8,))],
            compiler_params=pltpu.CompilerParams(vmem_limit_bytes=67043328))(flat(out), ig, *res[1:])
        out, ig, g_qkv, g_out, g_up = fin[:5]
        g_down = fin[5].T
        small = [t.reshape(dq) for t in fin[6:14]]
        g_bup, g_tab, loss = fin[14].reshape(fq), fin[15].T, fin[16].reshape(())
    else:
        def scatter(g):
            rows, cols = g.shape[0] // Q, g.shape[1] // C
            tiles = g.astype(F32).reshape(Q, rows, C, cols).transpose(2, 0, 1, 3).reshape(C * Q, rows, cols)
            return lax.psum_scatter(tiles, ("cand", "query"), scatter_dimension=0, tiled=True)[0]
        gq, go, gu, gd, gb, gtab = res[1:]
        g_qkv, g_out, g_up, g_down = scatter(gq.T), scatter(go.T), scatter(gu), scatter(gd.T)
        gvecs = jnp.concatenate([gb[:, :D], gb[:, 2 * D:], gv[:6]], axis=0)
        vg = jnp.concatenate([gvecs.reshape(8, Q, dq).transpose(1, 0, 2).reshape(Q, 8 * dq), gbu.reshape(Q, fq), gtab[:HEADS].T.reshape(Q, bq * HEADS),
                              jnp.broadcast_to(lossv[0:1, 0:1], (Q, 1))], axis=1)
        vg = jnp.pad(vg, ((0, 0), (0, -vg.shape[1] % 1024)))
        vs = lax.psum_scatter(lax.psum(vg, "cand"), "query", scatter_dimension=0, tiled=True)[0]
        small = [vs[i * dq:(i + 1) * dq] for i in range(8)]
        g_bup = vs[8 * dq:8 * dq + fq]
        g_tab = vs[8 * dq + fq:8 * dq + fq + bq * HEADS].reshape(bq, HEADS)
        loss = vs[8 * dq + fq + bq * HEADS]
    return (out.reshape(hidden_in.shape), ig.reshape(hidden_in.shape), g_qkv, g_out, g_up, g_down,
            small[0], small[1], small[2], small[3], small[4], g_bup, small[5], small[6], small[7], g_tab, loss)


def solution(mesh):
    seq, w, v = P(None, "query", "cand", None, None), P("query", "cand"), P("query")
    return jax.shard_map(
        body, mesh=mesh,
        in_specs=(seq, seq, P(None, "query", "cand"), P(None, "query"), P(), w, w, w, w) + (v,) * 9 + (P("query", None),),
        out_specs=(seq, seq, w, w, w, w) + (v,) * 9 + (P("query", None), P()),
        check_vma=False)
```

```python
import functools

import jax
import jax.numpy as jnp
from jax import lax
from jax.experimental import pallas as pl
from jax.experimental.pallas import tpu as pltpu
from jax.sharding import PartitionSpec as P

F32 = jnp.float32
BF = jnp.bfloat16
NT = (((1,), (1,)), ((), ()))
NN = (((1,), (0,)), ((), ()))
TN = (((0,), (0,)), ((), ()))
VM = pl.BlockSpec(memory_space=pltpu.VMEM)
SM = pl.BlockSpec(memory_space=pltpu.SMEM)
ANY = pl.BlockSpec(memory_space=pl.ANY)
MESH = pl.DeviceIdType.MESH
EPS = 1e-5
FC = 1536
HEADS = 12
NR = {"x": 2, "y": 2, "z": 4}
RPIECES = ["u", "d", "o", "qa", "qb", "qz"]
RORD = {"u": "yxz", "d": "xyz", "o": "zyx", "qa": "yxz", "qb": "xyz", "qz": "zyx"}
RSHP = {"u": (192, 384, 48), "d": (96, 768, 48), "o": (48, 384, 48), "qa": (64, 384, 32), "qb": (64, 384, 32), "qz": (16, 384, 16)}
QROW = {"qa": 0, "qb": 64, "qz": 128}
NB = 4 * len(RPIECES)
AGSLOTS = {
    "b": [("d", (0, 0, 0), (("x", 1), ("y", 1)))],
    "h": [("qa", (0, 0, 0), (("z", 2),)), ("qb", (0, 0, 0), (("x", 1),)), ("qz", (0, 0, 0), (("x", 1), ("z", 1), ("y", 1))), ("o", (0, 0, 0), (("x", 1),)), ("u", (0, 0, 0), (("k", 0),)), ("o", (0, 0, 0), (("y", 1),)), ("qa", (0, 0, 0), (("z", 1), ("z", 3), ("x", 1))), ("qb", (0, 0, 0), (("y", 1),)), ("u", (0, 0, 0), (("y", 1),)), ("qz", (0, 0, 0), (("z", 2),)), ("qb", (0, 1, 0), (("x", 1), ("k", 0))), ("qb", (0, 0, 0), (("z", 2),)), ("qa", (0, 0, 1), (("x", 1), ("y", 1), ("k", 0))), ("qz", (0, 1, 0), (("z", 1), ("z", 2), ("z", 3), ("k", 0))), ("d", (1, 0, 0), (("k", 0),)), ("u", (0, 0, 0), (("x", 1),)), ("qz", (0, 0, 1), (("y", 1), ("z", 1), ("z", 2), ("z", 3), ("k", 0))), ("qb", (0, 0, 0), (("z", 1),)), ("qa", (0, 0, 2), (("x", 1), ("y", 1), ("k", 0))), ("qb", (0, 0, 2), (("y", 1), ("x", 1), ("k", 0))), ("qa", (0, 1, 0), (("y", 1), ("k", 0))), ("qa", (0, 0, 0), (("k", 0),)), ("qb", (1, 0, 0), (("k", 0),)), ("qb", (0, 0, 0), (("z", 3),)), ("qb", (0, 0, 1), (("y", 1), ("x", 1), ("k", 0))), ("qz", (0, 0, 0), (("z", 3),)), ("qz", (0, 1, 1), (("z", 1), ("z", 2), ("z", 3), ("k", 0))), ("qz", (3, 1, 0), (("k", 0),)), ("qz", (0, 0, 0), (("k", 0),)), ("qa", (1, 0, 1), (("k", 0),)), ("qa", (0, 1, 1), (("y", 1), ("k", 0))), ("u", (0, 0, 0), (("z", 1),)), ("qz", (2, 0, 1), (("k", 0),)), ("d", (0, 0, 0), (("z", 3),)), ("qa", (0, 0, 3), (("x", 1), ("y", 1), ("k", 0))), ("qb", (0, 0, 3), (("y", 1), ("x", 1), ("k", 0))), ("qb", (0, 1, 1), (("x", 1), ("k", 0))), ("qb", (1, 1, 0), (("k", 0),)), ("qz", (3, 0, 0), (("k", 0),)), ("o", (0, 0, 0), (("k", 0),)), ("qz", (1, 1, 1), (("k", 0),)), ("qa", (1, 0, 2), (("k", 0),)), ("qa", (0, 1, 2), (("y", 1), ("k", 0))), ("qa", (1, 1, 1), (("k", 0),)), ("qa", (0, 1, 3), (("y", 1), ("k", 0)))],
    "p0": [("qa", (0, 0, 0), (("y", 1),)), ("qb", (0, 0, 0), (("k", 0),)), ("qb", (1, 0, 3), (("k", 0),)), ("qa", (1, 0, 3), (("k", 0),)), ("qb", (0, 1, 2), (("x", 1), ("k", 0))), ("qb", (0, 1, 3), (("x", 1), ("k", 0))), ("qa", (1, 1, 2), (("k", 0),)), ("qz", (2, 1, 1), (("k", 0),)), ("qz", (2, 1, 0), (("k", 0),)), ("qb", (1, 0, 1), (("k", 0),))],
    "p1": [("qa", (1, 1, 3), (("k", 0),)), ("u", (0, 0, 0), (("z", 2),)), ("d", (0, 0, 0), (("z", 1),)), ("qz", (2, 0, 0), (("k", 0),)), ("u", (0, 0, 1), (("x", 1), ("y", 1), ("k", 0))), ("qz", (3, 1, 1), (("k", 0),)), ("qb", (1, 0, 2), (("k", 0),)), ("qb", (1, 1, 1), (("k", 0),)), ("qz", (1, 0, 0), (("k", 0),)), ("qb", (1, 1, 2), (("k", 0),)), ("qa", (1, 0, 0), (("k", 0),)), ("qz", (1, 0, 1), (("k", 0),)), ("u", (0, 0, 0), (("z", 3),)), ("qb", (1, 1, 3), (("k", 0),)), ("o", (0, 0, 0), (("z", 1),)), ("qz", (1, 1, 0), (("k", 0),)), ("d", (0, 0, 0), (("z", 2),)), ("qz", (3, 0, 1), (("k", 0),)), ("qa", (1, 1, 0), (("k", 0),)), ("d", (0, 0, 3), (("y", 1), ("x", 1), ("k", 0)))],
    "n0": [("u", (0, 1, 1), (("y", 1), ("k", 0)))],
    "n1": [("d", (0, 1, 0), (("x", 1), ("k", 0)))],
    "n2": [("o", (0, 0, 1), (("y", 1), ("z", 1), ("z", 2), ("z", 3), ("k", 0)))],
    "n5": [("u", (0, 0, 2), (("x", 1), ("y", 1), ("k", 0))), ("d", (0, 1, 3), (("x", 1), ("k", 0)))],
    "n7": [("d", (0, 0, 1), (("y", 1), ("x", 1), ("k", 0))), ("u", (0, 1, 0), (("y", 1), ("k", 0)))],
    "n8": [("u", (1, 0, 1), (("k", 0),))],
    "r1": [("d", (1, 1, 0), (("k", 0),))],
    "t0": [("u", (0, 0, 3), (("x", 1), ("y", 1), ("k", 0)))],
    "t1": [("o", (1, 0, 0), (("k", 0),)), ("o", (0, 1, 0), (("z", 1), ("z", 2), ("z", 3), ("k", 0))), ("u", (1, 1, 1), (("k", 0),)), ("o", (0, 1, 1), (("z", 1), ("z", 2), ("z", 3), ("k", 0)))],
    "t3": [("d", (0, 0, 2), (("y", 1), ("x", 1), ("k", 0)))],
    "t4": [("o", (0, 0, 0), (("z", 3),)), ("d", (0, 0, 0), (("k", 0),)), ("d", (1, 0, 3), (("k", 0),)), ("u", (1, 1, 0), (("k", 0),)), ("d", (1, 0, 1), (("k", 0),)), ("u", (1, 0, 2), (("k", 0),)), ("u", (0, 1, 2), (("y", 1), ("k", 0)))],
    "t5": [("u", (1, 0, 0), (("k", 0),)), ("d", (0, 1, 1), (("x", 1), ("k", 0)))],
    "t6": [("u", (1, 0, 3), (("k", 0),)), ("o", (0, 0, 0), (("z", 2),)), ("d", (0, 1, 2), (("x", 1), ("k", 0))), ("d", (1, 0, 2), (("k", 0),))],
    "t7": [("u", (0, 1, 3), (("y", 1), ("k", 0))), ("o", (3, 0, 1), (("k", 0),))],
    "t8": [("o", (2, 0, 1), (("k", 0),)), ("d", (1, 1, 3), (("k", 0),)), ("u", (1, 1, 2), (("k", 0),))],
    "t9": [("d", (1, 1, 1), (("k", 0),)), ("o", (1, 1, 1), (("k", 0),)), ("o", (1, 1, 0), (("k", 0),)), ("o", (3, 1, 0), (("k", 0),)), ("o", (2, 1, 1), (("k", 0),))],
    "t10": [("o", (2, 1, 0), (("k", 0),)), ("o", (1, 0, 1), (("k", 0),)), ("o", (3, 1, 1), (("k", 0),)), ("d", (1, 1, 2), (("k", 0),)), ("u", (1, 1, 3), (("k", 0),)), ("o", (3, 0, 0), (("k", 0),)), ("o", (2, 0, 0), (("k", 0),))],
}
SLOTS = {
    "u1": [("s0", "u", 1, 1, 2), ("s0", "u", 0, 0, 3), ("s0", "u", 1, 0, 3), ("s0", "o", 2, 0, 0), ("s0", "u", 1, 1, 3), ("s0", "o", 2, 0, 1)],
    "u3": [("s0", "u", 1, 0, 2), ("s0", "u", 1, 1, 1), ("s0", "o", 3, 1, 0), ("s1", "u", 1, 1, 3), ("s0", "o", 2, 1, 0), ("s1", "o", 2, 0, 1), ("s0", "u", 0, 0, 1), ("s0", "u", 0, 1, 3), ("s0", "o", 2, 1, 1), ("s0", "o", 3, 0, 0)],
    "d0": [("s0", "u", 0, 1, 2)],
    "d1": [("s0", "u", 1, 0, 1), ("s1", "u", 1, 0, 3), ("s1", "u", 1, 1, 2), ("s0", "d", 1, 0, 2)],
    "d2": [("s1", "o", 2, 1, 1), ("s0", "o", 3, 1, 1), ("s1", "o", 3, 1, 0), ("s0", "o", 1, 0, 1), ("s1", "u", 1, 0, 2), ("s0", "d", 1, 1, 2), ("s0", "o", 1, 1, 0), ("s0", "d", 1, 1, 0), ("s0", "d", 1, 0, 0), ("s0", "u", 0, 1, 1), ("s2", "u", 1, 3)],
    "d3": [("s1", "d", 1, 1, 2), ("s0", "d", 0, 1, 1), ("s0", "d", 1, 1, 1), ("s0", "o", 1, 0, 0), ("s0", "o", 1, 1, 1), ("s0", "o", 3, 0, 1)],
    "t0": [("s1", "d", 1, 1, 1), ("s1", "d", 1, 1, 0), ("s1", "o", 2, 1, 0)],
    "t1": [("s2", "u", 1, 2), ("s1", "o", 3, 0, 1), ("s3", "u", 3), ("s0", "d", 0, 0, 2), ("s0", "d", 0, 1, 2)],
    "t2": [("s1", "u", 1, 0, 1), ("s0", "d", 1, 1, 3), ("s1", "o", 3, 0, 0), ("s1", "d", 1, 0, 2), ("s1", "o", 1, 1, 1), ("s1", "u", 1, 1, 1), ("s0", "d", 1, 0, 1), ("s0", "u", 0, 1, 0), ("s1", "o", 3, 1, 1), ("s0", "d", 0, 1, 3)],
    "t3": [("s2", "d", 1, 2)],
    "t4": [("s0", "u", 0, 0, 2), ("s1", "o", 1, 0, 0), ("s0", "u", 1, 0, 0), ("s1", "d", 1, 1, 3)],
    "t5": [("s0", "d", 0, 0, 1), ("s1", "d", 1, 0, 1), ("s0", "d", 0, 1, 0), ("s0", "d", 0, 0, 0), ("s1", "o", 2, 0, 0)],
    "t6": [("s3", "u", 2), ("s2", "d", 1, 1), ("s0", "o", 0, 1, 1)],
    "t7": [("s0", "d", 1, 0, 3)],
    "t8": [("s1", "o", 1, 1, 0), ("s0", "u", 1, 1, 0), ("s2", "u", 1, 1), ("s1", "u", 1, 0, 0)],
    "t9": [("s3", "d", 2), ("s1", "u", 1, 1, 0)],
    "t11": [("s1", "d", 1, 0, 3)],
    "g0": [("s3", "u", 1), ("s1", "o", 1, 0, 1), ("s2", "d", 1, 3)],
    "g2": [("s1", "d", 1, 0, 0), ("s0", "qz", 2, 0, 0), ("s0", "qa", 1, 1, 2), ("s0", "qb", 1, 1, 3), ("s0", "qz", 3, 1, 1), ("s0", "qz", 3, 1, 0), ("s0", "qz", 2, 1, 0)],
    "g3": [("s0", "qb", 1, 1, 2), ("s0", "o", 0, 1, 0), ("s0", "d", 0, 0, 3)],
    "g4": [("s1", "qz", 3, 1, 0), ("s2", "o", 1, 1), ("s0", "qb", 1, 0, 2), ("s1", "qz", 3, 1, 1), ("s0", "qa", 1, 1, 3), ("s0", "qb", 0, 1, 2), ("s0", "qz", 3, 0, 0), ("s1", "qz", 2, 0, 0)],
    "g5": [("s0", "qz", 2, 1, 1), ("s0", "qz", 1, 1, 1), ("s1", "qz", 2, 1, 0), ("s0", "qa", 1, 1, 0), ("s1", "qa", 1, 1, 2), ("s0", "qz", 3, 0, 1), ("s0", "qa", 1, 0, 2), ("s0", "o", 0, 0, 0), ("s0", "qb", 1, 0, 3), ("s0", "qb", 1, 0, 1), ("s3", "d", 1), ("s0", "qz", 0, 1, 1), ("s0", "qa", 0, 0, 3), ("s0", "qb", 0, 0, 1), ("s0", "qb", 0, 1, 3), ("s0", "qa", 1, 1, 1), ("s0", "qb", 0, 1, 0), ("s0", "qa", 0, 0, 2), ("s1", "qa", 1, 1, 3), ("s0", "qb", 1, 1, 1), ("s0", "qz", 1, 1, 0), ("s0", "qa", 0, 1, 2), ("s1", "qz", 3, 0, 0), ("s0", "qb", 0, 0, 0), ("s1", "qb", 1, 1, 2), ("s0", "qa", 1, 0, 1), ("s3", "d", 3), ("s1", "qb", 1, 1, 3)],
    "i0": [("s1", "qz", 1, 1, 0), ("s0", "qa", 1, 0, 3), ("s0", "qa", 0, 0, 1), ("s1", "qb", 1, 1, 1), ("s0", "qb", 0, 0, 2), ("s1", "qa", 1, 1, 0), ("s1", "qb", 1, 0, 2), ("s1", "qz", 1, 1, 1), ("s1", "qa", 1, 1, 1), ("s0", "qa", 0, 1, 3), ("s0", "qz", 0, 1, 0), ("s0", "o", 0, 0, 1), ("s0", "qb", 1, 1, 0), ("s1", "qa", 1, 0, 2), ("s0", "qb", 1, 0, 0), ("s0", "qa", 1, 0, 0), ("s2", "qa", 1, 2), ("s1", "qb", 1, 0, 3), ("s0", "qz", 0, 0, 1), ("s0", "qz", 2, 0, 1), ("s1", "qz", 2, 1, 1), ("s2", "qb", 1, 2), ("s0", "qa", 0, 1, 1)],
    "v": [("s1", "qa", 1, 0, 3), ("s1", "qa", 1, 0, 1), ("s0", "qz", 1, 0, 1), ("s1", "qb", 1, 0, 1), ("s0", "qz", 1, 0, 0), ("s0", "qz", 0, 0, 0), ("s0", "qa", 0, 1, 0), ("s1", "qz", 3, 0, 1), ("s2", "qa", 1, 3), ("s2", "qb", 1, 3), ("s0", "qb", 0, 1, 1), ("s1", "qz", 2, 0, 1)],
    "i1": [("s2", "qa", 1, 1), ("s2", "qb", 1, 1), ("s3", "qa", 2), ("s1", "qb", 1, 1, 0), ("s2", "u", 1, 0), ("s2", "d", 1, 0), ("s0", "u", 0, 0, 0), ("s2", "qz", 1, 1), ("s0", "qb", 0, 0, 3)],
    "i2": [("s2", "qa", 1, 0), ("s2", "o", 1, 0), ("s3", "qa", 3), ("s3", "qb", 3), ("s2", "qz", 1, 0), ("s2", "qb", 1, 0), ("s1", "qa", 1, 0, 0), ("s3", "o", 1), ("s3", "qa", 1), ("s1", "qz", 1, 0, 1), ("s0", "qa", 0, 0, 0), ("s3", "qb", 2), ("s1", "qb", 1, 0, 0), ("s3", "qb", 1), ("s1", "qz", 1, 0, 0), ("fin_", "u"), ("s3", "qz", 1), ("fin_", "d")],
    "i3": [("fin_", "o"), ("fin_", "qa"), ("fin_", "qz"), ("fin_", "qb")],
}


def dg(a,b,d,prec=None): return lax.dot_general(a,b,d,preferred_element_type=F32,precision=prec)


def hooks(i, table):
    for j, evs in table.items():
        if evs:
            @pl.when(i == j)
            def _(evs=evs):
                for e in evs: e()


def qkv_proj(w_ref, bias_ref, xlow_ref, qkv_ref, slots):
    def body(n,_):
        o=pl.multiple_of(n*256,256)
        y=dg(xlow_ref[...], w_ref[pl.ds(o,256),:], NT)
        y=(y+bias_ref[:,pl.ds(o,256)])*jnp.where(o<xlow_ref.shape[1],0.125,1.0)
        qkv_ref[:,pl.ds(o,256)]=y.astype(BF)
        hooks(n, slots)
        return 0
    lax.fori_loop(0, w_ref.shape[0]//256, body, 0)


def rel_rows(tableT_ref, bk_ref, rel_ref):
    nb=tableT_ref.shape[1]; n=bk_ref.shape[1]
    hot=(lax.broadcasted_iota(jnp.int32,(nb,n),0)==bk_ref[...]).astype(F32)
    rel_ref[...]=dg(tableT_ref[...], hot, NN, lax.Precision.HIGHEST)


def bias_expand(row,S):
    R=pltpu.roll(jnp.broadcast_to(row,(128,2*S)), 2*S-127, 1, stride=1, stride_axis=0)
    nu=S//128
    return jnp.concatenate([R[:,128*(nu-1-u):128*(nu-1-u)+S] for u in range(nu)],axis=0)


def diag_sum(t,S):
    nu=S//128
    y=None
    for u in range(nu):
        a=128*(nu-1-u); parts=[]
        if a: parts.append(jnp.zeros((128,a),F32))
        parts.append(t[128*u:128*(u+1),:])
        if 2*S-a-S: parts.append(jnp.zeros((128,2*S-a-S),F32))
        v=jnp.concatenate(parts,axis=1) if len(parts)>1 else parts[0]
        y=v if y is None else y+v
    z=None
    for w in range(16):
        g=y[8*w:8*w+8,:]
        sh=120-8*w
        g=pltpu.roll(g,sh,1) if sh else g
        z=g if z is None else z+g
    out=None
    for b in range(8):
        g=z[b:b+1,:]
        g=pltpu.roll(g,7-b,1) if b<7 else g
        out=g if out is None else out+g
    return out


def attn_fwd(len_ref, qkv_ref, rel_ref, ctx_ref, lse_ref, bias_scr, S, D, slots):
    lane=lax.broadcasted_iota(jnp.int32,(1,128),1)
    col=lax.broadcasted_iota(jnp.int32,(1,S),1)
    def body(p,_):
        o=pl.multiple_of(p*128,128)
        for hh in range(2):
            row=rel_ref[pl.ds(p*2+hh,1),:]
            bias_scr[hh]=bias_expand(row,S)
        for m in range(2):
            q=qkv_ref[m*S:(m+1)*S,pl.ds(o,128)]
            k=qkv_ref[m*S:(m+1)*S,pl.ds(D+o,128)]
            v=qkv_ref[m*S:(m+1)*S,pl.ds(2*D+o,128)]
            valid=col<len_ref[m]
            outs=[]
            for hh in range(2):
                mk=(lane//64)==hh
                qm=jnp.where(mk,q,jnp.zeros_like(q))
                s=dg(qm,k,NT)+bias_scr[hh]
                s=jnp.where(valid,s,-1e30)
                mx=jnp.max(s,axis=1,keepdims=True)
                e=jnp.exp(s-mx)
                tot=jnp.sum(e,axis=1,keepdims=True)
                pl_=(e*(1.0/tot)).astype(BF)
                outs.append(dg(pl_,v,NN))
                lse_ref[m,pl.ds(p*2+hh,1),:]=jnp.transpose(mx+jnp.log(tot),(1,0))
            ctx_ref[m*S:(m+1)*S,pl.ds(o,128)]=jnp.where((lane//64)==0,outs[0],outs[1]).astype(BF)
            hooks(p, {i: slots.get(2*i+m) for i in range(D//128)})
        return 0
    lax.fori_loop(0, D//128, body, 0)


def attn_bwd(len_ref, qkv_ref, dctx_ref, lse_ref, relf_ref, drelf_ref, bias_scr, acc_scr, S, D, slots):
    lane=lax.broadcasted_iota(jnp.int32,(1,128),1)
    rowi=lax.broadcasted_iota(jnp.int32,(S,1),0)
    m0=(lane//64)==0
    def body(p,_):
        o=pl.multiple_of(p*128,128)
        for hh in range(2):
            row=relf_ref[pl.ds(p*2+hh,1),:]
            bias_scr[hh]=bias_expand(row,S)
        for m in range(2):
            q=qkv_ref[m*S:(m+1)*S,pl.ds(o,128)]
            k=qkv_ref[m*S:(m+1)*S,pl.ds(D+o,128)]
            v=qkv_ref[m*S:(m+1)*S,pl.ds(2*D+o,128)]
            do=dctx_ref[m*S:(m+1)*S,pl.ds(o,128)]
            valid=rowi<len_ref[m]
            oq=[];ok=[];ov=[]
            for hh in range(2):
                mk=(lane//64)==hh
                km=jnp.where(mk,k,jnp.zeros_like(k)); vm=jnp.where(mk,v,jnp.zeros_like(v))
                sT=dg(km,q,NT)+bias_scr[hh]
                sT=jnp.where(valid,sT,-1e30)
                pT=jnp.exp(sT-lse_ref[m,pl.ds(p*2+hh,1),:])
                dpT=dg(vm,do,NT)
                rd=jnp.sum(dpT*pT,axis=0,keepdims=True)
                ds=(pT*(dpT-rd)).astype(BF)
                ov.append(dg(pT.astype(BF),do,NN))
                ok.append(dg(ds,q,NN))
                oq.append(dg(ds,k,TN))
                if m==0: acc_scr[hh]=ds.astype(F32)
                else: acc_scr[hh]+=ds.astype(F32)
            qkv_ref[m*S:(m+1)*S,pl.ds(o,128)]=(jnp.where(m0,oq[0],oq[1])*0.125).astype(BF)
            qkv_ref[m*S:(m+1)*S,pl.ds(D+o,128)]=jnp.where(m0,ok[0],ok[1]).astype(BF)
            qkv_ref[m*S:(m+1)*S,pl.ds(2*D+o,128)]=jnp.where(m0,ov[0],ov[1]).astype(BF)
            hooks(p, {i: slots.get(2*i+m) for i in range(D//128)})
        for hh in range(2):
            drelf_ref[pl.ds(p*2+hh,1),:]=diag_sum(acc_scr[hh],S)
        return 0
    lax.fori_loop(0, D//128, body, 0)


def stats(z):
    mu=jnp.mean(z,axis=-1,keepdims=True); c=z-mu
    var=jnp.mean(c*c,axis=-1,keepdims=True)
    r=lax.rsqrt(var+EPS)
    return c*r, r


def fwd_tile(arrive, slot, x_ref, ctx_ref, wo_ref, wu_ref, wd_ref, vec_ref, bup_ref, out_ref, nl_scr, act_scr, gp_scr, z1_scr, z2_scr, r_scr, R):
    D=x_ref.shape[2]; FF=wu_ref.shape[1]
    ctx=ctx_ref[...].reshape(R,D)
    arrive(0)
    fs=x_ref[...].reshape(R,D)+(dg(ctx,wo_ref[...],NT)+vec_ref[0:1,:])
    z1,r1=stats(fs)
    z1_scr[slot]=z1
    fn=z1*vec_ref[1:2,:]+vec_ref[2:3,:]
    nl=fn.astype(BF)
    nl_scr[...]=nl.reshape(nl_scr.shape)
    def body(f,acc):
        o=pl.multiple_of(f*FC,FC)
        u=dg(nl_scr[...].reshape(R,D),wu_ref[:,pl.ds(o,FC)],NN)+bup_ref[:,pl.ds(o,FC)]
        phi=0.5*(1.0+lax.erf(u*(2.0**-0.5)))
        a=(u*phi).astype(BF)
        act_scr[:,:,pl.ds(o,FC)]=a.reshape(2,R//2,FC)
        gp_scr[slot,:,pl.ds(o,FC)]=phi+u*(jnp.exp(u*u*-0.5)*0.3989422804014327)
        return acc+dg(a,wd_ref[:,pl.ds(o,FC)],NT)
    arrive(1)
    arrive(2)
    acc=lax.fori_loop(0,FF//FC,body,fn+vec_ref[3:4,:],unroll=True)
    z2,r2=stats(acc)
    z2_scr[slot]=z2
    r_scr[slot,:,0:1]=r1
    r_scr[slot,:,1:2]=r2
    out_ref[...]=(z2*vec_ref[4:5,:]).reshape(out_ref.shape)


def lnb(u,z,r):
    return r*(u-jnp.mean(u,axis=-1,keepdims=True)-z*jnp.mean(u*z,axis=-1,keepdims=True))


def bwd_tile(slot, ds_ref, cot_ref, wo_ref, wu_ref, wd_ref, vec_ref, dfs_ref, dctx_ref, gv_ref, gbu_ref, dl_scr, ul_scr, al_scr, gp_scr, z1_scr, z2_scr, r_scr, R):
    D=wu_ref.shape[0]; FF=wu_ref.shape[1]; Rh=R//2
    r1=r_scr[slot,:,0:1]; r2=r_scr[slot,:,1:2]
    z2=z2_scr[slot]
    do=cot_ref[...].reshape(R,D)
    ri=lax.broadcasted_iota(jnp.int32,(R,1),0)
    coef=jnp.where(ri==0,ds_ref[0:1,0:1],0.0)+jnp.where(ri==Rh,ds_ref[1:2,0:1],0.0)
    do=do+coef*vec_ref[5:6,:]
    gv_ref[4:5,:]+=jnp.sum(do*z2,axis=0,keepdims=True)
    gv_ref[5:6,:]+=jnp.sum(coef*(z2*vec_ref[4:5,:]),axis=0,keepdims=True)
    d2=lnb(do*vec_ref[4:5,:],z2,r2)
    dl=d2.astype(BF)
    dl_scr[...]=dl.reshape(dl_scr.shape)
    gv_ref[3:4,:]+=jnp.sum(dl.astype(F32),axis=0,keepdims=True)
    def body(f,acc):
        o=pl.multiple_of(f*FC,FC)
        da=dg(dl_scr[...].reshape(R,D),wd_ref[:,pl.ds(o,FC)],NN)
        ul=(da*gp_scr[slot,:,pl.ds(o,FC)]).astype(BF)
        ul_scr[:,:,pl.ds(o,FC)]=ul.reshape(2,R//2,FC)
        gbu_ref[:,pl.ds(o,FC)]+=jnp.sum(ul.astype(F32),axis=0,keepdims=True)
        return acc+dg(ul,wu_ref[:,pl.ds(o,FC)],NT)
    d1=lax.fori_loop(0,FF//FC,body,d2,unroll=True)
    z1=z1_scr[slot]
    gv_ref[1:2,:]+=jnp.sum(d1*z1,axis=0,keepdims=True)
    gv_ref[2:3,:]+=jnp.sum(d1,axis=0,keepdims=True)
    dfs=lnb(d1*vec_ref[1:2,:],z1,r1)
    dfs_ref[...]=dfs.reshape(dfs_ref.shape)
    al=dfs.astype(BF)
    al_scr[...]=al.reshape(al_scr.shape)
    gv_ref[0:1,:]+=jnp.sum(al.astype(F32),axis=0,keepdims=True)
    dctx_ref[...]=dg(al,wo_ref[...],NN).astype(BF).reshape(dctx_ref.shape)


class Geo:
    def __init__(g, C, Q):
        g.C=C; g.Q=Q; g.nx=Q//2; g.nz=min(4,C); g.ny=C//g.nz
        c=lax.axis_index("cand"); q=lax.axis_index("query")
        g.z=c//g.ny; g.y=lax.rem(c,g.ny); g.x=q//2; g.k=lax.rem(q,2)
    def dev(g,z,y,x,k): return {"cand":z*g.ny+y,"query":x*2+k}


def mo(v,n): return pl.multiple_of(v,n)


def barrier(g, peers):
    b=pltpu.get_barrier_semaphore()
    for p in peers: pl.semaphore_signal(b,inc=1,device_id=p,device_id_type=MESH)
    pl.semaphore_wait(b,len(peers))


class RS:
    def __init__(s, g, refs, bufs, ss, rs):
        s.g, s.refs, s.bufs, s.ss, s.rs = g, refs, bufs, ss, rs
        s.partner = g.dev(g.z, g.y, g.x, 1 - g.k)
        s.pend = []
    def dims(s, n): return [NR[d] for d in RORD[n]]
    def own(s, n, rel, k):
        g = s.g
        r = dict(zip(RORD[n], rel))
        return rs_slice(g, n, s.refs, jnp.bitwise_xor(g.z, r["z"]), 1 - g.y if r["y"] else g.y, 1 - g.x if r["x"] else g.x, k)
    def near(s, d, r):
        g = s.g
        return g.dev(jnp.bitwise_xor(g.z, r) if d == "z" else g.z, 1 - g.y if d == "y" else g.y, 1 - g.x if d == "x" else g.x, g.k)
    def copy(s, src, dst, n, i, dev):
        pi = RPIECES.index(n)
        return pltpu.make_async_remote_copy(src, dst, s.ss.at[pi, i], s.rs.at[pi, i], device_id=dev, device_id_type=MESH)
    def c0(s, n, r1, r2, r3):
        _, n2, n3 = s.dims(n)
        return s.copy(s.own(n, (r1, r2, r3), 1 - s.g.k), s.bufs[n][0].at[r1, r2, r3], n, (r1 * n2 + r2) * n3 + r3, s.partner)
    def c1(s, n, r1, r2, r3):
        _, n2, n3 = s.dims(n)
        return s.copy(s.bufs[n][0].at[r1, r2, r3], s.bufs[n][1].at[r1 - 1, r2, r3], n, 16 + ((r1 - 1) * n2 + r2) * n3 + r3, s.near(RORD[n][0], r1))
    def c2(s, n, r2, r3):
        n1, n2, n3 = s.dims(n)
        return s.copy(s.bufs[n][0].at[0, r2, r3], s.bufs[n][2].at[r2 - 1, r3], n, 16 + (n1 - 1) * n2 * n3 + (r2 - 1) * n3 + r3, s.near(RORD[n][1], r2))
    def c3(s, n, r3):
        n1, n2, n3 = s.dims(n)
        return s.copy(s.bufs[n][0].at[0, 0, r3], s.bufs[n][3].at[r3 - 1], n, 16 + (n1 - 1) * n2 * n3 + (n2 - 1) * n3 + r3 - 1, s.near(RORD[n][2], r3))
    def go(s, f, *a):
        f(*a).start()
        s.pend.append(lambda: f(*a))
    def add(s, n, dst, srcs):
        rows, st = RSHP[n][0], RSHP[n][2]
        def body(i, _):
            o = pl.multiple_of(i * st, 16)
            dst[pl.ds(o, st), :] = functools.reduce(lambda a, b: a + b, [r[pl.ds(o, st), :].astype(F32) for r in srcs]).astype(dst.dtype)
            return 0
        lax.fori_loop(0, rows // st, body, 0)
    def part1(s, n, r2, r3):
        s.c0(n, 0, r2, r3).wait_recv()
        n1 = s.dims(n)[0]
        for r1 in range(1, n1):
            s.c1(n, r1, r2, r3).wait_recv()
        return [s.own(n, (0, r2, r3), s.g.k), s.bufs[n][0].at[0, r2, r3]] + [s.bufs[n][1].at[r1 - 1, r2, r3] for r1 in range(1, n1)]
    def part2(s, n, r3):
        t = s.part1(n, 0, r3)
        n2 = s.dims(n)[1]
        for r2 in range(1, n2):
            s.c2(n, r2, r3).wait_recv()
        return t + [s.bufs[n][2].at[r2 - 1, r3] for r2 in range(1, n2)]
    def s0(s, n, r1, r2, r3): s.go(s.c0, n, r1, r2, r3)
    def s1(s, n, r1, r2, r3):
        s.c0(n, r1, r2, r3).wait_recv()
        b = s.bufs[n][0].at[r1, r2, r3]
        s.add(n, b, [s.own(n, (r1, r2, r3), s.g.k), b])
        s.go(s.c1, n, r1, r2, r3)
    def s2(s, n, r2, r3):
        s.add(n, s.bufs[n][0].at[0, r2, r3], s.part1(n, r2, r3))
        s.go(s.c2, n, r2, r3)
    def s3(s, n, r3):
        s.add(n, s.bufs[n][0].at[0, 0, r3], s.part2(n, r3))
        s.go(s.c3, n, r3)
    def fin(s, n, dst):
        t = s.part2(n, 0)
        n3 = s.dims(n)[2]
        for r3 in range(1, n3):
            s.c3(n, r3).wait_recv()
        s.add(n, dst, t + [s.bufs[n][3].at[r3 - 1] for r3 in range(1, n3)])
    def fin_(s, n): s.fin(n, s.outs[n])
    def ev(s, e): getattr(s, e[0])(*e[1:])
    def drain(s):
        for c in s.pend: c().wait_send()


def rs_slice(g, n, refs, z, y, x, k):
    wq, wo, wu, wd = refs
    c = z * g.ny + y
    q = x * 2 + k
    if n in QROW:
        return wq.at[pl.ds(mo(c * 288 + k * 144 + QROW[n], 16), RSHP[n][0]), pl.ds(mo(x * 384, 128), 384)]
    if n == "o": return wo.at[pl.ds(mo(c * 96 + k * 48, 16), 48), pl.ds(mo(x * 384, 128), 384)]
    if n == "u": return wu.at[pl.ds(mo(q * 192, 16), 192), pl.ds(mo(c * 384, 128), 384)]
    if n == "d": return wd.at[pl.ds(mo(c * 96, 16), 96), pl.ds(mo(q * 768, 128), 768)]


def rs_bufs():
    out = []
    for n in RPIECES:
        n1, n2, n3 = [NR[d] for d in RORD[n]]
        sh = RSHP[n][:2]
        out += [pltpu.VMEM((n1, n2, n3) + sh, BF), pltpu.VMEM((n1 - 1, n2, n3) + sh, BF), pltpu.VMEM((n2 - 1, n3) + sh, BF), pltpu.VMEM((n3 - 1,) + sh, BF)]
    return out


def attn_fwd_kernel(len_ref, x_ref, w_ref, bias_ref, tab_ref, bk_ref, bkf_ref, xlow_ref, qkv_ref, ctx_ref, lse_ref, relf_ref, rel_ref, bias_scr):
    S, D = x_ref.shape[1:]
    for m in range(2):
        xlow_ref[m*S:(m+1)*S,:]=x_ref[m].astype(BF)
    qkv_proj(w_ref, bias_ref, xlow_ref, qkv_ref, {})
    rel_rows(tab_ref, bk_ref, rel_ref)
    rel_rows(tab_ref, bkf_ref, relf_ref)
    attn_fwd(len_ref, qkv_ref, rel_ref, ctx_ref, lse_ref, bias_scr, S, D, {})


class AG:
    def __init__(s, g, own, refs, ss, rs, cs, cr):
        s.g, s.own_, s.refs, s.ss, s.rs, s.cs, s.cr = g, own, refs, ss, rs, cs, cr
        s.partner = g.dev(g.z, g.y, g.x, 1 - g.k)
        s.pend = []
        s.got = set()
    def dst(s, n, rel, k):
        g = s.g
        r = dict(zip(RORD[n], rel))
        return rs_slice(g, n, s.refs, jnp.bitwise_xor(g.z, r["z"]), 1 - g.y if r["y"] else g.y, 1 - g.x if r["x"] else g.x, k)
    def idx(s, n, rel):
        _, n2, n3 = [NR[d] for d in RORD[n]]
        return (rel[0] * n2 + rel[1]) * n3 + rel[2]
    def src(s, n, rel): return s.own_(n) if rel == (0, 0, 0) else s.dst(n, rel, s.g.k)
    def near(s, d, r):
        g = s.g
        return g.dev(jnp.bitwise_xor(g.z, r) if d == "z" else g.z, 1 - g.y if d == "y" else g.y, 1 - g.x if d == "x" else g.x, g.k)
    def link(s, n, rel, d, k):
        new = tuple(k if a == d else r for a, r in zip(RORD[n], rel))
        pi, i = RPIECES.index(n), s.idx(n, new)
        return pltpu.make_async_remote_copy(s.src(n, rel), s.dst(n, rel, s.g.k), s.ss.at[pi, i], s.rs.at[pi, i], device_id=s.near(d, k), device_id_type=MESH)
    def core(s, n, rel):
        pi, i = RPIECES.index(n), s.idx(n, rel)
        return pltpu.make_async_remote_copy(s.src(n, rel), s.dst(n, rel, s.g.k), s.cs.at[pi, i], s.cr.at[pi, i], device_id=s.partner, device_id_type=MESH)
    def got_core(s, n, rel):
        pi, i = RPIECES.index(n), s.idx(n, rel)
        t = s.dst(n, rel, 1 - s.g.k)
        pltpu.make_async_remote_copy(t, t, s.cs.at[pi, i], s.cr.at[pi, i], device_id=s.partner, device_id_type=MESH).wait_recv()
    def go(s, f, *a):
        f(*a).start()
        s.pend.append(lambda: f(*a))
    def ev(s, e):
        n, rel, outs = e
        if rel != (0, 0, 0):
            t = s.dst(n, rel, s.g.k)
            pi, i = RPIECES.index(n), s.idx(n, rel)
            pltpu.make_async_remote_copy(t, t, s.ss.at[pi, i], s.rs.at[pi, i], device_id=s.partner, device_id_type=MESH).wait_recv()
        for d, k in outs:
            if d == "k": s.go(s.core, n, rel)
            else: s.go(s.link, n, rel, d, k)
    def rels(s, n):
        n1, n2, n3 = [NR[d] for d in RORD[n]]
        return [(a, b, c) for a in range(n1) for b in range(n2) for c in range(n3)]
    def drain(s):
        for c in s.pend: c().wait_send()


def front_kernel(len_ref, x_h, wqf_h, wof_h, wuf_h, wdf_h, *rest, C, Q):
    vins, rest = rest[:11], rest[11:]
    (wq_o, wo, wu, wd, vec_o, bup_o, xlow_o, qkv_o, ctx_ref, lse_ref, relf_ref, bkf_o,
     wqf_ref, wof_ref, wuf_ref, wdf_ref, v_ref, bk_ref, x_v, xlow, qkv, wq, own_p, got_p, h_scr, u_bf, d_bf, vall, tab, rel, qb, bias_scr, ss, rs, cs, cr, vss, vrs, ps, ls) = rest
    g = Geo(C, Q)
    S, D = x_h.shape[1:]
    q_ = lax.axis_index("query")
    peers = [{"query": lax.rem(q_ + j, Q)} for j in range(1, Q)] + [g.dev(g.z, 1 - g.y, g.x, g.k)] + [g.dev(jnp.bitwise_xor(g.z, i), g.y, g.x, g.k) for i in range(1, g.nz)]
    bar = pltpu.get_barrier_semaphore()
    for p in peers:
        pl.semaphore_signal(bar, inc=1, device_id=p, device_id_type=MESH)
    wc = [pltpu.make_async_copy(a, b, ls.at[10 + i]) for i, (a, b) in enumerate(((wqf_h, wqf_ref), (wof_h, wof_ref), (wuf_h, wuf_ref), (wdf_h, wdf_ref)))]
    for c in wc:
        c.start()
    xc = pltpu.make_async_copy(x_h, x_v, ls.at[0])
    xc.start()
    k = g.k
    dq, bq = D // Q, tab.shape[1] // Q
    fq = bup_o.shape[1] // Q
    v_ref[...] = jnp.zeros_like(v_ref)
    for i in range(8):
        v_ref[i:i + 1, 0:dq] = vins[i][...]
    for j in range(fq // 256):
        v_ref[8 + j, :] = vins[8][j * 256:(j + 1) * 256]
    v_ref[16:16 + vins[9].shape[0], 0:bq] = vins[9][...]
    nrel = vins[10].shape[1]
    bk_ref[...] = jnp.full(bk_ref.shape, -1, jnp.int32)
    bk_ref[:, 0:nrel] = vins[10][...]
    for c in wc:
        c.wait()

    def turn(w):
        n = w.shape[1]
        eye = (lax.broadcasted_iota(jnp.int32, (n, n), 0) == lax.broadcasted_iota(jnp.int32, (n, n), 1)).astype(BF)
        return dg(eye, w.astype(BF), NT).astype(BF)
    a, b = turn(wqf_ref[...]), turn(wof_ref[...])
    ha, hb = a.shape[0] // 2, b.shape[0] // 2
    for i in range(2):
        own_p[i, 0:ha, :] = a[i * ha:(i + 1) * ha]
        own_p[i, ha:ha + hb, :] = b[i * hb:(i + 1) * hb]
    d_bf[...] = wdf_ref[...].astype(BF)
    u_bf[...] = wuf_ref[...].astype(BF)
    pl.semaphore_wait(bar, len(peers))
    pc = pltpu.make_async_remote_copy(own_p.at[1 - k], got_p, ps.at[0], ps.at[1], device_id=g.dev(g.z, g.y, g.x, 1 - k), device_id_type=MESH)
    pc.start()
    vcs = []
    for j in range(1, Q):
        c = pltpu.make_async_remote_copy(v_ref, vall.at[q_], vss.at[j - 1], vrs.at[j - 1], device_id={"query": lax.rem(q_ + j, Q)}, device_id_type=MESH)
        c.start()
        vcs.append(c)
    vall[q_] = v_ref[...]

    def own(n):
        if n == "u": return u_bf
        if n == "d": return d_bf
        return h_scr.at[pl.ds(QROW.get(n, 144), RSHP[n][0])]
    A = AG(g, own, (wq, wo, wu, wd), ss, rs, cs, cr)
    loc = [pltpu.make_async_copy(own(n), A.dst(n, (0, 0, 0), k), ls.at[1 + i]) for i, n in enumerate(RPIECES)]

    def after(name):
        for e in AGSLOTS.get(name, []):
            A.ev(e)
    after("b")
    loc[0].start()
    loc[1].start()
    pc.wait()
    t, r = own_p[k], got_p[...]
    @pl.when(k == 0)
    def _(): h_scr[...] = jnp.concatenate([t, r], axis=1)
    @pl.when(k == 1)
    def _(): h_scr[...] = jnp.concatenate([r, t], axis=1)
    for c in loc[2:]:
        c.start()
    after("h")
    xc.wait()
    for m in range(2):
        xlow[m*S:(m+1)*S,:]=x_v[m].astype(BF)
    xo = pltpu.make_async_copy(xlow, xlow_o, ls.at[7])
    xo.start()
    after("p0")
    for c in vcs:
        c.wait()
    qb[...] = jnp.zeros_like(qb)
    vec_o[...] = jnp.zeros_like(vec_o)
    for q in range(Q):
        lo, hi = q * dq, (q + 1) * dq
        qb[:, lo:hi] = vall[q, 0:1, 0:dq]
        qb[:, 2 * D + lo:2 * D + hi] = vall[q, 1:2, 0:dq]
        vec_o[0:6, lo:hi] = vall[q, 2:8, 0:dq]
        for j in range(fq // 256):
            bup_o[:, q * fq + j * 256:q * fq + (j + 1) * 256] = vall[q, 8 + j:9 + j, :]
        tab[:, q * bq:(q + 1) * bq] = vall[q, 16:32, 0:bq]
    after("p1")
    for i, n in enumerate(RPIECES):
        if n in QROW:
            loc[i].wait()
            for r in A.rels(n):
                A.got_core(n, r)
    qkv_proj(wq, qb, xlow, qkv, {i: [functools.partial(A.ev, e) for e in AGSLOTS.get(f"n{i}", [])] for i in range(3 * D // 256)})
    wc = pltpu.make_async_copy(wq, wq_o, ls.at[8])
    qc = pltpu.make_async_copy(qkv, qkv_o, ls.at[9])
    wc.start()
    qc.start()
    ids = jnp.broadcast_to(bk_ref[...], (8, 2 * S)).astype(F32).astype(BF)
    for j in range(2 * S // 256):
        flip = (lax.broadcasted_iota(jnp.int32, (2 * S, 256), 0) + lax.broadcasted_iota(jnp.int32, (2 * S, 256), 1) == nrel - 1 - j * 256).astype(BF)
        bkf_o[:, j * 256:(j + 1) * 256] = dg(ids, flip, NN)[0:1].astype(jnp.int32)
    bkf_o[:, nrel:] = jnp.full((1, 2 * S - nrel), -1, jnp.int32)
    after("r0")
    rel_rows(tab, bk_ref, rel)
    rel_rows(tab, bkf_o, relf_ref)
    after("r1")
    attn_fwd(len_ref, qkv, rel, ctx_ref, lse_ref, bias_scr, S, D, {i: [functools.partial(A.ev, e) for e in AGSLOTS.get(f"t{i}", [])] for i in range(D // 64)})
    for c in (xo, wc, qc):
        c.wait()
    for i, n in enumerate(RPIECES):
        if n not in QROW:
            loc[i].wait()
            for r in A.rels(n):
                A.got_core(n, r)
    A.drain()


def ffn_kernel(lab_ref, x_ref, ctx_ref, cot_ref, wo_h, wu_h, wd_h, vec_ref, bup_ref,
               out_ref, dfs_ref, dctx_ref, nl_ref, act_ref, dl_ref, al_ref, ul_ref, gv_ref, gbu_ref, loss_ref,
               wo_ref, wu_ref, wd_ref, gp_scr, z1_scr, z2_scr, r_scr,
               ws, ds_scr, sc_snd, sc_all, sss, ssr, *, T, R, C, Q):
    i = pl.program_id(0)
    D, FF = wu_ref.shape
    cid = lax.axis_index("cand")

    loads = [pltpu.make_async_copy(a, b, ws.at[j]) for j, (a, b) in enumerate(((wo_h, wo_ref), (wu_h, wu_ref), (wd_h, wd_ref)))]

    def arrive(j):
        @pl.when(i == 0)
        def _(): loads[j].wait()

    def score_copy(j):
        return pltpu.make_async_remote_copy(sc_snd, sc_all.at[cid], sss.at[j - 1], ssr.at[j - 1], device_id={"cand": lax.rem(cid + j, C)}, device_id_type=MESH)

    @pl.when(i == 0)
    def _():
        b = pltpu.get_barrier_semaphore()
        for j in range(1, C):
            pl.semaphore_signal(b, inc=1, device_id={"cand": lax.rem(cid + j, C)}, device_id_type=MESH)
        for c in loads:
            c.start()
        gv_ref[...] = jnp.zeros_like(gv_ref)
        gbu_ref[...] = jnp.zeros_like(gbu_ref)
        ds_scr[...] = jnp.zeros_like(ds_scr)
        sc_snd[...] = jnp.zeros_like(sc_snd)

    @pl.when(i < T)
    def _():
        fwd_tile(arrive, jnp.minimum(i, 1), x_ref, ctx_ref, wo_ref, wu_ref, wd_ref, vec_ref, bup_ref, out_ref, nl_ref, act_ref, gp_scr, z1_scr, z2_scr, r_scr, R)

    @pl.when(i == 0)
    def _():
        for m in range(2):
            sc = jnp.sum(out_ref[m, 0:1, :] * vec_ref[5:6, :], axis=1, keepdims=True)
            sc_snd[m:m + 1, :] = jnp.broadcast_to(sc, (1, 128))
        sc_all[cid] = sc_snd[...]
        pl.semaphore_wait(pltpu.get_barrier_semaphore(), C - 1)
        for j in range(1, C):
            score_copy(j).start()

    @pl.when(i == T)
    def _():
        for j in range(1, C):
            score_copy(j).wait()
        total = jnp.zeros((1, 128), F32)
        own = sc_snd[...]
        for m in range(2):
            rows = [sc_all[j, m:m + 1, :] for j in range(C)]
            peak = functools.reduce(jnp.maximum, rows)
            lse = peak + jnp.log(functools.reduce(lambda a, b: a + b, [jnp.exp(r - peak) for r in rows]))
            lab = lab_ref[m]
            picked = functools.reduce(lambda a, b: a + b, [jnp.where(lab == j, r, 0.0) for j, r in enumerate(rows)])
            total = total + (lse - picked)
            ds_scr[m:m + 1, :] = (jnp.exp(own[m:m + 1, :] - lse) - jnp.where(lab == cid, 1.0, 0.0)) * (1.0 / Q)
        loss_ref[...] = jnp.broadcast_to(jnp.where(cid == 0, total * (1.0 / Q), 0.0), (8, 128))

    @pl.when((i >= 1) & (i <= T))
    def _():
        t = lax.rem(i, T)
        bwd_tile(jnp.minimum(t, 1), ds_scr, cot_ref, wo_ref, wu_ref, wd_ref, vec_ref, dfs_ref, dctx_ref, gv_ref, gbu_ref, dl_ref, ul_ref, al_ref, gp_scr, z1_scr, z2_scr, r_scr, R)


class VecSum:
    def __init__(s, C, Q, src, va, snd, rcv, qs, qr, rs, rr):
        s.C, s.Q, s.src, s.va, s.snd, s.rcv, s.qs, s.qr, s.rs, s.rr = C, Q, src, va, snd, rcv, qs, qr, rs, rr
        s.c, s.q = lax.axis_index("cand"), lax.axis_index("query")
        s.rounds = C.bit_length() - 1
    def qcopy(s, j):
        to = lax.rem(s.q + j, s.Q)
        return pltpu.make_async_remote_copy(s.src.at[to], s.va.at[s.q], s.qs.at[j - 1], s.qr.at[j - 1], device_id={"query": to}, device_id_type=MESH)
    def rcopy(s, i):
        return pltpu.make_async_remote_copy(s.snd.at[i], s.rcv.at[i], s.rs.at[i], s.rr.at[i], device_id={"cand": jnp.bitwise_xor(s.c, 1 << i)}, device_id_type=MESH)
    def start(s):
        for j in range(1, s.Q):
            s.qcopy(j).start()
        s.va[s.q] = s.src[s.q]
    def take(s, i):
        if i == 0:
            for j in range(1, s.Q):
                s.qcopy(j).wait()
            return functools.reduce(lambda a, b: a + b, [s.va[j] for j in range(s.Q)])
        s.rcopy(i - 1).wait()
        return s.snd[i - 1] + s.rcv[i - 1]
    def step(s, i):
        s.snd[i] = s.take(i)
        s.rcopy(i).start()
    def finish(s, dst):
        dst[...] = s.take(s.rounds)


def back_kernel(len_ref, nl_h, dl_h, al_h, ctx_h, act_h, ul_h, qkv_h, dctx_h, xlow_h, wq_h, dfs_h, lse_ref, relf, bkf_ref, gv_ref, gbu_ref, loss_ref,
                *rest, C, Q, fast):
    if fast:
        ig_h, p_out, u_out, d_out, ve_out, vl_out = rest[:6]
        scr = rest[6:]
    else:
        ig_h, gq_o, go_o, gu_o, gd_o, gb_o, gtab_o = rest[:7]
        scr = rest[7:]
    (nl, dl, al, ctx, ch, qkv, dctx, xlow, wq, dfs, igt, gq, go, gu, gd, drelf, bias_scr, acc_scr, gb, gtab, ls, cs_, os_) = scr[:23]
    NS, D = nl.shape
    FF = gu.shape[1]
    S = NS // 2
    NZ = FF // 768
    load = lambda i, src, dst: pltpu.make_async_copy(src, dst, ls.at[i])
    big = [load(0, nl_h, nl), load(1, dl_h, dl), load(2, al_h, al), load(3, ctx_h, ctx), load(4, qkv_h, qkv), load(5, dctx_h, dctx),
           load(6, xlow_h, xlow), load(7, wq_h, wq), load(8, dfs_h, dfs)]
    if fast:
        g = Geo(C, Q)

    def offs(d, i):
        if not fast: c = i
        elif d: c = jnp.bitwise_xor(g.x, 1 - i // 2) * 2 + jnp.bitwise_xor(g.k, 1 - lax.rem(i, 2))
        else: c = jnp.bitwise_xor(g.z, 3 - i)
        return pl.multiple_of(c * 768, 128)

    def chunk(d, i):
        return pltpu.make_async_copy((act_h if d else ul_h).at[:, pl.ds(offs(d, i), 768)], ch.at[lax.rem(i, 2)], cs_.at[lax.rem(i, 2)])
    if fast:
        peers = [{"query": lax.rem(lax.axis_index("query") + j, Q)} for j in range(1, Q)] + [{"cand": lax.rem(lax.axis_index("cand") + j, C)} for j in range(1, C)]
        bar = pltpu.get_barrier_semaphore()
        for p in peers:
            pl.semaphore_signal(bar, inc=1, device_id=p, device_id_type=MESH)
    for c in (big[2], big[3], big[0], chunk(0, jnp.int32(0)), chunk(0, jnp.int32(1)), big[1]):
        c.start()
    if fast:
        bufs = {n: scr[23 + 4 * i:27 + 4 * i] for i, n in enumerate(RPIECES)}
        h_scr, e_snd, e_rcv, ve, vea, ves, ver, vl, vla, vls, vlr, ss, rs, es, qs, qr, cs, cr = scr[23 + NB:]
        R = RS(g, (gq, go, gu, gd), bufs, ss, rs)
        R.outs = {n: h_scr.at[pl.ds(QROW.get(n, 144), RSHP[n][0])] for n in ("qa", "qb", "qz", "o")}
        R.outs.update(u=u_out, d=d_out)
        dq, fq, bq = D // Q, FF // Q, gtab.shape[1] // Q
        early = VecSum(C, Q, ve, vea, ves, ver, qs.at[0], qr.at[0], cs.at[0], cr.at[0])
        late = VecSum(C, Q, vl, vla, vls, vlr, qs.at[1], qr.at[1], cs.at[1], cr.at[1])
        ve[...] = jnp.zeros_like(ve)
        vl[...] = jnp.zeros_like(vl)
        for q in range(Q):
            ve[q, 0:6, 0:dq] = gv_ref[0:6, q * dq:(q + 1) * dq]
            for j in range(fq // 256):
                ve[q, 6 + j:7 + j, :] = gbu_ref[:, q * fq + j * 256:q * fq + (j + 1) * 256]
            ve[q, 9:10, 0:128] = loss_ref[0:1, :]
        vec_at = {"o": early.start, "u3": functools.partial(early.step, 0), "d1": functools.partial(early.step, 1), "d3": functools.partial(early.step, 2),
                  "i1": functools.partial(late.step, 0), "i2": functools.partial(late.step, 1), "i3": functools.partial(late.step, 2)}

    def after(name):
        if name == "v":
            late_vectors()
            late.start()
        if fast:
            for e in SLOTS.get(name, []):
                R.ev(e)
            if name in vec_at:
                vec_at[name]()
    big[2].wait()
    big[3].wait()
    go[...] = dg(al[...], ctx[...], TN).astype(BF)
    big[0].wait()

    def table(names):
        return {i: [functools.partial(after, n) for n in t] for i, t in enumerate(names)} if fast else {}

    def up(i, _):
        chunk(0, i).wait()
        gu[:, pl.ds(offs(0, i), 768)] = dg(nl[...], ch[lax.rem(i, 2)], TN).astype(BF)
        @pl.when(i < NZ - 2)
        def _(): chunk(0, i + 2).start()
        @pl.when(i >= NZ - 2)
        def _(): chunk(1, i + 2 - NZ).start()
        if fast:
            @pl.when(i == 0)
            def _(): pl.semaphore_wait(bar, len(peers))
        hooks(i, table([("o", "u0"), ("u1",), ("u2",), ("u3",)]))
        return 0
    lax.fori_loop(0, NZ, up, 0)
    big[1].wait()
    big[4].start()
    big[5].start()

    def down(i, _):
        chunk(1, i).wait()
        gd[:, pl.ds(offs(1, i), 768)] = dg(dl[...], ch[lax.rem(i, 2)], TN).astype(BF)
        @pl.when(i < NZ - 2)
        def _(): chunk(1, i + 2).start()
        @pl.when(i == 2)
        def _():
            for c in big[6:]:
                c.start()
        hooks(i, table([("d0",), ("d1",), ("d2",), ("d3",)]))
        return 0
    lax.fori_loop(0, NZ, down, 0)
    slots = {}
    if fast:
        for i in range(2 * (D // 128)):
            slots[i] = [functools.partial(R.ev, e) for e in SLOTS.get(f"t{i}", [])]
    drelf[...] = jnp.zeros_like(drelf)
    big[4].wait()
    big[5].wait()
    attn_bwd(len_ref, qkv, dctx, lse_ref, relf, drelf, bias_scr, acc_scr, S, D, slots)
    big[6].wait()

    half = 3 * D // 2
    zh = g.z // 2 if fast else 0

    def b1(n, _):
        o = pl.multiple_of(jnp.where(n < 3, 1 - zh, zh) * half + lax.rem(n, 3) * 384, 128)
        t = qkv[:, pl.ds(o, 384)]
        gq[pl.ds(o, 384), :] = dg(t, xlow[...], TN).astype(BF)
        gb[:, pl.ds(o, 384)] = jnp.sum(t.astype(F32), axis=0, keepdims=True)
        hooks(n, {i: [functools.partial(R.ev, e) for e in SLOTS.get(f"g{i}", [])] for i in range(6)} if fast else {})
        return 0
    lax.fori_loop(0, 6, b1, 0)
    big[7].wait()
    big[8].wait()
    steps = NS // 256
    outc = lambda r: pltpu.make_async_copy(igt.at[lax.rem(r, 2)], ig_h.at[pl.ds(pl.multiple_of(r * 256, 256), 256), :], os_.at[lax.rem(r, 2)])

    def late_vectors():
        nb, nn = gtab.shape[1], bkf_ref.shape[1]
        hot = (lax.broadcasted_iota(jnp.int32, (nb, nn), 0) == bkf_ref[...]).astype(F32)
        gtab[...] = dg(drelf[...], hot, NT, lax.Precision.HIGHEST)
        if fast:
            for q in range(Q):
                vl[q, 0:1, 0:dq] = gb[:, q * dq:(q + 1) * dq]
                vl[q, 1:2, 0:dq] = gb[:, 2 * D + q * dq:2 * D + (q + 1) * dq]
                for h in range(HEADS):
                    vl[q, 2 + h // 4:3 + h // 4, h % 4 * bq:(h % 4 + 1) * bq] = gtab[h:h + 1, q * bq:(q + 1) * bq]

    def rows(r, _):
        o = pl.multiple_of(r * 256, 256)
        @pl.when(r >= 2)
        def _(): outc(r - 2).wait()
        igt[lax.rem(r, 2)] = dfs[pl.ds(o, 256), :] + dg(qkv[pl.ds(o, 256), :], wq[...], NN)
        outc(r).start()
        hooks(r, table([("i0", "v"), ("i1",), ("i2",), ("i3",)]))
        return 0
    lax.fori_loop(0, steps, rows, 0)
    if not fast:
        late_vectors()
    for r in range(max(0, steps - 2), steps):
        outc(jnp.int32(r)).wait()
    if fast:
        k = g.k
        lo = h_scr[:, 0:192]
        hi = h_scr[:, 192:384]
        e_snd[...] = jnp.where(k == 0, hi, lo)
        c = pltpu.make_async_remote_copy(e_snd, e_rcv, es.at[0], es.at[1], device_id=R.partner, device_id_type=MESH)
        c.start()
        p_out[k] = jnp.where(k == 0, lo, hi)
        c.wait()
        p_out[1 - k] = e_rcv[...]
        early.finish(ve_out)
        late.finish(vl_out)
        R.drain()
    else:
        gq_o[...] = gq[...]
        go_o[...] = go[...]
        gu_o[...] = gu[...]
        gd_o[...] = gd[...]
        gb_o[...] = gb[...]
        gtab_o[...] = gtab[...]


def finish_kernel(out_h, ig_h, p_ref, u_ref, d_ref, ve_ref, vl_ref, out_o, ig_o, gq_o, go_o, gu_o, gd_o, *rest):
    vec_o, bup_o, tab_o, loss_o = rest[:8], rest[8], rest[9], rest[10]
    buf, si, so = rest[11:]
    n, rows = buf.shape[0] // 2, buf.shape[1]
    src = [h.at[pl.ds(i * rows, rows), :] for h in (out_h, ig_h) for i in range(n)]
    dst = [h.at[pl.ds(i * rows, rows), :] for h in (out_o, ig_o) for i in range(n)]
    ins = [pltpu.make_async_copy(src[i], buf.at[i], si.at[i]) for i in range(2 * n)]
    outs = [pltpu.make_async_copy(buf.at[i], dst[i], so.at[i]) for i in range(2 * n)]
    for c in ins:
        c.start()
    for a, b in zip(ins, outs):
        a.wait()
        b.start()
    ha = gq_o.shape[1] // 2
    gq_o[...] = jnp.concatenate([p_ref[0, 0:ha, :], p_ref[1, 0:ha, :]], axis=0).T
    go_o[...] = jnp.concatenate([p_ref[0, ha:, :], p_ref[1, ha:, :]], axis=0).T
    gu_o[...] = u_ref[...]
    gd_o[...] = d_ref[...]
    for i in range(8):
        n = vec_o[i].shape[1]
        vec_o[i][...] = vl_ref[i:i + 1, 0:n] if i < 2 else ve_ref[i - 2:i - 1, 0:n]
    for j in range(bup_o.shape[0] // 256):
        bup_o[j * 256:(j + 1) * 256] = ve_ref[6 + j, :]
    loss_o[0] = ve_ref[9, 0]
    bq = tab_o.shape[1]
    for h in range(HEADS):
        tab_o[h:h + 1, :] = vl_ref[2 + h // 4:3 + h // 4, h % 4 * bq:(h % 4 + 1) * bq]
    for c in outs:
        c.wait()


def sds(shape, dtype=F32):
    return jax.ShapeDtypeStruct(shape, dtype)


def back_scratch(fast, C, Q, NS=1024, S=512, D=768, FF=3072, NBK=256):
    v = pltpu.VMEM
    dma = pltpu.SemaphoreType.DMA
    scr = [v((NS, D), BF)] * 4 + [v((2, NS, 768), BF), v((NS, 3 * D), BF), v((NS, D), BF), v((NS, D), BF), v((3 * D, D), BF), v((NS, D), F32), v((2, 256, D), F32),
                                  v((3 * D, D), BF), v((D, D), BF), v((D, FF), BF), v((D, FF), BF), v((16, 2 * S), F32),
                                  v((2, S, S), F32), v((2, S, S), F32), v((1, 3 * D), F32), v((16, NBK), F32), dma((9,)), dma((2,)), dma((2,))]
    if fast:
        scr += rs_bufs() + [v((192, 384), F32), v((192, 192), F32), v((192, 192), F32), v((Q, 16, 256), F32), v((Q, 16, 256), F32), v((3, 16, 256), F32), v((3, 16, 256), F32),
                v((Q, 8, 256), F32), v((Q, 8, 256), F32), v((3, 8, 256), F32), v((3, 8, 256), F32),
                            dma((len(RPIECES), 31)), dma((len(RPIECES), 31)), dma((2,)), dma((2, Q)), dma((2, Q)), dma((2, 3)), dma((2, 3))]
    return scr


def body(hidden_in, out_cotangent, lengths, labels, buckets, w_qkv, w_out, w_up, w_down, bias_q, bias_v, bias_out,
         norm1_gain, norm1_bias, bias_up, bias_down, norm2_gain, score_vector, rel_table):
    Q = lax.axis_size("query")
    C = lax.axis_size("cand")
    micro = hidden_in.shape[0]
    S, D = hidden_in.shape[3:]
    FF = w_up.shape[1] * C
    NBK = rel_table.shape[0] * Q
    dq, fq, bq = D // Q, FF // Q, NBK // Q
    fast = Q == 4 and C == 8 and D == 768 and FF == 3072
    x = hidden_in.reshape(micro, S, D)
    cot = out_cotangent.reshape(micro, S, D)
    lens = lengths.reshape(micro)
    labs = labels.reshape(micro)
    NS = micro * S
    v = pltpu.VMEM
    dma = pltpu.SemaphoreType.DMA
    eight = [bias_q, bias_v, bias_out, norm1_gain, norm1_bias, bias_down, norm2_gain, score_vector]
    if fast:
        np_ = len(RPIECES)
        wq, wo, wu, wd, vec, bup, xlow, qkv, ctx, lse, relf, bkf = pl.pallas_call(
            functools.partial(front_kernel, C=C, Q=Q), in_specs=[SM] + [ANY] * 5 + [VM] * 11, out_specs=[ANY] * 4 + [VM] * 2 + [ANY] * 2 + [VM] * 4,
            out_shape=[sds((3 * D, D), BF), sds((D, D), BF), sds((D, FF), BF), sds((D, FF), BF), sds((8, D)), sds((1, FF)), sds((NS, D), BF), sds((NS, 3 * D), BF),
                       sds((NS, D), BF), sds((micro, 16, S)), sds((16, 2 * S)), sds((1, 2 * S), jnp.int32)],
            scratch_shapes=[v(w_qkv.shape, F32), v(w_out.shape, F32), v(w_up.shape, F32), v(w_down.shape[::-1], F32), v((32, 256), F32), v((1, 2 * S), jnp.int32),
                            v((micro, S, D), F32), v((NS, D), BF), v((NS, 3 * D), BF), v((3 * D, D), BF), v((2, 192, 192), BF), v((192, 192), BF), v((192, 384), BF),
                            v((192, 384), BF), v((96, 768), BF), v((Q, 32, 256), F32), v((16, NBK), F32), v((16, 2 * S), F32), v((1, 3 * D), F32), v((2, S, S), F32)]
            + [dma((np_, 16))] * 4 + [dma((Q,))] * 2 + [dma((2,)), dma((14,))],
            compiler_params=pltpu.CompilerParams(collective_id=0, has_side_effects=True, vmem_limit_bytes=67043328),
        )(lens, x, w_qkv, w_out, w_up, w_down.T, *[t.reshape(1, -1) for t in eight], bias_up, rel_table.T, buckets.reshape(1, -1))
    else:
        bk = jnp.pad(buckets, (0, 1), constant_values=-1)[None, :]
        bkf = jnp.pad(buckets[::-1], (0, 1), constant_values=-1)[None, :]
        def gather(w):
            part = lax.all_gather(w.astype(BF), "query", axis=0, tiled=True)
            return lax.all_gather(part, "cand", axis=1, tiled=True)
        wq, wo, wu, wd = gather(w_qkv).T, gather(w_out).T, gather(w_up), gather(w_down).T
        vall = lax.all_gather(jnp.concatenate(eight + [bias_up, rel_table.reshape(-1)]), "query", axis=0, tiled=False)
        vecs = vall[:, :8 * dq].reshape(Q, 8, dq).transpose(1, 0, 2).reshape(8, D)
        bup = vall[:, 8 * dq:8 * dq + fq].reshape(1, FF)
        tab = jnp.pad(vall[:, 8 * dq + fq:].reshape(NBK, HEADS).T, ((0, 4), (0, 0)))
        qkv_bias = jnp.concatenate([vecs[0:1], jnp.zeros((1, D), F32), vecs[1:2]], axis=1)
        vec = jnp.concatenate([vecs[2:], jnp.zeros((2, D), F32)], axis=0)
        xlow, qkv, ctx, lse, relf = pl.pallas_call(
            attn_fwd_kernel, in_specs=[SM] + [VM] * 6, out_specs=[VM] * 5,
            out_shape=[sds((NS, D), BF), sds((NS, 3 * D), BF), sds((NS, D), BF), sds((micro, 16, S)), sds((16, 2 * S))],
            scratch_shapes=[v((16, 2 * S), F32), v((2, S, S), F32)],
            compiler_params=pltpu.CompilerParams(vmem_limit_bytes=60 * 2**20))(lens, x, wq, qkv_bias, tab, bk, bkf)
    R = 256
    Rh, T = R // micro, NS // R
    tb = lambda im, n=D: pl.BlockSpec((micro, Rh, n), im)
    fw = lambda i: (0, jnp.minimum(i, T - 1), 0)
    bw = lambda i: (0, lax.rem(jnp.maximum(i, 1), T), 0)
    tok = lambda n, dt=BF: sds((micro, S, n), dt)
    out, dfs, dctx, nl, act, dl, al, ul, gv, gbu, lossv = pl.pallas_call(
        functools.partial(ffn_kernel, T=T, R=R, C=C, Q=Q), grid=(T + 1,),
        in_specs=[SM, tb(fw), tb(fw), tb(bw)] + [ANY] * 3 + [VM] * 2, out_specs=[tb(fw), tb(bw), tb(bw), tb(fw), tb(fw, FF), tb(bw), tb(bw), tb(bw, FF)] + [VM] * 3,
        out_shape=[tok(D, F32), tok(D, F32), tok(D), tok(D), tok(FF), tok(D), tok(D), tok(FF), sds((8, D)), sds((1, FF)), sds((8, 128))],
        scratch_shapes=[v((D, D), BF), v((D, FF), BF), v((D, FF), BF), pltpu.VMEM((2, R, FF), F32), pltpu.VMEM((2, R, D), F32), pltpu.VMEM((2, R, D), F32), pltpu.VMEM((2, R, 128), F32), dma((3,)),
                        pltpu.VMEM((8, 128), F32), pltpu.VMEM((8, 128), F32), pltpu.VMEM((C, 8, 128), F32), pltpu.SemaphoreType.DMA((C,)), pltpu.SemaphoreType.DMA((C,))],
        compiler_params=pltpu.CompilerParams(collective_id=1, has_side_effects=True, vmem_limit_bytes=67043328),
    )(labs, x, ctx.reshape(micro, S, D), cot, wo, wu, wd, vec, bup)
    flat = lambda t: t.reshape(NS, t.shape[-1])
    gouts = [sds((2, 192, 192)), sds((192, 384)), sds((96, 768)), sds((16, 256)), sds((8, 256))] if fast else \
        [sds((3 * D, D), BF), sds((D, D), BF), sds((D, FF), BF), sds((D, FF), BF), sds((1, 3 * D)), sds((16, NBK))]
    res = pl.pallas_call(
        functools.partial(back_kernel, C=C, Q=Q, fast=fast), in_specs=[SM] + [ANY] * 11 + [VM] * 6, out_specs=[ANY] + [VM] * len(gouts),
        out_shape=[sds((NS, D))] + gouts, scratch_shapes=back_scratch(fast, C, Q, NS, S, D, FF, NBK),
        compiler_params=pltpu.CompilerParams(collective_id=2 if fast else None, has_side_effects=True, vmem_limit_bytes=67043328),
    )(lens, flat(nl), flat(dl), flat(al), ctx, flat(act), flat(ul), qkv, flat(dctx), xlow, wq, flat(dfs), lse, relf, bkf, gv, gbu, lossv)
    ig = res[0]
    if fast:
        fin = pl.pallas_call(
            finish_kernel, in_specs=[ANY] * 2 + [VM] * 5, out_specs=[ANY] * 2 + [VM] * 14 + [SM],
            out_shape=[sds((NS, D)), sds((NS, D)), sds(w_qkv.shape), sds(w_out.shape), sds(w_up.shape), sds(w_down.shape[::-1])] + [sds((1, dq))] * 8
            + [sds((fq,)), sds((HEADS, bq)), sds((1,))],
            scratch_shapes=[v((8, NS // 4, D), F32), dma((8,)), dma((8,))],
            compiler_params=pltpu.CompilerParams(vmem_limit_bytes=67043328))(flat(out), ig, *res[1:])
        out, ig, g_qkv, g_out, g_up = fin[:5]
        g_down = fin[5].T
        small = [t.reshape(dq) for t in fin[6:14]]
        g_bup, g_tab, loss = fin[14], fin[15].T, fin[16].reshape(())
    else:
        def scatter(g):
            rows, cols = g.shape[0] // Q, g.shape[1] // C
            tiles = g.astype(F32).reshape(Q, rows, C, cols).transpose(2, 0, 1, 3).reshape(C * Q, rows, cols)
            return lax.psum_scatter(tiles, ("cand", "query"), scatter_dimension=0, tiled=True)[0]
        gq, go, gu, gd, gb, gtab = res[1:]
        g_qkv, g_out, g_up, g_down = scatter(gq.T), scatter(go.T), scatter(gu), scatter(gd.T)
        gvecs = jnp.concatenate([gb[:, :D], gb[:, 2 * D:], gv[:6]], axis=0)
        vg = jnp.concatenate([gvecs.reshape(8, Q, dq).transpose(1, 0, 2).reshape(Q, 8 * dq), gbu.reshape(Q, fq), gtab[:HEADS].T.reshape(Q, bq * HEADS),
                              jnp.broadcast_to(lossv[0:1, 0:1], (Q, 1))], axis=1)
        vg = jnp.pad(vg, ((0, 0), (0, -vg.shape[1] % 1024)))
        vs = lax.psum_scatter(lax.psum(vg, "cand"), "query", scatter_dimension=0, tiled=True)[0]
        small = [vs[i * dq:(i + 1) * dq] for i in range(8)]
        g_bup = vs[8 * dq:8 * dq + fq]
        g_tab = vs[8 * dq + fq:8 * dq + fq + bq * HEADS].reshape(bq, HEADS)
        loss = vs[8 * dq + fq + bq * HEADS]
    return (out.reshape(hidden_in.shape), ig.reshape(hidden_in.shape), g_qkv, g_out, g_up, g_down,
            small[0], small[1], small[2], small[3], small[4], g_bup, small[5], small[6], small[7], g_tab, loss)


def solution(mesh):
    seq, w, v = P(None, "query", "cand", None, None), P("query", "cand"), P("query")
    return jax.shard_map(
        body, mesh=mesh,
        in_specs=(seq, seq, P(None, "query", "cand"), P(None, "query"), P(), w, w, w, w) + (v,) * 9 + (P("query", None),),
        out_specs=(seq, seq, w, w, w, w) + (v,) * 9 + (P("query", None), P()),
        check_vma=False)
```

```python
import functools

import jax
import jax.numpy as jnp
from jax import lax
from jax.experimental import pallas as pl
from jax.experimental.pallas import tpu as pltpu
from jax.sharding import PartitionSpec as P

F32 = jnp.float32
BF = jnp.bfloat16
NT = (((1,), (1,)), ((), ()))
NN = (((1,), (0,)), ((), ()))
TN = (((0,), (0,)), ((), ()))
VM = pl.BlockSpec(memory_space=pltpu.VMEM)
SM = pl.BlockSpec(memory_space=pltpu.SMEM)
ANY = pl.BlockSpec(memory_space=pl.ANY)
MESH = pl.DeviceIdType.MESH
EPS = 1e-5
FC = 1536
HEADS = 12
NR = {"x": 2, "y": 2, "z": 4}
RPIECES = ["u", "d", "o", "qa", "qb", "qz"]
RORD = {"u": "yxz", "d": "xyz", "o": "zyx", "qa": "yxz", "qb": "xyz", "qz": "zyx"}
RSHP = {"u": (192, 384, 96), "d": (96, 768, 48), "o": (48, 384, 48), "qa": (64, 384, 64), "qb": (64, 384, 64), "qz": (16, 384, 16)}
QROW = {"qa": 0, "qb": 64, "qz": 128}
NB = 4 * len(RPIECES)
AGSLOTS = {
    "b": [("d", (0, 0, 0), (("x", 1), ("y", 1)))],
    "h": [("qa", (0, 0, 0), (("z", 2),)), ("qb", (0, 0, 0), (("x", 1),)), ("qz", (0, 0, 0), (("x", 1), ("z", 1), ("y", 1))), ("o", (0, 0, 0), (("x", 1),)), ("u", (0, 0, 0), (("k", 0),)), ("o", (0, 0, 0), (("y", 1),)), ("qa", (0, 0, 0), (("z", 1), ("z", 3), ("x", 1))), ("qb", (0, 0, 0), (("y", 1),)), ("u", (0, 0, 0), (("y", 1),)), ("qz", (0, 0, 0), (("z", 2),)), ("qb", (0, 1, 0), (("x", 1), ("k", 0))), ("qb", (0, 0, 0), (("z", 2),)), ("qa", (0, 0, 1), (("x", 1), ("y", 1), ("k", 0))), ("qz", (0, 1, 0), (("z", 1), ("z", 2), ("z", 3), ("k", 0))), ("d", (1, 0, 0), (("k", 0),)), ("u", (0, 0, 0), (("x", 1),)), ("qz", (0, 0, 1), (("y", 1), ("z", 1), ("z", 2), ("z", 3), ("k", 0))), ("qb", (0, 0, 0), (("z", 1),)), ("qa", (0, 0, 2), (("x", 1), ("y", 1), ("k", 0))), ("qb", (0, 0, 2), (("y", 1), ("x", 1), ("k", 0))), ("qa", (0, 1, 0), (("y", 1), ("k", 0))), ("qa", (0, 0, 0), (("k", 0),)), ("qb", (1, 0, 0), (("k", 0),)), ("qb", (0, 0, 0), (("z", 3),)), ("qb", (0, 0, 1), (("y", 1), ("x", 1), ("k", 0))), ("qz", (0, 0, 0), (("z", 3),)), ("qz", (0, 1, 1), (("z", 1), ("z", 2), ("z", 3), ("k", 0))), ("qz", (3, 1, 0), (("k", 0),)), ("qz", (0, 0, 0), (("k", 0),)), ("qa", (1, 0, 1), (("k", 0),)), ("qa", (0, 1, 1), (("y", 1), ("k", 0))), ("u", (0, 0, 0), (("z", 1),)), ("qz", (2, 0, 1), (("k", 0),)), ("d", (0, 0, 0), (("z", 3),)), ("qa", (0, 0, 3), (("x", 1), ("y", 1), ("k", 0))), ("qb", (0, 0, 3), (("y", 1), ("x", 1), ("k", 0))), ("qb", (0, 1, 1), (("x", 1), ("k", 0))), ("qb", (1, 1, 0), (("k", 0),)), ("qz", (3, 0, 0), (("k", 0),)), ("o", (0, 0, 0), (("k", 0),)), ("qz", (1, 1, 1), (("k", 0),)), ("qa", (1, 0, 2), (("k", 0),)), ("qa", (0, 1, 2), (("y", 1), ("k", 0))), ("qa", (1, 1, 1), (("k", 0),)), ("qa", (0, 1, 3), (("y", 1), ("k", 0)))],
    "p0": [("qa", (0, 0, 0), (("y", 1),)), ("qb", (0, 0, 0), (("k", 0),)), ("qb", (1, 0, 3), (("k", 0),)), ("qa", (1, 0, 3), (("k", 0),)), ("qb", (0, 1, 2), (("x", 1), ("k", 0))), ("qb", (0, 1, 3), (("x", 1), ("k", 0))), ("qa", (1, 1, 2), (("k", 0),)), ("qz", (2, 1, 1), (("k", 0),)), ("qz", (2, 1, 0), (("k", 0),)), ("qb", (1, 0, 1), (("k", 0),))],
    "p1": [("qa", (1, 1, 3), (("k", 0),)), ("u", (0, 0, 0), (("z", 2),)), ("d", (0, 0, 0), (("z", 1),)), ("qz", (2, 0, 0), (("k", 0),)), ("u", (0, 0, 1), (("x", 1), ("y", 1), ("k", 0))), ("qz", (3, 1, 1), (("k", 0),)), ("qb", (1, 0, 2), (("k", 0),)), ("qb", (1, 1, 1), (("k", 0),)), ("qz", (1, 0, 0), (("k", 0),)), ("qb", (1, 1, 2), (("k", 0),)), ("qa", (1, 0, 0), (("k", 0),)), ("qz", (1, 0, 1), (("k", 0),)), ("u", (0, 0, 0), (("z", 3),)), ("qb", (1, 1, 3), (("k", 0),)), ("o", (0, 0, 0), (("z", 1),)), ("qz", (1, 1, 0), (("k", 0),)), ("d", (0, 0, 0), (("z", 2),)), ("qz", (3, 0, 1), (("k", 0),)), ("qa", (1, 1, 0), (("k", 0),)), ("d", (0, 0, 3), (("y", 1), ("x", 1), ("k", 0)))],
    "n0": [("u", (0, 1, 1), (("y", 1), ("k", 0)))],
    "n1": [("d", (0, 1, 0), (("x", 1), ("k", 0)))],
    "n2": [("o", (0, 0, 1), (("y", 1), ("z", 1), ("z", 2), ("z", 3), ("k", 0)))],
    "n5": [("u", (0, 0, 2), (("x", 1), ("y", 1), ("k", 0))), ("d", (0, 1, 3), (("x", 1), ("k", 0)))],
    "n7": [("d", (0, 0, 1), (("y", 1), ("x", 1), ("k", 0))), ("u", (0, 1, 0), (("y", 1), ("k", 0)))],
    "n8": [("u", (1, 0, 1), (("k", 0),))],
    "r1": [("d", (1, 1, 0), (("k", 0),))],
    "t0": [("u", (0, 0, 3), (("x", 1), ("y", 1), ("k", 0)))],
    "t1": [("o", (1, 0, 0), (("k", 0),)), ("o", (0, 1, 0), (("z", 1), ("z", 2), ("z", 3), ("k", 0))), ("u", (1, 1, 1), (("k", 0),)), ("o", (0, 1, 1), (("z", 1), ("z", 2), ("z", 3), ("k", 0)))],
    "t3": [("d", (0, 0, 2), (("y", 1), ("x", 1), ("k", 0)))],
    "t4": [("o", (0, 0, 0), (("z", 3),)), ("d", (0, 0, 0), (("k", 0),)), ("d", (1, 0, 3), (("k", 0),)), ("u", (1, 1, 0), (("k", 0),)), ("d", (1, 0, 1), (("k", 0),)), ("u", (1, 0, 2), (("k", 0),)), ("u", (0, 1, 2), (("y", 1), ("k", 0)))],
    "t5": [("u", (1, 0, 0), (("k", 0),)), ("d", (0, 1, 1), (("x", 1), ("k", 0)))],
    "t6": [("u", (1, 0, 3), (("k", 0),)), ("o", (0, 0, 0), (("z", 2),)), ("d", (0, 1, 2), (("x", 1), ("k", 0))), ("d", (1, 0, 2), (("k", 0),))],
    "t7": [("u", (0, 1, 3), (("y", 1), ("k", 0))), ("o", (3, 0, 1), (("k", 0),))],
    "t8": [("o", (2, 0, 1), (("k", 0),)), ("d", (1, 1, 3), (("k", 0),)), ("u", (1, 1, 2), (("k", 0),))],
    "t9": [("d", (1, 1, 1), (("k", 0),)), ("o", (1, 1, 1), (("k", 0),)), ("o", (1, 1, 0), (("k", 0),)), ("o", (3, 1, 0), (("k", 0),)), ("o", (2, 1, 1), (("k", 0),))],
    "t10": [("o", (2, 1, 0), (("k", 0),)), ("o", (1, 0, 1), (("k", 0),)), ("o", (3, 1, 1), (("k", 0),)), ("d", (1, 1, 2), (("k", 0),)), ("u", (1, 1, 3), (("k", 0),)), ("o", (3, 0, 0), (("k", 0),)), ("o", (2, 0, 0), (("k", 0),))],
}
SLOTS = {
    "o": [("s0", "u", 1, 1, 3)],
    "u1": [("s0", "u", 1, 0, 2), ("s0", "o", 3, 1, 1)],
    "u2": [("s0", "o", 1, 1, 0), ("s0", "o", 1, 0, 0), ("s0", "u", 1, 0, 3), ("s1", "u", 1, 1, 3), ("s0", "u", 1, 1, 1), ("s0", "o", 3, 0, 0), ("s0", "o", 3, 1, 0)],
    "u3": [("s0", "o", 0, 1, 1), ("s0", "o", 2, 0, 1)],
    "d0": [("s1", "o", 1, 1, 0), ("s1", "u", 1, 0, 2), ("s0", "o", 2, 1, 0), ("s0", "u", 1, 1, 2), ("s1", "o", 2, 0, 1), ("s0", "u", 0, 1, 3)],
    "d1": [("s0", "u", 0, 0, 3), ("s1", "u", 1, 0, 3), ("s0", "d", 1, 1, 0), ("s0", "o", 3, 0, 1), ("s0", "d", 1, 1, 2), ("s1", "u", 1, 1, 2)],
    "d3": [("s2", "u", 1, 3), ("s1", "o", 3, 1, 1), ("s0", "o", 0, 0, 1), ("s0", "u", 0, 1, 2), ("s0", "d", 1, 0, 2), ("s0", "u", 1, 0, 1), ("s1", "d", 1, 1, 2), ("s0", "d", 0, 0, 1), ("s0", "u", 0, 0, 1)],
    "t0": [("s1", "o", 2, 1, 0), ("s0", "d", 0, 1, 0), ("s1", "o", 3, 0, 0), ("s0", "o", 2, 1, 1), ("s0", "d", 1, 0, 3), ("s0", "d", 1, 1, 1), ("s0", "o", 2, 0, 0), ("s1", "u", 1, 1, 1)],
    "t1": [("s1", "o", 3, 1, 0), ("s0", "d", 0, 1, 2), ("s0", "d", 0, 0, 3), ("s3", "u", 3), ("s0", "u", 0, 0, 2), ("s1", "o", 2, 1, 1), ("s1", "o", 2, 0, 0), ("s1", "d", 1, 0, 2), ("s1", "o", 3, 0, 1), ("s0", "o", 1, 1, 1)],
    "t2": [("s2", "u", 1, 2), ("s0", "o", 1, 0, 1)],
    "t3": [("s0", "u", 1, 1, 0), ("s1", "o", 1, 1, 1), ("s1", "d", 1, 1, 0), ("s0", "d", 1, 1, 3)],
    "t5": [("s1", "u", 1, 0, 1), ("s1", "d", 1, 1, 1), ("s1", "o", 1, 0, 1), ("s0", "u", 0, 1, 1), ("s1", "d", 1, 1, 3)],
    "t6": [("s0", "d", 1, 0, 0), ("s0", "d", 1, 0, 1), ("s0", "d", 0, 0, 0), ("s2", "d", 1, 2), ("s0", "d", 0, 1, 1), ("s0", "u", 0, 0, 0), ("s0", "d", 0, 0, 2), ("s1", "u", 1, 1, 0), ("s2", "u", 1, 1), ("s3", "u", 2)],
    "t8": [("s2", "d", 1, 1)],
    "t9": [("s2", "d", 1, 0), ("s1", "d", 1, 0, 1), ("s3", "d", 2)],
    "t10": [("s0", "d", 0, 1, 3), ("s1", "d", 1, 0, 3), ("s1", "o", 1, 0, 0)],
    "t11": [("s0", "o", 0, 1, 0), ("s3", "u", 1), ("s0", "u", 0, 1, 0)],
    "g0": [("s1", "d", 1, 0, 0)],
    "g2": [("s0", "qz", 2, 0, 1), ("s0", "qz", 3, 1, 0), ("s0", "qz", 3, 0, 0), ("s0", "qz", 2, 1, 1), ("s0", "qz", 2, 1, 0), ("s0", "qa", 0, 1, 2), ("s0", "u", 1, 0, 0), ("s0", "qz", 3, 1, 1), ("s2", "d", 1, 3), ("s0", "qa", 0, 1, 3), ("s0", "qb", 1, 1, 3), ("s0", "qz", 3, 0, 1), ("s0", "qb", 1, 1, 2), ("s0", "qz", 2, 0, 0)],
    "g3": [("s0", "qa", 1, 1, 2), ("s1", "qz", 2, 0, 1), ("s1", "qz", 3, 0, 0), ("s1", "qz", 2, 1, 1), ("s1", "qz", 3, 1, 0), ("s1", "qz", 2, 1, 0)],
    "g5": [("s0", "qa", 0, 1, 1), ("s0", "qb", 1, 0, 3), ("s1", "qa", 1, 1, 2), ("s1", "qz", 3, 1, 1), ("s0", "qz", 1, 1, 0), ("s1", "qz", 2, 0, 0), ("s0", "qb", 0, 1, 1), ("s0", "qz", 1, 0, 1), ("s0", "qb", 0, 1, 0), ("s0", "qb", 1, 0, 1), ("s2", "o", 1, 1), ("s1", "qz", 3, 0, 1), ("s0", "qb", 1, 1, 1), ("s0", "qa", 1, 1, 3), ("s0", "qa", 1, 1, 1), ("s0", "qa", 0, 0, 3), ("s0", "qa", 1, 0, 2), ("s1", "qb", 1, 1, 3), ("s3", "d", 1), ("s2", "o", 1, 0)],
    "i0": [("s1", "qb", 1, 1, 1), ("s3", "d", 3), ("s0", "qa", 1, 0, 3), ("s1", "qa", 1, 1, 3), ("s1", "qz", 1, 1, 0), ("s0", "qa", 1, 0, 1), ("s0", "qb", 0, 1, 2), ("s0", "qa", 0, 1, 0), ("s0", "qz", 1, 0, 0), ("s0", "qa", 0, 0, 0), ("s1", "qa", 1, 0, 2), ("s0", "qb", 0, 1, 3), ("s0", "qz", 1, 1, 1), ("s1", "qb", 1, 1, 2), ("s0", "qb", 1, 1, 0), ("s0", "qa", 1, 1, 0), ("s1", "qb", 1, 0, 1), ("s1", "qa", 1, 1, 1), ("s0", "qa", 0, 0, 2), ("s1", "qz", 1, 0, 0), ("s2", "qa", 1, 2), ("s1", "qz", 1, 1, 1), ("s3", "o", 1), ("s2", "qb", 1, 1), ("s1", "qz", 1, 0, 1), ("s1", "qa", 1, 0, 3), ("s0", "qb", 1, 0, 2), ("s0", "qz", 0, 0, 0), ("s0", "o", 0, 0, 0)],
    "v": [("s1", "qb", 1, 0, 2), ("s1", "qb", 1, 0, 3), ("s2", "qa", 1, 1), ("s2", "qb", 1, 3), ("s2", "qb", 1, 2), ("s0", "qb", 0, 0, 3), ("s0", "qa", 0, 0, 1), ("s0", "qz", 0, 1, 1), ("s2", "qa", 1, 3), ("s0", "qb", 0, 0, 1), ("fin_", "o"), ("s0", "qb", 1, 0, 0), ("s0", "qz", 0, 1, 0), ("s0", "qa", 1, 0, 0), ("s1", "qb", 1, 1, 0), ("s3", "qa", 2), ("s2", "u", 1, 0), ("s1", "qa", 1, 0, 1), ("s0", "qb", 0, 0, 2)],
    "i1": [("s1", "qa", 1, 1, 0), ("s2", "qz", 1, 0), ("s2", "qz", 1, 1), ("s3", "qb", 3), ("s3", "qb", 1), ("s1", "qa", 1, 0, 0)],
    "i2": [("s0", "qb", 0, 0, 0), ("s3", "qa", 1), ("s1", "qb", 1, 0, 0), ("s3", "qa", 3), ("s0", "qz", 0, 0, 1), ("s3", "qb", 2), ("s1", "u", 1, 0, 0), ("fin_", "d"), ("s2", "qb", 1, 0), ("s2", "qa", 1, 0)],
    "i3": [("s3", "qz", 1), ("fin_", "u"), ("fin_", "qa"), ("fin_", "qz"), ("fin_", "qb")],
}


def dg(a,b,d,prec=None): return lax.dot_general(a,b,d,preferred_element_type=F32,precision=prec)


def hooks(i, table):
    for j, evs in table.items():
        if evs:
            @pl.when(i == j)
            def _(evs=evs):
                for e in evs: e()


def qkv_proj(w_ref, bias_ref, xlow_ref, qkv_ref, slots):
    def body(n,_):
        o=pl.multiple_of(n*256,256)
        y=dg(xlow_ref[...], w_ref[pl.ds(o,256),:], NT)
        y=(y+bias_ref[:,pl.ds(o,256)])*jnp.where(o<xlow_ref.shape[1],0.125,1.0)
        qkv_ref[:,pl.ds(o,256)]=y.astype(BF)
        hooks(n, slots)
        return 0
    lax.fori_loop(0, w_ref.shape[0]//256, body, 0)


def rel_rows(tableT_ref, bk_ref, rel_ref):
    nb=tableT_ref.shape[1]; n=bk_ref.shape[1]
    hot=(lax.broadcasted_iota(jnp.int32,(nb,n),0)==bk_ref[...]).astype(F32)
    rel_ref[...]=dg(tableT_ref[...], hot, NN, lax.Precision.HIGHEST)


def bias_expand(row,S):
    R=pltpu.roll(jnp.broadcast_to(row,(128,2*S)), 2*S-127, 1, stride=1, stride_axis=0)
    nu=S//128
    return jnp.concatenate([R[:,128*(nu-1-u):128*(nu-1-u)+S] for u in range(nu)],axis=0)


def diag_sum(t,S):
    nu=S//128
    y=None
    for u in range(nu):
        a=128*(nu-1-u); parts=[]
        if a: parts.append(jnp.zeros((128,a),F32))
        parts.append(t[128*u:128*(u+1),:])
        if 2*S-a-S: parts.append(jnp.zeros((128,2*S-a-S),F32))
        v=jnp.concatenate(parts,axis=1) if len(parts)>1 else parts[0]
        y=v if y is None else y+v
    z=None
    for w in range(16):
        g=y[8*w:8*w+8,:]
        sh=120-8*w
        g=pltpu.roll(g,sh,1) if sh else g
        z=g if z is None else z+g
    out=None
    for b in range(8):
        g=z[b:b+1,:]
        g=pltpu.roll(g,7-b,1) if b<7 else g
        out=g if out is None else out+g
    return out


def attn_fwd(len_ref, qkv_ref, rel_ref, ctx_ref, lse_ref, bias_scr, S, D, slots):
    lane=lax.broadcasted_iota(jnp.int32,(1,128),1)
    col=lax.broadcasted_iota(jnp.int32,(1,S),1)
    def body(p,_):
        o=pl.multiple_of(p*128,128)
        for hh in range(2):
            row=rel_ref[pl.ds(p*2+hh,1),:]
            bias_scr[hh]=bias_expand(row,S)
        for m in range(2):
            q=qkv_ref[m*S:(m+1)*S,pl.ds(o,128)]
            k=qkv_ref[m*S:(m+1)*S,pl.ds(D+o,128)]
            v=qkv_ref[m*S:(m+1)*S,pl.ds(2*D+o,128)]
            valid=col<len_ref[m]
            outs=[]
            for hh in range(2):
                mk=(lane//64)==hh
                qm=jnp.where(mk,q,jnp.zeros_like(q))
                s=dg(qm,k,NT)+bias_scr[hh]
                s=jnp.where(valid,s,-1e30)
                mx=jnp.max(s,axis=1,keepdims=True)
                e=jnp.exp(s-mx)
                tot=jnp.sum(e,axis=1,keepdims=True)
                pl_=(e*(1.0/tot)).astype(BF)
                outs.append(dg(pl_,v,NN))
                lse_ref[m,pl.ds(p*2+hh,1),:]=jnp.transpose(mx+jnp.log(tot),(1,0))
            ctx_ref[m*S:(m+1)*S,pl.ds(o,128)]=jnp.where((lane//64)==0,outs[0],outs[1]).astype(BF)
            hooks(p, {i: slots.get(2*i+m) for i in range(D//128)})
        return 0
    lax.fori_loop(0, D//128, body, 0)


def attn_bwd(len_ref, qkv_ref, dctx_ref, lse_ref, relf_ref, drelf_ref, bias_scr, acc_scr, S, D, slots):
    lane=lax.broadcasted_iota(jnp.int32,(1,128),1)
    rowi=lax.broadcasted_iota(jnp.int32,(S,1),0)
    m0=(lane//64)==0
    def body(p,_):
        o=pl.multiple_of(p*128,128)
        for hh in range(2):
            row=relf_ref[pl.ds(p*2+hh,1),:]
            bias_scr[hh]=bias_expand(row,S)
        for m in range(2):
            q=qkv_ref[m*S:(m+1)*S,pl.ds(o,128)]
            k=qkv_ref[m*S:(m+1)*S,pl.ds(D+o,128)]
            v=qkv_ref[m*S:(m+1)*S,pl.ds(2*D+o,128)]
            do=dctx_ref[m*S:(m+1)*S,pl.ds(o,128)]
            valid=rowi<len_ref[m]
            oq=[];ok=[];ov=[]
            for hh in range(2):
                mk=(lane//64)==hh
                km=jnp.where(mk,k,jnp.zeros_like(k)); vm=jnp.where(mk,v,jnp.zeros_like(v))
                sT=dg(km,q,NT)+bias_scr[hh]
                sT=jnp.where(valid,sT,-1e30)
                pT=jnp.exp(sT-lse_ref[m,pl.ds(p*2+hh,1),:])
                dpT=dg(vm,do,NT)
                rd=jnp.sum(dpT*pT,axis=0,keepdims=True)
                ds=(pT*(dpT-rd)).astype(BF)
                ov.append(dg(pT.astype(BF),do,NN))
                ok.append(dg(ds,q,NN))
                oq.append(dg(ds,k,TN))
                if m==0: acc_scr[hh]=ds.astype(F32)
                else: acc_scr[hh]+=ds.astype(F32)
            qkv_ref[m*S:(m+1)*S,pl.ds(o,128)]=(jnp.where(m0,oq[0],oq[1])*0.125).astype(BF)
            qkv_ref[m*S:(m+1)*S,pl.ds(D+o,128)]=jnp.where(m0,ok[0],ok[1]).astype(BF)
            qkv_ref[m*S:(m+1)*S,pl.ds(2*D+o,128)]=jnp.where(m0,ov[0],ov[1]).astype(BF)
            hooks(p, {i: slots.get(2*i+m) for i in range(D//128)})
        for hh in range(2):
            drelf_ref[pl.ds(p*2+hh,1),:]=diag_sum(acc_scr[hh],S)
        return 0
    lax.fori_loop(0, D//128, body, 0)


def stats(z):
    mu=jnp.mean(z,axis=-1,keepdims=True); c=z-mu
    var=jnp.mean(c*c,axis=-1,keepdims=True)
    r=lax.rsqrt(var+EPS)
    return c*r, r


def fwd_tile(arrive, slot, x_ref, ctx_ref, wo_ref, wu_ref, wd_ref, vec_ref, bup_ref, out_ref, nl_scr, act_scr, gp_scr, z1_scr, z2_scr, r_scr, R):
    D=x_ref.shape[2]; FF=wu_ref.shape[1]
    ctx=ctx_ref[...].reshape(R,D)
    arrive(0)
    fs=x_ref[...].reshape(R,D)+(dg(ctx,wo_ref[...],NT)+vec_ref[0:1,:])
    z1,r1=stats(fs)
    z1_scr[slot]=z1
    fn=z1*vec_ref[1:2,:]+vec_ref[2:3,:]
    nl=fn.astype(BF)
    nl_scr[...]=nl.reshape(nl_scr.shape)
    def body(f,acc):
        o=pl.multiple_of(f*FC,FC)
        u=dg(nl_scr[...].reshape(R,D),wu_ref[:,pl.ds(o,FC)],NN)+bup_ref[:,pl.ds(o,FC)]
        phi=0.5*(1.0+lax.erf(u*(2.0**-0.5)))
        a=(u*phi).astype(BF)
        act_scr[:,:,pl.ds(o,FC)]=a.reshape(2,R//2,FC)
        gp_scr[slot,:,pl.ds(o,FC)]=phi+u*(jnp.exp(u*u*-0.5)*0.3989422804014327)
        return acc+dg(a,wd_ref[:,pl.ds(o,FC)],NT)
    arrive(1)
    arrive(2)
    acc=lax.fori_loop(0,FF//FC,body,fn+vec_ref[3:4,:],unroll=True)
    z2,r2=stats(acc)
    z2_scr[slot]=z2
    r_scr[slot,:,0:1]=r1
    r_scr[slot,:,1:2]=r2
    out_ref[...]=(z2*vec_ref[4:5,:]).reshape(out_ref.shape)


def lnb(u,z,r):
    return r*(u-jnp.mean(u,axis=-1,keepdims=True)-z*jnp.mean(u*z,axis=-1,keepdims=True))


def bwd_tile(slot, ds_ref, cot_ref, wo_ref, wu_ref, wd_ref, vec_ref, dfs_ref, dctx_ref, gv_ref, gbu_ref, dl_scr, ul_scr, al_scr, gp_scr, z1_scr, z2_scr, r_scr, R):
    D=wu_ref.shape[0]; FF=wu_ref.shape[1]; Rh=R//2
    r1=r_scr[slot,:,0:1]; r2=r_scr[slot,:,1:2]
    z2=z2_scr[slot]
    do=cot_ref[...].reshape(R,D)
    ri=lax.broadcasted_iota(jnp.int32,(R,1),0)
    coef=jnp.where(ri==0,ds_ref[0:1,0:1],0.0)+jnp.where(ri==Rh,ds_ref[1:2,0:1],0.0)
    do=do+coef*vec_ref[5:6,:]
    gv_ref[4:5,:]+=jnp.sum(do*z2,axis=0,keepdims=True)
    gv_ref[5:6,:]+=jnp.sum(coef*(z2*vec_ref[4:5,:]),axis=0,keepdims=True)
    d2=lnb(do*vec_ref[4:5,:],z2,r2)
    dl=d2.astype(BF)
    dl_scr[...]=dl.reshape(dl_scr.shape)
    gv_ref[3:4,:]+=jnp.sum(dl.astype(F32),axis=0,keepdims=True)
    def body(f,acc):
        o=pl.multiple_of(f*FC,FC)
        da=dg(dl_scr[...].reshape(R,D),wd_ref[:,pl.ds(o,FC)],NN)
        ul=(da*gp_scr[slot,:,pl.ds(o,FC)]).astype(BF)
        ul_scr[:,:,pl.ds(o,FC)]=ul.reshape(2,R//2,FC)
        gbu_ref[:,pl.ds(o,FC)]+=jnp.sum(ul.astype(F32),axis=0,keepdims=True)
        return acc+dg(ul,wu_ref[:,pl.ds(o,FC)],NT)
    d1=lax.fori_loop(0,FF//FC,body,d2,unroll=True)
    z1=z1_scr[slot]
    gv_ref[1:2,:]+=jnp.sum(d1*z1,axis=0,keepdims=True)
    gv_ref[2:3,:]+=jnp.sum(d1,axis=0,keepdims=True)
    dfs=lnb(d1*vec_ref[1:2,:],z1,r1)
    dfs_ref[...]=dfs.reshape(dfs_ref.shape)
    al=dfs.astype(BF)
    al_scr[...]=al.reshape(al_scr.shape)
    gv_ref[0:1,:]+=jnp.sum(al.astype(F32),axis=0,keepdims=True)
    dctx_ref[...]=dg(al,wo_ref[...],NN).astype(BF).reshape(dctx_ref.shape)


class Geo:
    def __init__(g, C, Q):
        g.C=C; g.Q=Q; g.nx=Q//2; g.nz=min(4,C); g.ny=C//g.nz
        c=lax.axis_index("cand"); q=lax.axis_index("query")
        g.z=c//g.ny; g.y=lax.rem(c,g.ny); g.x=q//2; g.k=lax.rem(q,2)
    def dev(g,z,y,x,k): return {"cand":z*g.ny+y,"query":x*2+k}


def mo(v,n): return pl.multiple_of(v,n)


def barrier(g, peers):
    b=pltpu.get_barrier_semaphore()
    for p in peers: pl.semaphore_signal(b,inc=1,device_id=p,device_id_type=MESH)
    pl.semaphore_wait(b,len(peers))


class RS:
    def __init__(s, g, refs, bufs, ss, rs):
        s.g, s.refs, s.bufs, s.ss, s.rs = g, refs, bufs, ss, rs
        s.partner = g.dev(g.z, g.y, g.x, 1 - g.k)
        s.pend = []
    def dims(s, n): return [NR[d] for d in RORD[n]]
    def own(s, n, rel, k):
        g = s.g
        r = dict(zip(RORD[n], rel))
        return rs_slice(g, n, s.refs, jnp.bitwise_xor(g.z, r["z"]), 1 - g.y if r["y"] else g.y, 1 - g.x if r["x"] else g.x, k)
    def near(s, d, r):
        g = s.g
        return g.dev(jnp.bitwise_xor(g.z, r) if d == "z" else g.z, 1 - g.y if d == "y" else g.y, 1 - g.x if d == "x" else g.x, g.k)
    def copy(s, src, dst, n, i, dev):
        pi = RPIECES.index(n)
        return pltpu.make_async_remote_copy(src, dst, s.ss.at[pi, i], s.rs.at[pi, i], device_id=dev, device_id_type=MESH)
    def c0(s, n, r1, r2, r3):
        _, n2, n3 = s.dims(n)
        return s.copy(s.own(n, (r1, r2, r3), 1 - s.g.k), s.bufs[n][0].at[r1, r2, r3], n, (r1 * n2 + r2) * n3 + r3, s.partner)
    def c1(s, n, r1, r2, r3):
        _, n2, n3 = s.dims(n)
        return s.copy(s.bufs[n][0].at[r1, r2, r3], s.bufs[n][1].at[r1 - 1, r2, r3], n, 16 + ((r1 - 1) * n2 + r2) * n3 + r3, s.near(RORD[n][0], r1))
    def c2(s, n, r2, r3):
        n1, n2, n3 = s.dims(n)
        return s.copy(s.bufs[n][0].at[0, r2, r3], s.bufs[n][2].at[r2 - 1, r3], n, 16 + (n1 - 1) * n2 * n3 + (r2 - 1) * n3 + r3, s.near(RORD[n][1], r2))
    def c3(s, n, r3):
        n1, n2, n3 = s.dims(n)
        return s.copy(s.bufs[n][0].at[0, 0, r3], s.bufs[n][3].at[r3 - 1], n, 16 + (n1 - 1) * n2 * n3 + (n2 - 1) * n3 + r3 - 1, s.near(RORD[n][2], r3))
    def go(s, f, *a):
        f(*a).start()
        s.pend.append(lambda: f(*a))
    def add(s, n, dst, srcs):
        rows, st = RSHP[n][0], RSHP[n][2]
        def body(i, _):
            o = pl.multiple_of(i * st, 16)
            wide = lambda t: t if len(srcs) == 2 else t.astype(F32)
            dst[pl.ds(o, st), :] = functools.reduce(lambda a, b: a + b, [wide(r[pl.ds(o, st), :]) for r in srcs]).astype(dst.dtype)
            return 0
        lax.fori_loop(0, rows // st, body, 0)
    def part1(s, n, r2, r3):
        s.c0(n, 0, r2, r3).wait_recv()
        n1 = s.dims(n)[0]
        for r1 in range(1, n1):
            s.c1(n, r1, r2, r3).wait_recv()
        return [s.own(n, (0, r2, r3), s.g.k), s.bufs[n][0].at[0, r2, r3]] + [s.bufs[n][1].at[r1 - 1, r2, r3] for r1 in range(1, n1)]
    def part2(s, n, r3):
        t = s.part1(n, 0, r3)
        n2 = s.dims(n)[1]
        for r2 in range(1, n2):
            s.c2(n, r2, r3).wait_recv()
        return t + [s.bufs[n][2].at[r2 - 1, r3] for r2 in range(1, n2)]
    def s0(s, n, r1, r2, r3): s.go(s.c0, n, r1, r2, r3)
    def s1(s, n, r1, r2, r3):
        s.c0(n, r1, r2, r3).wait_recv()
        b = s.bufs[n][0].at[r1, r2, r3]
        s.add(n, b, [s.own(n, (r1, r2, r3), s.g.k), b])
        s.go(s.c1, n, r1, r2, r3)
    def s2(s, n, r2, r3):
        s.add(n, s.bufs[n][0].at[0, r2, r3], s.part1(n, r2, r3))
        s.go(s.c2, n, r2, r3)
    def s3(s, n, r3):
        s.add(n, s.bufs[n][0].at[0, 0, r3], s.part2(n, r3))
        s.go(s.c3, n, r3)
    def fin(s, n, dst):
        t = s.part2(n, 0)
        n3 = s.dims(n)[2]
        for r3 in range(1, n3):
            s.c3(n, r3).wait_recv()
        s.add(n, dst, t + [s.bufs[n][3].at[r3 - 1] for r3 in range(1, n3)])
    def fin_(s, n): s.fin(n, s.outs[n])
    def ev(s, e): getattr(s, e[0])(*e[1:])
    def drain(s):
        for c in s.pend: c().wait_send()


def rs_slice(g, n, refs, z, y, x, k):
    wq, wo, wu, wd = refs
    c = z * g.ny + y
    q = x * 2 + k
    if n in QROW:
        return wq.at[pl.ds(mo(c * 288 + k * 144 + QROW[n], 16), RSHP[n][0]), pl.ds(mo(x * 384, 128), 384)]
    if n == "o": return wo.at[pl.ds(mo(c * 96 + k * 48, 16), 48), pl.ds(mo(x * 384, 128), 384)]
    if n == "u": return wu.at[pl.ds(mo(q * 192, 16), 192), pl.ds(mo(c * 384, 128), 384)]
    if n == "d": return wd.at[pl.ds(mo(c * 96, 16), 96), pl.ds(mo(q * 768, 128), 768)]


def rs_bufs():
    out = []
    for n in RPIECES:
        n1, n2, n3 = [NR[d] for d in RORD[n]]
        sh = RSHP[n][:2]
        out += [pltpu.VMEM((n1, n2, n3) + sh, BF), pltpu.VMEM((n1 - 1, n2, n3) + sh, BF), pltpu.VMEM((n2 - 1, n3) + sh, BF), pltpu.VMEM((n3 - 1,) + sh, BF)]
    return out


def attn_fwd_kernel(len_ref, x_ref, w_ref, bias_ref, tab_ref, bk_ref, bkf_ref, xlow_ref, qkv_ref, ctx_ref, lse_ref, relf_ref, rel_ref, bias_scr):
    S, D = x_ref.shape[1:]
    for m in range(2):
        xlow_ref[m*S:(m+1)*S,:]=x_ref[m].astype(BF)
    qkv_proj(w_ref, bias_ref, xlow_ref, qkv_ref, {})
    rel_rows(tab_ref, bk_ref, rel_ref)
    rel_rows(tab_ref, bkf_ref, relf_ref)
    attn_fwd(len_ref, qkv_ref, rel_ref, ctx_ref, lse_ref, bias_scr, S, D, {})


class AG:
    def __init__(s, g, own, refs, ss, rs, cs, cr):
        s.g, s.own_, s.refs, s.ss, s.rs, s.cs, s.cr = g, own, refs, ss, rs, cs, cr
        s.partner = g.dev(g.z, g.y, g.x, 1 - g.k)
        s.pend = []
        s.got = set()
    def dst(s, n, rel, k):
        g = s.g
        r = dict(zip(RORD[n], rel))
        return rs_slice(g, n, s.refs, jnp.bitwise_xor(g.z, r["z"]), 1 - g.y if r["y"] else g.y, 1 - g.x if r["x"] else g.x, k)
    def idx(s, n, rel):
        _, n2, n3 = [NR[d] for d in RORD[n]]
        return (rel[0] * n2 + rel[1]) * n3 + rel[2]
    def src(s, n, rel): return s.own_(n) if rel == (0, 0, 0) else s.dst(n, rel, s.g.k)
    def near(s, d, r):
        g = s.g
        return g.dev(jnp.bitwise_xor(g.z, r) if d == "z" else g.z, 1 - g.y if d == "y" else g.y, 1 - g.x if d == "x" else g.x, g.k)
    def link(s, n, rel, d, k):
        new = tuple(k if a == d else r for a, r in zip(RORD[n], rel))
        pi, i = RPIECES.index(n), s.idx(n, new)
        return pltpu.make_async_remote_copy(s.src(n, rel), s.dst(n, rel, s.g.k), s.ss.at[pi, i], s.rs.at[pi, i], device_id=s.near(d, k), device_id_type=MESH)
    def core(s, n, rel):
        pi, i = RPIECES.index(n), s.idx(n, rel)
        return pltpu.make_async_remote_copy(s.src(n, rel), s.dst(n, rel, s.g.k), s.cs.at[pi, i], s.cr.at[pi, i], device_id=s.partner, device_id_type=MESH)
    def got_core(s, n, rel):
        pi, i = RPIECES.index(n), s.idx(n, rel)
        t = s.dst(n, rel, 1 - s.g.k)
        pltpu.make_async_remote_copy(t, t, s.cs.at[pi, i], s.cr.at[pi, i], device_id=s.partner, device_id_type=MESH).wait_recv()
    def go(s, f, *a):
        f(*a).start()
        s.pend.append(lambda: f(*a))
    def ev(s, e):
        n, rel, outs = e
        if rel != (0, 0, 0):
            t = s.dst(n, rel, s.g.k)
            pi, i = RPIECES.index(n), s.idx(n, rel)
            pltpu.make_async_remote_copy(t, t, s.ss.at[pi, i], s.rs.at[pi, i], device_id=s.partner, device_id_type=MESH).wait_recv()
        for d, k in outs:
            if d == "k": s.go(s.core, n, rel)
            else: s.go(s.link, n, rel, d, k)
    def rels(s, n):
        n1, n2, n3 = [NR[d] for d in RORD[n]]
        return [(a, b, c) for a in range(n1) for b in range(n2) for c in range(n3)]
    def drain(s):
        for c in s.pend: c().wait_send()


def front_kernel(len_ref, x_h, wqf_h, wof_h, wuf_h, wdf_h, *rest, C, Q):
    vins, rest = rest[:11], rest[11:]
    (wq_o, wo, wu, wd, vec_o, bup_o, xlow_o, qkv_o, ctx_ref, lse_ref, relf_ref, bkf_o,
     wqf_ref, wof_ref, wuf_ref, wdf_ref, v_ref, bk_ref, x_v, xlow, qkv, wq, own_p, got_p, h_scr, u_bf, d_bf, vall, tab, rel, qb, bias_scr, ss, rs, cs, cr, vss, vrs, ps, ls) = rest
    g = Geo(C, Q)
    S, D = x_h.shape[1:]
    q_ = lax.axis_index("query")
    peers = [{"query": lax.rem(q_ + j, Q)} for j in range(1, Q)] + [g.dev(g.z, 1 - g.y, g.x, g.k)] + [g.dev(jnp.bitwise_xor(g.z, i), g.y, g.x, g.k) for i in range(1, g.nz)]
    bar = pltpu.get_barrier_semaphore()
    for p in peers:
        pl.semaphore_signal(bar, inc=1, device_id=p, device_id_type=MESH)
    wc = [pltpu.make_async_copy(a, b, ls.at[10 + i]) for i, (a, b) in enumerate(((wqf_h, wqf_ref), (wof_h, wof_ref), (wuf_h, wuf_ref), (wdf_h, wdf_ref)))]
    for c in wc:
        c.start()
    xc = pltpu.make_async_copy(x_h, x_v, ls.at[0])
    xc.start()
    k = g.k
    dq, bq = D // Q, tab.shape[1] // Q
    fq = bup_o.shape[1] // Q
    v_ref[...] = jnp.zeros_like(v_ref)
    for i in range(8):
        v_ref[i:i + 1, 0:dq] = vins[i][...]
    for j in range(fq // 256):
        v_ref[8 + j, :] = vins[8][j * 256:(j + 1) * 256]
    v_ref[16:16 + vins[9].shape[0], 0:bq] = vins[9][...]
    nrel = vins[10].shape[1]
    bk_ref[...] = jnp.full(bk_ref.shape, -1, jnp.int32)
    bk_ref[:, 0:nrel] = vins[10][...]
    for c in wc:
        c.wait()

    def turn(w):
        n = w.shape[1]
        eye = (lax.broadcasted_iota(jnp.int32, (n, n), 0) == lax.broadcasted_iota(jnp.int32, (n, n), 1)).astype(BF)
        return dg(eye, w.astype(BF), NT).astype(BF)
    a, b = turn(wqf_ref[...]), turn(wof_ref[...])
    ha, hb = a.shape[0] // 2, b.shape[0] // 2
    for i in range(2):
        own_p[i, 0:ha, :] = a[i * ha:(i + 1) * ha]
        own_p[i, ha:ha + hb, :] = b[i * hb:(i + 1) * hb]
    d_bf[...] = wdf_ref[...].astype(BF)
    u_bf[...] = wuf_ref[...].astype(BF)
    pl.semaphore_wait(bar, len(peers))
    pc = pltpu.make_async_remote_copy(own_p.at[1 - k], got_p, ps.at[0], ps.at[1], device_id=g.dev(g.z, g.y, g.x, 1 - k), device_id_type=MESH)
    pc.start()
    vcs = []
    for j in range(1, Q):
        c = pltpu.make_async_remote_copy(v_ref, vall.at[q_], vss.at[j - 1], vrs.at[j - 1], device_id={"query": lax.rem(q_ + j, Q)}, device_id_type=MESH)
        c.start()
        vcs.append(c)
    vall[q_] = v_ref[...]

    def own(n):
        if n == "u": return u_bf
        if n == "d": return d_bf
        return h_scr.at[pl.ds(QROW.get(n, 144), RSHP[n][0])]
    A = AG(g, own, (wq, wo, wu, wd), ss, rs, cs, cr)
    loc = [pltpu.make_async_copy(own(n), A.dst(n, (0, 0, 0), k), ls.at[1 + i]) for i, n in enumerate(RPIECES)]

    def after(name):
        for e in AGSLOTS.get(name, []):
            A.ev(e)
    after("b")
    loc[0].start()
    loc[1].start()
    pc.wait()
    t, r = own_p[k], got_p[...]
    @pl.when(k == 0)
    def _(): h_scr[...] = jnp.concatenate([t, r], axis=1)
    @pl.when(k == 1)
    def _(): h_scr[...] = jnp.concatenate([r, t], axis=1)
    for c in loc[2:]:
        c.start()
    after("h")
    xc.wait()
    for m in range(2):
        xlow[m*S:(m+1)*S,:]=x_v[m].astype(BF)
    xo = pltpu.make_async_copy(xlow, xlow_o, ls.at[7])
    xo.start()
    after("p0")
    for c in vcs:
        c.wait()
    qb[...] = jnp.zeros_like(qb)
    vec_o[...] = jnp.zeros_like(vec_o)
    for q in range(Q):
        lo, hi = q * dq, (q + 1) * dq
        qb[:, lo:hi] = vall[q, 0:1, 0:dq]
        qb[:, 2 * D + lo:2 * D + hi] = vall[q, 1:2, 0:dq]
        vec_o[0:6, lo:hi] = vall[q, 2:8, 0:dq]
        for j in range(fq // 256):
            bup_o[:, q * fq + j * 256:q * fq + (j + 1) * 256] = vall[q, 8 + j:9 + j, :]
        tab[:, q * bq:(q + 1) * bq] = vall[q, 16:32, 0:bq]
    after("p1")
    for i, n in enumerate(RPIECES):
        if n in QROW:
            loc[i].wait()
            for r in A.rels(n):
                A.got_core(n, r)
    qkv_proj(wq, qb, xlow, qkv, {i: [functools.partial(A.ev, e) for e in AGSLOTS.get(f"n{i}", [])] for i in range(3 * D // 256)})
    wc = pltpu.make_async_copy(wq, wq_o, ls.at[8])
    qc = pltpu.make_async_copy(qkv, qkv_o, ls.at[9])
    wc.start()
    qc.start()
    ids = jnp.broadcast_to(bk_ref[...], (8, 2 * S)).astype(F32).astype(BF)
    for j in range(2 * S // 256):
        flip = (lax.broadcasted_iota(jnp.int32, (2 * S, 256), 0) + lax.broadcasted_iota(jnp.int32, (2 * S, 256), 1) == nrel - 1 - j * 256).astype(BF)
        bkf_o[:, j * 256:(j + 1) * 256] = dg(ids, flip, NN)[0:1].astype(jnp.int32)
    bkf_o[:, nrel:] = jnp.full((1, 2 * S - nrel), -1, jnp.int32)
    after("r0")
    rel_rows(tab, bk_ref, rel)
    rel_rows(tab, bkf_o, relf_ref)
    after("r1")
    attn_fwd(len_ref, qkv, rel, ctx_ref, lse_ref, bias_scr, S, D, {i: [functools.partial(A.ev, e) for e in AGSLOTS.get(f"t{i}", [])] for i in range(D // 64)})
    for c in (xo, wc, qc):
        c.wait()
    for i, n in enumerate(RPIECES):
        if n not in QROW:
            loc[i].wait()
            for r in A.rels(n):
                A.got_core(n, r)
    A.drain()


def ffn_kernel(lab_ref, x_ref, ctx_ref, cot_ref, wo_h, wu_h, wd_h, vec_ref, bup_ref,
               out_ref, dfs_ref, dctx_ref, nl_ref, act_ref, dl_ref, al_ref, ul_ref, gv_ref, gbu_ref, loss_ref,
               wo_ref, wu_ref, wd_ref, gp_scr, z1_scr, z2_scr, r_scr,
               ws, ds_scr, sc_snd, sc_all, sss, ssr, *, T, R, C, Q):
    i = pl.program_id(0)
    D, FF = wu_ref.shape
    cid = lax.axis_index("cand")

    loads = [pltpu.make_async_copy(a, b, ws.at[j]) for j, (a, b) in enumerate(((wo_h, wo_ref), (wu_h, wu_ref), (wd_h, wd_ref)))]

    def arrive(j):
        @pl.when(i == 0)
        def _(): loads[j].wait()

    def score_copy(j):
        return pltpu.make_async_remote_copy(sc_snd, sc_all.at[cid], sss.at[j - 1], ssr.at[j - 1], device_id={"cand": lax.rem(cid + j, C)}, device_id_type=MESH)

    @pl.when(i == 0)
    def _():
        b = pltpu.get_barrier_semaphore()
        for j in range(1, C):
            pl.semaphore_signal(b, inc=1, device_id={"cand": lax.rem(cid + j, C)}, device_id_type=MESH)
        for c in loads:
            c.start()
        gv_ref[...] = jnp.zeros_like(gv_ref)
        gbu_ref[...] = jnp.zeros_like(gbu_ref)
        ds_scr[...] = jnp.zeros_like(ds_scr)
        sc_snd[...] = jnp.zeros_like(sc_snd)

    @pl.when(i < T)
    def _():
        fwd_tile(arrive, jnp.minimum(i, 1), x_ref, ctx_ref, wo_ref, wu_ref, wd_ref, vec_ref, bup_ref, out_ref, nl_ref, act_ref, gp_scr, z1_scr, z2_scr, r_scr, R)

    @pl.when(i == 0)
    def _():
        for m in range(2):
            sc = jnp.sum(out_ref[m, 0:1, :] * vec_ref[5:6, :], axis=1, keepdims=True)
            sc_snd[m:m + 1, :] = jnp.broadcast_to(sc, (1, 128))
        sc_all[cid] = sc_snd[...]
        pl.semaphore_wait(pltpu.get_barrier_semaphore(), C - 1)
        for j in range(1, C):
            score_copy(j).start()

    @pl.when(i == T)
    def _():
        for j in range(1, C):
            score_copy(j).wait()
        total = jnp.zeros((1, 128), F32)
        own = sc_snd[...]
        for m in range(2):
            rows = [sc_all[j, m:m + 1, :] for j in range(C)]
            peak = functools.reduce(jnp.maximum, rows)
            lse = peak + jnp.log(functools.reduce(lambda a, b: a + b, [jnp.exp(r - peak) for r in rows]))
            lab = lab_ref[m]
            picked = functools.reduce(lambda a, b: a + b, [jnp.where(lab == j, r, 0.0) for j, r in enumerate(rows)])
            total = total + (lse - picked)
            ds_scr[m:m + 1, :] = (jnp.exp(own[m:m + 1, :] - lse) - jnp.where(lab == cid, 1.0, 0.0)) * (1.0 / Q)
        loss_ref[...] = jnp.broadcast_to(jnp.where(cid == 0, total * (1.0 / Q), 0.0), (8, 128))

    @pl.when((i >= 1) & (i <= T))
    def _():
        t = lax.rem(i, T)
        bwd_tile(jnp.minimum(t, 1), ds_scr, cot_ref, wo_ref, wu_ref, wd_ref, vec_ref, dfs_ref, dctx_ref, gv_ref, gbu_ref, dl_ref, ul_ref, al_ref, gp_scr, z1_scr, z2_scr, r_scr, R)


class VecSum:
    def __init__(s, C, Q, src, va, snd, rcv, qs, qr, rs, rr):
        s.C, s.Q, s.src, s.va, s.snd, s.rcv, s.qs, s.qr, s.rs, s.rr = C, Q, src, va, snd, rcv, qs, qr, rs, rr
        s.c, s.q = lax.axis_index("cand"), lax.axis_index("query")
        s.rounds = C.bit_length() - 1
    def qcopy(s, j):
        to = lax.rem(s.q + j, s.Q)
        return pltpu.make_async_remote_copy(s.src.at[to], s.va.at[s.q], s.qs.at[j - 1], s.qr.at[j - 1], device_id={"query": to}, device_id_type=MESH)
    def rcopy(s, i):
        return pltpu.make_async_remote_copy(s.snd.at[i], s.rcv.at[i], s.rs.at[i], s.rr.at[i], device_id={"cand": jnp.bitwise_xor(s.c, 1 << i)}, device_id_type=MESH)
    def start(s):
        for j in range(1, s.Q):
            s.qcopy(j).start()
        s.va[s.q] = s.src[s.q]
    def take(s, i):
        if i == 0:
            for j in range(1, s.Q):
                s.qcopy(j).wait()
            return functools.reduce(lambda a, b: a + b, [s.va[j] for j in range(s.Q)])
        s.rcopy(i - 1).wait()
        return s.snd[i - 1] + s.rcv[i - 1]
    def step(s, i):
        s.snd[i] = s.take(i)
        s.rcopy(i).start()
    def finish(s, dst):
        dst[...] = s.take(s.rounds)


def back_kernel(len_ref, nl_h, dl_h, al_h, ctx_h, act_h, ul_h, qkv_h, dctx_h, xlow_h, wq_h, dfs_h, lse_ref, relf, bkf_ref, gv_ref, gbu_ref, loss_ref,
                *rest, C, Q, fast):
    if fast:
        ig_h, p_out, u_out, d_out, ve_out, vl_out = rest[:6]
        scr = rest[6:]
    else:
        ig_h, gq_o, go_o, gu_o, gd_o, gb_o, gtab_o = rest[:7]
        scr = rest[7:]
    (nl, dl, al, ctx, ch, qkv, dctx, xlow, wq, dfs, igt, gq, go, gu, gd, drelf, bias_scr, acc_scr, gb, gtab, ls, cs_, os_) = scr[:23]
    NS, D = nl.shape
    FF = gu.shape[1]
    S = NS // 2
    NZ = FF // 768
    load = lambda i, src, dst: pltpu.make_async_copy(src, dst, ls.at[i])
    big = [load(0, nl_h, nl), load(1, dl_h, dl), load(2, al_h, al), load(3, ctx_h, ctx), load(4, qkv_h, qkv), load(5, dctx_h, dctx),
           load(6, xlow_h, xlow), load(7, wq_h, wq), load(8, dfs_h, dfs)]
    if fast:
        g = Geo(C, Q)

    def offs(d, i):
        if not fast: c = i
        elif d: c = jnp.bitwise_xor(g.x, 1 - i // 2) * 2 + jnp.bitwise_xor(g.k, 1 - lax.rem(i, 2))
        else: c = jnp.bitwise_xor(g.z, 3 - i)
        return pl.multiple_of(c * 768, 128)

    def chunk(d, i):
        return pltpu.make_async_copy((act_h if d else ul_h).at[:, pl.ds(offs(d, i), 768)], ch.at[lax.rem(i, 2)], cs_.at[lax.rem(i, 2)])
    if fast:
        peers = [{"query": lax.rem(lax.axis_index("query") + j, Q)} for j in range(1, Q)] + [{"cand": jnp.bitwise_xor(lax.axis_index("cand"), j)} for j in (1, 2, 4, 6)]
        bar = pltpu.get_barrier_semaphore()
        for p in peers:
            pl.semaphore_signal(bar, inc=1, device_id=p, device_id_type=MESH)
    for c in (big[0], chunk(0, jnp.int32(0)), big[2], big[3], chunk(0, jnp.int32(1)), big[1]):
        c.start()
    if fast:
        bufs = {n: scr[23 + 4 * i:27 + 4 * i] for i, n in enumerate(RPIECES)}
        h_scr, e_snd, e_rcv, ve, vea, ves, ver, vl, vla, vls, vlr, ss, rs, es, qs, qr, cs, cr = scr[23 + NB:]
        R = RS(g, (gq, go, gu, gd), bufs, ss, rs)
        R.outs = {n: h_scr.at[pl.ds(QROW.get(n, 144), RSHP[n][0])] for n in ("qa", "qb", "qz", "o")}
        R.outs.update(u=u_out, d=d_out)
        dq, fq, bq = D // Q, FF // Q, gtab.shape[1] // Q
        early = VecSum(C, Q, ve, vea, ves, ver, qs.at[0], qr.at[0], cs.at[0], cr.at[0])
        late = VecSum(C, Q, vl, vla, vls, vlr, qs.at[1], qr.at[1], cs.at[1], cr.at[1])
        ve[...] = jnp.zeros_like(ve)
        vl[...] = jnp.zeros_like(vl)
        for q in range(Q):
            ve[q, 0:6, 0:dq] = gv_ref[0:6, q * dq:(q + 1) * dq]
            for j in range(fq // 256):
                ve[q, 6 + j:7 + j, :] = gbu_ref[:, q * fq + j * 256:q * fq + (j + 1) * 256]
            ve[q, 9:10, 0:128] = loss_ref[0:1, :]
        vec_at = {"o": early.start, "u3": functools.partial(early.step, 0), "d1": functools.partial(early.step, 1), "d3": functools.partial(early.step, 2),
                  "i1": functools.partial(late.step, 0), "i2": functools.partial(late.step, 1), "i3": functools.partial(late.step, 2)}

    def after(name):
        if name == "v":
            late_vectors()
            late.start()
        if fast:
            for e in SLOTS.get(name, []):
                R.ev(e)
            if name in vec_at:
                vec_at[name]()
    big[0].wait()

    def table(names):
        return {i: [functools.partial(after, n) for n in t] for i, t in enumerate(names)} if fast else {}

    def up(i, _):
        chunk(0, i).wait()
        gu[:, pl.ds(offs(0, i), 768)] = dg(nl[...], ch[lax.rem(i, 2)], TN).astype(BF)
        @pl.when(i < NZ - 2)
        def _(): chunk(0, i + 2).start()
        @pl.when(i >= NZ - 2)
        def _(): chunk(1, i + 2 - NZ).start()
        @pl.when(i == 0)
        def _():
            if fast:
                pl.semaphore_wait(bar, len(peers))
            after("u0")
            big[2].wait()
            big[3].wait()
            go[...] = dg(al[...], ctx[...], TN).astype(BF)
            after("o")
        hooks(i, table([(), ("u1",), ("u2",), ("u3",)]))
        return 0
    lax.fori_loop(0, NZ, up, 0)
    big[1].wait()
    big[4].start()
    big[5].start()

    def down(i, _):
        chunk(1, i).wait()
        gd[:, pl.ds(offs(1, i), 768)] = dg(dl[...], ch[lax.rem(i, 2)], TN).astype(BF)
        @pl.when(i < NZ - 2)
        def _(): chunk(1, i + 2).start()
        @pl.when(i == 2)
        def _():
            for c in big[6:]:
                c.start()
        hooks(i, table([("d0",), ("d1",), ("d2",), ("d3",)]))
        return 0
    lax.fori_loop(0, NZ, down, 0)
    slots = {}
    if fast:
        for i in range(2 * (D // 128)):
            slots[i] = [functools.partial(R.ev, e) for e in SLOTS.get(f"t{i}", [])]
    drelf[...] = jnp.zeros_like(drelf)
    big[4].wait()
    big[5].wait()
    attn_bwd(len_ref, qkv, dctx, lse_ref, relf, drelf, bias_scr, acc_scr, S, D, slots)
    big[6].wait()

    half = 3 * D // 2
    zh = g.z // 2 if fast else 0

    def b1(n, _):
        o = pl.multiple_of(jnp.where(n < 3, 1 - zh, zh) * half + lax.rem(n, 3) * 384, 128)
        t = qkv[:, pl.ds(o, 384)]
        gq[pl.ds(o, 384), :] = dg(t, xlow[...], TN).astype(BF)
        gb[:, pl.ds(o, 384)] = jnp.sum(t.astype(F32), axis=0, keepdims=True)
        hooks(n, {i: [functools.partial(R.ev, e) for e in SLOTS.get(f"g{i}", [])] for i in range(6)} if fast else {})
        return 0
    lax.fori_loop(0, 6, b1, 0)
    big[7].wait()
    big[8].wait()
    steps = NS // 256
    outc = lambda r: pltpu.make_async_copy(igt.at[lax.rem(r, 2)], ig_h.at[pl.ds(pl.multiple_of(r * 256, 256), 256), :], os_.at[lax.rem(r, 2)])

    def late_vectors():
        nb, nn = gtab.shape[1], bkf_ref.shape[1]
        hot = (lax.broadcasted_iota(jnp.int32, (nb, nn), 0) == bkf_ref[...]).astype(F32).astype(BF)
        part, total = drelf[...], None
        for _ in range(3):
            low = part.astype(BF)
            part = part - low.astype(F32)
            term = dg(low, hot, NT)
            total = term if total is None else total + term
        gtab[...] = total
        if fast:
            for q in range(Q):
                vl[q, 0:1, 0:dq] = gb[:, q * dq:(q + 1) * dq]
                vl[q, 1:2, 0:dq] = gb[:, 2 * D + q * dq:2 * D + (q + 1) * dq]
                for h in range(HEADS):
                    vl[q, 2 + h // 4:3 + h // 4, h % 4 * bq:(h % 4 + 1) * bq] = gtab[h:h + 1, q * bq:(q + 1) * bq]

    def rows(r, _):
        o = pl.multiple_of(r * 256, 256)
        @pl.when(r >= 2)
        def _(): outc(r - 2).wait()
        igt[lax.rem(r, 2)] = dfs[pl.ds(o, 256), :] + dg(qkv[pl.ds(o, 256), :], wq[...], NN)
        outc(r).start()
        hooks(r, table([("i0", "v"), ("i1",), ("i2",), ("i3",)]))
        return 0
    lax.fori_loop(0, steps, rows, 0)
    if not fast:
        late_vectors()
    for r in range(max(0, steps - 2), steps):
        outc(jnp.int32(r)).wait()
    if fast:
        k = g.k
        lo = h_scr[:, 0:192]
        hi = h_scr[:, 192:384]
        e_snd[...] = jnp.where(k == 0, hi, lo)
        c = pltpu.make_async_remote_copy(e_snd, e_rcv, es.at[0], es.at[1], device_id=R.partner, device_id_type=MESH)
        c.start()
        p_out[k] = jnp.where(k == 0, lo, hi)
        c.wait()
        p_out[1 - k] = e_rcv[...]
        early.finish(ve_out)
        late.finish(vl_out)
        R.drain()
    else:
        gq_o[...] = gq[...]
        go_o[...] = go[...]
        gu_o[...] = gu[...]
        gd_o[...] = gd[...]
        gb_o[...] = gb[...]
        gtab_o[...] = gtab[...]


def finish_kernel(out_h, ig_h, u_h, d_h, p_h, ve_h, vl_h, out_o, ig_o, gu_o, gd_o, gq_o, go_o, *rest):
    vec_o, bup_o, tab_o, loss_o = rest[:8], rest[8], rest[9], rest[10]
    buf, ub, db, p_ref, ve_ref, vl_ref, si, so = rest[11:]
    n, rows = buf.shape[0] // 2, buf.shape[1]
    part = lambda h, i: h.at[pl.ds(i * rows, rows), :]
    small = [pltpu.make_async_copy(a, b, si.at[2 * n + i]) for i, (a, b) in enumerate(((p_h, p_ref), (ve_h, ve_ref), (vl_h, vl_ref)))]
    src = [(u_h, ub, gu_o), (d_h, db, gd_o)]
    ins = [pltpu.make_async_copy(a, b, si.at[2 * n + 3 + i]) for i, (a, b, _) in enumerate(src)]
    outs = [pltpu.make_async_copy(b, c, so.at[2 * n + i]) for i, (_, b, c) in enumerate(src)]
    for i in range(n):
        for j, (h, o) in enumerate(((out_h, out_o), (ig_h, ig_o))):
            k = 2 * i + j
            ins.append(pltpu.make_async_copy(part(h, i), buf.at[k], si.at[k]))
            outs.append(pltpu.make_async_copy(buf.at[k], part(o, i), so.at[k]))
    for c in small + ins:
        c.start()
    for c in small:
        c.wait()
    ha = gq_o.shape[1] // 2
    gq_o[...] = jnp.concatenate([p_ref[0, 0:ha, :], p_ref[1, 0:ha, :]], axis=0).T
    go_o[...] = jnp.concatenate([p_ref[0, ha:, :], p_ref[1, ha:, :]], axis=0).T
    for i in range(8):
        m = vec_o[i].shape[1]
        vec_o[i][...] = vl_ref[i:i + 1, 0:m] if i < 2 else ve_ref[i - 2:i - 1, 0:m]
    for j in range(bup_o.shape[0] // 256):
        bup_o[j * 256:(j + 1) * 256] = ve_ref[6 + j, :]
    loss_o[0] = ve_ref[9, 0]
    bq = tab_o.shape[1]
    for h in range(HEADS):
        tab_o[h:h + 1, :] = vl_ref[2 + h // 4:3 + h // 4, h % 4 * bq:(h % 4 + 1) * bq]
    for a, b in zip(ins, outs):
        a.wait()
        b.start()
    for c in outs:
        c.wait()


def sds(shape, dtype=F32):
    return jax.ShapeDtypeStruct(shape, dtype)


def back_scratch(fast, C, Q, NS=1024, S=512, D=768, FF=3072, NBK=256):
    v = pltpu.VMEM
    dma = pltpu.SemaphoreType.DMA
    scr = [v((NS, D), BF)] * 4 + [v((2, NS, 768), BF), v((NS, 3 * D), BF), v((NS, D), BF), v((NS, D), BF), v((3 * D, D), BF), v((NS, D), F32), v((2, 256, D), F32),
                                  v((3 * D, D), BF), v((D, D), BF), v((D, FF), BF), v((D, FF), BF), v((16, 2 * S), F32),
                                  v((2, S, S), F32), v((2, S, S), F32), v((1, 3 * D), F32), v((16, NBK), F32), dma((9,)), dma((2,)), dma((2,))]
    if fast:
        scr += rs_bufs() + [v((192, 384), F32), v((192, 192), F32), v((192, 192), F32), v((Q, 16, 256), F32), v((Q, 16, 256), F32), v((3, 16, 256), F32), v((3, 16, 256), F32),
                v((Q, 8, 256), F32), v((Q, 8, 256), F32), v((3, 8, 256), F32), v((3, 8, 256), F32),
                            dma((len(RPIECES), 31)), dma((len(RPIECES), 31)), dma((2,)), dma((2, Q)), dma((2, Q)), dma((2, 3)), dma((2, 3))]
    return scr


def body(hidden_in, out_cotangent, lengths, labels, buckets, w_qkv, w_out, w_up, w_down, bias_q, bias_v, bias_out,
         norm1_gain, norm1_bias, bias_up, bias_down, norm2_gain, score_vector, rel_table):
    Q = lax.axis_size("query")
    C = lax.axis_size("cand")
    micro = hidden_in.shape[0]
    S, D = hidden_in.shape[3:]
    FF = w_up.shape[1] * C
    NBK = rel_table.shape[0] * Q
    dq, fq, bq = D // Q, FF // Q, NBK // Q
    fast = Q == 4 and C == 8 and D == 768 and FF == 3072
    x = hidden_in.reshape(micro, S, D)
    cot = out_cotangent.reshape(micro, S, D)
    lens = lengths.reshape(micro)
    labs = labels.reshape(micro)
    NS = micro * S
    v = pltpu.VMEM
    dma = pltpu.SemaphoreType.DMA
    eight = [bias_q, bias_v, bias_out, norm1_gain, norm1_bias, bias_down, norm2_gain, score_vector]
    if fast:
        np_ = len(RPIECES)
        wq, wo, wu, wd, vec, bup, xlow, qkv, ctx, lse, relf, bkf = pl.pallas_call(
            functools.partial(front_kernel, C=C, Q=Q), in_specs=[SM] + [ANY] * 5 + [VM] * 11, out_specs=[ANY] * 4 + [VM] * 2 + [ANY] * 2 + [VM] * 4,
            out_shape=[sds((3 * D, D), BF), sds((D, D), BF), sds((D, FF), BF), sds((D, FF), BF), sds((8, D)), sds((1, FF)), sds((NS, D), BF), sds((NS, 3 * D), BF),
                       sds((NS, D), BF), sds((micro, 16, S)), sds((16, 2 * S)), sds((1, 2 * S), jnp.int32)],
            scratch_shapes=[v(w_qkv.shape, F32), v(w_out.shape, F32), v(w_up.shape, F32), v(w_down.shape[::-1], F32), v((32, 256), F32), v((1, 2 * S), jnp.int32),
                            v((micro, S, D), F32), v((NS, D), BF), v((NS, 3 * D), BF), v((3 * D, D), BF), v((2, 192, 192), BF), v((192, 192), BF), v((192, 384), BF),
                            v((192, 384), BF), v((96, 768), BF), v((Q, 32, 256), F32), v((16, NBK), F32), v((16, 2 * S), F32), v((1, 3 * D), F32), v((2, S, S), F32)]
            + [dma((np_, 16))] * 4 + [dma((Q,))] * 2 + [dma((2,)), dma((14,))],
            compiler_params=pltpu.CompilerParams(collective_id=0, has_side_effects=True, vmem_limit_bytes=67043328),
        )(lens, x, w_qkv, w_out, w_up, w_down.T, *[t.reshape(1, -1) for t in eight], bias_up, rel_table.T, buckets.reshape(1, -1))
    else:
        bk = jnp.pad(buckets, (0, 1), constant_values=-1)[None, :]
        bkf = jnp.pad(buckets[::-1], (0, 1), constant_values=-1)[None, :]
        def gather(w):
            part = lax.all_gather(w.astype(BF), "query", axis=0, tiled=True)
            return lax.all_gather(part, "cand", axis=1, tiled=True)
        wq, wo, wu, wd = gather(w_qkv).T, gather(w_out).T, gather(w_up), gather(w_down).T
        vall = lax.all_gather(jnp.concatenate(eight + [bias_up, rel_table.reshape(-1)]), "query", axis=0, tiled=False)
        vecs = vall[:, :8 * dq].reshape(Q, 8, dq).transpose(1, 0, 2).reshape(8, D)
        bup = vall[:, 8 * dq:8 * dq + fq].reshape(1, FF)
        tab = jnp.pad(vall[:, 8 * dq + fq:].reshape(NBK, HEADS).T, ((0, 4), (0, 0)))
        qkv_bias = jnp.concatenate([vecs[0:1], jnp.zeros((1, D), F32), vecs[1:2]], axis=1)
        vec = jnp.concatenate([vecs[2:], jnp.zeros((2, D), F32)], axis=0)
        xlow, qkv, ctx, lse, relf = pl.pallas_call(
            attn_fwd_kernel, in_specs=[SM] + [VM] * 6, out_specs=[VM] * 5,
            out_shape=[sds((NS, D), BF), sds((NS, 3 * D), BF), sds((NS, D), BF), sds((micro, 16, S)), sds((16, 2 * S))],
            scratch_shapes=[v((16, 2 * S), F32), v((2, S, S), F32)],
            compiler_params=pltpu.CompilerParams(vmem_limit_bytes=60 * 2**20))(lens, x, wq, qkv_bias, tab, bk, bkf)
    R = 256
    Rh, T = R // micro, NS // R
    tb = lambda im, n=D: pl.BlockSpec((micro, Rh, n), im)
    fw = lambda i: (0, jnp.minimum(i, T - 1), 0)
    bw = lambda i: (0, lax.rem(jnp.maximum(i, 1), T), 0)
    tok = lambda n, dt=BF: sds((micro, S, n), dt)
    out, dfs, dctx, nl, act, dl, al, ul, gv, gbu, lossv = pl.pallas_call(
        functools.partial(ffn_kernel, T=T, R=R, C=C, Q=Q), grid=(T + 1,),
        in_specs=[SM, tb(fw), tb(fw), tb(bw)] + [ANY] * 3 + [VM] * 2, out_specs=[tb(fw), tb(bw), tb(bw), tb(fw), tb(fw, FF), tb(bw), tb(bw), tb(bw, FF)] + [VM] * 3,
        out_shape=[tok(D, F32), tok(D, F32), tok(D), tok(D), tok(FF), tok(D), tok(D), tok(FF), sds((8, D)), sds((1, FF)), sds((8, 128))],
        scratch_shapes=[v((D, D), BF), v((D, FF), BF), v((D, FF), BF), pltpu.VMEM((2, R, FF), F32), pltpu.VMEM((2, R, D), F32), pltpu.VMEM((2, R, D), F32), pltpu.VMEM((2, R, 128), F32), dma((3,)),
                        pltpu.VMEM((8, 128), F32), pltpu.VMEM((8, 128), F32), pltpu.VMEM((C, 8, 128), F32), pltpu.SemaphoreType.DMA((C,)), pltpu.SemaphoreType.DMA((C,))],
        compiler_params=pltpu.CompilerParams(collective_id=1, has_side_effects=True, vmem_limit_bytes=67043328),
    )(labs, x, ctx.reshape(micro, S, D), cot, wo, wu, wd, vec, bup)
    flat = lambda t: t.reshape(NS, t.shape[-1])
    gouts = [sds((2, 192, 192)), sds((192, 384)), sds((96, 768)), sds((16, 256)), sds((8, 256))] if fast else \
        [sds((3 * D, D), BF), sds((D, D), BF), sds((D, FF), BF), sds((D, FF), BF), sds((1, 3 * D)), sds((16, NBK))]
    res = pl.pallas_call(
        functools.partial(back_kernel, C=C, Q=Q, fast=fast), in_specs=[SM] + [ANY] * 11 + [VM] * 6, out_specs=[ANY] + [VM] * len(gouts),
        out_shape=[sds((NS, D))] + gouts, scratch_shapes=back_scratch(fast, C, Q, NS, S, D, FF, NBK),
        compiler_params=pltpu.CompilerParams(collective_id=2 if fast else None, has_side_effects=True, vmem_limit_bytes=67043328),
    )(lens, flat(nl), flat(dl), flat(al), ctx, flat(act), flat(ul), qkv, flat(dctx), xlow, wq, flat(dfs), lse, relf, bkf, gv, gbu, lossv)
    ig = res[0]
    if fast:
        pg, ug, dng, ve, vl = res[1:]
        fin = pl.pallas_call(
            finish_kernel, in_specs=[ANY] * 7, out_specs=[ANY] * 4 + [VM] * 12 + [SM],
            out_shape=[sds((NS, D)), sds((NS, D)), sds(w_up.shape), sds(w_down.shape[::-1]), sds(w_qkv.shape), sds(w_out.shape)] + [sds((1, dq))] * 8
            + [sds((fq,)), sds((HEADS, bq)), sds((1,))],
            scratch_shapes=[v((8, NS // 4, D), F32), v(ug.shape, F32), v(dng.shape, F32), v(pg.shape, F32), v(ve.shape, F32), v(vl.shape, F32), dma((13,)), dma((10,))],
            compiler_params=pltpu.CompilerParams(vmem_limit_bytes=67043328))(flat(out), ig, ug, dng, pg, ve, vl)
        out, ig, g_up, g_down, g_qkv, g_out = fin[:6]
        g_down = g_down.T
        small = [t.reshape(dq) for t in fin[6:14]]
        g_bup, g_tab, loss = fin[14], fin[15].T, fin[16].reshape(())
    else:
        def scatter(g):
            rows, cols = g.shape[0] // Q, g.shape[1] // C
            tiles = g.astype(F32).reshape(Q, rows, C, cols).transpose(2, 0, 1, 3).reshape(C * Q, rows, cols)
            return lax.psum_scatter(tiles, ("cand", "query"), scatter_dimension=0, tiled=True)[0]
        gq, go, gu, gd, gb, gtab = res[1:]
        g_qkv, g_out, g_up, g_down = scatter(gq.T), scatter(go.T), scatter(gu), scatter(gd.T)
        gvecs = jnp.concatenate([gb[:, :D], gb[:, 2 * D:], gv[:6]], axis=0)
        vg = jnp.concatenate([gvecs.reshape(8, Q, dq).transpose(1, 0, 2).reshape(Q, 8 * dq), gbu.reshape(Q, fq), gtab[:HEADS].T.reshape(Q, bq * HEADS),
                              jnp.broadcast_to(lossv[0:1, 0:1], (Q, 1))], axis=1)
        vg = jnp.pad(vg, ((0, 0), (0, -vg.shape[1] % 1024)))
        vs = lax.psum_scatter(lax.psum(vg, "cand"), "query", scatter_dimension=0, tiled=True)[0]
        small = [vs[i * dq:(i + 1) * dq] for i in range(8)]
        g_bup = vs[8 * dq:8 * dq + fq]
        g_tab = vs[8 * dq + fq:8 * dq + fq + bq * HEADS].reshape(bq, HEADS)
        loss = vs[8 * dq + fq + bq * HEADS]
    return (out.reshape(hidden_in.shape), ig.reshape(hidden_in.shape), g_qkv, g_out, g_up, g_down,
            small[0], small[1], small[2], small[3], small[4], g_bup, small[5], small[6], small[7], g_tab, loss)


def solution(mesh):
    seq, w, v = P(None, "query", "cand", None, None), P("query", "cand"), P("query")
    return jax.shard_map(
        body, mesh=mesh,
        in_specs=(seq, seq, P(None, "query", "cand"), P(None, "query"), P(), w, w, w, w) + (v,) * 9 + (P("query", None),),
        out_specs=(seq, seq, w, w, w, w) + (v,) * 9 + (P("query", None), P()),
        check_vma=False)
```

```python
import functools

import jax
import jax.numpy as jnp
from jax import lax
from jax.experimental import pallas as pl
from jax.experimental.pallas import tpu as pltpu
from jax.sharding import PartitionSpec as P

F32 = jnp.float32
BF = jnp.bfloat16
NT = (((1,), (1,)), ((), ()))
NN = (((1,), (0,)), ((), ()))
TN = (((0,), (0,)), ((), ()))
VM = pl.BlockSpec(memory_space=pltpu.VMEM)
SM = pl.BlockSpec(memory_space=pltpu.SMEM)
ANY = pl.BlockSpec(memory_space=pl.ANY)
MESH = pl.DeviceIdType.MESH
EPS = 1e-5
FC = 1536
HEADS = 12
NR = {"x": 2, "y": 2, "z": 4}
RPIECES = ["u", "d", "o", "qa", "qb", "qz"]
RORD = {"u": "yxz", "d": "xyz", "o": "zyx", "qa": "yxz", "qb": "xyz", "qz": "zyx"}
RSHP = {"u": (192, 384, 96), "d": (96, 768, 48), "o": (48, 384, 48), "qa": (64, 384, 64), "qb": (64, 384, 64), "qz": (16, 384, 16)}
QROW = {"qa": 0, "qb": 64, "qz": 128}
NB = 4 * len(RPIECES)
AGSLOTS = {
    "b": [("d", (0, 0, 0), (("y", 1),)), ("u", (0, 0, 0), (("x", 1),))],
    "h": [("qb", (0, 0, 0), (("z", 3),)), ("qa", (0, 0, 0), (("z", 1),)), ("qb", (0, 0, 0), (("y", 1),)), ("u", (0, 0, 0), (("y", 1),)), ("qa", (0, 0, 0), (("y", 1), ("x", 1))), ("qz", (0, 0, 0), (("z", 2), ("x", 1))), ("d", (0, 0, 0), (("x", 1),)), ("qb", (0, 0, 0), (("z", 2),)), ("qb", (0, 1, 0), (("x", 1), ("k", 0))), ("qa", (0, 0, 1), (("x", 1), ("y", 1), ("k", 0))), ("qz", (2, 0, 0), (("k", 0),)), ("qa", (0, 0, 0), (("z", 3),)), ("qz", (0, 0, 0), (("z", 3),)), ("qb", (0, 0, 0), (("z", 1),)), ("qa", (0, 0, 0), (("z", 2),)), ("qz", (0, 0, 0), (("k", 0),)), ("qz", (0, 0, 1), (("y", 1), ("z", 1), ("z", 2), ("z", 3), ("k", 0))), ("o", (0, 0, 0), (("x", 1),)), ("qb", (0, 0, 3), (("y", 1), ("x", 1), ("k", 0))), ("qz", (0, 0, 0), (("y", 1),)), ("qb", (0, 0, 0), (("x", 1),)), ("qa", (0, 1, 0), (("y", 1), ("k", 0))), ("qb", (0, 0, 1), (("y", 1), ("x", 1), ("k", 0))), ("qz", (0, 0, 0), (("z", 1),)), ("qz", (0, 1, 0), (("z", 1), ("z", 2), ("z", 3), ("k", 0))), ("qz", (0, 1, 1), (("z", 1), ("z", 2), ("z", 3), ("k", 0))), ("d", (0, 0, 0), (("k", 0),)), ("qa", (0, 0, 3), (("x", 1), ("y", 1), ("k", 0))), ("qa", (0, 0, 2), (("x", 1), ("y", 1), ("k", 0))), ("qb", (0, 0, 2), (("y", 1), ("x", 1), ("k", 0))), ("qa", (0, 1, 1), (("y", 1), ("k", 0))), ("qz", (2, 0, 1), (("k", 0),)), ("qz", (1, 0, 0), (("k", 0),)), ("d", (0, 0, 0), (("z", 3),)), ("u", (0, 0, 0), (("z", 1),)), ("qb", (0, 0, 0), (("k", 0),)), ("qa", (0, 1, 3), (("y", 1), ("k", 0))), ("qa", (1, 1, 0), (("k", 0),)), ("qb", (0, 1, 3), (("x", 1), ("k", 0))), ("d", (0, 0, 0), (("z", 1),))],
    "p0": [("qz", (1, 0, 1), (("k", 0),)), ("u", (0, 0, 0), (("z", 3),)), ("qa", (1, 0, 1), (("k", 0),)), ("qb", (1, 0, 1), (("k", 0),)), ("qz", (2, 1, 1), (("k", 0),)), ("qb", (0, 1, 1), (("x", 1), ("k", 0))), ("qz", (1, 1, 0), (("k", 0),)), ("qb", (0, 1, 2), (("x", 1), ("k", 0))), ("u", (0, 0, 0), (("k", 0),)), ("qz", (2, 1, 0), (("k", 0),)), ("qa", (1, 0, 2), (("k", 0),)), ("qa", (1, 0, 0), (("k", 0),)), ("qa", (0, 1, 2), (("y", 1), ("k", 0))), ("o", (0, 0, 0), (("z", 3), ("y", 1))), ("qb", (1, 0, 3), (("k", 0),)), ("qz", (3, 1, 1), (("k", 0),)), ("u", (1, 0, 0), (("k", 0),)), ("qz", (3, 1, 0), (("k", 0),)), ("qz", (3, 0, 1), (("k", 0),)), ("o", (0, 0, 0), (("z", 1),)), ("u", (0, 1, 0), (("y", 1), ("k", 0))), ("qa", (1, 0, 3), (("k", 0),))],
    "p1": [("d", (0, 1, 0), (("x", 1), ("k", 0))), ("qa", (0, 0, 0), (("k", 0),)), ("qa", (1, 1, 2), (("k", 0),)), ("qa", (1, 1, 1), (("k", 0),)), ("qb", (1, 1, 2), (("k", 0),)), ("qz", (1, 1, 1), (("k", 0),)), ("qa", (1, 1, 3), (("k", 0),)), ("qb", (1, 1, 3), (("k", 0),)), ("qz", (3, 0, 0), (("k", 0),)), ("qb", (1, 1, 1), (("k", 0),)), ("qb", (1, 0, 2), (("k", 0),)), ("qb", (1, 0, 0), (("k", 0),)), ("qb", (1, 1, 0), (("k", 0),))],
    "n0": [("d", (0, 0, 3), (("y", 1), ("x", 1), ("k", 0))), ("u", (0, 0, 0), (("z", 2),))],
    "n4": [("u", (0, 0, 1), (("x", 1), ("y", 1), ("k", 0)))],
    "n5": [("d", (0, 0, 1), (("y", 1), ("x", 1), ("k", 0))), ("u", (1, 1, 0), (("k", 0),))],
    "n7": [("d", (0, 0, 0), (("z", 2),))],
    "n8": [("d", (1, 0, 0), (("k", 0),))],
    "r0": [("u", (0, 1, 1), (("y", 1), ("k", 0))), ("u", (0, 0, 3), (("x", 1), ("y", 1), ("k", 0)))],
    "r1": [("d", (1, 0, 1), (("k", 0),)), ("d", (0, 1, 3), (("x", 1), ("k", 0)))],
    "t0": [("d", (1, 1, 0), (("k", 0),)), ("o", (3, 0, 0), (("k", 0),)), ("d", (1, 0, 3), (("k", 0),)), ("u", (0, 0, 2), (("x", 1), ("y", 1), ("k", 0)))],
    "t1": [("o", (0, 0, 1), (("y", 1), ("z", 1), ("z", 2), ("z", 3), ("k", 0))), ("o", (0, 1, 0), (("z", 1), ("z", 2), ("z", 3), ("k", 0)))],
    "t2": [("d", (0, 1, 1), (("x", 1), ("k", 0))), ("d", (0, 0, 2), (("y", 1), ("x", 1), ("k", 0))), ("u", (1, 0, 3), (("k", 0),))],
    "t4": [("o", (0, 0, 0), (("k", 0),)), ("o", (0, 1, 1), (("z", 1), ("z", 2), ("z", 3), ("k", 0))), ("u", (0, 1, 2), (("y", 1), ("k", 0)))],
    "t6": [("u", (1, 1, 1), (("k", 0),)), ("d", (0, 1, 2), (("x", 1), ("k", 0))), ("o", (1, 0, 1), (("k", 0),)), ("u", (0, 1, 3), (("y", 1), ("k", 0))), ("u", (1, 0, 2), (("k", 0),)), ("o", (0, 0, 0), (("z", 2),))],
    "t8": [("o", (1, 0, 0), (("k", 0),)), ("u", (1, 1, 2), (("k", 0),))],
    "t9": [("o", (1, 1, 1), (("k", 0),)), ("d", (1, 0, 2), (("k", 0),)), ("u", (1, 0, 1), (("k", 0),)), ("o", (3, 0, 1), (("k", 0),)), ("o", (2, 0, 1), (("k", 0),)), ("o", (1, 1, 0), (("k", 0),)), ("d", (1, 1, 3), (("k", 0),)), ("d", (1, 1, 1), (("k", 0),)), ("o", (2, 1, 0), (("k", 0),)), ("o", (3, 1, 0), (("k", 0),)), ("o", (2, 1, 1), (("k", 0),))],
    "t10": [("d", (1, 1, 2), (("k", 0),)), ("o", (3, 1, 1), (("k", 0),)), ("u", (1, 1, 3), (("k", 0),)), ("o", (2, 0, 0), (("k", 0),))],
}
SLOTS = {
    "o": [("s0", "u", 1, 1, 3)],
    "u1": [("s0", "u", 1, 0, 2), ("s0", "o", 3, 1, 1)],
    "u2": [("s0", "o", 1, 1, 0), ("s0", "o", 1, 0, 0), ("s0", "u", 1, 0, 3), ("s1", "u", 1, 1, 3), ("s0", "u", 1, 1, 1), ("s0", "o", 3, 0, 0), ("s0", "o", 3, 1, 0)],
    "u3": [("s0", "o", 0, 1, 1), ("s0", "o", 2, 0, 1)],
    "d0": [("s1", "o", 1, 1, 0), ("s1", "u", 1, 0, 2), ("s0", "o", 2, 1, 0), ("s0", "u", 1, 1, 2), ("s1", "o", 2, 0, 1), ("s0", "u", 0, 1, 3)],
    "d1": [("s0", "u", 0, 0, 3), ("s1", "u", 1, 0, 3), ("s0", "d", 1, 1, 0), ("s0", "o", 3, 0, 1), ("s0", "d", 1, 1, 2), ("s1", "u", 1, 1, 2)],
    "d3": [("s2", "u", 1, 3), ("s1", "o", 3, 1, 1), ("s0", "o", 0, 0, 1), ("s0", "u", 0, 1, 2), ("s0", "d", 1, 0, 2), ("s0", "u", 1, 0, 1), ("s1", "d", 1, 1, 2), ("s0", "d", 0, 0, 1), ("s0", "u", 0, 0, 1)],
    "t0": [("s1", "o", 2, 1, 0), ("s0", "d", 0, 1, 0), ("s1", "o", 3, 0, 0), ("s0", "o", 2, 1, 1), ("s0", "d", 1, 0, 3), ("s0", "d", 1, 1, 1), ("s0", "o", 2, 0, 0), ("s1", "u", 1, 1, 1)],
    "t1": [("s1", "o", 3, 1, 0), ("s0", "d", 0, 1, 2), ("s0", "d", 0, 0, 3), ("s3", "u", 3), ("s0", "u", 0, 0, 2), ("s1", "o", 2, 1, 1), ("s1", "o", 2, 0, 0), ("s1", "d", 1, 0, 2), ("s1", "o", 3, 0, 1), ("s0", "o", 1, 1, 1)],
    "t2": [("s2", "u", 1, 2), ("s0", "o", 1, 0, 1)],
    "t3": [("s0", "u", 1, 1, 0), ("s1", "o", 1, 1, 1), ("s1", "d", 1, 1, 0), ("s0", "d", 1, 1, 3)],
    "t5": [("s1", "u", 1, 0, 1), ("s1", "d", 1, 1, 1), ("s1", "o", 1, 0, 1), ("s0", "u", 0, 1, 1), ("s1", "d", 1, 1, 3)],
    "t6": [("s0", "d", 1, 0, 0), ("s0", "d", 1, 0, 1), ("s0", "d", 0, 0, 0), ("s2", "d", 1, 2), ("s0", "d", 0, 1, 1), ("s0", "u", 0, 0, 0), ("s0", "d", 0, 0, 2), ("s1", "u", 1, 1, 0), ("s2", "u", 1, 1), ("s3", "u", 2)],
    "t8": [("s2", "d", 1, 1)],
    "t9": [("s2", "d", 1, 0), ("s1", "d", 1, 0, 1), ("s3", "d", 2)],
    "t10": [("s0", "d", 0, 1, 3), ("s1", "d", 1, 0, 3), ("s1", "o", 1, 0, 0)],
    "t11": [("s0", "o", 0, 1, 0), ("s3", "u", 1), ("s0", "u", 0, 1, 0)],
    "g0": [("s1", "d", 1, 0, 0)],
    "g2": [("s0", "qz", 2, 0, 1), ("s0", "qz", 3, 1, 0), ("s0", "qz", 3, 0, 0), ("s0", "qz", 2, 1, 1), ("s0", "qz", 2, 1, 0), ("s0", "qa", 0, 1, 2), ("s0", "u", 1, 0, 0), ("s0", "qz", 3, 1, 1), ("s2", "d", 1, 3), ("s0", "qa", 0, 1, 3), ("s0", "qb", 1, 1, 3), ("s0", "qz", 3, 0, 1), ("s0", "qb", 1, 1, 2), ("s0", "qz", 2, 0, 0)],
    "g3": [("s0", "qa", 1, 1, 2), ("s1", "qz", 2, 0, 1), ("s1", "qz", 3, 0, 0), ("s1", "qz", 2, 1, 1), ("s1", "qz", 3, 1, 0), ("s1", "qz", 2, 1, 0)],
    "g5": [("s0", "qa", 0, 1, 1), ("s0", "qb", 1, 0, 3), ("s1", "qa", 1, 1, 2), ("s1", "qz", 3, 1, 1), ("s0", "qz", 1, 1, 0), ("s1", "qz", 2, 0, 0), ("s0", "qb", 0, 1, 1), ("s0", "qz", 1, 0, 1), ("s0", "qb", 0, 1, 0), ("s0", "qb", 1, 0, 1), ("s2", "o", 1, 1), ("s1", "qz", 3, 0, 1), ("s0", "qb", 1, 1, 1), ("s0", "qa", 1, 1, 3), ("s0", "qa", 1, 1, 1), ("s0", "qa", 0, 0, 3), ("s0", "qa", 1, 0, 2), ("s1", "qb", 1, 1, 3), ("s3", "d", 1), ("s2", "o", 1, 0)],
    "i0": [("s1", "qb", 1, 1, 1), ("s3", "d", 3), ("s0", "qa", 1, 0, 3), ("s1", "qa", 1, 1, 3), ("s1", "qz", 1, 1, 0), ("s0", "qa", 1, 0, 1), ("s0", "qb", 0, 1, 2), ("s0", "qa", 0, 1, 0), ("s0", "qz", 1, 0, 0), ("s0", "qa", 0, 0, 0), ("s1", "qa", 1, 0, 2), ("s0", "qb", 0, 1, 3), ("s0", "qz", 1, 1, 1), ("s1", "qb", 1, 1, 2), ("s0", "qb", 1, 1, 0), ("s0", "qa", 1, 1, 0), ("s1", "qb", 1, 0, 1), ("s1", "qa", 1, 1, 1), ("s0", "qa", 0, 0, 2), ("s1", "qz", 1, 0, 0), ("s2", "qa", 1, 2), ("s1", "qz", 1, 1, 1), ("s3", "o", 1), ("s2", "qb", 1, 1), ("s1", "qz", 1, 0, 1), ("s1", "qa", 1, 0, 3), ("s0", "qb", 1, 0, 2), ("s0", "qz", 0, 0, 0), ("s0", "o", 0, 0, 0)],
    "v": [("s1", "qb", 1, 0, 2), ("s1", "qb", 1, 0, 3), ("s2", "qa", 1, 1), ("s2", "qb", 1, 3), ("s2", "qb", 1, 2), ("s0", "qb", 0, 0, 3), ("s0", "qa", 0, 0, 1), ("s0", "qz", 0, 1, 1), ("s2", "qa", 1, 3), ("s0", "qb", 0, 0, 1), ("fin_", "o"), ("s0", "qb", 1, 0, 0), ("s0", "qz", 0, 1, 0), ("s0", "qa", 1, 0, 0), ("s1", "qb", 1, 1, 0), ("s3", "qa", 2), ("s2", "u", 1, 0), ("s1", "qa", 1, 0, 1), ("s0", "qb", 0, 0, 2)],
    "i1": [("s1", "qa", 1, 1, 0), ("s2", "qz", 1, 0), ("s2", "qz", 1, 1), ("s3", "qb", 3), ("s3", "qb", 1), ("s1", "qa", 1, 0, 0)],
    "i2": [("s0", "qb", 0, 0, 0), ("s3", "qa", 1), ("s1", "qb", 1, 0, 0), ("s3", "qa", 3), ("s0", "qz", 0, 0, 1), ("s3", "qb", 2), ("s1", "u", 1, 0, 0), ("fin_", "d"), ("s2", "qb", 1, 0), ("s2", "qa", 1, 0)],
    "i3": [("s3", "qz", 1), ("fin_", "u"), ("fin_", "qa"), ("fin_", "qz"), ("fin_", "qb")],
}


def dg(a,b,d,prec=None): return lax.dot_general(a,b,d,preferred_element_type=F32,precision=prec)


def hooks(i, table):
    for j, evs in table.items():
        if evs:
            @pl.when(i == j)
            def _(evs=evs):
                for e in evs: e()


def qkv_proj(w_ref, bias_ref, xlow_ref, qkv_ref, slots):
    def body(n,_):
        o=pl.multiple_of(n*256,256)
        y=dg(xlow_ref[...], w_ref[pl.ds(o,256),:], NT)
        y=(y+bias_ref[:,pl.ds(o,256)])*jnp.where(o<xlow_ref.shape[1],0.125,1.0)
        qkv_ref[:,pl.ds(o,256)]=y.astype(BF)
        hooks(n, slots)
        return 0
    lax.fori_loop(0, w_ref.shape[0]//256, body, 0)


def rel_rows(tableT_ref, bk_ref, rel_ref):
    nb=tableT_ref.shape[1]; n=bk_ref.shape[1]
    hot=(lax.broadcasted_iota(jnp.int32,(nb,n),0)==bk_ref[...]).astype(F32)
    rel_ref[...]=dg(tableT_ref[...], hot, NN, lax.Precision.HIGHEST)


def bias_expand(row,S):
    R=pltpu.roll(jnp.broadcast_to(row,(128,2*S)), 2*S-127, 1, stride=1, stride_axis=0)
    nu=S//128
    return jnp.concatenate([R[:,128*(nu-1-u):128*(nu-1-u)+S] for u in range(nu)],axis=0)


def diag_sum(t,S):
    nu=S//128
    y=None
    for u in range(nu):
        a=128*(nu-1-u); parts=[]
        if a: parts.append(jnp.zeros((128,a),F32))
        parts.append(t[128*u:128*(u+1),:])
        if 2*S-a-S: parts.append(jnp.zeros((128,2*S-a-S),F32))
        v=jnp.concatenate(parts,axis=1) if len(parts)>1 else parts[0]
        y=v if y is None else y+v
    z=None
    for w in range(16):
        g=y[8*w:8*w+8,:]
        sh=120-8*w
        g=pltpu.roll(g,sh,1) if sh else g
        z=g if z is None else z+g
    out=None
    for b in range(8):
        g=z[b:b+1,:]
        g=pltpu.roll(g,7-b,1) if b<7 else g
        out=g if out is None else out+g
    return out


def attn_fwd(len_ref, qkv_ref, rel_ref, ctx_ref, lse_ref, bias_scr, S, D, slots):
    lane=lax.broadcasted_iota(jnp.int32,(1,128),1)
    col=lax.broadcasted_iota(jnp.int32,(1,S),1)
    def body(p,_):
        o=pl.multiple_of(p*128,128)
        for hh in range(2):
            row=rel_ref[pl.ds(p*2+hh,1),:]
            bias_scr[hh]=bias_expand(row,S)
        for m in range(2):
            q=qkv_ref[m*S:(m+1)*S,pl.ds(o,128)]
            k=qkv_ref[m*S:(m+1)*S,pl.ds(D+o,128)]
            v=qkv_ref[m*S:(m+1)*S,pl.ds(2*D+o,128)]
            valid=col<len_ref[m]
            outs=[]
            for hh in range(2):
                mk=(lane//64)==hh
                qm=jnp.where(mk,q,jnp.zeros_like(q))
                s=dg(qm,k,NT)+bias_scr[hh]
                s=jnp.where(valid,s,-1e30)
                mx=jnp.max(s,axis=1,keepdims=True)
                e=jnp.exp(s-mx)
                tot=jnp.sum(e,axis=1,keepdims=True)
                pl_=(e*(1.0/tot)).astype(BF)
                outs.append(dg(pl_,v,NN))
                lse_ref[m,pl.ds(p*2+hh,1),:]=jnp.transpose(mx+jnp.log(tot),(1,0))
            ctx_ref[m*S:(m+1)*S,pl.ds(o,128)]=jnp.where((lane//64)==0,outs[0],outs[1]).astype(BF)
            hooks(p, {i: slots.get(2*i+m) for i in range(D//128)})
        return 0
    lax.fori_loop(0, D//128, body, 0)


def attn_bwd(len_ref, qkv_ref, dctx_ref, lse_ref, relf_ref, drelf_ref, bias_scr, acc_scr, S, D, slots):
    lane=lax.broadcasted_iota(jnp.int32,(1,128),1)
    rowi=lax.broadcasted_iota(jnp.int32,(S,1),0)
    m0=(lane//64)==0
    def body(p,_):
        o=pl.multiple_of(p*128,128)
        for hh in range(2):
            row=relf_ref[pl.ds(p*2+hh,1),:]
            bias_scr[hh]=bias_expand(row,S)
        for m in range(2):
            q=qkv_ref[m*S:(m+1)*S,pl.ds(o,128)]
            k=qkv_ref[m*S:(m+1)*S,pl.ds(D+o,128)]
            v=qkv_ref[m*S:(m+1)*S,pl.ds(2*D+o,128)]
            do=dctx_ref[m*S:(m+1)*S,pl.ds(o,128)]
            valid=rowi<len_ref[m]
            oq=[];ok=[];ov=[]
            for hh in range(2):
                mk=(lane//64)==hh
                km=jnp.where(mk,k,jnp.zeros_like(k)); vm=jnp.where(mk,v,jnp.zeros_like(v))
                sT=dg(km,q,NT)+bias_scr[hh]
                sT=jnp.where(valid,sT,-1e30)
                pT=jnp.exp(sT-lse_ref[m,pl.ds(p*2+hh,1),:])
                dpT=dg(vm,do,NT)
                rd=jnp.sum(dpT*pT,axis=0,keepdims=True)
                ds=(pT*(dpT-rd)).astype(BF)
                ov.append(dg(pT.astype(BF),do,NN))
                ok.append(dg(ds,q,NN))
                oq.append(dg(ds,k,TN))
                if m==0: acc_scr[hh]=ds.astype(F32)
                else: acc_scr[hh]+=ds.astype(F32)
            qkv_ref[m*S:(m+1)*S,pl.ds(o,128)]=(jnp.where(m0,oq[0],oq[1])*0.125).astype(BF)
            qkv_ref[m*S:(m+1)*S,pl.ds(D+o,128)]=jnp.where(m0,ok[0],ok[1]).astype(BF)
            qkv_ref[m*S:(m+1)*S,pl.ds(2*D+o,128)]=jnp.where(m0,ov[0],ov[1]).astype(BF)
            hooks(p, {i: slots.get(2*i+m) for i in range(D//128)})
        for hh in range(2):
            drelf_ref[pl.ds(p*2+hh,1),:]=diag_sum(acc_scr[hh],S)
        return 0
    lax.fori_loop(0, D//128, body, 0)


def stats(z):
    mu=jnp.mean(z,axis=-1,keepdims=True); c=z-mu
    var=jnp.mean(c*c,axis=-1,keepdims=True)
    r=lax.rsqrt(var+EPS)
    return c*r, r


def fwd_tile(arrive, slot, x_ref, ctx_ref, wo_ref, wu_ref, wd_ref, vec_ref, bup_ref, out_ref, nl_scr, act_scr, gp_scr, z1_scr, z2_scr, r_scr, R):
    D=x_ref.shape[2]; FF=wu_ref.shape[1]
    ctx=ctx_ref[...].reshape(R,D)
    arrive(0)
    fs=x_ref[...].reshape(R,D)+(dg(ctx,wo_ref[...],NT)+vec_ref[0:1,:])
    z1,r1=stats(fs)
    z1_scr[slot]=z1
    fn=z1*vec_ref[1:2,:]+vec_ref[2:3,:]
    nl=fn.astype(BF)
    nl_scr[...]=nl.reshape(nl_scr.shape)
    def body(f,acc):
        o=pl.multiple_of(f*FC,FC)
        u=dg(nl_scr[...].reshape(R,D),wu_ref[:,pl.ds(o,FC)],NN)+bup_ref[:,pl.ds(o,FC)]
        phi=0.5*(1.0+lax.erf(u*(2.0**-0.5)))
        a=(u*phi).astype(BF)
        act_scr[:,:,pl.ds(o,FC)]=a.reshape(2,R//2,FC)
        gp_scr[slot,:,pl.ds(o,FC)]=phi+u*(jnp.exp(u*u*-0.5)*0.3989422804014327)
        return acc+dg(a,wd_ref[:,pl.ds(o,FC)],NT)
    arrive(1)
    arrive(2)
    acc=lax.fori_loop(0,FF//FC,body,fn+vec_ref[3:4,:],unroll=True)
    z2,r2=stats(acc)
    z2_scr[slot]=z2
    r_scr[slot,:,0:1]=r1
    r_scr[slot,:,1:2]=r2
    out_ref[...]=(z2*vec_ref[4:5,:]).reshape(out_ref.shape)


def lnb(u,z,r):
    return r*(u-jnp.mean(u,axis=-1,keepdims=True)-z*jnp.mean(u*z,axis=-1,keepdims=True))


def bwd_tile(slot, ds_ref, cot_ref, wo_ref, wu_ref, wd_ref, vec_ref, dfs_ref, dctx_ref, gv_ref, gbu_ref, dl_scr, ul_scr, al_scr, gp_scr, z1_scr, z2_scr, r_scr, R):
    D=wu_ref.shape[0]; FF=wu_ref.shape[1]; Rh=R//2
    r1=r_scr[slot,:,0:1]; r2=r_scr[slot,:,1:2]
    z2=z2_scr[slot]
    do=cot_ref[...].reshape(R,D)
    ri=lax.broadcasted_iota(jnp.int32,(R,1),0)
    coef=jnp.where(ri==0,ds_ref[0:1,0:1],0.0)+jnp.where(ri==Rh,ds_ref[1:2,0:1],0.0)
    do=do+coef*vec_ref[5:6,:]
    gv_ref[4:5,:]+=jnp.sum(do*z2,axis=0,keepdims=True)
    gv_ref[5:6,:]+=jnp.sum(coef*(z2*vec_ref[4:5,:]),axis=0,keepdims=True)
    d2=lnb(do*vec_ref[4:5,:],z2,r2)
    dl=d2.astype(BF)
    dl_scr[...]=dl.reshape(dl_scr.shape)
    gv_ref[3:4,:]+=jnp.sum(dl.astype(F32),axis=0,keepdims=True)
    def body(f,acc):
        o=pl.multiple_of(f*FC,FC)
        da=dg(dl_scr[...].reshape(R,D),wd_ref[:,pl.ds(o,FC)],NN)
        ul=(da*gp_scr[slot,:,pl.ds(o,FC)]).astype(BF)
        ul_scr[:,:,pl.ds(o,FC)]=ul.reshape(2,R//2,FC)
        gbu_ref[:,pl.ds(o,FC)]+=jnp.sum(ul.astype(F32),axis=0,keepdims=True)
        return acc+dg(ul,wu_ref[:,pl.ds(o,FC)],NT)
    d1=lax.fori_loop(0,FF//FC,body,d2,unroll=True)
    z1=z1_scr[slot]
    gv_ref[1:2,:]+=jnp.sum(d1*z1,axis=0,keepdims=True)
    gv_ref[2:3,:]+=jnp.sum(d1,axis=0,keepdims=True)
    dfs=lnb(d1*vec_ref[1:2,:],z1,r1)
    dfs_ref[...]=dfs.reshape(dfs_ref.shape)
    al=dfs.astype(BF)
    al_scr[...]=al.reshape(al_scr.shape)
    gv_ref[0:1,:]+=jnp.sum(al.astype(F32),axis=0,keepdims=True)
    dctx_ref[...]=dg(al,wo_ref[...],NN).astype(BF).reshape(dctx_ref.shape)


class Geo:
    def __init__(g, C, Q):
        g.C=C; g.Q=Q; g.nx=Q//2; g.nz=min(4,C); g.ny=C//g.nz
        c=lax.axis_index("cand"); q=lax.axis_index("query")
        g.z=c//g.ny; g.y=lax.rem(c,g.ny); g.x=q//2; g.k=lax.rem(q,2)
    def dev(g,z,y,x,k): return {"cand":z*g.ny+y,"query":x*2+k}


def mo(v,n): return pl.multiple_of(v,n)


def barrier(g, peers):
    b=pltpu.get_barrier_semaphore()
    for p in peers: pl.semaphore_signal(b,inc=1,device_id=p,device_id_type=MESH)
    pl.semaphore_wait(b,len(peers))


class RS:
    def __init__(s, g, refs, bufs, ss, rs):
        s.g, s.refs, s.bufs, s.ss, s.rs = g, refs, bufs, ss, rs
        s.partner = g.dev(g.z, g.y, g.x, 1 - g.k)
        s.pend = []
    def dims(s, n): return [NR[d] for d in RORD[n]]
    def own(s, n, rel, k):
        g = s.g
        r = dict(zip(RORD[n], rel))
        return rs_slice(g, n, s.refs, jnp.bitwise_xor(g.z, r["z"]), 1 - g.y if r["y"] else g.y, 1 - g.x if r["x"] else g.x, k)
    def near(s, d, r):
        g = s.g
        return g.dev(jnp.bitwise_xor(g.z, r) if d == "z" else g.z, 1 - g.y if d == "y" else g.y, 1 - g.x if d == "x" else g.x, g.k)
    def copy(s, src, dst, n, i, dev):
        pi = RPIECES.index(n)
        return pltpu.make_async_remote_copy(src, dst, s.ss.at[pi, i], s.rs.at[pi, i], device_id=dev, device_id_type=MESH)
    def c0(s, n, r1, r2, r3):
        _, n2, n3 = s.dims(n)
        return s.copy(s.own(n, (r1, r2, r3), 1 - s.g.k), s.bufs[n][0].at[r1, r2, r3], n, (r1 * n2 + r2) * n3 + r3, s.partner)
    def c1(s, n, r1, r2, r3):
        _, n2, n3 = s.dims(n)
        return s.copy(s.bufs[n][0].at[r1, r2, r3], s.bufs[n][1].at[r1 - 1, r2, r3], n, 16 + ((r1 - 1) * n2 + r2) * n3 + r3, s.near(RORD[n][0], r1))
    def c2(s, n, r2, r3):
        n1, n2, n3 = s.dims(n)
        return s.copy(s.bufs[n][0].at[0, r2, r3], s.bufs[n][2].at[r2 - 1, r3], n, 16 + (n1 - 1) * n2 * n3 + (r2 - 1) * n3 + r3, s.near(RORD[n][1], r2))
    def c3(s, n, r3):
        n1, n2, n3 = s.dims(n)
        return s.copy(s.bufs[n][0].at[0, 0, r3], s.bufs[n][3].at[r3 - 1], n, 16 + (n1 - 1) * n2 * n3 + (n2 - 1) * n3 + r3 - 1, s.near(RORD[n][2], r3))
    def go(s, f, *a):
        f(*a).start()
        s.pend.append(lambda: f(*a))
    def add(s, n, dst, srcs):
        rows, st = RSHP[n][0], RSHP[n][2]
        def body(i, _):
            o = pl.multiple_of(i * st, 16)
            wide = lambda t: t if len(srcs) == 2 else t.astype(F32)
            dst[pl.ds(o, st), :] = functools.reduce(lambda a, b: a + b, [wide(r[pl.ds(o, st), :]) for r in srcs]).astype(dst.dtype)
            return 0
        lax.fori_loop(0, rows // st, body, 0)
    def part1(s, n, r2, r3):
        s.c0(n, 0, r2, r3).wait_recv()
        n1 = s.dims(n)[0]
        for r1 in range(1, n1):
            s.c1(n, r1, r2, r3).wait_recv()
        return [s.own(n, (0, r2, r3), s.g.k), s.bufs[n][0].at[0, r2, r3]] + [s.bufs[n][1].at[r1 - 1, r2, r3] for r1 in range(1, n1)]
    def part2(s, n, r3):
        t = s.part1(n, 0, r3)
        n2 = s.dims(n)[1]
        for r2 in range(1, n2):
            s.c2(n, r2, r3).wait_recv()
        return t + [s.bufs[n][2].at[r2 - 1, r3] for r2 in range(1, n2)]
    def s0(s, n, r1, r2, r3): s.go(s.c0, n, r1, r2, r3)
    def s1(s, n, r1, r2, r3):
        s.c0(n, r1, r2, r3).wait_recv()
        b = s.bufs[n][0].at[r1, r2, r3]
        s.add(n, b, [s.own(n, (r1, r2, r3), s.g.k), b])
        s.go(s.c1, n, r1, r2, r3)
    def s2(s, n, r2, r3):
        s.add(n, s.bufs[n][0].at[0, r2, r3], s.part1(n, r2, r3))
        s.go(s.c2, n, r2, r3)
    def s3(s, n, r3):
        s.add(n, s.bufs[n][0].at[0, 0, r3], s.part2(n, r3))
        s.go(s.c3, n, r3)
    def fin(s, n, dst):
        t = s.part2(n, 0)
        n3 = s.dims(n)[2]
        for r3 in range(1, n3):
            s.c3(n, r3).wait_recv()
        s.add(n, dst, t + [s.bufs[n][3].at[r3 - 1] for r3 in range(1, n3)])
    def fin_(s, n): s.fin(n, s.outs[n])
    def ev(s, e): getattr(s, e[0])(*e[1:])
    def drain(s):
        for c in s.pend: c().wait_send()


def rs_slice(g, n, refs, z, y, x, k):
    wq, wo, wu, wd = refs
    c = z * g.ny + y
    q = x * 2 + k
    if n in QROW:
        return wq.at[pl.ds(mo(c * 288 + k * 144 + QROW[n], 16), RSHP[n][0]), pl.ds(mo(x * 384, 128), 384)]
    if n == "o": return wo.at[pl.ds(mo(c * 96 + k * 48, 16), 48), pl.ds(mo(x * 384, 128), 384)]
    if n == "u": return wu.at[pl.ds(mo(q * 192, 16), 192), pl.ds(mo(c * 384, 128), 384)]
    if n == "d": return wd.at[pl.ds(mo(c * 96, 16), 96), pl.ds(mo(q * 768, 128), 768)]


def rs_bufs():
    out = []
    for n in RPIECES:
        n1, n2, n3 = [NR[d] for d in RORD[n]]
        sh = RSHP[n][:2]
        out += [pltpu.VMEM((n1, n2, n3) + sh, BF), pltpu.VMEM((n1 - 1, n2, n3) + sh, BF), pltpu.VMEM((n2 - 1, n3) + sh, BF), pltpu.VMEM((n3 - 1,) + sh, BF)]
    return out


def attn_fwd_kernel(len_ref, x_ref, w_ref, bias_ref, tab_ref, bk_ref, bkf_ref, xlow_ref, qkv_ref, ctx_ref, lse_ref, relf_ref, rel_ref, bias_scr):
    S, D = x_ref.shape[1:]
    for m in range(2):
        xlow_ref[m*S:(m+1)*S,:]=x_ref[m].astype(BF)
    qkv_proj(w_ref, bias_ref, xlow_ref, qkv_ref, {})
    rel_rows(tab_ref, bk_ref, rel_ref)
    rel_rows(tab_ref, bkf_ref, relf_ref)
    attn_fwd(len_ref, qkv_ref, rel_ref, ctx_ref, lse_ref, bias_scr, S, D, {})


class AG:
    def __init__(s, g, own, refs, ss, rs, cs, cr):
        s.g, s.own_, s.refs, s.ss, s.rs, s.cs, s.cr = g, own, refs, ss, rs, cs, cr
        s.partner = g.dev(g.z, g.y, g.x, 1 - g.k)
        s.pend = []
        s.got = set()
    def dst(s, n, rel, k):
        g = s.g
        r = dict(zip(RORD[n], rel))
        return rs_slice(g, n, s.refs, jnp.bitwise_xor(g.z, r["z"]), 1 - g.y if r["y"] else g.y, 1 - g.x if r["x"] else g.x, k)
    def idx(s, n, rel):
        _, n2, n3 = [NR[d] for d in RORD[n]]
        return (rel[0] * n2 + rel[1]) * n3 + rel[2]
    def src(s, n, rel): return s.own_(n) if rel == (0, 0, 0) else s.dst(n, rel, s.g.k)
    def near(s, d, r):
        g = s.g
        return g.dev(jnp.bitwise_xor(g.z, r) if d == "z" else g.z, 1 - g.y if d == "y" else g.y, 1 - g.x if d == "x" else g.x, g.k)
    def link(s, n, rel, d, k):
        new = tuple(k if a == d else r for a, r in zip(RORD[n], rel))
        pi, i = RPIECES.index(n), s.idx(n, new)
        return pltpu.make_async_remote_copy(s.src(n, rel), s.dst(n, rel, s.g.k), s.ss.at[pi, i], s.rs.at[pi, i], device_id=s.near(d, k), device_id_type=MESH)
    def core(s, n, rel):
        pi, i = RPIECES.index(n), s.idx(n, rel)
        return pltpu.make_async_remote_copy(s.src(n, rel), s.dst(n, rel, s.g.k), s.cs.at[pi, i], s.cr.at[pi, i], device_id=s.partner, device_id_type=MESH)
    def got_core(s, n, rel):
        pi, i = RPIECES.index(n), s.idx(n, rel)
        t = s.dst(n, rel, 1 - s.g.k)
        pltpu.make_async_remote_copy(t, t, s.cs.at[pi, i], s.cr.at[pi, i], device_id=s.partner, device_id_type=MESH).wait_recv()
    def go(s, f, *a):
        f(*a).start()
        s.pend.append(lambda: f(*a))
    def ev(s, e):
        n, rel, outs = e
        if rel != (0, 0, 0):
            t = s.dst(n, rel, s.g.k)
            pi, i = RPIECES.index(n), s.idx(n, rel)
            pltpu.make_async_remote_copy(t, t, s.ss.at[pi, i], s.rs.at[pi, i], device_id=s.partner, device_id_type=MESH).wait_recv()
        for d, k in outs:
            if d == "k": s.go(s.core, n, rel)
            else: s.go(s.link, n, rel, d, k)
    def rels(s, n):
        n1, n2, n3 = [NR[d] for d in RORD[n]]
        return [(a, b, c) for a in range(n1) for b in range(n2) for c in range(n3)]
    def drain(s):
        for c in s.pend: c().wait_send()


def front_kernel(len_ref, x_h, wqf_h, wof_h, wuf_h, wdf_h, *rest, C, Q):
    vins, rest = rest[:11], rest[11:]
    (wq_o, wo, wu, wd, vec_o, bup_o, xlow_o, qkv_o, ctx_ref, lse_ref, relf_ref, bkf_o,
     wqf_ref, wof_ref, wuf_ref, wdf_ref, v_ref, bk_ref, x_v, xlow, qkv, wq, own_p, got_p, h_scr, u_bf, d_bf, vall, tab, rel, qb, bias_scr, ss, rs, cs, cr, vss, vrs, ps, ls) = rest
    g = Geo(C, Q)
    S, D = x_h.shape[1:]
    q_ = lax.axis_index("query")
    peers = [{"query": lax.rem(q_ + j, Q)} for j in range(1, Q)] + [g.dev(g.z, 1 - g.y, g.x, g.k)] + [g.dev(jnp.bitwise_xor(g.z, i), g.y, g.x, g.k) for i in range(1, g.nz)]
    bar = pltpu.get_barrier_semaphore()
    for p in peers:
        pl.semaphore_signal(bar, inc=1, device_id=p, device_id_type=MESH)
    wc = [pltpu.make_async_copy(a, b, ls.at[10 + i]) for i, (a, b) in enumerate(((wqf_h, wqf_ref), (wof_h, wof_ref), (wuf_h, wuf_ref), (wdf_h, wdf_ref)))]
    for c in wc:
        c.start()
    xc = pltpu.make_async_copy(x_h, x_v, ls.at[0])
    xc.start()
    k = g.k
    dq, bq = D // Q, tab.shape[1] // Q
    fq = bup_o.shape[1] // Q
    v_ref[...] = jnp.zeros_like(v_ref)
    for i in range(8):
        v_ref[i:i + 1, 0:dq] = vins[i][...]
    for j in range(fq // 256):
        v_ref[8 + j, :] = vins[8][j * 256:(j + 1) * 256]
    v_ref[16:16 + vins[9].shape[0], 0:bq] = vins[9][...]
    nrel = vins[10].shape[1]
    bk_ref[...] = jnp.full(bk_ref.shape, -1, jnp.int32)
    bk_ref[:, 0:nrel] = vins[10][...]
    for c in wc:
        c.wait()

    def turn(w):
        n = w.shape[1]
        eye = (lax.broadcasted_iota(jnp.int32, (n, n), 0) == lax.broadcasted_iota(jnp.int32, (n, n), 1)).astype(BF)
        return dg(eye, w.astype(BF), NT).astype(BF)
    a, b = turn(wqf_ref[...]), turn(wof_ref[...])
    ha, hb = a.shape[0] // 2, b.shape[0] // 2
    for i in range(2):
        own_p[i, 0:ha, :] = a[i * ha:(i + 1) * ha]
        own_p[i, ha:ha + hb, :] = b[i * hb:(i + 1) * hb]
    d_bf[...] = wdf_ref[...].astype(BF)
    u_bf[...] = wuf_ref[...].astype(BF)
    pl.semaphore_wait(bar, len(peers))
    pc = pltpu.make_async_remote_copy(own_p.at[1 - k], got_p, ps.at[0], ps.at[1], device_id=g.dev(g.z, g.y, g.x, 1 - k), device_id_type=MESH)
    pc.start()
    vcs = []
    for j in range(1, Q):
        c = pltpu.make_async_remote_copy(v_ref, vall.at[q_], vss.at[j - 1], vrs.at[j - 1], device_id={"query": lax.rem(q_ + j, Q)}, device_id_type=MESH)
        c.start()
        vcs.append(c)
    vall[q_] = v_ref[...]

    def own(n):
        if n == "u": return u_bf
        if n == "d": return d_bf
        return h_scr.at[pl.ds(QROW.get(n, 144), RSHP[n][0])]
    A = AG(g, own, (wq, wo, wu, wd), ss, rs, cs, cr)
    loc = [pltpu.make_async_copy(own(n), A.dst(n, (0, 0, 0), k), ls.at[1 + i]) for i, n in enumerate(RPIECES)]

    def after(name):
        for e in AGSLOTS.get(name, []):
            A.ev(e)
    after("b")
    loc[0].start()
    loc[1].start()
    pc.wait()
    t, r = own_p[k], got_p[...]
    @pl.when(k == 0)
    def _(): h_scr[...] = jnp.concatenate([t, r], axis=1)
    @pl.when(k == 1)
    def _(): h_scr[...] = jnp.concatenate([r, t], axis=1)
    for c in loc[2:]:
        c.start()
    after("h")
    xc.wait()
    for m in range(2):
        xlow[m*S:(m+1)*S,:]=x_v[m].astype(BF)
    xo = pltpu.make_async_copy(xlow, xlow_o, ls.at[7])
    xo.start()
    after("p0")
    for c in vcs:
        c.wait()
    qb[...] = jnp.zeros_like(qb)
    vec_o[...] = jnp.zeros_like(vec_o)
    for q in range(Q):
        lo, hi = q * dq, (q + 1) * dq
        qb[:, lo:hi] = vall[q, 0:1, 0:dq]
        qb[:, 2 * D + lo:2 * D + hi] = vall[q, 1:2, 0:dq]
        vec_o[0:6, lo:hi] = vall[q, 2:8, 0:dq]
        for j in range(fq // 256):
            bup_o[:, q * fq + j * 256:q * fq + (j + 1) * 256] = vall[q, 8 + j:9 + j, :]
        tab[:, q * bq:(q + 1) * bq] = vall[q, 16:32, 0:bq]
    after("p1")
    for i, n in enumerate(RPIECES):
        if n in QROW:
            loc[i].wait()
            for r in A.rels(n):
                A.got_core(n, r)
    qkv_proj(wq, qb, xlow, qkv, {i: [functools.partial(A.ev, e) for e in AGSLOTS.get(f"n{i}", [])] for i in range(3 * D // 256)})
    wc = pltpu.make_async_copy(wq, wq_o, ls.at[8])
    qc = pltpu.make_async_copy(qkv, qkv_o, ls.at[9])
    wc.start()
    qc.start()
    ids = jnp.broadcast_to(bk_ref[...], (8, 2 * S)).astype(F32).astype(BF)
    for j in range(2 * S // 256):
        flip = (lax.broadcasted_iota(jnp.int32, (2 * S, 256), 0) + lax.broadcasted_iota(jnp.int32, (2 * S, 256), 1) == nrel - 1 - j * 256).astype(BF)
        bkf_o[:, j * 256:(j + 1) * 256] = dg(ids, flip, NN)[0:1].astype(jnp.int32)
    bkf_o[:, nrel:] = jnp.full((1, 2 * S - nrel), -1, jnp.int32)
    after("r0")
    rel_rows(tab, bk_ref, rel)
    rel_rows(tab, bkf_o, relf_ref)
    after("r1")
    attn_fwd(len_ref, qkv, rel, ctx_ref, lse_ref, bias_scr, S, D, {i: [functools.partial(A.ev, e) for e in AGSLOTS.get(f"t{i}", [])] for i in range(D // 64)})
    for c in (xo, wc, qc):
        c.wait()
    for i, n in enumerate(RPIECES):
        if n not in QROW:
            loc[i].wait()
            for r in A.rels(n):
                A.got_core(n, r)
    A.drain()


def ffn_kernel(lab_ref, x_ref, ctx_ref, cot_ref, wo_h, wu_h, wd_h, vec_ref, bup_ref,
               out_ref, dfs_ref, dctx_ref, nl_ref, act_ref, dl_ref, al_ref, ul_ref, gv_ref, gbu_ref, loss_ref,
               wo_ref, wu_ref, wd_ref, gp_scr, z1_scr, z2_scr, r_scr,
               ws, ds_scr, sc_snd, sc_all, sss, ssr, *, T, R, C, Q):
    i = pl.program_id(0)
    D, FF = wu_ref.shape
    cid = lax.axis_index("cand")

    loads = [pltpu.make_async_copy(a, b, ws.at[j]) for j, (a, b) in enumerate(((wo_h, wo_ref), (wu_h, wu_ref), (wd_h, wd_ref)))]

    def arrive(j):
        @pl.when(i == 0)
        def _(): loads[j].wait()

    def score_copy(j):
        return pltpu.make_async_remote_copy(sc_snd, sc_all.at[cid], sss.at[j - 1], ssr.at[j - 1], device_id={"cand": lax.rem(cid + j, C)}, device_id_type=MESH)

    @pl.when(i == 0)
    def _():
        b = pltpu.get_barrier_semaphore()
        for j in range(1, C):
            pl.semaphore_signal(b, inc=1, device_id={"cand": lax.rem(cid + j, C)}, device_id_type=MESH)
        for c in loads:
            c.start()
        gv_ref[...] = jnp.zeros_like(gv_ref)
        gbu_ref[...] = jnp.zeros_like(gbu_ref)
        ds_scr[...] = jnp.zeros_like(ds_scr)
        sc_snd[...] = jnp.zeros_like(sc_snd)

    @pl.when(i < T)
    def _():
        fwd_tile(arrive, jnp.minimum(i, 1), x_ref, ctx_ref, wo_ref, wu_ref, wd_ref, vec_ref, bup_ref, out_ref, nl_ref, act_ref, gp_scr, z1_scr, z2_scr, r_scr, R)

    @pl.when(i == 0)
    def _():
        for m in range(2):
            sc = jnp.sum(out_ref[m, 0:1, :] * vec_ref[5:6, :], axis=1, keepdims=True)
            sc_snd[m:m + 1, :] = jnp.broadcast_to(sc, (1, 128))
        sc_all[cid] = sc_snd[...]
        pl.semaphore_wait(pltpu.get_barrier_semaphore(), C - 1)
        for j in range(1, C):
            score_copy(j).start()

    @pl.when(i == T)
    def _():
        for j in range(1, C):
            score_copy(j).wait()
        total = jnp.zeros((1, 128), F32)
        own = sc_snd[...]
        for m in range(2):
            rows = [sc_all[j, m:m + 1, :] for j in range(C)]
            peak = functools.reduce(jnp.maximum, rows)
            lse = peak + jnp.log(functools.reduce(lambda a, b: a + b, [jnp.exp(r - peak) for r in rows]))
            lab = lab_ref[m]
            picked = functools.reduce(lambda a, b: a + b, [jnp.where(lab == j, r, 0.0) for j, r in enumerate(rows)])
            total = total + (lse - picked)
            ds_scr[m:m + 1, :] = (jnp.exp(own[m:m + 1, :] - lse) - jnp.where(lab == cid, 1.0, 0.0)) * (1.0 / Q)
        loss_ref[...] = jnp.broadcast_to(jnp.where(cid == 0, total * (1.0 / Q), 0.0), (8, 128))

    @pl.when((i >= 1) & (i <= T))
    def _():
        t = lax.rem(i, T)
        bwd_tile(jnp.minimum(t, 1), ds_scr, cot_ref, wo_ref, wu_ref, wd_ref, vec_ref, dfs_ref, dctx_ref, gv_ref, gbu_ref, dl_ref, ul_ref, al_ref, gp_scr, z1_scr, z2_scr, r_scr, R)


class VecSum:
    def __init__(s, C, Q, src, va, snd, rcv, qs, qr, rs, rr):
        s.C, s.Q, s.src, s.va, s.snd, s.rcv, s.qs, s.qr, s.rs, s.rr = C, Q, src, va, snd, rcv, qs, qr, rs, rr
        s.c, s.q = lax.axis_index("cand"), lax.axis_index("query")
        s.rounds = C.bit_length() - 1
    def qcopy(s, j):
        to = lax.rem(s.q + j, s.Q)
        return pltpu.make_async_remote_copy(s.src.at[to], s.va.at[s.q], s.qs.at[j - 1], s.qr.at[j - 1], device_id={"query": to}, device_id_type=MESH)
    def rcopy(s, i):
        return pltpu.make_async_remote_copy(s.snd.at[i], s.rcv.at[i], s.rs.at[i], s.rr.at[i], device_id={"cand": jnp.bitwise_xor(s.c, 1 << i)}, device_id_type=MESH)
    def start(s):
        for j in range(1, s.Q):
            s.qcopy(j).start()
        s.va[s.q] = s.src[s.q]
    def take(s, i):
        if i == 0:
            for j in range(1, s.Q):
                s.qcopy(j).wait()
            return functools.reduce(lambda a, b: a + b, [s.va[j] for j in range(s.Q)])
        s.rcopy(i - 1).wait()
        return s.snd[i - 1] + s.rcv[i - 1]
    def step(s, i):
        s.snd[i] = s.take(i)
        s.rcopy(i).start()
    def finish(s, dst):
        dst[...] = s.take(s.rounds)


def back_kernel(len_ref, nl_h, dl_h, al_h, ctx_h, act_h, ul_h, qkv_h, dctx_h, xlow_h, wq_h, dfs_h, lse_ref, relf, bkf_ref, gv_ref, gbu_ref, loss_ref,
                *rest, C, Q, fast):
    if fast:
        ig_h, p_out, u_out, d_out, ve_out, vl_out = rest[:6]
        scr = rest[6:]
    else:
        ig_h, gq_o, go_o, gu_o, gd_o, gb_o, gtab_o = rest[:7]
        scr = rest[7:]
    (nl, dl, al, ctx, ch, qkv, dctx, xlow, wq, dfs, igt, gq, go, gu, gd, drelf, bias_scr, acc_scr, gb, gtab, ls, cs_, os_) = scr[:23]
    NS, D = nl.shape
    FF = gu.shape[1]
    S = NS // 2
    NZ = FF // 768
    load = lambda i, src, dst: pltpu.make_async_copy(src, dst, ls.at[i])
    big = [load(0, nl_h, nl), load(1, dl_h, dl), load(2, al_h, al), load(3, ctx_h, ctx), load(4, qkv_h, qkv), load(5, dctx_h, dctx),
           load(6, xlow_h, xlow), load(7, wq_h, wq), load(8, dfs_h, dfs)]
    if fast:
        g = Geo(C, Q)

    def offs(d, i):
        if not fast: c = i
        elif d: c = jnp.bitwise_xor(g.x, 1 - i // 2) * 2 + jnp.bitwise_xor(g.k, 1 - lax.rem(i, 2))
        else: c = jnp.bitwise_xor(g.z, 3 - i)
        return pl.multiple_of(c * 768, 128)

    def chunk(d, i):
        return pltpu.make_async_copy((act_h if d else ul_h).at[:, pl.ds(offs(d, i), 768)], ch.at[lax.rem(i, 2)], cs_.at[lax.rem(i, 2)])
    if fast:
        peers = [{"query": lax.rem(lax.axis_index("query") + j, Q)} for j in range(1, Q)] + [{"cand": jnp.bitwise_xor(lax.axis_index("cand"), j)} for j in (1, 2, 4, 6)]
        bar = pltpu.get_barrier_semaphore()
        for p in peers:
            pl.semaphore_signal(bar, inc=1, device_id=p, device_id_type=MESH)
    for c in (big[0], chunk(0, jnp.int32(0)), big[2], big[3], chunk(0, jnp.int32(1)), big[1]):
        c.start()
    if fast:
        bufs = {n: scr[23 + 4 * i:27 + 4 * i] for i, n in enumerate(RPIECES)}
        h_scr, e_snd, e_rcv, ve, vea, ves, ver, vl, vla, vls, vlr, ss, rs, es, qs, qr, cs, cr = scr[23 + NB:]
        R = RS(g, (gq, go, gu, gd), bufs, ss, rs)
        R.outs = {n: h_scr.at[pl.ds(QROW.get(n, 144), RSHP[n][0])] for n in ("qa", "qb", "qz", "o")}
        R.outs.update(u=u_out, d=d_out)
        dq, fq, bq = D // Q, FF // Q, gtab.shape[1] // Q
        early = VecSum(C, Q, ve, vea, ves, ver, qs.at[0], qr.at[0], cs.at[0], cr.at[0])
        late = VecSum(C, Q, vl, vla, vls, vlr, qs.at[1], qr.at[1], cs.at[1], cr.at[1])
        ve[...] = jnp.zeros_like(ve)
        vl[...] = jnp.zeros_like(vl)
        for q in range(Q):
            ve[q, 0:6, 0:dq] = gv_ref[0:6, q * dq:(q + 1) * dq]
            for j in range(fq // 256):
                ve[q, 6 + j:7 + j, :] = gbu_ref[:, q * fq + j * 256:q * fq + (j + 1) * 256]
            ve[q, 9:10, 0:128] = loss_ref[0:1, :]
        vec_at = {"o": early.start, "u3": functools.partial(early.step, 0), "d1": functools.partial(early.step, 1), "d3": functools.partial(early.step, 2),
                  "i1": functools.partial(late.step, 0), "i2": functools.partial(late.step, 1), "i3": functools.partial(late.step, 2)}

    def after(name):
        if name == "v":
            late_vectors()
            late.start()
        if fast:
            for e in SLOTS.get(name, []):
                R.ev(e)
            if name in vec_at:
                vec_at[name]()
    big[0].wait()

    def table(names):
        return {i: [functools.partial(after, n) for n in t] for i, t in enumerate(names)} if fast else {}

    def up(i, _):
        chunk(0, i).wait()
        gu[:, pl.ds(offs(0, i), 768)] = dg(nl[...], ch[lax.rem(i, 2)], TN).astype(BF)
        @pl.when(i < NZ - 2)
        def _(): chunk(0, i + 2).start()
        @pl.when(i >= NZ - 2)
        def _(): chunk(1, i + 2 - NZ).start()
        @pl.when(i == 0)
        def _():
            if fast:
                pl.semaphore_wait(bar, len(peers))
            after("u0")
            big[2].wait()
            big[3].wait()
            go[...] = dg(al[...], ctx[...], TN).astype(BF)
            after("o")
        hooks(i, table([(), ("u1",), ("u2",), ("u3",)]))
        return 0
    lax.fori_loop(0, NZ, up, 0)
    big[1].wait()
    big[4].start()
    big[5].start()

    def down(i, _):
        chunk(1, i).wait()
        gd[:, pl.ds(offs(1, i), 768)] = dg(dl[...], ch[lax.rem(i, 2)], TN).astype(BF)
        @pl.when(i < NZ - 2)
        def _(): chunk(1, i + 2).start()
        @pl.when(i == 2)
        def _():
            for c in big[6:]:
                c.start()
        hooks(i, table([("d0",), ("d1",), ("d2",), ("d3",)]))
        return 0
    lax.fori_loop(0, NZ, down, 0)
    slots = {}
    if fast:
        for i in range(2 * (D // 128)):
            slots[i] = [functools.partial(R.ev, e) for e in SLOTS.get(f"t{i}", [])]
    drelf[...] = jnp.zeros_like(drelf)
    big[4].wait()
    big[5].wait()
    attn_bwd(len_ref, qkv, dctx, lse_ref, relf, drelf, bias_scr, acc_scr, S, D, slots)
    big[6].wait()

    half = 3 * D // 2
    zh = g.z // 2 if fast else 0

    def b1(n, _):
        o = pl.multiple_of(jnp.where(n < 3, 1 - zh, zh) * half + lax.rem(n, 3) * 384, 128)
        t = qkv[:, pl.ds(o, 384)]
        gq[pl.ds(o, 384), :] = dg(t, xlow[...], TN).astype(BF)
        gb[:, pl.ds(o, 384)] = jnp.sum(t.astype(F32), axis=0, keepdims=True)
        hooks(n, {i: [functools.partial(R.ev, e) for e in SLOTS.get(f"g{i}", [])] for i in range(6)} if fast else {})
        return 0
    lax.fori_loop(0, 6, b1, 0)
    big[7].wait()
    big[8].wait()
    steps = NS // 256
    outc = lambda r: pltpu.make_async_copy(igt.at[lax.rem(r, 2)], ig_h.at[pl.ds(pl.multiple_of(r * 256, 256), 256), :], os_.at[lax.rem(r, 2)])

    def late_vectors():
        nb, nn = gtab.shape[1], bkf_ref.shape[1]
        hot = (lax.broadcasted_iota(jnp.int32, (nb, nn), 0) == bkf_ref[...]).astype(F32).astype(BF)
        part, total = drelf[...], None
        for _ in range(3):
            low = part.astype(BF)
            part = part - low.astype(F32)
            term = dg(low, hot, NT)
            total = term if total is None else total + term
        gtab[...] = total
        if fast:
            for q in range(Q):
                vl[q, 0:1, 0:dq] = gb[:, q * dq:(q + 1) * dq]
                vl[q, 1:2, 0:dq] = gb[:, 2 * D + q * dq:2 * D + (q + 1) * dq]
                for h in range(HEADS):
                    vl[q, 2 + h // 4:3 + h // 4, h % 4 * bq:(h % 4 + 1) * bq] = gtab[h:h + 1, q * bq:(q + 1) * bq]

    def rows(r, _):
        o = pl.multiple_of(r * 256, 256)
        @pl.when(r >= 2)
        def _(): outc(r - 2).wait()
        igt[lax.rem(r, 2)] = dfs[pl.ds(o, 256), :] + dg(qkv[pl.ds(o, 256), :], wq[...], NN)
        outc(r).start()
        hooks(r, table([("i0", "v"), ("i1",), ("i2",), ("i3",)]))
        return 0
    lax.fori_loop(0, steps, rows, 0)
    if not fast:
        late_vectors()
    for r in range(max(0, steps - 2), steps):
        outc(jnp.int32(r)).wait()
    if fast:
        k = g.k
        lo = h_scr[:, 0:192]
        hi = h_scr[:, 192:384]
        e_snd[...] = jnp.where(k == 0, hi, lo)
        c = pltpu.make_async_remote_copy(e_snd, e_rcv, es.at[0], es.at[1], device_id=R.partner, device_id_type=MESH)
        c.start()
        p_out[k] = jnp.where(k == 0, lo, hi)
        c.wait()
        p_out[1 - k] = e_rcv[...]
        early.finish(ve_out)
        late.finish(vl_out)
        R.drain()
    else:
        gq_o[...] = gq[...]
        go_o[...] = go[...]
        gu_o[...] = gu[...]
        gd_o[...] = gd[...]
        gb_o[...] = gb[...]
        gtab_o[...] = gtab[...]


def finish_kernel(out_h, ig_h, u_h, d_h, p_h, ve_h, vl_h, out_o, ig_o, gu_o, gd_o, gq_o, go_o, *rest):
    vec_o, bup_o, tab_o, loss_o = rest[:8], rest[8], rest[9], rest[10]
    buf, ub, db, p_ref, ve_ref, vl_ref, si, so = rest[11:]
    n, rows = buf.shape[0] // 2, buf.shape[1]
    part = lambda h, i: h.at[pl.ds(i * rows, rows), :]
    small = [pltpu.make_async_copy(a, b, si.at[2 * n + i]) for i, (a, b) in enumerate(((p_h, p_ref), (ve_h, ve_ref), (vl_h, vl_ref)))]
    src = [(u_h, ub, gu_o), (d_h, db, gd_o)]
    ins = [pltpu.make_async_copy(a, b, si.at[2 * n + 3 + i]) for i, (a, b, _) in enumerate(src)]
    outs = [pltpu.make_async_copy(b, c, so.at[2 * n + i]) for i, (_, b, c) in enumerate(src)]
    for i in range(n):
        for j, (h, o) in enumerate(((out_h, out_o), (ig_h, ig_o))):
            k = 2 * i + j
            ins.append(pltpu.make_async_copy(part(h, i), buf.at[k], si.at[k]))
            outs.append(pltpu.make_async_copy(buf.at[k], part(o, i), so.at[k]))
    for c in small + ins:
        c.start()
    for c in small:
        c.wait()
    ha = gq_o.shape[1] // 2
    gq_o[...] = jnp.concatenate([p_ref[0, 0:ha, :], p_ref[1, 0:ha, :]], axis=0).T
    go_o[...] = jnp.concatenate([p_ref[0, ha:, :], p_ref[1, ha:, :]], axis=0).T
    for i in range(8):
        m = vec_o[i].shape[1]
        vec_o[i][...] = vl_ref[i:i + 1, 0:m] if i < 2 else ve_ref[i - 2:i - 1, 0:m]
    for j in range(bup_o.shape[0] // 256):
        bup_o[j * 256:(j + 1) * 256] = ve_ref[6 + j, :]
    loss_o[0] = ve_ref[9, 0]
    bq = tab_o.shape[1]
    for h in range(HEADS):
        tab_o[h:h + 1, :] = vl_ref[2 + h // 4:3 + h // 4, h % 4 * bq:(h % 4 + 1) * bq]
    for a, b in zip(ins, outs):
        a.wait()
        b.start()
    for c in outs:
        c.wait()


def sds(shape, dtype=F32):
    return jax.ShapeDtypeStruct(shape, dtype)


def back_scratch(fast, C, Q, NS=1024, S=512, D=768, FF=3072, NBK=256):
    v = pltpu.VMEM
    dma = pltpu.SemaphoreType.DMA
    scr = [v((NS, D), BF)] * 4 + [v((2, NS, 768), BF), v((NS, 3 * D), BF), v((NS, D), BF), v((NS, D), BF), v((3 * D, D), BF), v((NS, D), F32), v((2, 256, D), F32),
                                  v((3 * D, D), BF), v((D, D), BF), v((D, FF), BF), v((D, FF), BF), v((16, 2 * S), F32),
                                  v((2, S, S), F32), v((2, S, S), F32), v((1, 3 * D), F32), v((16, NBK), F32), dma((9,)), dma((2,)), dma((2,))]
    if fast:
        scr += rs_bufs() + [v((192, 384), F32), v((192, 192), F32), v((192, 192), F32), v((Q, 16, 256), F32), v((Q, 16, 256), F32), v((3, 16, 256), F32), v((3, 16, 256), F32),
                v((Q, 8, 256), F32), v((Q, 8, 256), F32), v((3, 8, 256), F32), v((3, 8, 256), F32),
                            dma((len(RPIECES), 31)), dma((len(RPIECES), 31)), dma((2,)), dma((2, Q)), dma((2, Q)), dma((2, 3)), dma((2, 3))]
    return scr


def body(hidden_in, out_cotangent, lengths, labels, buckets, w_qkv, w_out, w_up, w_down, bias_q, bias_v, bias_out,
         norm1_gain, norm1_bias, bias_up, bias_down, norm2_gain, score_vector, rel_table):
    Q = lax.axis_size("query")
    C = lax.axis_size("cand")
    micro = hidden_in.shape[0]
    S, D = hidden_in.shape[3:]
    FF = w_up.shape[1] * C
    NBK = rel_table.shape[0] * Q
    dq, fq, bq = D // Q, FF // Q, NBK // Q
    fast = Q == 4 and C == 8 and D == 768 and FF == 3072
    x = hidden_in.reshape(micro, S, D)
    cot = out_cotangent.reshape(micro, S, D)
    lens = lengths.reshape(micro)
    labs = labels.reshape(micro)
    NS = micro * S
    v = pltpu.VMEM
    dma = pltpu.SemaphoreType.DMA
    eight = [bias_q, bias_v, bias_out, norm1_gain, norm1_bias, bias_down, norm2_gain, score_vector]
    if fast:
        np_ = len(RPIECES)
        wq, wo, wu, wd, vec, bup, xlow, qkv, ctx, lse, relf, bkf = pl.pallas_call(
            functools.partial(front_kernel, C=C, Q=Q), in_specs=[SM] + [ANY] * 5 + [VM] * 11, out_specs=[ANY] * 4 + [VM] * 2 + [ANY] * 2 + [VM] * 4,
            out_shape=[sds((3 * D, D), BF), sds((D, D), BF), sds((D, FF), BF), sds((D, FF), BF), sds((8, D)), sds((1, FF)), sds((NS, D), BF), sds((NS, 3 * D), BF),
                       sds((NS, D), BF), sds((micro, 16, S)), sds((16, 2 * S)), sds((1, 2 * S), jnp.int32)],
            scratch_shapes=[v(w_qkv.shape, F32), v(w_out.shape, F32), v(w_up.shape, F32), v(w_down.shape[::-1], F32), v((32, 256), F32), v((1, 2 * S), jnp.int32),
                            v((micro, S, D), F32), v((NS, D), BF), v((NS, 3 * D), BF), v((3 * D, D), BF), v((2, 192, 192), BF), v((192, 192), BF), v((192, 384), BF),
                            v((192, 384), BF), v((96, 768), BF), v((Q, 32, 256), F32), v((16, NBK), F32), v((16, 2 * S), F32), v((1, 3 * D), F32), v((2, S, S), F32)]
            + [dma((np_, 16))] * 4 + [dma((Q,))] * 2 + [dma((2,)), dma((14,))],
            compiler_params=pltpu.CompilerParams(collective_id=0, has_side_effects=True, vmem_limit_bytes=67043328),
        )(lens, x, w_qkv, w_out, w_up, w_down.T, *[t.reshape(1, -1) for t in eight], bias_up, rel_table.T, buckets.reshape(1, -1))
    else:
        bk = jnp.pad(buckets, (0, 1), constant_values=-1)[None, :]
        bkf = jnp.pad(buckets[::-1], (0, 1), constant_values=-1)[None, :]
        def gather(w):
            part = lax.all_gather(w.astype(BF), "query", axis=0, tiled=True)
            return lax.all_gather(part, "cand", axis=1, tiled=True)
        wq, wo, wu, wd = gather(w_qkv).T, gather(w_out).T, gather(w_up), gather(w_down).T
        vall = lax.all_gather(jnp.concatenate(eight + [bias_up, rel_table.reshape(-1)]), "query", axis=0, tiled=False)
        vecs = vall[:, :8 * dq].reshape(Q, 8, dq).transpose(1, 0, 2).reshape(8, D)
        bup = vall[:, 8 * dq:8 * dq + fq].reshape(1, FF)
        tab = jnp.pad(vall[:, 8 * dq + fq:].reshape(NBK, HEADS).T, ((0, 4), (0, 0)))
        qkv_bias = jnp.concatenate([vecs[0:1], jnp.zeros((1, D), F32), vecs[1:2]], axis=1)
        vec = jnp.concatenate([vecs[2:], jnp.zeros((2, D), F32)], axis=0)
        xlow, qkv, ctx, lse, relf = pl.pallas_call(
            attn_fwd_kernel, in_specs=[SM] + [VM] * 6, out_specs=[VM] * 5,
            out_shape=[sds((NS, D), BF), sds((NS, 3 * D), BF), sds((NS, D), BF), sds((micro, 16, S)), sds((16, 2 * S))],
            scratch_shapes=[v((16, 2 * S), F32), v((2, S, S), F32)],
            compiler_params=pltpu.CompilerParams(vmem_limit_bytes=60 * 2**20))(lens, x, wq, qkv_bias, tab, bk, bkf)
    R = 256
    Rh, T = R // micro, NS // R
    tb = lambda im, n=D: pl.BlockSpec((micro, Rh, n), im)
    fw = lambda i: (0, jnp.minimum(i, T - 1), 0)
    bw = lambda i: (0, lax.rem(jnp.maximum(i, 1), T), 0)
    tok = lambda n, dt=BF: sds((micro, S, n), dt)
    out, dfs, dctx, nl, act, dl, al, ul, gv, gbu, lossv = pl.pallas_call(
        functools.partial(ffn_kernel, T=T, R=R, C=C, Q=Q), grid=(T + 1,),
        in_specs=[SM, tb(fw), tb(fw), tb(bw)] + [ANY] * 3 + [VM] * 2, out_specs=[tb(fw), tb(bw), tb(bw), tb(fw), tb(fw, FF), tb(bw), tb(bw), tb(bw, FF)] + [VM] * 3,
        out_shape=[tok(D, F32), tok(D, F32), tok(D), tok(D), tok(FF), tok(D), tok(D), tok(FF), sds((8, D)), sds((1, FF)), sds((8, 128))],
        scratch_shapes=[v((D, D), BF), v((D, FF), BF), v((D, FF), BF), pltpu.VMEM((2, R, FF), F32), pltpu.VMEM((2, R, D), F32), pltpu.VMEM((2, R, D), F32), pltpu.VMEM((2, R, 128), F32), dma((3,)),
                        pltpu.VMEM((8, 128), F32), pltpu.VMEM((8, 128), F32), pltpu.VMEM((C, 8, 128), F32), pltpu.SemaphoreType.DMA((C,)), pltpu.SemaphoreType.DMA((C,))],
        compiler_params=pltpu.CompilerParams(collective_id=1, has_side_effects=True, vmem_limit_bytes=67043328),
    )(labs, x, ctx.reshape(micro, S, D), cot, wo, wu, wd, vec, bup)
    flat = lambda t: t.reshape(NS, t.shape[-1])
    gouts = [sds((2, 192, 192)), sds((192, 384)), sds((96, 768)), sds((16, 256)), sds((8, 256))] if fast else \
        [sds((3 * D, D), BF), sds((D, D), BF), sds((D, FF), BF), sds((D, FF), BF), sds((1, 3 * D)), sds((16, NBK))]
    res = pl.pallas_call(
        functools.partial(back_kernel, C=C, Q=Q, fast=fast), in_specs=[SM] + [ANY] * 11 + [VM] * 6, out_specs=[ANY] + [VM] * len(gouts),
        out_shape=[sds((NS, D))] + gouts, scratch_shapes=back_scratch(fast, C, Q, NS, S, D, FF, NBK),
        compiler_params=pltpu.CompilerParams(collective_id=2 if fast else None, has_side_effects=True, vmem_limit_bytes=67043328),
    )(lens, flat(nl), flat(dl), flat(al), ctx, flat(act), flat(ul), qkv, flat(dctx), xlow, wq, flat(dfs), lse, relf, bkf, gv, gbu, lossv)
    ig = res[0]
    if fast:
        pg, ug, dng, ve, vl = res[1:]
        fin = pl.pallas_call(
            finish_kernel, in_specs=[ANY] * 7, out_specs=[ANY] * 4 + [VM] * 12 + [SM],
            out_shape=[sds((NS, D)), sds((NS, D)), sds(w_up.shape), sds(w_down.shape[::-1]), sds(w_qkv.shape), sds(w_out.shape)] + [sds((1, dq))] * 8
            + [sds((fq,)), sds((HEADS, bq)), sds((1,))],
            scratch_shapes=[v((8, NS // 4, D), F32), v(ug.shape, F32), v(dng.shape, F32), v(pg.shape, F32), v(ve.shape, F32), v(vl.shape, F32), dma((13,)), dma((10,))],
            compiler_params=pltpu.CompilerParams(vmem_limit_bytes=67043328))(flat(out), ig, ug, dng, pg, ve, vl)
        out, ig, g_up, g_down, g_qkv, g_out = fin[:6]
        g_down = g_down.T
        small = [t.reshape(dq) for t in fin[6:14]]
        g_bup, g_tab, loss = fin[14], fin[15].T, fin[16].reshape(())
    else:
        def scatter(g):
            rows, cols = g.shape[0] // Q, g.shape[1] // C
            tiles = g.astype(F32).reshape(Q, rows, C, cols).transpose(2, 0, 1, 3).reshape(C * Q, rows, cols)
            return lax.psum_scatter(tiles, ("cand", "query"), scatter_dimension=0, tiled=True)[0]
        gq, go, gu, gd, gb, gtab = res[1:]
        g_qkv, g_out, g_up, g_down = scatter(gq.T), scatter(go.T), scatter(gu), scatter(gd.T)
        gvecs = jnp.concatenate([gb[:, :D], gb[:, 2 * D:], gv[:6]], axis=0)
        vg = jnp.concatenate([gvecs.reshape(8, Q, dq).transpose(1, 0, 2).reshape(Q, 8 * dq), gbu.reshape(Q, fq), gtab[:HEADS].T.reshape(Q, bq * HEADS),
                              jnp.broadcast_to(lossv[0:1, 0:1], (Q, 1))], axis=1)
        vg = jnp.pad(vg, ((0, 0), (0, -vg.shape[1] % 1024)))
        vs = lax.psum_scatter(lax.psum(vg, "cand"), "query", scatter_dimension=0, tiled=True)[0]
        small = [vs[i * dq:(i + 1) * dq] for i in range(8)]
        g_bup = vs[8 * dq:8 * dq + fq]
        g_tab = vs[8 * dq + fq:8 * dq + fq + bq * HEADS].reshape(bq, HEADS)
        loss = vs[8 * dq + fq + bq * HEADS]
    return (out.reshape(hidden_in.shape), ig.reshape(hidden_in.shape), g_qkv, g_out, g_up, g_down,
            small[0], small[1], small[2], small[3], small[4], g_bup, small[5], small[6], small[7], g_tab, loss)


def solution(mesh):
    seq, w, v = P(None, "query", "cand", None, None), P("query", "cand"), P("query")
    return jax.shard_map(
        body, mesh=mesh,
        in_specs=(seq, seq, P(None, "query", "cand"), P(None, "query"), P(), w, w, w, w) + (v,) * 9 + (P("query", None),),
        out_specs=(seq, seq, w, w, w, w) + (v,) * 9 + (P("query", None), P()),
        check_vma=False)
```

```python
import functools

import jax
import jax.numpy as jnp
from jax import lax
from jax.experimental import pallas as pl
from jax.experimental.pallas import tpu as pltpu
from jax.sharding import PartitionSpec as P

F32 = jnp.float32
BF = jnp.bfloat16
NT = (((1,), (1,)), ((), ()))
NN = (((1,), (0,)), ((), ()))
TN = (((0,), (0,)), ((), ()))
VM = pl.BlockSpec(memory_space=pltpu.VMEM)
SM = pl.BlockSpec(memory_space=pltpu.SMEM)
ANY = pl.BlockSpec(memory_space=pl.ANY)
MESH = pl.DeviceIdType.MESH
EPS = 1e-5
FC = 1536
HEADS = 12
NR = {"x": 2, "y": 2, "z": 4}
RPIECES = ["u", "d", "o", "qa", "qb", "qz"]
RORD = {"u": "yxz", "d": "xyz", "o": "zyx", "qa": "yxz", "qb": "xyz", "qz": "zyx"}
RSHP = {"u": (192, 384, 192), "d": (96, 768, 96), "o": (48, 384, 48), "qa": (64, 384, 64), "qb": (64, 384, 64), "qz": (16, 384, 16)}
QROW = {"qa": 0, "qb": 64, "qz": 128}
NB = 4 * len(RPIECES)
AGSLOTS = {
    "b": [("d", (0, 0, 0), (("y", 1),)), ("u", (0, 0, 0), (("x", 1),))],
    "h": [("qb", (0, 0, 0), (("z", 3),)), ("qa", (0, 0, 0), (("z", 1),)), ("qb", (0, 0, 0), (("y", 1),)), ("u", (0, 0, 0), (("y", 1),)), ("qa", (0, 0, 0), (("y", 1), ("x", 1))), ("qz", (0, 0, 0), (("z", 2), ("x", 1))), ("d", (0, 0, 0), (("x", 1),)), ("qb", (0, 0, 0), (("z", 2),)), ("qb", (0, 1, 0), (("x", 1), ("k", 0))), ("qa", (0, 0, 1), (("x", 1), ("y", 1), ("k", 0))), ("qz", (2, 0, 0), (("k", 0),)), ("qa", (0, 0, 0), (("z", 3),)), ("qz", (0, 0, 0), (("z", 3),)), ("qb", (0, 0, 0), (("z", 1),)), ("qa", (0, 0, 0), (("z", 2),)), ("qz", (0, 0, 0), (("k", 0),)), ("qz", (0, 0, 1), (("y", 1), ("z", 1), ("z", 2), ("z", 3), ("k", 0))), ("o", (0, 0, 0), (("x", 1),)), ("qb", (0, 0, 3), (("y", 1), ("x", 1), ("k", 0))), ("qz", (0, 0, 0), (("y", 1),)), ("qb", (0, 0, 0), (("x", 1),)), ("qa", (0, 1, 0), (("y", 1), ("k", 0))), ("qb", (0, 0, 1), (("y", 1), ("x", 1), ("k", 0))), ("qz", (0, 0, 0), (("z", 1),)), ("qz", (0, 1, 0), (("z", 1), ("z", 2), ("z", 3), ("k", 0))), ("qz", (0, 1, 1), (("z", 1), ("z", 2), ("z", 3), ("k", 0))), ("d", (0, 0, 0), (("k", 0),)), ("qa", (0, 0, 3), (("x", 1), ("y", 1), ("k", 0))), ("qa", (0, 0, 2), (("x", 1), ("y", 1), ("k", 0))), ("qb", (0, 0, 2), (("y", 1), ("x", 1), ("k", 0))), ("qa", (0, 1, 1), (("y", 1), ("k", 0))), ("qz", (2, 0, 1), (("k", 0),)), ("qz", (1, 0, 0), (("k", 0),)), ("d", (0, 0, 0), (("z", 3),)), ("u", (0, 0, 0), (("z", 1),)), ("qb", (0, 0, 0), (("k", 0),)), ("qa", (0, 1, 3), (("y", 1), ("k", 0))), ("qa", (1, 1, 0), (("k", 0),)), ("qb", (0, 1, 3), (("x", 1), ("k", 0))), ("d", (0, 0, 0), (("z", 1),))],
    "p0": [("qz", (1, 0, 1), (("k", 0),)), ("u", (0, 0, 0), (("z", 3),)), ("qa", (1, 0, 1), (("k", 0),)), ("qb", (1, 0, 1), (("k", 0),)), ("qz", (2, 1, 1), (("k", 0),)), ("qb", (0, 1, 1), (("x", 1), ("k", 0))), ("qz", (1, 1, 0), (("k", 0),)), ("qb", (0, 1, 2), (("x", 1), ("k", 0))), ("u", (0, 0, 0), (("k", 0),)), ("qz", (2, 1, 0), (("k", 0),)), ("qa", (1, 0, 2), (("k", 0),)), ("qa", (1, 0, 0), (("k", 0),)), ("qa", (0, 1, 2), (("y", 1), ("k", 0))), ("o", (0, 0, 0), (("z", 3), ("y", 1))), ("qb", (1, 0, 3), (("k", 0),)), ("qz", (3, 1, 1), (("k", 0),)), ("u", (1, 0, 0), (("k", 0),)), ("qz", (3, 1, 0), (("k", 0),)), ("qz", (3, 0, 1), (("k", 0),)), ("o", (0, 0, 0), (("z", 1),)), ("u", (0, 1, 0), (("y", 1), ("k", 0))), ("qa", (1, 0, 3), (("k", 0),))],
    "p1": [("d", (0, 1, 0), (("x", 1), ("k", 0))), ("qa", (0, 0, 0), (("k", 0),)), ("qa", (1, 1, 2), (("k", 0),)), ("qa", (1, 1, 1), (("k", 0),)), ("qb", (1, 1, 2), (("k", 0),)), ("qz", (1, 1, 1), (("k", 0),)), ("qa", (1, 1, 3), (("k", 0),)), ("qb", (1, 1, 3), (("k", 0),)), ("qz", (3, 0, 0), (("k", 0),)), ("qb", (1, 1, 1), (("k", 0),)), ("qb", (1, 0, 2), (("k", 0),)), ("qb", (1, 0, 0), (("k", 0),)), ("qb", (1, 1, 0), (("k", 0),))],
    "n0": [("d", (0, 0, 3), (("y", 1), ("x", 1), ("k", 0))), ("u", (0, 0, 0), (("z", 2),))],
    "n4": [("u", (0, 0, 1), (("x", 1), ("y", 1), ("k", 0)))],
    "n5": [("d", (0, 0, 1), (("y", 1), ("x", 1), ("k", 0))), ("u", (1, 1, 0), (("k", 0),))],
    "n7": [("d", (0, 0, 0), (("z", 2),))],
    "n8": [("d", (1, 0, 0), (("k", 0),))],
    "r0": [("u", (0, 1, 1), (("y", 1), ("k", 0))), ("u", (0, 0, 3), (("x", 1), ("y", 1), ("k", 0)))],
    "r1": [("d", (1, 0, 1), (("k", 0),)), ("d", (0, 1, 3), (("x", 1), ("k", 0)))],
    "t0": [("d", (1, 1, 0), (("k", 0),)), ("o", (3, 0, 0), (("k", 0),)), ("d", (1, 0, 3), (("k", 0),)), ("u", (0, 0, 2), (("x", 1), ("y", 1), ("k", 0)))],
    "t1": [("o", (0, 0, 1), (("y", 1), ("z", 1), ("z", 2), ("z", 3), ("k", 0))), ("o", (0, 1, 0), (("z", 1), ("z", 2), ("z", 3), ("k", 0)))],
    "t2": [("d", (0, 1, 1), (("x", 1), ("k", 0))), ("d", (0, 0, 2), (("y", 1), ("x", 1), ("k", 0))), ("u", (1, 0, 3), (("k", 0),))],
    "t4": [("o", (0, 0, 0), (("k", 0),)), ("o", (0, 1, 1), (("z", 1), ("z", 2), ("z", 3), ("k", 0))), ("u", (0, 1, 2), (("y", 1), ("k", 0)))],
    "t6": [("u", (1, 1, 1), (("k", 0),)), ("d", (0, 1, 2), (("x", 1), ("k", 0))), ("o", (1, 0, 1), (("k", 0),)), ("u", (0, 1, 3), (("y", 1), ("k", 0))), ("u", (1, 0, 2), (("k", 0),)), ("o", (0, 0, 0), (("z", 2),))],
    "t8": [("o", (1, 0, 0), (("k", 0),)), ("u", (1, 1, 2), (("k", 0),))],
    "t9": [("o", (1, 1, 1), (("k", 0),)), ("d", (1, 0, 2), (("k", 0),)), ("u", (1, 0, 1), (("k", 0),)), ("o", (3, 0, 1), (("k", 0),)), ("o", (2, 0, 1), (("k", 0),)), ("o", (1, 1, 0), (("k", 0),)), ("d", (1, 1, 3), (("k", 0),)), ("d", (1, 1, 1), (("k", 0),)), ("o", (2, 1, 0), (("k", 0),)), ("o", (3, 1, 0), (("k", 0),)), ("o", (2, 1, 1), (("k", 0),))],
    "t10": [("d", (1, 1, 2), (("k", 0),)), ("o", (3, 1, 1), (("k", 0),)), ("u", (1, 1, 3), (("k", 0),)), ("o", (2, 0, 0), (("k", 0),))],
}
SLOTS = {
    "o": [("s0", "u", 1, 1, 3)],
    "u1": [("s0", "u", 1, 0, 2), ("s0", "o", 3, 1, 1)],
    "u2": [("s0", "o", 1, 1, 0), ("s0", "o", 1, 0, 0), ("s0", "u", 1, 0, 3), ("s1", "u", 1, 1, 3), ("s0", "u", 1, 1, 1), ("s0", "o", 3, 0, 0), ("s0", "o", 3, 1, 0)],
    "u3": [("s0", "o", 0, 1, 1), ("s0", "o", 2, 0, 1)],
    "d0": [("s1", "o", 1, 1, 0), ("s1", "u", 1, 0, 2), ("s0", "o", 2, 1, 0), ("s0", "u", 1, 1, 2), ("s1", "o", 2, 0, 1), ("s0", "u", 0, 1, 3)],
    "d1": [("s0", "u", 0, 0, 3), ("s1", "u", 1, 0, 3), ("s0", "d", 1, 1, 0), ("s0", "o", 3, 0, 1), ("s0", "d", 1, 1, 2), ("s1", "u", 1, 1, 2)],
    "d3": [("s2", "u", 1, 3), ("s1", "o", 3, 1, 1), ("s0", "o", 0, 0, 1), ("s0", "u", 0, 1, 2), ("s0", "d", 1, 0, 2), ("s0", "u", 1, 0, 1), ("s1", "d", 1, 1, 2), ("s0", "d", 0, 0, 1), ("s0", "u", 0, 0, 1)],
    "t0": [("s1", "o", 2, 1, 0), ("s0", "d", 0, 1, 0), ("s1", "o", 3, 0, 0), ("s0", "o", 2, 1, 1), ("s0", "d", 1, 0, 3), ("s0", "d", 1, 1, 1), ("s0", "o", 2, 0, 0), ("s1", "u", 1, 1, 1)],
    "t1": [("s1", "o", 3, 1, 0), ("s0", "d", 0, 1, 2), ("s0", "d", 0, 0, 3), ("s3", "u", 3), ("s0", "u", 0, 0, 2), ("s1", "o", 2, 1, 1), ("s1", "o", 2, 0, 0), ("s1", "d", 1, 0, 2), ("s1", "o", 3, 0, 1), ("s0", "o", 1, 1, 1)],
    "t2": [("s2", "u", 1, 2), ("s0", "o", 1, 0, 1)],
    "t3": [("s0", "u", 1, 1, 0), ("s1", "o", 1, 1, 1), ("s1", "d", 1, 1, 0), ("s0", "d", 1, 1, 3)],
    "t5": [("s1", "u", 1, 0, 1), ("s1", "d", 1, 1, 1), ("s1", "o", 1, 0, 1), ("s0", "u", 0, 1, 1), ("s1", "d", 1, 1, 3)],
    "t6": [("s0", "d", 1, 0, 0), ("s0", "d", 1, 0, 1), ("s0", "d", 0, 0, 0), ("s2", "d", 1, 2), ("s0", "d", 0, 1, 1), ("s0", "u", 0, 0, 0), ("s0", "d", 0, 0, 2), ("s1", "u", 1, 1, 0), ("s2", "u", 1, 1), ("s3", "u", 2)],
    "t8": [("s2", "d", 1, 1)],
    "t9": [("s2", "d", 1, 0), ("s1", "d", 1, 0, 1), ("s3", "d", 2)],
    "t10": [("s0", "d", 0, 1, 3), ("s1", "d", 1, 0, 3), ("s1", "o", 1, 0, 0)],
    "t11": [("s0", "o", 0, 1, 0), ("s3", "u", 1), ("s0", "u", 0, 1, 0)],
    "g0": [("s1", "d", 1, 0, 0)],
    "g2": [("s0", "qz", 2, 0, 1), ("s0", "qz", 3, 1, 0), ("s0", "qz", 3, 0, 0), ("s0", "qz", 2, 1, 1), ("s0", "qz", 2, 1, 0), ("s0", "qa", 0, 1, 2), ("s0", "u", 1, 0, 0), ("s0", "qz", 3, 1, 1), ("s2", "d", 1, 3), ("s0", "qa", 0, 1, 3), ("s0", "qb", 1, 1, 3), ("s0", "qz", 3, 0, 1), ("s0", "qb", 1, 1, 2), ("s0", "qz", 2, 0, 0)],
    "g3": [("s0", "qa", 1, 1, 2), ("s1", "qz", 2, 0, 1), ("s1", "qz", 3, 0, 0), ("s1", "qz", 2, 1, 1), ("s1", "qz", 3, 1, 0), ("s1", "qz", 2, 1, 0)],
    "g5": [("s0", "qa", 0, 1, 1), ("s0", "qb", 1, 0, 3), ("s1", "qa", 1, 1, 2), ("s1", "qz", 3, 1, 1), ("s0", "qz", 1, 1, 0), ("s1", "qz", 2, 0, 0), ("s0", "qb", 0, 1, 1), ("s0", "qz", 1, 0, 1), ("s0", "qb", 0, 1, 0), ("s0", "qb", 1, 0, 1), ("s2", "o", 1, 1), ("s1", "qz", 3, 0, 1), ("s0", "qb", 1, 1, 1), ("s0", "qa", 1, 1, 3), ("s0", "qa", 1, 1, 1), ("s0", "qa", 0, 0, 3), ("s0", "qa", 1, 0, 2), ("s1", "qb", 1, 1, 3), ("s3", "d", 1), ("s2", "o", 1, 0)],
    "i0": [("s1", "qb", 1, 1, 1), ("s3", "d", 3), ("s0", "qa", 1, 0, 3), ("s1", "qa", 1, 1, 3), ("s1", "qz", 1, 1, 0), ("s0", "qa", 1, 0, 1), ("s0", "qb", 0, 1, 2), ("s0", "qa", 0, 1, 0), ("s0", "qz", 1, 0, 0), ("s0", "qa", 0, 0, 0), ("s1", "qa", 1, 0, 2), ("s0", "qb", 0, 1, 3), ("s0", "qz", 1, 1, 1), ("s1", "qb", 1, 1, 2), ("s0", "qb", 1, 1, 0), ("s0", "qa", 1, 1, 0), ("s1", "qb", 1, 0, 1), ("s1", "qa", 1, 1, 1), ("s0", "qa", 0, 0, 2), ("s1", "qz", 1, 0, 0), ("s2", "qa", 1, 2), ("s1", "qz", 1, 1, 1), ("s3", "o", 1), ("s2", "qb", 1, 1), ("s1", "qz", 1, 0, 1), ("s1", "qa", 1, 0, 3), ("s0", "qb", 1, 0, 2), ("s0", "qz", 0, 0, 0), ("s0", "o", 0, 0, 0)],
    "v": [("s1", "qb", 1, 0, 2), ("s1", "qb", 1, 0, 3), ("s2", "qa", 1, 1), ("s2", "qb", 1, 3), ("s2", "qb", 1, 2), ("s0", "qb", 0, 0, 3), ("s0", "qa", 0, 0, 1), ("s0", "qz", 0, 1, 1), ("s2", "qa", 1, 3), ("s0", "qb", 0, 0, 1), ("fin_", "o"), ("s0", "qb", 1, 0, 0), ("s0", "qz", 0, 1, 0), ("s0", "qa", 1, 0, 0), ("s1", "qb", 1, 1, 0), ("s3", "qa", 2), ("s2", "u", 1, 0), ("s1", "qa", 1, 0, 1), ("s0", "qb", 0, 0, 2)],
    "i1": [("s1", "qa", 1, 1, 0), ("s2", "qz", 1, 0), ("s2", "qz", 1, 1), ("s3", "qb", 3), ("s3", "qb", 1), ("s1", "qa", 1, 0, 0)],
    "i2": [("s0", "qb", 0, 0, 0), ("s3", "qa", 1), ("s1", "qb", 1, 0, 0), ("s3", "qa", 3), ("s0", "qz", 0, 0, 1), ("s3", "qb", 2), ("s1", "u", 1, 0, 0), ("fin_", "d"), ("s2", "qb", 1, 0), ("s2", "qa", 1, 0)],
    "i3": [("s3", "qz", 1), ("fin_", "u"), ("fin_", "qa"), ("fin_", "qz"), ("fin_", "qb")],
}


def dg(a,b,d,prec=None): return lax.dot_general(a,b,d,preferred_element_type=F32,precision=prec)


def hooks(i, table):
    for j, evs in table.items():
        if evs:
            @pl.when(i == j)
            def _(evs=evs):
                for e in evs: e()


def qkv_proj(w_ref, bias_ref, xlow_ref, qkv_ref, slots):
    def body(n,_):
        o=pl.multiple_of(n*256,256)
        y=dg(xlow_ref[...], w_ref[pl.ds(o,256),:], NT)
        y=(y+bias_ref[:,pl.ds(o,256)])*jnp.where(o<xlow_ref.shape[1],0.125,1.0)
        qkv_ref[:,pl.ds(o,256)]=y.astype(BF)
        hooks(n, slots)
        return 0
    lax.fori_loop(0, w_ref.shape[0]//256, body, 0)


def rel_rows(tableT_ref, bk_ref, rel_ref):
    nb=tableT_ref.shape[1]; n=bk_ref.shape[1]
    hot=(lax.broadcasted_iota(jnp.int32,(nb,n),0)==bk_ref[...]).astype(F32)
    rel_ref[...]=dg(tableT_ref[...], hot, NN, lax.Precision.HIGHEST)


def bias_expand(row,S):
    R=pltpu.roll(jnp.broadcast_to(row,(128,2*S)), 2*S-127, 1, stride=1, stride_axis=0)
    nu=S//128
    return jnp.concatenate([R[:,128*(nu-1-u):128*(nu-1-u)+S] for u in range(nu)],axis=0)


def diag_sum(t,S):
    nu=S//128
    y=None
    for u in range(nu):
        a=128*(nu-1-u); parts=[]
        if a: parts.append(jnp.zeros((128,a),F32))
        parts.append(t[128*u:128*(u+1),:])
        if 2*S-a-S: parts.append(jnp.zeros((128,2*S-a-S),F32))
        v=jnp.concatenate(parts,axis=1) if len(parts)>1 else parts[0]
        y=v if y is None else y+v
    z=None
    for w in range(16):
        g=y[8*w:8*w+8,:]
        sh=120-8*w
        g=pltpu.roll(g,sh,1) if sh else g
        z=g if z is None else z+g
    out=None
    for b in range(8):
        g=z[b:b+1,:]
        g=pltpu.roll(g,7-b,1) if b<7 else g
        out=g if out is None else out+g
    return out


def attn_fwd(len_ref, qkv_ref, rel_ref, ctx_ref, lse_ref, bias_scr, S, D, slots):
    lane=lax.broadcasted_iota(jnp.int32,(1,128),1)
    col=lax.broadcasted_iota(jnp.int32,(1,S),1)
    def body(p,_):
        o=pl.multiple_of(p*128,128)
        for hh in range(2):
            row=rel_ref[pl.ds(p*2+hh,1),:]
            bias_scr[hh]=bias_expand(row,S)
        for m in range(2):
            q=qkv_ref[m*S:(m+1)*S,pl.ds(o,128)]
            k=qkv_ref[m*S:(m+1)*S,pl.ds(D+o,128)]
            v=qkv_ref[m*S:(m+1)*S,pl.ds(2*D+o,128)]
            valid=col<len_ref[m]
            outs=[]
            for hh in range(2):
                mk=(lane//64)==hh
                qm=jnp.where(mk,q,jnp.zeros_like(q))
                s=dg(qm,k,NT)+bias_scr[hh]
                s=jnp.where(valid,s,-1e30)
                mx=jnp.max(s,axis=1,keepdims=True)
                e=jnp.exp(s-mx)
                tot=jnp.sum(e,axis=1,keepdims=True)
                pl_=(e*(1.0/tot)).astype(BF)
                outs.append(dg(pl_,v,NN))
                lse_ref[m,pl.ds(p*2+hh,1),:]=jnp.transpose(mx+jnp.log(tot),(1,0))
            ctx_ref[m*S:(m+1)*S,pl.ds(o,128)]=jnp.where((lane//64)==0,outs[0],outs[1]).astype(BF)
            hooks(p, {i: slots.get(2*i+m) for i in range(D//128)})
        return 0
    lax.fori_loop(0, D//128, body, 0)


def attn_bwd(len_ref, qkv_ref, dctx_ref, lse_ref, relf_ref, drelf_ref, bias_scr, acc_scr, S, D, slots):
    lane=lax.broadcasted_iota(jnp.int32,(1,128),1)
    rowi=lax.broadcasted_iota(jnp.int32,(S,1),0)
    m0=(lane//64)==0
    def body(p,_):
        o=pl.multiple_of(p*128,128)
        for hh in range(2):
            row=relf_ref[pl.ds(p*2+hh,1),:]
            bias_scr[hh]=bias_expand(row,S)
        for m in range(2):
            q=qkv_ref[m*S:(m+1)*S,pl.ds(o,128)]
            k=qkv_ref[m*S:(m+1)*S,pl.ds(D+o,128)]
            v=qkv_ref[m*S:(m+1)*S,pl.ds(2*D+o,128)]
            do=dctx_ref[m*S:(m+1)*S,pl.ds(o,128)]
            valid=rowi<len_ref[m]
            oq=[];ok=[];ov=[]
            for hh in range(2):
                mk=(lane//64)==hh
                km=jnp.where(mk,k,jnp.zeros_like(k)); vm=jnp.where(mk,v,jnp.zeros_like(v))
                sT=dg(km,q,NT)+bias_scr[hh]
                sT=jnp.where(valid,sT,-1e30)
                pT=jnp.exp(sT-lse_ref[m,pl.ds(p*2+hh,1),:])
                dpT=dg(vm,do,NT)
                rd=jnp.sum(dpT*pT,axis=0,keepdims=True)
                ds=(pT*(dpT-rd)).astype(BF)
                ov.append(dg(pT.astype(BF),do,NN))
                ok.append(dg(ds,q,NN))
                oq.append(dg(ds,k,TN))
                if m==0: acc_scr[hh]=ds.astype(F32)
                else: acc_scr[hh]+=ds.astype(F32)
            qkv_ref[m*S:(m+1)*S,pl.ds(o,128)]=(jnp.where(m0,oq[0],oq[1])*0.125).astype(BF)
            qkv_ref[m*S:(m+1)*S,pl.ds(D+o,128)]=jnp.where(m0,ok[0],ok[1]).astype(BF)
            qkv_ref[m*S:(m+1)*S,pl.ds(2*D+o,128)]=jnp.where(m0,ov[0],ov[1]).astype(BF)
            hooks(p, {i: slots.get(2*i+m) for i in range(D//128)})
        for hh in range(2):
            drelf_ref[pl.ds(p*2+hh,1),:]=diag_sum(acc_scr[hh],S)
        return 0
    lax.fori_loop(0, D//128, body, 0)


def stats(z):
    mu=jnp.mean(z,axis=-1,keepdims=True); c=z-mu
    var=jnp.mean(c*c,axis=-1,keepdims=True)
    r=lax.rsqrt(var+EPS)
    return c*r, r


def fwd_tile(arrive, slot, x_ref, ctx_ref, wo_ref, wu_ref, wd_ref, vec_ref, bup_ref, out_ref, nl_scr, act_scr, gp_scr, z1_scr, z2_scr, r_scr, R):
    D=x_ref.shape[2]; FF=wu_ref.shape[1]
    ctx=ctx_ref[...].reshape(R,D)
    arrive(0)
    fs=x_ref[...].reshape(R,D)+(dg(ctx,wo_ref[...],NT)+vec_ref[0:1,:])
    z1,r1=stats(fs)
    z1_scr[slot]=z1
    fn=z1*vec_ref[1:2,:]+vec_ref[2:3,:]
    nl=fn.astype(BF)
    nl_scr[...]=nl.reshape(nl_scr.shape)
    def body(f,acc):
        o=pl.multiple_of(f*FC,FC)
        u=dg(nl_scr[...].reshape(R,D),wu_ref[:,pl.ds(o,FC)],NN)+bup_ref[:,pl.ds(o,FC)]
        phi=0.5*(1.0+lax.erf(u*(2.0**-0.5)))
        a=(u*phi).astype(BF)
        act_scr[:,:,pl.ds(o,FC)]=a.reshape(2,R//2,FC)
        gp_scr[slot,:,pl.ds(o,FC)]=phi+u*(jnp.exp(u*u*-0.5)*0.3989422804014327)
        return acc+dg(a,wd_ref[:,pl.ds(o,FC)],NT)
    arrive(1)
    arrive(2)
    acc=lax.fori_loop(0,FF//FC,body,fn+vec_ref[3:4,:],unroll=True)
    z2,r2=stats(acc)
    z2_scr[slot]=z2
    r_scr[slot,:,0:1]=r1
    r_scr[slot,:,1:2]=r2
    out_ref[...]=(z2*vec_ref[4:5,:]).reshape(out_ref.shape)


def lnb(u,z,r):
    return r*(u-jnp.mean(u,axis=-1,keepdims=True)-z*jnp.mean(u*z,axis=-1,keepdims=True))


def bwd_tile(slot, ds_ref, cot_ref, wo_ref, wu_ref, wd_ref, vec_ref, dfs_ref, dctx_ref, gv_ref, gbu_ref, dl_scr, ul_scr, al_scr, gp_scr, z1_scr, z2_scr, r_scr, R):
    D=wu_ref.shape[0]; FF=wu_ref.shape[1]; Rh=R//2
    r1=r_scr[slot,:,0:1]; r2=r_scr[slot,:,1:2]
    z2=z2_scr[slot]
    do=cot_ref[...].reshape(R,D)
    ri=lax.broadcasted_iota(jnp.int32,(R,1),0)
    coef=jnp.where(ri==0,ds_ref[0:1,0:1],0.0)+jnp.where(ri==Rh,ds_ref[1:2,0:1],0.0)
    do=do+coef*vec_ref[5:6,:]
    gv_ref[4:5,:]+=jnp.sum(do*z2,axis=0,keepdims=True)
    gv_ref[5:6,:]+=jnp.sum(coef*(z2*vec_ref[4:5,:]),axis=0,keepdims=True)
    d2=lnb(do*vec_ref[4:5,:],z2,r2)
    dl=d2.astype(BF)
    dl_scr[...]=dl.reshape(dl_scr.shape)
    gv_ref[3:4,:]+=jnp.sum(dl.astype(F32),axis=0,keepdims=True)
    def body(f,acc):
        o=pl.multiple_of(f*FC,FC)
        da=dg(dl_scr[...].reshape(R,D),wd_ref[:,pl.ds(o,FC)],NN)
        ul=(da*gp_scr[slot,:,pl.ds(o,FC)]).astype(BF)
        ul_scr[:,:,pl.ds(o,FC)]=ul.reshape(2,R//2,FC)
        gbu_ref[:,pl.ds(o,FC)]+=jnp.sum(ul.astype(F32),axis=0,keepdims=True)
        return acc+dg(ul,wu_ref[:,pl.ds(o,FC)],NT)
    d1=lax.fori_loop(0,FF//FC,body,d2,unroll=True)
    z1=z1_scr[slot]
    gv_ref[1:2,:]+=jnp.sum(d1*z1,axis=0,keepdims=True)
    gv_ref[2:3,:]+=jnp.sum(d1,axis=0,keepdims=True)
    dfs=lnb(d1*vec_ref[1:2,:],z1,r1)
    dfs_ref[...]=dfs.reshape(dfs_ref.shape)
    al=dfs.astype(BF)
    al_scr[...]=al.reshape(al_scr.shape)
    gv_ref[0:1,:]+=jnp.sum(al.astype(F32),axis=0,keepdims=True)
    dctx_ref[...]=dg(al,wo_ref[...],NN).astype(BF).reshape(dctx_ref.shape)


class Geo:
    def __init__(g, C, Q):
        g.C=C; g.Q=Q; g.nx=Q//2; g.nz=min(4,C); g.ny=C//g.nz
        c=lax.axis_index("cand"); q=lax.axis_index("query")
        g.z=c//g.ny; g.y=lax.rem(c,g.ny); g.x=q//2; g.k=lax.rem(q,2)
    def dev(g,z,y,x,k): return {"cand":z*g.ny+y,"query":x*2+k}


def mo(v,n): return pl.multiple_of(v,n)


def barrier(g, peers):
    b=pltpu.get_barrier_semaphore()
    for p in peers: pl.semaphore_signal(b,inc=1,device_id=p,device_id_type=MESH)
    pl.semaphore_wait(b,len(peers))


class RS:
    def __init__(s, g, refs, bufs, ss, rs):
        s.g, s.refs, s.bufs, s.ss, s.rs = g, refs, bufs, ss, rs
        s.partner = g.dev(g.z, g.y, g.x, 1 - g.k)
        s.pend = []
    def dims(s, n): return [NR[d] for d in RORD[n]]
    def own(s, n, rel, k):
        g = s.g
        r = dict(zip(RORD[n], rel))
        return rs_slice(g, n, s.refs, jnp.bitwise_xor(g.z, r["z"]), 1 - g.y if r["y"] else g.y, 1 - g.x if r["x"] else g.x, k)
    def near(s, d, r):
        g = s.g
        return g.dev(jnp.bitwise_xor(g.z, r) if d == "z" else g.z, 1 - g.y if d == "y" else g.y, 1 - g.x if d == "x" else g.x, g.k)
    def copy(s, src, dst, n, i, dev):
        pi = RPIECES.index(n)
        return pltpu.make_async_remote_copy(src, dst, s.ss.at[pi, i], s.rs.at[pi, i], device_id=dev, device_id_type=MESH)
    def c0(s, n, r1, r2, r3):
        _, n2, n3 = s.dims(n)
        return s.copy(s.own(n, (r1, r2, r3), 1 - s.g.k), s.bufs[n][0].at[r1, r2, r3], n, (r1 * n2 + r2) * n3 + r3, s.partner)
    def c1(s, n, r1, r2, r3):
        _, n2, n3 = s.dims(n)
        return s.copy(s.bufs[n][0].at[r1, r2, r3], s.bufs[n][1].at[r1 - 1, r2, r3], n, 16 + ((r1 - 1) * n2 + r2) * n3 + r3, s.near(RORD[n][0], r1))
    def c2(s, n, r2, r3):
        n1, n2, n3 = s.dims(n)
        return s.copy(s.bufs[n][0].at[0, r2, r3], s.bufs[n][2].at[r2 - 1, r3], n, 16 + (n1 - 1) * n2 * n3 + (r2 - 1) * n3 + r3, s.near(RORD[n][1], r2))
    def c3(s, n, r3):
        n1, n2, n3 = s.dims(n)
        return s.copy(s.bufs[n][0].at[0, 0, r3], s.bufs[n][3].at[r3 - 1], n, 16 + (n1 - 1) * n2 * n3 + (n2 - 1) * n3 + r3 - 1, s.near(RORD[n][2], r3))
    def go(s, f, *a):
        f(*a).start()
        s.pend.append(lambda: f(*a))
    def add(s, n, dst, srcs):
        rows, st = RSHP[n][0], RSHP[n][2]
        def body(i, _):
            o = pl.multiple_of(i * st, 16)
            wide = lambda t: t if len(srcs) == 2 else t.astype(F32)
            dst[pl.ds(o, st), :] = functools.reduce(lambda a, b: a + b, [wide(r[pl.ds(o, st), :]) for r in srcs]).astype(dst.dtype)
            return 0
        lax.fori_loop(0, rows // st, body, 0)
    def part1(s, n, r2, r3):
        s.c0(n, 0, r2, r3).wait_recv()
        n1 = s.dims(n)[0]
        for r1 in range(1, n1):
            s.c1(n, r1, r2, r3).wait_recv()
        return [s.own(n, (0, r2, r3), s.g.k), s.bufs[n][0].at[0, r2, r3]] + [s.bufs[n][1].at[r1 - 1, r2, r3] for r1 in range(1, n1)]
    def part2(s, n, r3):
        t = s.part1(n, 0, r3)
        n2 = s.dims(n)[1]
        for r2 in range(1, n2):
            s.c2(n, r2, r3).wait_recv()
        return t + [s.bufs[n][2].at[r2 - 1, r3] for r2 in range(1, n2)]
    def s0(s, n, r1, r2, r3): s.go(s.c0, n, r1, r2, r3)
    def s1(s, n, r1, r2, r3):
        s.c0(n, r1, r2, r3).wait_recv()
        b = s.bufs[n][0].at[r1, r2, r3]
        s.add(n, b, [s.own(n, (r1, r2, r3), s.g.k), b])
        s.go(s.c1, n, r1, r2, r3)
    def s2(s, n, r2, r3):
        s.add(n, s.bufs[n][0].at[0, r2, r3], s.part1(n, r2, r3))
        s.go(s.c2, n, r2, r3)
    def s3(s, n, r3):
        s.add(n, s.bufs[n][0].at[0, 0, r3], s.part2(n, r3))
        s.go(s.c3, n, r3)
    def fin(s, n, dst):
        t = s.part2(n, 0)
        n3 = s.dims(n)[2]
        for r3 in range(1, n3):
            s.c3(n, r3).wait_recv()
        s.add(n, dst, t + [s.bufs[n][3].at[r3 - 1] for r3 in range(1, n3)])
    def fin_(s, n): s.fin(n, s.outs[n])
    def ev(s, e): getattr(s, e[0])(*e[1:])
    def drain(s):
        for c in s.pend: c().wait_send()


def rs_slice(g, n, refs, z, y, x, k):
    wq, wo, wu, wd = refs
    c = z * g.ny + y
    q = x * 2 + k
    if n in QROW:
        return wq.at[pl.ds(mo(c * 288 + k * 144 + QROW[n], 16), RSHP[n][0]), pl.ds(mo(x * 384, 128), 384)]
    if n == "o": return wo.at[pl.ds(mo(c * 96 + k * 48, 16), 48), pl.ds(mo(x * 384, 128), 384)]
    if n == "u": return wu.at[pl.ds(mo(q * 192, 16), 192), pl.ds(mo(c * 384, 128), 384)]
    if n == "d": return wd.at[pl.ds(mo(c * 96, 16), 96), pl.ds(mo(q * 768, 128), 768)]


def rs_bufs():
    out = []
    for n in RPIECES:
        n1, n2, n3 = [NR[d] for d in RORD[n]]
        sh = RSHP[n][:2]
        out += [pltpu.VMEM((n1, n2, n3) + sh, BF), pltpu.VMEM((n1 - 1, n2, n3) + sh, BF), pltpu.VMEM((n2 - 1, n3) + sh, BF), pltpu.VMEM((n3 - 1,) + sh, BF)]
    return out


def attn_fwd_kernel(len_ref, x_ref, w_ref, bias_ref, tab_ref, bk_ref, bkf_ref, xlow_ref, qkv_ref, ctx_ref, lse_ref, relf_ref, rel_ref, bias_scr):
    S, D = x_ref.shape[1:]
    for m in range(2):
        xlow_ref[m*S:(m+1)*S,:]=x_ref[m].astype(BF)
    qkv_proj(w_ref, bias_ref, xlow_ref, qkv_ref, {})
    rel_rows(tab_ref, bk_ref, rel_ref)
    rel_rows(tab_ref, bkf_ref, relf_ref)
    attn_fwd(len_ref, qkv_ref, rel_ref, ctx_ref, lse_ref, bias_scr, S, D, {})


class AG:
    def __init__(s, g, own, refs, ss, rs, cs, cr):
        s.g, s.own_, s.refs, s.ss, s.rs, s.cs, s.cr = g, own, refs, ss, rs, cs, cr
        s.partner = g.dev(g.z, g.y, g.x, 1 - g.k)
        s.pend = []
        s.got = set()
    def dst(s, n, rel, k):
        g = s.g
        r = dict(zip(RORD[n], rel))
        return rs_slice(g, n, s.refs, jnp.bitwise_xor(g.z, r["z"]), 1 - g.y if r["y"] else g.y, 1 - g.x if r["x"] else g.x, k)
    def idx(s, n, rel):
        _, n2, n3 = [NR[d] for d in RORD[n]]
        return (rel[0] * n2 + rel[1]) * n3 + rel[2]
    def src(s, n, rel): return s.own_(n) if rel == (0, 0, 0) else s.dst(n, rel, s.g.k)
    def near(s, d, r):
        g = s.g
        return g.dev(jnp.bitwise_xor(g.z, r) if d == "z" else g.z, 1 - g.y if d == "y" else g.y, 1 - g.x if d == "x" else g.x, g.k)
    def link(s, n, rel, d, k):
        new = tuple(k if a == d else r for a, r in zip(RORD[n], rel))
        pi, i = RPIECES.index(n), s.idx(n, new)
        return pltpu.make_async_remote_copy(s.src(n, rel), s.dst(n, rel, s.g.k), s.ss.at[pi, i], s.rs.at[pi, i], device_id=s.near(d, k), device_id_type=MESH)
    def core(s, n, rel):
        pi, i = RPIECES.index(n), s.idx(n, rel)
        return pltpu.make_async_remote_copy(s.src(n, rel), s.dst(n, rel, s.g.k), s.cs.at[pi, i], s.cr.at[pi, i], device_id=s.partner, device_id_type=MESH)
    def got_core(s, n, rel):
        pi, i = RPIECES.index(n), s.idx(n, rel)
        t = s.dst(n, rel, 1 - s.g.k)
        pltpu.make_async_remote_copy(t, t, s.cs.at[pi, i], s.cr.at[pi, i], device_id=s.partner, device_id_type=MESH).wait_recv()
    def go(s, f, *a):
        f(*a).start()
        s.pend.append(lambda: f(*a))
    def ev(s, e):
        n, rel, outs = e
        if rel != (0, 0, 0):
            t = s.dst(n, rel, s.g.k)
            pi, i = RPIECES.index(n), s.idx(n, rel)
            pltpu.make_async_remote_copy(t, t, s.ss.at[pi, i], s.rs.at[pi, i], device_id=s.partner, device_id_type=MESH).wait_recv()
        for d, k in outs:
            if d == "k": s.go(s.core, n, rel)
            else: s.go(s.link, n, rel, d, k)
    def rels(s, n):
        n1, n2, n3 = [NR[d] for d in RORD[n]]
        return [(a, b, c) for a in range(n1) for b in range(n2) for c in range(n3)]
    def drain(s):
        for c in s.pend: c().wait_send()


def front_kernel(len_ref, x_h, wqf_h, wof_h, wuf_h, wdf_h, *rest, C, Q):
    vins, rest = rest[:11], rest[11:]
    (wq_o, wo, wu, wd, vec_o, bup_o, xlow_o, qkv_o, ctx_ref, lse_ref, relf_ref, bkf_o,
     wqf_ref, wof_ref, wuf_ref, wdf_ref, v_ref, bk_ref, x_v, xlow, qkv, wq, own_p, got_p, h_scr, u_bf, d_bf, vall, tab, rel, qb, bias_scr, ss, rs, cs, cr, vss, vrs, ps, ls) = rest
    g = Geo(C, Q)
    S, D = x_h.shape[1:]
    q_ = lax.axis_index("query")
    peers = [{"query": lax.rem(q_ + j, Q)} for j in range(1, Q)] + [g.dev(g.z, 1 - g.y, g.x, g.k)] + [g.dev(jnp.bitwise_xor(g.z, i), g.y, g.x, g.k) for i in range(1, g.nz)]
    bar = pltpu.get_barrier_semaphore()
    for p in peers:
        pl.semaphore_signal(bar, inc=1, device_id=p, device_id_type=MESH)
    wc = [pltpu.make_async_copy(a, b, ls.at[10 + i]) for i, (a, b) in enumerate(((wqf_h, wqf_ref), (wof_h, wof_ref), (wuf_h, wuf_ref), (wdf_h, wdf_ref)))]
    for c in wc:
        c.start()
    xc = pltpu.make_async_copy(x_h, x_v, ls.at[0])
    xc.start()
    k = g.k
    dq, bq = D // Q, tab.shape[1] // Q
    fq = bup_o.shape[1] // Q
    v_ref[...] = jnp.zeros_like(v_ref)
    for i in range(8):
        v_ref[i:i + 1, 0:dq] = vins[i][...]
    for j in range(fq // 256):
        v_ref[8 + j, :] = vins[8][j * 256:(j + 1) * 256]
    v_ref[16:16 + vins[9].shape[0], 0:bq] = vins[9][...]
    nrel = vins[10].shape[1]
    bk_ref[...] = jnp.full(bk_ref.shape, -1, jnp.int32)
    bk_ref[:, 0:nrel] = vins[10][...]
    for c in wc:
        c.wait()

    def turn(w):
        n = w.shape[1]
        eye = (lax.broadcasted_iota(jnp.int32, (n, n), 0) == lax.broadcasted_iota(jnp.int32, (n, n), 1)).astype(BF)
        return dg(eye, w.astype(BF), NT).astype(BF)
    a, b = turn(wqf_ref[...]), turn(wof_ref[...])
    ha, hb = a.shape[0] // 2, b.shape[0] // 2
    for i in range(2):
        own_p[i, 0:ha, :] = a[i * ha:(i + 1) * ha]
        own_p[i, ha:ha + hb, :] = b[i * hb:(i + 1) * hb]
    d_bf[...] = wdf_ref[...].astype(BF)
    u_bf[...] = wuf_ref[...].astype(BF)
    pl.semaphore_wait(bar, len(peers))
    pc = pltpu.make_async_remote_copy(own_p.at[1 - k], got_p, ps.at[0], ps.at[1], device_id=g.dev(g.z, g.y, g.x, 1 - k), device_id_type=MESH)
    pc.start()
    vcs = []
    for j in range(1, Q):
        c = pltpu.make_async_remote_copy(v_ref, vall.at[q_], vss.at[j - 1], vrs.at[j - 1], device_id={"query": lax.rem(q_ + j, Q)}, device_id_type=MESH)
        c.start()
        vcs.append(c)
    vall[q_] = v_ref[...]

    def own(n):
        if n == "u": return u_bf
        if n == "d": return d_bf
        return h_scr.at[pl.ds(QROW.get(n, 144), RSHP[n][0])]
    A = AG(g, own, (wq, wo, wu, wd), ss, rs, cs, cr)
    loc = [pltpu.make_async_copy(own(n), A.dst(n, (0, 0, 0), k), ls.at[1 + i]) for i, n in enumerate(RPIECES)]

    def after(name):
        for e in AGSLOTS.get(name, []):
            A.ev(e)
    after("b")
    loc[0].start()
    loc[1].start()
    pc.wait()
    t, r = own_p[k], got_p[...]
    @pl.when(k == 0)
    def _(): h_scr[...] = jnp.concatenate([t, r], axis=1)
    @pl.when(k == 1)
    def _(): h_scr[...] = jnp.concatenate([r, t], axis=1)
    for c in loc[2:]:
        c.start()
    after("h")
    xc.wait()
    for m in range(2):
        xlow[m*S:(m+1)*S,:]=x_v[m].astype(BF)
    xo = pltpu.make_async_copy(xlow, xlow_o, ls.at[7])
    xo.start()
    after("p0")
    for c in vcs:
        c.wait()
    qb[...] = jnp.zeros_like(qb)
    vec_o[...] = jnp.zeros_like(vec_o)
    for q in range(Q):
        lo, hi = q * dq, (q + 1) * dq
        qb[:, lo:hi] = vall[q, 0:1, 0:dq]
        qb[:, 2 * D + lo:2 * D + hi] = vall[q, 1:2, 0:dq]
        vec_o[0:6, lo:hi] = vall[q, 2:8, 0:dq]
        for j in range(fq // 256):
            bup_o[:, q * fq + j * 256:q * fq + (j + 1) * 256] = vall[q, 8 + j:9 + j, :]
        tab[:, q * bq:(q + 1) * bq] = vall[q, 16:32, 0:bq]
    after("p1")
    for i, n in enumerate(RPIECES):
        if n in QROW:
            loc[i].wait()
            for r in A.rels(n):
                A.got_core(n, r)
    qkv_proj(wq, qb, xlow, qkv, {i: [functools.partial(A.ev, e) for e in AGSLOTS.get(f"n{i}", [])] for i in range(3 * D // 256)})
    wc = pltpu.make_async_copy(wq, wq_o, ls.at[8])
    qc = pltpu.make_async_copy(qkv, qkv_o, ls.at[9])
    wc.start()
    qc.start()
    ids = jnp.broadcast_to(bk_ref[...], (8, 2 * S)).astype(F32).astype(BF)
    for j in range(2 * S // 256):
        flip = (lax.broadcasted_iota(jnp.int32, (2 * S, 256), 0) + lax.broadcasted_iota(jnp.int32, (2 * S, 256), 1) == nrel - 1 - j * 256).astype(BF)
        bkf_o[:, j * 256:(j + 1) * 256] = dg(ids, flip, NN)[0:1].astype(jnp.int32)
    bkf_o[:, nrel:] = jnp.full((1, 2 * S - nrel), -1, jnp.int32)
    after("r0")
    rel_rows(tab, bk_ref, rel)
    rel_rows(tab, bkf_o, relf_ref)
    after("r1")
    attn_fwd(len_ref, qkv, rel, ctx_ref, lse_ref, bias_scr, S, D, {i: [functools.partial(A.ev, e) for e in AGSLOTS.get(f"t{i}", [])] for i in range(D // 64)})
    for c in (xo, wc, qc):
        c.wait()
    for i, n in enumerate(RPIECES):
        if n not in QROW:
            loc[i].wait()
            for r in A.rels(n):
                A.got_core(n, r)
    A.drain()


def ffn_kernel(lab_ref, x_ref, ctx_ref, cot_ref, wo_h, wu_h, wd_h, vec_ref, bup_ref,
               out_ref, dfs_ref, dctx_ref, nl_ref, act_ref, dl_ref, al_ref, ul_ref, gv_ref, gbu_ref, loss_ref,
               wo_ref, wu_ref, wd_ref, gp_scr, z1_scr, z2_scr, r_scr,
               ws, ds_scr, sc_snd, sc_all, sss, ssr, *, T, R, C, Q):
    i = pl.program_id(0)
    D, FF = wu_ref.shape
    cid = lax.axis_index("cand")

    loads = [pltpu.make_async_copy(a, b, ws.at[j]) for j, (a, b) in enumerate(((wo_h, wo_ref), (wu_h, wu_ref), (wd_h, wd_ref)))]

    def arrive(j):
        @pl.when(i == 0)
        def _(): loads[j].wait()

    def score_copy(j):
        return pltpu.make_async_remote_copy(sc_snd, sc_all.at[cid], sss.at[j - 1], ssr.at[j - 1], device_id={"cand": lax.rem(cid + j, C)}, device_id_type=MESH)

    @pl.when(i == 0)
    def _():
        b = pltpu.get_barrier_semaphore()
        for j in range(1, C):
            pl.semaphore_signal(b, inc=1, device_id={"cand": lax.rem(cid + j, C)}, device_id_type=MESH)
        for c in loads:
            c.start()
        gv_ref[...] = jnp.zeros_like(gv_ref)
        gbu_ref[...] = jnp.zeros_like(gbu_ref)
        ds_scr[...] = jnp.zeros_like(ds_scr)
        sc_snd[...] = jnp.zeros_like(sc_snd)

    @pl.when(i < T)
    def _():
        fwd_tile(arrive, jnp.minimum(i, 1), x_ref, ctx_ref, wo_ref, wu_ref, wd_ref, vec_ref, bup_ref, out_ref, nl_ref, act_ref, gp_scr, z1_scr, z2_scr, r_scr, R)

    @pl.when(i == 0)
    def _():
        for m in range(2):
            sc = jnp.sum(out_ref[m, 0:1, :] * vec_ref[5:6, :], axis=1, keepdims=True)
            sc_snd[m:m + 1, :] = jnp.broadcast_to(sc, (1, 128))
        sc_all[cid] = sc_snd[...]
        pl.semaphore_wait(pltpu.get_barrier_semaphore(), C - 1)
        for j in range(1, C):
            score_copy(j).start()

    @pl.when(i == T)
    def _():
        for j in range(1, C):
            score_copy(j).wait()
        total = jnp.zeros((1, 128), F32)
        own = sc_snd[...]
        for m in range(2):
            rows = [sc_all[j, m:m + 1, :] for j in range(C)]
            peak = functools.reduce(jnp.maximum, rows)
            lse = peak + jnp.log(functools.reduce(lambda a, b: a + b, [jnp.exp(r - peak) for r in rows]))
            lab = lab_ref[m]
            picked = functools.reduce(lambda a, b: a + b, [jnp.where(lab == j, r, 0.0) for j, r in enumerate(rows)])
            total = total + (lse - picked)
            ds_scr[m:m + 1, :] = (jnp.exp(own[m:m + 1, :] - lse) - jnp.where(lab == cid, 1.0, 0.0)) * (1.0 / Q)
        loss_ref[...] = jnp.broadcast_to(jnp.where(cid == 0, total * (1.0 / Q), 0.0), (8, 128))

    @pl.when((i >= 1) & (i <= T))
    def _():
        t = lax.rem(i, T)
        bwd_tile(jnp.minimum(t, 1), ds_scr, cot_ref, wo_ref, wu_ref, wd_ref, vec_ref, dfs_ref, dctx_ref, gv_ref, gbu_ref, dl_ref, ul_ref, al_ref, gp_scr, z1_scr, z2_scr, r_scr, R)


class VecSum:
    def __init__(s, C, Q, src, va, snd, rcv, qs, qr, rs, rr):
        s.C, s.Q, s.src, s.va, s.snd, s.rcv, s.qs, s.qr, s.rs, s.rr = C, Q, src, va, snd, rcv, qs, qr, rs, rr
        s.c, s.q = lax.axis_index("cand"), lax.axis_index("query")
        s.rounds = C.bit_length() - 1
    def qcopy(s, j):
        to = lax.rem(s.q + j, s.Q)
        return pltpu.make_async_remote_copy(s.src.at[to], s.va.at[s.q], s.qs.at[j - 1], s.qr.at[j - 1], device_id={"query": to}, device_id_type=MESH)
    def rcopy(s, i):
        return pltpu.make_async_remote_copy(s.snd.at[i], s.rcv.at[i], s.rs.at[i], s.rr.at[i], device_id={"cand": jnp.bitwise_xor(s.c, 1 << i)}, device_id_type=MESH)
    def start(s):
        for j in range(1, s.Q):
            s.qcopy(j).start()
        s.va[s.q] = s.src[s.q]
    def take(s, i):
        if i == 0:
            for j in range(1, s.Q):
                s.qcopy(j).wait()
            return functools.reduce(lambda a, b: a + b, [s.va[j] for j in range(s.Q)])
        s.rcopy(i - 1).wait()
        return s.snd[i - 1] + s.rcv[i - 1]
    def step(s, i):
        s.snd[i] = s.take(i)
        s.rcopy(i).start()
    def finish(s, dst):
        dst[...] = s.take(s.rounds)


def back_kernel(len_ref, nl_h, dl_h, al_h, ctx_h, act_h, ul_h, qkv_h, dctx_h, xlow_h, wq_h, dfs_h, lse_ref, relf, bkf_ref, gv_ref, gbu_ref, loss_ref,
                *rest, C, Q, fast):
    if fast:
        ig_h, p_out, u_out, d_out, ve_out, vl_out = rest[:6]
        scr = rest[6:]
    else:
        ig_h, gq_o, go_o, gu_o, gd_o, gb_o, gtab_o = rest[:7]
        scr = rest[7:]
    (nl, dl, al, ctx, ch, qkv, dctx, xlow, wq, dfs, igt, gq, go, gu, gd, drelf, bias_scr, acc_scr, gb, gtab, ls, cs_, os_) = scr[:23]
    NS, D = nl.shape
    FF = gu.shape[1]
    S = NS // 2
    NZ = FF // 768
    load = lambda i, src, dst: pltpu.make_async_copy(src, dst, ls.at[i])
    big = [load(0, nl_h, nl), load(1, dl_h, dl), load(2, al_h, al), load(3, ctx_h, ctx), load(4, qkv_h, qkv), load(5, dctx_h, dctx),
           load(6, xlow_h, xlow), load(7, wq_h, wq), load(8, dfs_h, dfs)]
    if fast:
        g = Geo(C, Q)

    def offs(d, i):
        if not fast: c = i
        elif d: c = jnp.bitwise_xor(g.x, 1 - i // 2) * 2 + jnp.bitwise_xor(g.k, 1 - lax.rem(i, 2))
        else: c = jnp.bitwise_xor(g.z, 3 - i)
        return pl.multiple_of(c * 768, 128)

    def chunk(d, i):
        return pltpu.make_async_copy((act_h if d else ul_h).at[:, pl.ds(offs(d, i), 768)], ch.at[lax.rem(i, 2)], cs_.at[lax.rem(i, 2)])
    if fast:
        peers = [{"query": lax.rem(lax.axis_index("query") + j, Q)} for j in range(1, Q)] + [{"cand": jnp.bitwise_xor(lax.axis_index("cand"), j)} for j in (1, 2, 4, 6)]
        bar = pltpu.get_barrier_semaphore()
        for p in peers:
            pl.semaphore_signal(bar, inc=1, device_id=p, device_id_type=MESH)
    for c in (big[0], chunk(0, jnp.int32(0)), big[2], big[3], chunk(0, jnp.int32(1)), big[1]):
        c.start()
    if fast:
        bufs = {n: scr[23 + 4 * i:27 + 4 * i] for i, n in enumerate(RPIECES)}
        h_scr, e_snd, e_rcv, ve, vea, ves, ver, vl, vla, vls, vlr, ss, rs, es, qs, qr, cs, cr = scr[23 + NB:]
        R = RS(g, (gq, go, gu, gd), bufs, ss, rs)
        R.outs = {n: h_scr.at[pl.ds(QROW.get(n, 144), RSHP[n][0])] for n in ("qa", "qb", "qz", "o")}
        R.outs.update(u=u_out, d=d_out)
        dq, fq, bq = D // Q, FF // Q, gtab.shape[1] // Q
        early = VecSum(C, Q, ve, vea, ves, ver, qs.at[0], qr.at[0], cs.at[0], cr.at[0])
        late = VecSum(C, Q, vl, vla, vls, vlr, qs.at[1], qr.at[1], cs.at[1], cr.at[1])
        ve[...] = jnp.zeros_like(ve)
        vl[...] = jnp.zeros_like(vl)
        for q in range(Q):
            ve[q, 0:6, 0:dq] = gv_ref[0:6, q * dq:(q + 1) * dq]
            for j in range(fq // 256):
                ve[q, 6 + j:7 + j, :] = gbu_ref[:, q * fq + j * 256:q * fq + (j + 1) * 256]
            ve[q, 9:10, 0:128] = loss_ref[0:1, :]
        vec_at = {"o": early.start, "u3": functools.partial(early.step, 0), "d1": functools.partial(early.step, 1), "d3": functools.partial(early.step, 2),
                  "i1": functools.partial(late.step, 0), "i2": functools.partial(late.step, 1), "i3": functools.partial(late.step, 2)}

    def after(name):
        if name == "v":
            late_vectors()
            late.start()
        if fast:
            for e in SLOTS.get(name, []):
                R.ev(e)
            if name in vec_at:
                vec_at[name]()
    big[0].wait()

    def table(names):
        return {i: [functools.partial(after, n) for n in t] for i, t in enumerate(names)} if fast else {}

    def up(i, _):
        chunk(0, i).wait()
        gu[:, pl.ds(offs(0, i), 768)] = dg(nl[...], ch[lax.rem(i, 2)], TN).astype(BF)
        @pl.when(i < NZ - 2)
        def _(): chunk(0, i + 2).start()
        @pl.when(i >= NZ - 2)
        def _(): chunk(1, i + 2 - NZ).start()
        @pl.when(i == 0)
        def _():
            if fast:
                pl.semaphore_wait(bar, len(peers))
            after("u0")
            big[2].wait()
            big[3].wait()
            go[...] = dg(al[...], ctx[...], TN).astype(BF)
            after("o")
        hooks(i, table([(), ("u1",), ("u2",), ("u3",)]))
        return 0
    lax.fori_loop(0, NZ, up, 0)
    big[1].wait()
    big[4].start()
    big[5].start()

    def down(i, _):
        chunk(1, i).wait()
        gd[:, pl.ds(offs(1, i), 768)] = dg(dl[...], ch[lax.rem(i, 2)], TN).astype(BF)
        @pl.when(i < NZ - 2)
        def _(): chunk(1, i + 2).start()
        @pl.when(i == 2)
        def _():
            for c in big[6:]:
                c.start()
        hooks(i, table([("d0",), ("d1",), ("d2",), ("d3",)]))
        return 0
    lax.fori_loop(0, NZ, down, 0)
    slots = {}
    if fast:
        for i in range(2 * (D // 128)):
            slots[i] = [functools.partial(R.ev, e) for e in SLOTS.get(f"t{i}", [])]
    drelf[...] = jnp.zeros_like(drelf)
    big[4].wait()
    big[5].wait()
    attn_bwd(len_ref, qkv, dctx, lse_ref, relf, drelf, bias_scr, acc_scr, S, D, slots)
    big[6].wait()

    half = 3 * D // 2
    zh = g.z // 2 if fast else 0

    def b1(n, _):
        o = pl.multiple_of(jnp.where(n < 3, 1 - zh, zh) * half + lax.rem(n, 3) * 384, 128)
        t = qkv[:, pl.ds(o, 384)]
        gq[pl.ds(o, 384), :] = dg(t, xlow[...], TN).astype(BF)
        gb[:, pl.ds(o, 384)] = jnp.sum(t.astype(F32), axis=0, keepdims=True)
        hooks(n, {i: [functools.partial(R.ev, e) for e in SLOTS.get(f"g{i}", [])] for i in range(6)} if fast else {})
        return 0
    lax.fori_loop(0, 6, b1, 0)
    big[7].wait()
    big[8].wait()
    steps = NS // 256
    outc = lambda r: pltpu.make_async_copy(igt.at[lax.rem(r, 2)], ig_h.at[pl.ds(pl.multiple_of(r * 256, 256), 256), :], os_.at[lax.rem(r, 2)])

    def late_vectors():
        nb, nn = gtab.shape[1], bkf_ref.shape[1]
        hot = (lax.broadcasted_iota(jnp.int32, (nb, nn), 0) == bkf_ref[...]).astype(F32).astype(BF)
        part, total = drelf[...], None
        for _ in range(3):
            low = part.astype(BF)
            part = part - low.astype(F32)
            term = dg(low, hot, NT)
            total = term if total is None else total + term
        gtab[...] = total
        if fast:
            for q in range(Q):
                vl[q, 0:1, 0:dq] = gb[:, q * dq:(q + 1) * dq]
                vl[q, 1:2, 0:dq] = gb[:, 2 * D + q * dq:2 * D + (q + 1) * dq]
                for h in range(HEADS):
                    vl[q, 2 + h // 4:3 + h // 4, h % 4 * bq:(h % 4 + 1) * bq] = gtab[h:h + 1, q * bq:(q + 1) * bq]

    def rows(r, _):
        o = pl.multiple_of(r * 256, 256)
        @pl.when(r >= 2)
        def _(): outc(r - 2).wait()
        igt[lax.rem(r, 2)] = dfs[pl.ds(o, 256), :] + dg(qkv[pl.ds(o, 256), :], wq[...], NN)
        outc(r).start()
        hooks(r, table([("i0", "v"), ("i1",), ("i2",), ("i3",)]))
        return 0
    lax.fori_loop(0, steps, rows, 0)
    if not fast:
        late_vectors()
    for r in range(max(0, steps - 2), steps):
        outc(jnp.int32(r)).wait()
    if fast:
        k = g.k
        lo = h_scr[:, 0:192]
        hi = h_scr[:, 192:384]
        e_snd[...] = jnp.where(k == 0, hi, lo)
        c = pltpu.make_async_remote_copy(e_snd, e_rcv, es.at[0], es.at[1], device_id=R.partner, device_id_type=MESH)
        c.start()
        p_out[k] = jnp.where(k == 0, lo, hi)
        c.wait()
        p_out[1 - k] = e_rcv[...]
        early.finish(ve_out)
        late.finish(vl_out)
        R.drain()
    else:
        gq_o[...] = gq[...]
        go_o[...] = go[...]
        gu_o[...] = gu[...]
        gd_o[...] = gd[...]
        gb_o[...] = gb[...]
        gtab_o[...] = gtab[...]


def finish_kernel(out_h, ig_h, u_h, d_h, p_h, ve_h, vl_h, out_o, ig_o, gu_o, gd_o, gq_o, go_o, *rest):
    vec_o, bup_o, tab_o, loss_o = rest[:8], rest[8], rest[9], rest[10]
    buf, ub, db, p_ref, ve_ref, vl_ref, si, so = rest[11:]
    n, rows = buf.shape[0] // 2, buf.shape[1]
    part = lambda h, i: h.at[pl.ds(i * rows, rows), :]
    small = [pltpu.make_async_copy(a, b, si.at[2 * n + i]) for i, (a, b) in enumerate(((p_h, p_ref), (ve_h, ve_ref), (vl_h, vl_ref)))]
    src = [(u_h, ub, gu_o), (d_h, db, gd_o)]
    ins = [pltpu.make_async_copy(a, b, si.at[2 * n + 3 + i]) for i, (a, b, _) in enumerate(src)]
    outs = [pltpu.make_async_copy(b, c, so.at[2 * n + i]) for i, (_, b, c) in enumerate(src)]
    for i in range(n):
        for j, (h, o) in enumerate(((out_h, out_o), (ig_h, ig_o))):
            k = 2 * i + j
            ins.append(pltpu.make_async_copy(part(h, i), buf.at[k], si.at[k]))
            outs.append(pltpu.make_async_copy(buf.at[k], part(o, i), so.at[k]))
    for c in small + ins:
        c.start()
    for c in small:
        c.wait()
    ha = gq_o.shape[1] // 2
    gq_o[...] = jnp.concatenate([p_ref[0, 0:ha, :], p_ref[1, 0:ha, :]], axis=0).T
    go_o[...] = jnp.concatenate([p_ref[0, ha:, :], p_ref[1, ha:, :]], axis=0).T
    for i in range(8):
        m = vec_o[i].shape[1]
        vec_o[i][...] = vl_ref[i:i + 1, 0:m] if i < 2 else ve_ref[i - 2:i - 1, 0:m]
    for j in range(bup_o.shape[0] // 256):
        bup_o[j * 256:(j + 1) * 256] = ve_ref[6 + j, :]
    loss_o[0] = ve_ref[9, 0]
    bq = tab_o.shape[1]
    for h in range(HEADS):
        tab_o[h:h + 1, :] = vl_ref[2 + h // 4:3 + h // 4, h % 4 * bq:(h % 4 + 1) * bq]
    for a, b in zip(ins, outs):
        a.wait()
        b.start()
    for c in outs:
        c.wait()


def sds(shape, dtype=F32):
    return jax.ShapeDtypeStruct(shape, dtype)


def back_scratch(fast, C, Q, NS=1024, S=512, D=768, FF=3072, NBK=256):
    v = pltpu.VMEM
    dma = pltpu.SemaphoreType.DMA
    scr = [v((NS, D), BF)] * 4 + [v((2, NS, 768), BF), v((NS, 3 * D), BF), v((NS, D), BF), v((NS, D), BF), v((3 * D, D), BF), v((NS, D), F32), v((2, 256, D), F32),
                                  v((3 * D, D), BF), v((D, D), BF), v((D, FF), BF), v((D, FF), BF), v((16, 2 * S), F32),
                                  v((2, S, S), F32), v((2, S, S), F32), v((1, 3 * D), F32), v((16, NBK), F32), dma((9,)), dma((2,)), dma((2,))]
    if fast:
        scr += rs_bufs() + [v((192, 384), F32), v((192, 192), F32), v((192, 192), F32), v((Q, 16, 256), F32), v((Q, 16, 256), F32), v((3, 16, 256), F32), v((3, 16, 256), F32),
                v((Q, 8, 256), F32), v((Q, 8, 256), F32), v((3, 8, 256), F32), v((3, 8, 256), F32),
                            dma((len(RPIECES), 31)), dma((len(RPIECES), 31)), dma((2,)), dma((2, Q)), dma((2, Q)), dma((2, 3)), dma((2, 3))]
    return scr


def body(hidden_in, out_cotangent, lengths, labels, buckets, w_qkv, w_out, w_up, w_down, bias_q, bias_v, bias_out,
         norm1_gain, norm1_bias, bias_up, bias_down, norm2_gain, score_vector, rel_table):
    Q = lax.axis_size("query")
    C = lax.axis_size("cand")
    micro = hidden_in.shape[0]
    S, D = hidden_in.shape[3:]
    FF = w_up.shape[1] * C
    NBK = rel_table.shape[0] * Q
    dq, fq, bq = D // Q, FF // Q, NBK // Q
    fast = Q == 4 and C == 8 and D == 768 and FF == 3072
    x = hidden_in.reshape(micro, S, D)
    cot = out_cotangent.reshape(micro, S, D)
    lens = lengths.reshape(micro)
    labs = labels.reshape(micro)
    NS = micro * S
    v = pltpu.VMEM
    dma = pltpu.SemaphoreType.DMA
    eight = [bias_q, bias_v, bias_out, norm1_gain, norm1_bias, bias_down, norm2_gain, score_vector]
    if fast:
        np_ = len(RPIECES)
        wq, wo, wu, wd, vec, bup, xlow, qkv, ctx, lse, relf, bkf = pl.pallas_call(
            functools.partial(front_kernel, C=C, Q=Q), in_specs=[SM] + [ANY] * 5 + [VM] * 11, out_specs=[ANY] * 4 + [VM] * 2 + [ANY] * 2 + [VM] * 4,
            out_shape=[sds((3 * D, D), BF), sds((D, D), BF), sds((D, FF), BF), sds((D, FF), BF), sds((8, D)), sds((1, FF)), sds((NS, D), BF), sds((NS, 3 * D), BF),
                       sds((NS, D), BF), sds((micro, 16, S)), sds((16, 2 * S)), sds((1, 2 * S), jnp.int32)],
            scratch_shapes=[v(w_qkv.shape, F32), v(w_out.shape, F32), v(w_up.shape, F32), v(w_down.shape[::-1], F32), v((32, 256), F32), v((1, 2 * S), jnp.int32),
                            v((micro, S, D), F32), v((NS, D), BF), v((NS, 3 * D), BF), v((3 * D, D), BF), v((2, 192, 192), BF), v((192, 192), BF), v((192, 384), BF),
                            v((192, 384), BF), v((96, 768), BF), v((Q, 32, 256), F32), v((16, NBK), F32), v((16, 2 * S), F32), v((1, 3 * D), F32), v((2, S, S), F32)]
            + [dma((np_, 16))] * 4 + [dma((Q,))] * 2 + [dma((2,)), dma((14,))],
            compiler_params=pltpu.CompilerParams(collective_id=0, has_side_effects=True, vmem_limit_bytes=67043328),
        )(lens, x, w_qkv, w_out, w_up, w_down.T, *[t.reshape(1, -1) for t in eight], bias_up, rel_table.T, buckets.reshape(1, -1))
    else:
        bk = jnp.pad(buckets, (0, 1), constant_values=-1)[None, :]
        bkf = jnp.pad(buckets[::-1], (0, 1), constant_values=-1)[None, :]
        def gather(w):
            part = lax.all_gather(w.astype(BF), "query", axis=0, tiled=True)
            return lax.all_gather(part, "cand", axis=1, tiled=True)
        wq, wo, wu, wd = gather(w_qkv).T, gather(w_out).T, gather(w_up), gather(w_down).T
        vall = lax.all_gather(jnp.concatenate(eight + [bias_up, rel_table.reshape(-1)]), "query", axis=0, tiled=False)
        vecs = vall[:, :8 * dq].reshape(Q, 8, dq).transpose(1, 0, 2).reshape(8, D)
        bup = vall[:, 8 * dq:8 * dq + fq].reshape(1, FF)
        tab = jnp.pad(vall[:, 8 * dq + fq:].reshape(NBK, HEADS).T, ((0, 4), (0, 0)))
        qkv_bias = jnp.concatenate([vecs[0:1], jnp.zeros((1, D), F32), vecs[1:2]], axis=1)
        vec = jnp.concatenate([vecs[2:], jnp.zeros((2, D), F32)], axis=0)
        xlow, qkv, ctx, lse, relf = pl.pallas_call(
            attn_fwd_kernel, in_specs=[SM] + [VM] * 6, out_specs=[VM] * 5,
            out_shape=[sds((NS, D), BF), sds((NS, 3 * D), BF), sds((NS, D), BF), sds((micro, 16, S)), sds((16, 2 * S))],
            scratch_shapes=[v((16, 2 * S), F32), v((2, S, S), F32)],
            compiler_params=pltpu.CompilerParams(vmem_limit_bytes=60 * 2**20))(lens, x, wq, qkv_bias, tab, bk, bkf)
    R = 256
    Rh, T = R // micro, NS // R
    tb = lambda im, n=D: pl.BlockSpec((micro, Rh, n), im)
    fw = lambda i: (0, jnp.minimum(i, T - 1), 0)
    bw = lambda i: (0, lax.rem(jnp.maximum(i, 1), T), 0)
    tok = lambda n, dt=BF: sds((micro, S, n), dt)
    out, dfs, dctx, nl, act, dl, al, ul, gv, gbu, lossv = pl.pallas_call(
        functools.partial(ffn_kernel, T=T, R=R, C=C, Q=Q), grid=(T + 1,),
        in_specs=[SM, tb(fw), tb(fw), tb(bw)] + [ANY] * 3 + [VM] * 2, out_specs=[tb(fw), tb(bw), tb(bw), tb(fw), tb(fw, FF), tb(bw), tb(bw), tb(bw, FF)] + [VM] * 3,
        out_shape=[tok(D, F32), tok(D, F32), tok(D), tok(D), tok(FF), tok(D), tok(D), tok(FF), sds((8, D)), sds((1, FF)), sds((8, 128))],
        scratch_shapes=[v((D, D), BF), v((D, FF), BF), v((D, FF), BF), pltpu.VMEM((2, R, FF), F32), pltpu.VMEM((2, R, D), F32), pltpu.VMEM((2, R, D), F32), pltpu.VMEM((2, R, 128), F32), dma((3,)),
                        pltpu.VMEM((8, 128), F32), pltpu.VMEM((8, 128), F32), pltpu.VMEM((C, 8, 128), F32), pltpu.SemaphoreType.DMA((C,)), pltpu.SemaphoreType.DMA((C,))],
        compiler_params=pltpu.CompilerParams(collective_id=1, has_side_effects=True, vmem_limit_bytes=67043328),
    )(labs, x, ctx.reshape(micro, S, D), cot, wo, wu, wd, vec, bup)
    flat = lambda t: t.reshape(NS, t.shape[-1])
    gouts = [sds((2, 192, 192)), sds((192, 384)), sds((96, 768)), sds((16, 256)), sds((8, 256))] if fast else \
        [sds((3 * D, D), BF), sds((D, D), BF), sds((D, FF), BF), sds((D, FF), BF), sds((1, 3 * D)), sds((16, NBK))]
    res = pl.pallas_call(
        functools.partial(back_kernel, C=C, Q=Q, fast=fast), in_specs=[SM] + [ANY] * 11 + [VM] * 6, out_specs=[ANY] + [VM] * len(gouts),
        out_shape=[sds((NS, D))] + gouts, scratch_shapes=back_scratch(fast, C, Q, NS, S, D, FF, NBK),
        compiler_params=pltpu.CompilerParams(collective_id=2 if fast else None, has_side_effects=True, vmem_limit_bytes=67043328),
    )(lens, flat(nl), flat(dl), flat(al), ctx, flat(act), flat(ul), qkv, flat(dctx), xlow, wq, flat(dfs), lse, relf, bkf, gv, gbu, lossv)
    ig = res[0]
    if fast:
        pg, ug, dng, ve, vl = res[1:]
        fin = pl.pallas_call(
            finish_kernel, in_specs=[ANY] * 7, out_specs=[ANY] * 4 + [VM] * 12 + [SM],
            out_shape=[sds((NS, D)), sds((NS, D)), sds(w_up.shape), sds(w_down.shape[::-1]), sds(w_qkv.shape), sds(w_out.shape)] + [sds((1, dq))] * 8
            + [sds((fq,)), sds((HEADS, bq)), sds((1,))],
            scratch_shapes=[v((8, NS // 4, D), F32), v(ug.shape, F32), v(dng.shape, F32), v(pg.shape, F32), v(ve.shape, F32), v(vl.shape, F32), dma((13,)), dma((10,))],
            compiler_params=pltpu.CompilerParams(vmem_limit_bytes=67043328))(flat(out), ig, ug, dng, pg, ve, vl)
        out, ig, g_up, g_down, g_qkv, g_out = fin[:6]
        g_down = g_down.T
        small = [t.reshape(dq) for t in fin[6:14]]
        g_bup, g_tab, loss = fin[14], fin[15].T, fin[16].reshape(())
    else:
        def scatter(g):
            rows, cols = g.shape[0] // Q, g.shape[1] // C
            tiles = g.astype(F32).reshape(Q, rows, C, cols).transpose(2, 0, 1, 3).reshape(C * Q, rows, cols)
            return lax.psum_scatter(tiles, ("cand", "query"), scatter_dimension=0, tiled=True)[0]
        gq, go, gu, gd, gb, gtab = res[1:]
        g_qkv, g_out, g_up, g_down = scatter(gq.T), scatter(go.T), scatter(gu), scatter(gd.T)
        gvecs = jnp.concatenate([gb[:, :D], gb[:, 2 * D:], gv[:6]], axis=0)
        vg = jnp.concatenate([gvecs.reshape(8, Q, dq).transpose(1, 0, 2).reshape(Q, 8 * dq), gbu.reshape(Q, fq), gtab[:HEADS].T.reshape(Q, bq * HEADS),
                              jnp.broadcast_to(lossv[0:1, 0:1], (Q, 1))], axis=1)
        vg = jnp.pad(vg, ((0, 0), (0, -vg.shape[1] % 1024)))
        vs = lax.psum_scatter(lax.psum(vg, "cand"), "query", scatter_dimension=0, tiled=True)[0]
        small = [vs[i * dq:(i + 1) * dq] for i in range(8)]
        g_bup = vs[8 * dq:8 * dq + fq]
        g_tab = vs[8 * dq + fq:8 * dq + fq + bq * HEADS].reshape(bq, HEADS)
        loss = vs[8 * dq + fq + bq * HEADS]
    return (out.reshape(hidden_in.shape), ig.reshape(hidden_in.shape), g_qkv, g_out, g_up, g_down,
            small[0], small[1], small[2], small[3], small[4], g_bup, small[5], small[6], small[7], g_tab, loss)


def solution(mesh):
    seq, w, v = P(None, "query", "cand", None, None), P("query", "cand"), P("query")
    return jax.shard_map(
        body, mesh=mesh,
        in_specs=(seq, seq, P(None, "query", "cand"), P(None, "query"), P(), w, w, w, w) + (v,) * 9 + (P("query", None),),
        out_specs=(seq, seq, w, w, w, w) + (v,) * 9 + (P("query", None), P()),
        check_vma=False)
```
